32 devices in a mesh: grp: 4 (over y, x), dp: 8 (over z, core).
Axes of the slice: x: 2, y: 2, z: 4, core: 2. Of those that a mesh axis runs over, the one named last changes fastest.
Arguments:
- inputs: bfloat16 [32768, 384], P(('grp', 'dp'))
- cotangent: bfloat16 [32768, 384], P(('grp', 'dp')), may hold values from -6 to 6
- group_interval: int32 [4], replicated, may hold values from 0 to 2, as said below
- sample_counts: int32 [4], replicated, may hold values from 100 to 999
- rollout_start: int32 [4], replicated, may hold values from 0 to 18, as said below
- lead_table: float32 [3, 384], replicated, may hold values from -5 to 5
- qkv_master: float32 [442368], P('dp'), may hold values from -0.3125 to 0.3125
- proj_master: float32 [147456], P('dp'), may hold values from -1.25 to 1.25
- up_master: float32 [589824], P('dp'), may hold values from -0.3125 to 0.3125
- down_master: float32 [589824], P('dp'), may hold values from -0.15625 to 0.15625
- ada_master: float32 [884736], P('dp'), may hold values from -0.3125 to 0.3125
- bias_master: float32 [5376], P('dp'), may hold values from -0.6 to 0.6
- qkv_first: float32 [442368], P('dp'), may hold values from -4 to 4
- proj_first: float32 [147456], P('dp'), may hold values from -4 to 4
- up_first: float32 [589824], P('dp'), may hold values from -4 to 4
- down_first: float32 [589824], P('dp'), may hold values from -4 to 4
- ada_first: float32 [884736], P('dp'), may hold values from -4 to 4
- bias_first: float32 [5376], P('dp'), may hold values from -4 to 4
- qkv_second: float32 [442368], P('dp'), may hold values from 1 to 4
- proj_second: float32 [147456], P('dp'), may hold values from 1 to 4
- up_second: float32 [589824], P('dp'), may hold values from 1 to 4
- down_second: float32 [589824], P('dp'), may hold values from 1 to 4
- ada_second: float32 [884736], P('dp'), may hold values from 1 to 4
- bias_second: float32 [5376], P('dp'), may hold values from 1 to 4
Outputs:
- block_output: float32 [32768, 384], P(('grp', 'dp'))
- input_grad: float32 [32768, 384], P(('grp', 'dp'))
- grad_norm: float32 [], replicated
- qkv_new: float32 [442368], P('dp')
- proj_new: float32 [147456], P('dp')
- up_new: float32 [589824], P('dp')
- down_new: float32 [589824], P('dp')
- ada_new: float32 [884736], P('dp')
- bias_new: float32 [5376], P('dp')
- qkv_first_new: float32 [442368], P('dp')
- proj_first_new: float32 [147456], P('dp')
- up_first_new: float32 [589824], P('dp')
- down_first_new: float32 [589824], P('dp')
- ada_first_new: float32 [884736], P('dp')
- bias_first_new: float32 [5376], P('dp')
- qkv_second_new: float32 [442368], P('dp')
- proj_second_new: float32 [147456], P('dp')
- up_second_new: float32 [589824], P('dp')
- down_second_new: float32 [589824], P('dp')
- ada_second_new: float32 [884736], P('dp')
- bias_second_new: float32 [5376], P('dp')
- qkv_copy: bfloat16 [442368], P('dp')
- proj_copy: bfloat16 [147456], P('dp')
- up_copy: bfloat16 [589824], P('dp')
- down_copy: bfloat16 [589824], P('dp')
- ada_copy: bfloat16 [884736], P('dp')
- bias_copy: bfloat16 [5376], P('dp')
The draws below stay inside these ranges and needn't reach their ends.
Inputs may be any that keep to these rules, and one draw needn't show every extreme that they name: `group_interval`: every interval 0 to 2 is used by some group. `rollout_start`: even numbers; both 0 and 18 occur.
All inputs are finite; a program needn't handle non-finite values.
Results may differ from the reference program's by a relative error of at most 0.015.
The reference program's roundings to bfloat16 on the way count: a program that leaves them out, or rounds other values in their place, can miss the bound.
Values may be sent and summed in bfloat16 or wider, within the bound.
A program may use at most 192 MiB of HBM per device.

```python
import math
import jax
import jax.numpy as jnp
from jax import lax

D = 384
HEADS = 6
FF = 1536
SEQ = 1024
ROLLOUT = 2
INTERVALS = 3
MAX_START = 18
ADAM_STEP = 10
HEAD_DIM = 64
GROUPS = 4
TOKENS = 32768
NBIAS = 5376
NPARAM = 2659584
N_DP = 8


def draw_group_interval(key, part):
    order = jax.random.permutation(jax.random.fold_in(key, 5), GROUPS)
    extra = jax.random.randint(jax.random.fold_in(key, 7), (GROUPS,), 0, INTERVALS)
    return jnp.where(order < INTERVALS, order, extra).astype(jnp.int32)


def draw_rollout_start(key, part):
    order = jax.random.permutation(jax.random.fold_in(key, 21), GROUPS)
    extra = 2 * jax.random.randint(jax.random.fold_in(key, 23), (GROUPS,), 0, MAX_START // 2 + 1)
    chosen = jnp.where(order == 0, 0, jnp.where(order == 1, MAX_START, extra))
    return chosen.astype(jnp.int32)


def draw_inputs(key, part):
    noise_key = jax.random.fold_in(key, 11)
    row_key = jax.random.fold_in(key, 12)
    column = jnp.arange(D, dtype=jnp.float32) / (D - 1)
    column_scale = 0.5 * jnp.exp(column * math.log(8.0))
    row_scale = jnp.exp(jax.random.uniform(row_key, (TOKENS, 1), minval=math.log(0.5), maxval=math.log(5.0)))
    noise = jax.random.normal(noise_key, (TOKENS, D))
    return (noise * row_scale * column_scale[None, :]).astype(jnp.bfloat16)


def plant(drawn, key, least, high):
    spot = [jax.random.randint(jax.random.fold_in(key, axis), (), 0, length) for axis, length in enumerate(drawn.shape)]
    widest = drawn.shape.index(max(drawn.shape))
    next_to = spot[:widest] + [(spot[widest] + 1) % drawn.shape[widest]] + spot[widest + 1:]
    return drawn.at[tuple(spot)].set(least).at[tuple(next_to)].set(high)


def steps_of(rng, dims, shards, low, largest):
    factor_of, own = 1.0, jax.random.fold_in(rng, 6)
    for position, parts in shards:
        heights = jnp.exp(jax.random.uniform(jax.random.fold_in(own, position), (parts,), jnp.float32, low / len(shards), largest / len(shards)))
        factor_of = factor_of * jnp.repeat(heights, dims[position] // parts).reshape([-1 if axis == position else 1 for axis in range(len(dims))])
    return factor_of


def normal_values(own_key, extent, scale, reach, cuts=(), kind=jnp.bfloat16):
    drawn = jax.random.normal(own_key, extent, jnp.float32) * scale
    if len(cuts) > 0:
        drawn = steps_of(own_key, extent, cuts, -0.22, 0.18) * drawn
    return jnp.clip(drawn, min=-reach, max=reach).astype(kind)


def setup_inputs(seed: int = 0) -> dict:
    streams_of = jax.random.split(jax.random.key(seed), 25)
    inputs = draw_inputs(jax.random.fold_in(streams_of[24], 71), 0)
    cotangent = normal_values(streams_of[1], (TOKENS, D), 1.0, 6.0, ((0, 32),))
    group_interval = draw_group_interval(jax.random.fold_in(streams_of[24], 71), 0)
    sample_counts = plant(jax.random.randint(streams_of[3], (GROUPS,), 100, 1000), jax.random.fold_in(streams_of[3], 1), 100, 999).astype(jnp.int32)
    rollout_start = draw_rollout_start(jax.random.fold_in(streams_of[24], 71), 0)
    lead_table = normal_values(streams_of[5], (INTERVALS, D), 1.0, 5.0, (), jnp.float32)
    qkv_master = normal_values(streams_of[6], (3 * D * D,), D ** -0.5, 0.3125, ((0, 8),), jnp.float32)
    proj_master = normal_values(streams_of[7], (D * D,), (D // 16) ** -0.5, 1.25, ((0, 8),), jnp.float32)
    up_master = normal_values(streams_of[8], (D * FF,), D ** -0.5, 0.3125, ((0, 8),), jnp.float32)
    down_master = normal_values(streams_of[9], (FF * D,), FF ** -0.5, 0.15625, ((0, 8),), jnp.float32)
    ada_master = normal_values(streams_of[10], (6 * D * D,), D ** -0.5, 0.3125, ((0, 8),), jnp.float32)
    bias_master = normal_values(streams_of[11], (NBIAS,), 0.1, 0.6, ((0, 8),), jnp.float32)
    qkv_first = normal_values(streams_of[12], (3 * D * D,), 1.0, 4.0, ((0, 8),), jnp.float32)
    proj_first = normal_values(streams_of[13], (D * D,), 1.0, 4.0, ((0, 8),), jnp.float32)
    up_first = normal_values(streams_of[14], (D * FF,), 1.0, 4.0, ((0, 8),), jnp.float32)
    down_first = normal_values(streams_of[15], (FF * D,), 1.0, 4.0, ((0, 8),), jnp.float32)
    ada_first = normal_values(streams_of[16], (6 * D * D,), 1.0, 4.0, ((0, 8),), jnp.float32)
    bias_first = normal_values(streams_of[17], (NBIAS,), 1.0, 4.0, ((0, 8),), jnp.float32)
    qkv_second = jnp.clip(jnp.exp(math.log(4.0) - 1.3862944 * jax.random.uniform(streams_of[18], (3 * D * D,), jnp.float32) ** steps_of(streams_of[18], (3 * D * D,), ((0, 8),), -0.2, 0.2)), 1.0, 4.0)
    proj_second = jnp.clip(jnp.exp(math.log(4.0) - 1.3862944 * jax.random.uniform(streams_of[19], (D * D,), jnp.float32) ** steps_of(streams_of[19], (D * D,), ((0, 8),), -0.2, 0.2)), 1.0, 4.0)
    up_second = jnp.clip(jnp.exp(math.log(4.0) - 1.3862944 * jax.random.uniform(streams_of[20], (D * FF,), jnp.float32) ** steps_of(streams_of[20], (D * FF,), ((0, 8),), -0.2, 0.2)), 1.0, 4.0)
    down_second = jnp.clip(jnp.exp(math.log(4.0) - 1.3862944 * jax.random.uniform(streams_of[21], (FF * D,), jnp.float32) ** steps_of(streams_of[21], (FF * D,), ((0, 8),), -0.2, 0.2)), 1.0, 4.0)
    ada_second = jnp.clip(jnp.exp(math.log(4.0) - 1.3862944 * jax.random.uniform(streams_of[22], (6 * D * D,), jnp.float32) ** steps_of(streams_of[22], (6 * D * D,), ((0, 8),), -0.2, 0.2)), 1.0, 4.0)
    bias_second = jnp.clip(jnp.exp(math.log(4.0) - 1.3862944 * jax.random.uniform(streams_of[23], (NBIAS,), jnp.float32) ** steps_of(streams_of[23], (NBIAS,), ((0, 8),), -0.2, 0.2)), 1.0, 4.0)
    return dict(inputs=inputs, cotangent=cotangent, group_interval=group_interval, sample_counts=sample_counts, rollout_start=rollout_start, lead_table=lead_table, qkv_master=qkv_master, proj_master=proj_master, up_master=up_master, down_master=down_master, ada_master=ada_master, bias_master=bias_master, qkv_first=qkv_first, proj_first=proj_first, up_first=up_first, down_first=down_first, ada_first=ada_first, bias_first=bias_first, qkv_second=qkv_second, proj_second=proj_second, up_second=up_second, down_second=down_second, ada_second=ada_second, bias_second=bias_second)


@jax.custom_vjp
def low(v):
    return lax.optimization_barrier(v.astype(jnp.bfloat16)).astype(jnp.float32)

@jax.custom_vjp
def low_back(v):
    return v

def low_keep(v):
    return (low(v), None)

def low_pass(kept, grad):
    return (grad,)

def back_keep(v):
    return (v, None)

def back_low(kept, grad):
    return (low(grad),)
low.defvjp(low_keep, low_pass)
low_back.defvjp(back_keep, back_low)
exact_prec = lax.Precision.HIGHEST
norm_eps = 1e-06
learn_rate = 0.05
adam_eps = 1e-08

def exact_dot(left, right):
    return jnp.dot(left, right, precision=exact_prec, preferred_element_type=jnp.float32)

def low_both(value):
    return low_back(low(value))

def normalize(stream):
    centred = stream - lax.optimization_barrier(jnp.mean(stream, axis=-1, keepdims=True))
    return centred * lax.rsqrt(lax.optimization_barrier(jnp.mean(centred * centred, axis=-1, keepdims=True)) + norm_eps)

def step_embedding(moment):
    half_width = D // 2
    freqs = jnp.exp(-math.log(10000.0) * jnp.arange(half_width, dtype=jnp.float32) / half_width)
    angles = moment * freqs
    return jnp.concatenate([jnp.sin(angles), jnp.cos(angles)])

def one_step(stream, condition, params):
    w_qkv, w_proj, w_up, w_down, w_ada, biases = params
    b_query = biases[0:D]
    b_value = biases[D:2 * D]
    b_proj = biases[2 * D:3 * D]
    b_up = biases[3 * D:3 * D + FF]
    b_down = biases[3 * D + FF:4 * D + FF]
    b_ada = biases[4 * D + FF:]
    modulation = exact_dot(low(jax.nn.silu(condition))[None, :], w_ada)[0] + b_ada
    shift_one, scale_one, gate_one, shift_two, scale_two, gate_two = jnp.split(modulation, 6)
    hidden_one = low(normalize(stream) * (1.0 + scale_one) + shift_one)
    zero_bias = jnp.zeros((D,), jnp.float32)
    qkv_all = low_both(exact_dot(hidden_one, w_qkv) + jnp.concatenate([b_query, zero_bias, b_value]))
    queries = qkv_all[:, :D].reshape(-1, HEADS, HEAD_DIM)
    key_rows = qkv_all[:, D:2 * D].reshape(-1, HEADS, HEAD_DIM)
    value_rows = qkv_all[:, 2 * D:].reshape(-1, HEADS, HEAD_DIM)
    scores = low_back(jnp.einsum('qhd,khd->hqk', queries, key_rows, precision=exact_prec) * HEAD_DIM ** (-0.5))
    weights_soft = jax.nn.softmax(scores, axis=-1)
    attended = low_both(jnp.einsum('hqk,khd->qhd', low(weights_soft), value_rows, precision=exact_prec).reshape(-1, D))
    branch_one = low_back(exact_dot(attended, w_proj) + b_proj)
    middle = stream + gate_one * branch_one
    hidden_two = low(normalize(middle) * (1.0 + scale_two) + shift_two)
    upward = low_back(exact_dot(hidden_two, w_up) + b_up)
    activated = low(jax.nn.gelu(upward, approximate=False))
    branch_two = low_back(exact_dot(activated, w_down) + b_down)
    return middle + gate_two * branch_two

def rollout(params, stream, conditions):
    for offset in range(ROLLOUT):
        stream = one_step(stream, conditions[offset], params)
    return stream

def reference(inputs, cotangent, group_interval, sample_counts, rollout_start, lead_table, qkv_master, proj_master, up_master, down_master, ada_master, bias_master, qkv_first, proj_first, up_first, down_first, ada_first, bias_first, qkv_second, proj_second, up_second, down_second, ada_second, bias_second):
    masters = (qkv_master, proj_master, up_master, down_master, ada_master, bias_master)
    firsts = (qkv_first, proj_first, up_first, down_first, ada_first, bias_first)
    seconds = (qkv_second, proj_second, up_second, down_second, ada_second, bias_second)
    rounded = [lax.optimization_barrier(master.astype(jnp.bfloat16)).astype(jnp.float32) for master in masters]
    params = (rounded[0].reshape(D, 3 * D), rounded[1].reshape(D, D), rounded[2].reshape(D, FF), rounded[3].reshape(FF, D), rounded[4].reshape(D, 6 * D), rounded[5])
    counts = sample_counts.astype(jnp.float32)
    shares = GROUPS * counts / jnp.sum(counts)
    cond_rows = jnp.stack([jnp.stack([lead_table[group_interval[group_pos]] + step_embedding(rollout_start[group_pos].astype(jnp.float32) + offset) for offset in range(ROLLOUT)]) for group_pos in range(GROUPS)])
    total_seqs = GROUPS * N_DP
    streams = inputs.astype(jnp.float32).reshape(total_seqs, SEQ, D)
    cot_rows = cotangent.astype(jnp.float32).reshape(total_seqs, SEQ, D)
    cond_all = jnp.repeat(cond_rows, N_DP, axis=0)
    share_all = jnp.repeat(shares, N_DP)

    def visit_one(totals, pieces):
        stream, cot_seq, cond_seq, seq_share = pieces

        def forward_seq(param_set, stream_in):
            return rollout(param_set, stream_in, cond_seq)
        result, pull_back = jax.vjp(forward_seq, params, stream)
        param_grads, stream_grad = pull_back(cot_seq)
        totals = tuple((total_part + seq_share * grad_part for total_part, grad_part in zip(totals, param_grads)))
        return (totals, (result, stream_grad))
    zero_grads = tuple((jnp.zeros_like(param) for param in params))
    totals, (results, input_grads) = lax.scan(visit_one, zero_grads, (streams, cot_rows, cond_all, share_all))
    flats = [total_part.reshape(-1) for total_part in totals]
    grad_norm = jnp.sqrt(sum((jnp.sum(piece * piece) for piece in flats)))
    limit = math.sqrt(NPARAM)
    clip_scale = limit / jnp.maximum(grad_norm, limit)
    correction = 1.0 - 0.5 ** ADAM_STEP
    decays = [0.1, 0.1, 0.1, 0.1, 0.1, 0.0]
    news = []
    first_news = []
    second_news = []
    copies = []
    for index_w in range(6):
        clipped = flats[index_w] * clip_scale
        first_new = 0.5 * firsts[index_w] + 0.5 * clipped
        second_new = 0.5 * seconds[index_w] + 0.5 * clipped * clipped
        update = first_new / correction / (jnp.sqrt(second_new / correction) + adam_eps)
        new_master = masters[index_w] - learn_rate * (update + decays[index_w] * masters[index_w])
        news.append(new_master)
        first_news.append(first_new)
        second_news.append(second_new)
        copies.append(new_master.astype(jnp.bfloat16))
    block_output = results.reshape(TOKENS, D)
    input_grad = input_grads.reshape(TOKENS, D)
    return (block_output, input_grad, grad_norm, news[0], news[1], news[2], news[3], news[4], news[5], first_news[0], first_news[1], first_news[2], first_news[3], first_news[4], first_news[5], second_news[0], second_news[1], second_news[2], second_news[3], second_news[4], second_news[5], copies[0], copies[1], copies[2], copies[3], copies[4], copies[5])
```

```python
import functools
import math

import jax
import jax.numpy as jnp
from jax import lax
from jax.experimental import pallas as pl
from jax.experimental.pallas import tpu as pltpu
from jax.sharding import PartitionSpec as P

D = 384
HEADS = 6
FF = 1536
ROLLOUT = 2
INTERVALS = 3
ADAM_STEP = 10
HEAD_DIM = 64
NPARAM = 2659584

norm_eps = 1e-06
learn_rate = 0.05
adam_eps = 1e-08

BF = jnp.bfloat16
F32 = jnp.float32
NN = (((1,), (0,)), ((), ()))
NT = (((1,), (1,)), ((), ()))
TN = (((0,), (0,)), ((), ()))

ROWS = 256
SHIFT1, SCALE1, GATE1, SHIFT2, SCALE2, GATE2 = range(6)


def dot(left, right, dims=NN):
    return lax.dot_general(left, right, dims, preferred_element_type=F32)


def layer_norm(stream):
    centred = stream - jnp.mean(stream, axis=-1, keepdims=True)
    inverse = lax.rsqrt(jnp.mean(centred * centred, axis=-1, keepdims=True) + norm_eps)
    return (centred * inverse, inverse)


def norm_back(normed, inverse, grad_out):
    mean_grad = jnp.mean(grad_out, axis=-1, keepdims=True)
    mean_prod = jnp.mean(grad_out * normed, axis=-1, keepdims=True)
    return inverse * (grad_out - mean_grad - normed * mean_prod)


def col_sum(value):
    return jnp.sum(value, axis=0, keepdims=True)


def modulated(normed, mods, scale_row, shift_row):
    return (normed * (1.0 + mods(scale_row)) + mods(shift_row)).astype(BF)


def mod_reader(mod_ref, step):
    return lambda row: mod_ref[pl.ds(8 * step + row, 1), :]


def gelu_pair(value):
    cdf = 0.5 + 0.5 * lax.erf(value * (2.0**-0.5))
    density = jnp.exp(-0.5 * value * value) * (1.0 / math.sqrt(2.0 * math.pi))
    return (value * cdf, cdf + value * density)


def first_kernel(x_ref, mod_ref, wqkv_ref, bqkv_ref, qkv_ref):
    mods = mod_reader(mod_ref, 0)
    normed, _ = layer_norm(x_ref[...].astype(F32))
    hidden = modulated(normed, mods, SCALE1, SHIFT1)
    qkv_ref[...] = (dot(hidden, wqkv_ref[...]) + bqkv_ref[...]).astype(BF)


def middle_kernel(
    x_ref, att_ref, mod_ref, wproj_ref, wup_ref, wdown_ref, wqkv_ref,
    bproj_ref, bup_ref, bdown_ref, bqkv_ref,
    a_ref, gp_ref, act_ref, f_ref, next_ref, qkv_ref,
):
    mods = mod_reader(mod_ref, 0)
    later = mod_reader(mod_ref, 1)
    branch = dot(att_ref[...], wproj_ref[...]) + bproj_ref[...]
    a_ref[...] = branch
    middle = x_ref[...].astype(F32) + mods(GATE1) * branch
    normed, _ = layer_norm(middle)
    hidden = modulated(normed, mods, SCALE2, SHIFT2)
    upward = dot(hidden, wup_ref[...]) + bup_ref[...]
    act, slope = gelu_pair(upward)
    gp_ref[...] = slope
    act = act.astype(BF)
    act_ref[...] = act
    branch = dot(act, wdown_ref[...]) + bdown_ref[...]
    f_ref[...] = branch
    stream = middle + mods(GATE2) * branch
    next_ref[...] = stream
    normed, _ = layer_norm(stream)
    hidden = modulated(normed, later, SCALE1, SHIFT1)
    qkv_ref[...] = (dot(hidden, wqkv_ref[...]) + bqkv_ref[...]).astype(BF)


def ffn_back(
    mods, grad, branch_two, act, slope, normed, inverse, hidden, branch_one, att,
    wproj_ref, wup_ref, wdown_ref, gdown_ref, gup_ref, gproj_ref, wide_ref, narrow_ref,
    dmid_ref, datt_ref,
):
    df = (mods(GATE2) * grad).astype(BF)
    narrow_ref[pl.ds(GATE2, 1), :] += col_sum(grad * branch_two)
    narrow_ref[pl.ds(7, 1), :] += col_sum(df.astype(F32))
    gdown_ref[...] += dot(act, df, TN)
    dact = dot(df, wdown_ref[...], NT)
    du = (dact * slope).astype(BF)
    wide_ref[pl.ds(0, 1), :] += col_sum(du.astype(F32))
    gup_ref[...] += dot(hidden, du, TN)
    dh = dot(du, wup_ref[...], NT)
    narrow_ref[pl.ds(SHIFT2, 1), :] += col_sum(dh)
    narrow_ref[pl.ds(SCALE2, 1), :] += col_sum(dh * normed)
    dmid = grad + norm_back(normed, inverse, dh * (1.0 + mods(SCALE2)))
    dmid_ref[...] = dmid
    da = (mods(GATE1) * dmid).astype(BF)
    narrow_ref[pl.ds(GATE1, 1), :] += col_sum(dmid * branch_one)
    narrow_ref[pl.ds(6, 1), :] += col_sum(da.astype(F32))
    gproj_ref[...] += dot(att, da, TN)
    datt_ref[...] = dot(da, wproj_ref[...], NT).astype(BF)


def turn_kernel(
    x_ref, att_ref, cot_ref, mod_ref, wproj_ref, wup_ref, wdown_ref,
    bproj_ref, bup_ref, bdown_ref,
    out_ref, dmid_ref, datt_ref, gdown_ref, gup_ref, gproj_ref, wide_ref, narrow_ref,
):
    @pl.when(pl.program_id(0) == 0)
    def _():
        for ref in (gdown_ref, gup_ref, gproj_ref, wide_ref, narrow_ref):
            ref[...] = jnp.zeros_like(ref)

    mods = mod_reader(mod_ref, 1)
    att = att_ref[...]
    branch_one = dot(att, wproj_ref[...]) + bproj_ref[...]
    middle = x_ref[...] + mods(GATE1) * branch_one
    normed, inverse = layer_norm(middle)
    hidden = modulated(normed, mods, SCALE2, SHIFT2)
    act, slope = gelu_pair(dot(hidden, wup_ref[...]) + bup_ref[...])
    act = act.astype(BF)
    branch_two = dot(act, wdown_ref[...]) + bdown_ref[...]
    out_ref[...] = middle + mods(GATE2) * branch_two
    ffn_back(
        mods, cot_ref[...].astype(F32), branch_two, act, slope, normed, inverse, hidden,
        branch_one, att, wproj_ref, wup_ref, wdown_ref, gdown_ref, gup_ref, gproj_ref,
        wide_ref, narrow_ref, dmid_ref, datt_ref,
    )


def qkv_back(mods, stream, dmid, dqkv, wqkv_ref, gqkv_ref, narrow_ref, bias_ref):
    normed, inverse = layer_norm(stream)
    hidden = modulated(normed, mods, SCALE1, SHIFT1)
    bias_ref[pl.ds(0, 1), :] += col_sum(dqkv.astype(F32))
    gqkv_ref[...] += dot(hidden, dqkv, TN)
    dh = dot(dqkv, wqkv_ref[...], NT)
    narrow_ref[pl.ds(SHIFT1, 1), :] += col_sum(dh)
    narrow_ref[pl.ds(SCALE1, 1), :] += col_sum(dh * normed)
    return dmid + norm_back(normed, inverse, dh * (1.0 + mods(SCALE1)))


def join_kernel(
    dq_ref, dk_ref, dv_ref, x1_ref, dmid1_ref, x0_ref, a_ref, gp_ref, act_ref, f_ref, att_ref,
    mod_ref, wproj_ref, wup_ref, wdown_ref, wqkv_ref, gdown_in, gup_in, gproj_in,
    dmid_ref, datt_ref, gqkv_ref, gdown_ref, gup_ref, gproj_ref, wide_ref, narrow1_ref,
    narrow_ref, bias_ref,
):
    @pl.when(pl.program_id(0) == 0)
    def _():
        for ref in (gqkv_ref, wide_ref, narrow1_ref, narrow_ref, bias_ref):
            ref[...] = jnp.zeros_like(ref)
        gdown_ref[...] = gdown_in[...]
        gup_ref[...] = gup_in[...]
        gproj_ref[...] = gproj_in[...]

    dqkv = jnp.concatenate([dq_ref[...], dk_ref[...], dv_ref[...]], axis=1)
    grad = qkv_back(
        mod_reader(mod_ref, 1), x1_ref[...], dmid1_ref[...], dqkv, wqkv_ref, gqkv_ref,
        narrow1_ref, bias_ref,
    )
    mods = mod_reader(mod_ref, 0)
    branch_one = a_ref[...]
    middle = x0_ref[...].astype(F32) + mods(GATE1) * branch_one
    normed, inverse = layer_norm(middle)
    hidden = modulated(normed, mods, SCALE2, SHIFT2)
    ffn_back(
        mods, grad, f_ref[...], act_ref[...], gp_ref[...], normed, inverse, hidden,
        branch_one, att_ref[...], wproj_ref, wup_ref, wdown_ref, gdown_ref, gup_ref, gproj_ref,
        wide_ref, narrow_ref, dmid_ref, datt_ref,
    )


def last_kernel(
    dq_ref, dk_ref, dv_ref, x_ref, dmid_ref, mod_ref, wqkv_ref, gqkv_in,
    dx_ref, gqkv_ref, narrow_ref, bias_ref,
):
    @pl.when(pl.program_id(0) == 0)
    def _():
        narrow_ref[...] = jnp.zeros_like(narrow_ref)
        bias_ref[...] = jnp.zeros_like(bias_ref)
        gqkv_ref[...] = gqkv_in[...]

    dqkv = jnp.concatenate([dq_ref[...], dk_ref[...], dv_ref[...]], axis=1)
    dx_ref[...] = qkv_back(
        mod_reader(mod_ref, 0), x_ref[...].astype(F32), dmid_ref[...], dqkv, wqkv_ref,
        gqkv_ref, narrow_ref, bias_ref,
    )


def rows_call(kernel, name, row_args, whole_args, row_outs, whole_outs):
    length = row_args[0].shape[0]
    row_spec = lambda width: pl.BlockSpec((ROWS, width), lambda i: (i, 0))
    whole_in = lambda shape: pl.BlockSpec(shape, lambda i: (0, 0), pipeline_mode=pl.Buffered(1))
    whole_out = lambda shape: pl.BlockSpec(shape, lambda i: (0, 0))
    return pl.pallas_call(
        kernel,
        grid=(length // ROWS,),
        in_specs=[row_spec(a.shape[1]) for a in row_args] + [whole_in(a.shape) for a in whole_args],
        out_specs=[row_spec(w) for w, _ in row_outs] + [whole_out(s) for s in whole_outs],
        out_shape=[jax.ShapeDtypeStruct((length, w), t) for w, t in row_outs]
        + [jax.ShapeDtypeStruct(s, F32) for s in whole_outs],
        name=name,
    )(*row_args, *whole_args)


def head_lanes(rows):
    lane = lax.broadcasted_iota(jnp.int32, (rows, 2 * HEAD_DIM), 1)
    return (lane < HEAD_DIM, lane >= HEAD_DIM)


def turned_heads(rows_f32, out_ref):
    turned = jnp.transpose(rows_f32)
    row = lax.broadcasted_iota(jnp.int32, turned.shape, 0)
    out_ref[0] = jnp.where(row < HEAD_DIM, turned, 0.0).astype(BF)
    out_ref[1] = jnp.where(row >= HEAD_DIM, turned, 0.0).astype(BF)


score_scale = HEAD_DIM**-0.5


def attend_kernel(q_ref, k_ref, v_ref, o_ref, p_ref, vt_ref):
    @pl.when(pl.program_id(1) == 0)
    def _():
        turned_heads(v_ref[...].astype(F32), vt_ref)

    queries = q_ref[...] * BF(score_scale)
    mixed = None
    for half, lanes in enumerate(head_lanes(queries.shape[0])):
        scores = dot(k_ref[...], jnp.where(lanes, queries, BF(0)), NT)
        top = jnp.max(scores, axis=0, keepdims=True)
        weights = jnp.exp(scores - top)
        total = jnp.sum(weights, axis=0, keepdims=True)
        low = (weights * (1.0 / total)).astype(BF)
        p_ref[half] = low
        part = dot(vt_ref[half], low)
        mixed = part if mixed is None else mixed + part
    o_ref[...] = jnp.transpose(mixed).astype(BF)


def attend(qkv, block):
    length = qkv.shape[0]
    pairs = HEADS // 2
    return pl.pallas_call(
        attend_kernel,
        grid=(pairs, length // block),
        in_specs=[
            pl.BlockSpec((block, 128), lambda h, i: (i, h)),
            pl.BlockSpec((length, 128), lambda h, i: (0, pairs + h)),
            pl.BlockSpec((length, 128), lambda h, i: (0, 2 * pairs + h)),
        ],
        out_specs=[
            pl.BlockSpec((block, 128), lambda h, i: (i, h)),
            pl.BlockSpec((2, length, block), lambda h, i: (h, 0, i)),
        ],
        out_shape=[
            jax.ShapeDtypeStruct((length, D), BF),
            jax.ShapeDtypeStruct((HEADS, length, length), BF),
        ],
        scratch_shapes=[pltpu.VMEM((2, 128, length), BF)],
        name="attend",
    )(qkv, qkv, qkv)


def attend_back_kernel(
    q_ref, k_ref, v_ref, do_ref, p_ref, dq_ref, dk_ref, dv_ref, kt_ref, dk_sum, dv_sum
):
    block_id = pl.program_id(1)

    @pl.when(block_id == 0)
    def _():
        turned_heads(k_ref[...].astype(F32) * score_scale, kt_ref)
        dk_sum[...] = jnp.zeros_like(dk_sum)
        dv_sum[...] = jnp.zeros_like(dv_sum)

    queries = q_ref[...] * BF(score_scale)
    grads = do_ref[...]
    dq_turned = None
    for half, lanes in enumerate(head_lanes(queries.shape[0])):
        grad = jnp.where(lanes, grads, BF(0))
        query = jnp.where(lanes, queries, BF(0))
        low = p_ref[half]
        weight_grad = dot(v_ref[...], grad, NT)
        weights = low.astype(F32)
        delta = jnp.sum(weights * weight_grad, axis=0, keepdims=True)
        score_grad = (weights * (weight_grad - delta)).astype(BF)
        dk_sum[...] += dot(score_grad, query)
        dv_sum[...] += dot(low, grad)
        part = dot(kt_ref[half], score_grad)
        dq_turned = part if dq_turned is None else dq_turned + part
    dq_ref[...] = jnp.transpose(dq_turned).astype(BF)

    @pl.when(block_id == pl.num_programs(1) - 1)
    def _():
        dk_ref[...] = dk_sum[...].astype(BF)
        dv_ref[...] = dv_sum[...].astype(BF)


def attend_back(qkv, grads, weights, block):
    length = qkv.shape[0]
    pairs = HEADS // 2
    return pl.pallas_call(
        attend_back_kernel,
        grid=(pairs, length // block),
        in_specs=[
            pl.BlockSpec((block, 128), lambda h, i: (i, h)),
            pl.BlockSpec((length, 128), lambda h, i: (0, pairs + h)),
            pl.BlockSpec((length, 128), lambda h, i: (0, 2 * pairs + h)),
            pl.BlockSpec((block, 128), lambda h, i: (i, h)),
            pl.BlockSpec((2, length, block), lambda h, i: (h, 0, i)),
        ],
        out_specs=[
            pl.BlockSpec((block, 128), lambda h, i: (i, h)),
            pl.BlockSpec((length, 128), lambda h, i: (0, h)),
            pl.BlockSpec((length, 128), lambda h, i: (0, h)),
        ],
        out_shape=[jax.ShapeDtypeStruct((length, D), BF)] * 3,
        scratch_shapes=[
            pltpu.VMEM((2, 128, length), BF),
            pltpu.VMEM((length, 128), F32),
            pltpu.VMEM((length, 128), F32),
        ],
        name="attend_back",
    )(qkv, qkv, qkv, grads, weights)


def step_embedding(moment):
    half_width = D // 2
    freqs = jnp.exp(-math.log(10000.0) * jnp.arange(half_width, dtype=F32) / half_width)
    angles = moment[:, None] * freqs[None, :]
    return jnp.concatenate([jnp.sin(angles), jnp.cos(angles)], axis=1)


def all_conditions(group_interval, rollout_start, lead_table):
    chosen = group_interval[:, None] == jnp.arange(INTERVALS)[None, :]
    lead_rows = jnp.sum(jnp.where(chosen[:, :, None], lead_table[None], 0.0), axis=1)
    start = rollout_start.astype(F32)
    rows = [lead_rows + step_embedding(start + offset) for offset in range(ROLLOUT)]
    return jax.nn.silu(jnp.stack(rows, axis=1)).astype(BF)


def block_pass(inputs, cotangent, mods, matrices, biases):
    w_qkv, w_proj, w_up, w_down = matrices
    b_qkv, b_proj, b_up, b_down = biases
    block = inputs.shape[0]
    (qkv0,) = rows_call(
        first_kernel, "first", [inputs], [mods, w_qkv, b_qkv], [(3 * D, BF)], []
    )
    att0, p0 = attend(qkv0, block)
    a0, gp0, act0, f0, x1, qkv1 = rows_call(
        middle_kernel, "middle", [inputs, att0],
        [mods, w_proj, w_up, w_down, w_qkv, b_proj, b_up, b_down, b_qkv],
        [(D, F32), (FF, F32), (FF, BF), (D, F32), (D, F32), (3 * D, BF)], [],
    )
    att1, p1 = attend(qkv1, block)
    result, dmid1, datt1, gdown, gup, gproj, wide1, narrow1 = rows_call(
        turn_kernel, "turn", [x1, att1, cotangent],
        [mods, w_proj, w_up, w_down, b_proj, b_up, b_down],
        [(D, F32), (D, F32), (D, BF)],
        [(FF, D), (D, FF), (D, D), (8, FF), (8, D)],
    )
    dq, dk, dv = attend_back(qkv1, datt1, p1, block)
    dmid0, datt0, gqkv, gdown, gup, gproj, wide0, narrow1b, narrow0, bias1 = rows_call(
        join_kernel, "join",
        [dq, dk, dv, x1, dmid1, inputs, a0, gp0, act0, f0, att0],
        [mods, w_proj, w_up, w_down, w_qkv, gdown, gup, gproj],
        [(D, F32), (D, BF)],
        [(D, 3 * D), (FF, D), (D, FF), (D, D), (8, FF), (8, D), (8, D), (8, 3 * D)],
    )
    dq, dk, dv = attend_back(qkv0, datt0, p0, block)
    input_grad, gqkv, narrow0b, bias0 = rows_call(
        last_kernel, "last", [dq, dk, dv, inputs, dmid0], [mods, w_qkv, gqkv],
        [(D, F32)], [(D, 3 * D), (8, D), (8, 3 * D)],
    )
    narrow = jnp.stack([narrow0 + narrow0b, narrow1 + narrow1b])
    both = narrow[0] + narrow[1]
    qkv_bias = bias0[0] + bias1[0]
    branch_bias = jnp.concatenate(
        [qkv_bias[:D], qkv_bias[2 * D :], both[6], wide0[0] + wide1[0], both[7]]
    )
    dmod = narrow[:, :6].reshape(ROLLOUT, 6 * D)
    return (result, input_grad, (gqkv, gproj, gup, gdown), branch_bias, dmod)


def per_device(
    inputs,
    cotangent,
    group_interval,
    sample_counts,
    rollout_start,
    lead_table,
    *state,
):
    masters, firsts, seconds = (state[0:6], state[6:12], state[12:18])
    low = [master.astype(BF) for master in masters]
    group_index = lax.axis_index("grp")
    owner = lax.axis_index("dp")
    owners = lax.axis_size("dp")
    groups = lax.axis_size("grp")
    own_rows = D // owners
    counts = sample_counts.astype(F32)
    share = lax.dynamic_index_in_dim(groups * counts / jnp.sum(counts), group_index, keepdims=False)
    conditions = all_conditions(group_interval, rollout_start, lead_table)
    owner_columns = lax.dynamic_slice_in_dim(conditions, owner * own_rows, own_rows, axis=2)
    own_condition = lax.dynamic_index_in_dim(owner_columns, group_index, keepdims=False)

    part = dot(own_condition, low[4].reshape(own_rows, 6 * D))
    modulation = lax.psum(part, "dp")
    gathered = [lax.all_gather(low[index], "dp", axis=0, tiled=True) for index in (0, 1, 2, 3, 5)]
    matrices = (
        gathered[0].reshape(D, 3 * D),
        gathered[1].reshape(D, D),
        gathered[2].reshape(D, FF),
        gathered[3].reshape(FF, D),
    )
    bias = gathered[4].astype(F32)
    modulation = modulation + bias[4 * D + FF :][None]
    mods = jnp.pad(modulation.reshape(ROLLOUT, 6, D), ((0, 0), (0, 2), (0, 0))).reshape(-1, D)
    b_qkv = jnp.concatenate([bias[:D], jnp.zeros((D,), F32), bias[D : 2 * D]])
    biases = (
        b_qkv[None],
        bias[2 * D : 3 * D][None],
        bias[3 * D : 3 * D + FF][None],
        bias[3 * D + FF : 4 * D + FF][None],
    )
    result, input_grad, grads, branch_bias, dmod = block_pass(
        inputs, cotangent, mods, matrices, biases
    )

    dmod = lax.psum(dmod * share, "dp")
    dmod_all = lax.all_gather(dmod, "grp")
    vectors = jnp.concatenate([branch_bias * share, jnp.zeros((6 * D,), F32)])
    bias_sum = lax.psum(vectors, ("grp", "dp"))
    bias_sum = bias_sum + jnp.pad(jnp.sum(dmod_all, axis=(0, 1)), (4 * D + FF, 0))
    bias_grad = lax.dynamic_slice_in_dim(bias_sum, owner * masters[5].shape[0], masters[5].shape[0])
    ada_grad = jnp.einsum(
        "gsr,gsc->rc", owner_columns.astype(F32), dmod_all, precision=lax.Precision.HIGHEST
    )
    shares = []
    for grad in grads:
        summed = lax.psum((grad * share).astype(BF).reshape(-1), "grp").astype(F32)
        shares.append(lax.psum_scatter(summed, "dp", scatter_dimension=0, tiled=True))
    shares = shares + [ada_grad.reshape(-1), bias_grad]

    local_square = sum((jnp.sum(piece * piece) for piece in shares))
    grad_norm = jnp.sqrt(lax.psum(local_square, "dp"))
    limit = math.sqrt(NPARAM)
    clip_scale = limit / jnp.maximum(grad_norm, limit)
    correction = 1.0 - 0.5**ADAM_STEP
    decays = [0.1, 0.1, 0.1, 0.1, 0.1, 0.0]
    news = []
    first_news = []
    second_news = []
    copies = []
    for index_w in range(6):
        clipped = shares[index_w] * clip_scale
        first_new = 0.5 * firsts[index_w] + 0.5 * clipped
        second_new = 0.5 * seconds[index_w] + 0.5 * clipped * clipped
        update = first_new / correction / (jnp.sqrt(second_new / correction) + adam_eps)
        new_master = masters[index_w] - learn_rate * (update + decays[index_w] * masters[index_w])
        news.append(new_master)
        first_news.append(first_new)
        second_news.append(second_new)
        copies.append(new_master.astype(BF))
    return (result, input_grad, grad_norm, *news, *first_news, *second_news, *copies)


def solution(mesh):
    rows = P(("grp", "dp"), None)
    return jax.shard_map(
        per_device,
        mesh=mesh,
        in_specs=(rows, rows, P(), P(), P(), P(), *[P("dp")] * 18),
        out_specs=(rows, rows, P(), *[P("dp")] * 24),
        check_vma=False,
    )
```

```python
import functools
import math

import jax
import jax.numpy as jnp
from jax import lax
from jax.experimental import pallas as pl
from jax.experimental.pallas import tpu as pltpu
from jax.sharding import PartitionSpec as P

D = 384
HEADS = 6
FF = 1536
ROLLOUT = 2
INTERVALS = 3
ADAM_STEP = 10
HEAD_DIM = 64
NPARAM = 2659584

norm_eps = 1e-06
learn_rate = 0.05
adam_eps = 1e-08

BF = jnp.bfloat16
F32 = jnp.float32
NN = (((1,), (0,)), ((), ()))
NT = (((1,), (1,)), ((), ()))
TN = (((0,), (0,)), ((), ()))

ROWS = 256
SLAB = 48
PART = 384
ROW_SHARE = 6
ROW_BQKV, ROW_BPROJ, ROW_BUP, ROW_BDOWN = 16, 19, 20, 24
SHIFT1, SCALE1, GATE1, SHIFT2, SCALE2, GATE2 = range(6)


def dot(left, right, dims=NN):
    return lax.dot_general(left, right, dims, preferred_element_type=F32)


def layer_norm(stream):
    centred = stream - jnp.mean(stream, axis=-1, keepdims=True)
    inverse = lax.rsqrt(jnp.mean(centred * centred, axis=-1, keepdims=True) + norm_eps)
    return (centred * inverse, inverse)


def norm_back(normed, inverse, grad_out):
    mean_grad = jnp.mean(grad_out, axis=-1, keepdims=True)
    mean_prod = jnp.mean(grad_out * normed, axis=-1, keepdims=True)
    return inverse * (grad_out - mean_grad - normed * mean_prod)


def col_sum(value):
    return jnp.sum(value, axis=0, keepdims=True)


def modulated(normed, mods, scale_row, shift_row):
    return (normed * (1.0 + mods(scale_row)) + mods(shift_row)).astype(BF)


def mod_reader(mod_ref, step):
    return lambda row: mod_ref[pl.ds(8 * step + row, 1), :]


def gelu_pair(value):
    cdf = 0.5 + 0.5 * lax.erf(value * (2.0**-0.5))
    density = jnp.exp(-0.5 * value * value) * (1.0 / math.sqrt(2.0 * math.pi))
    return (value * cdf, cdf + value * density)


def side_by_side(ref, first, count):
    return jnp.concatenate([ref[row : row + 1, :] for row in range(first, first + count)], axis=1)


def first_kernel(x_ref, rows_ref, wa_ref, qkv_ref):
    mods = mod_reader(rows_ref, 0)
    normed, _ = layer_norm(x_ref[...].astype(F32))
    hidden = modulated(normed, mods, SCALE1, SHIFT1)
    qkv = dot(hidden, wa_ref[:, : 3 * D]) + side_by_side(rows_ref, ROW_BQKV, 3)
    qkv_ref[...] = qkv.astype(BF)


def middle_kernel(
    x_ref, att_ref, rows_ref, wa_ref, wup_ref, wdown_ref,
    a_ref, gp_ref, act_ref, f_ref, next_ref, qkv_ref,
):
    mods = mod_reader(rows_ref, 0)
    later = mod_reader(rows_ref, 1)
    branch = dot(att_ref[...], wa_ref[:, 3 * D :]) + mods(ROW_BPROJ)
    a_ref[...] = branch
    middle = x_ref[...].astype(F32) + mods(GATE1) * branch
    normed, _ = layer_norm(middle)
    hidden = modulated(normed, mods, SCALE2, SHIFT2)
    upward = dot(hidden, wup_ref[...]) + side_by_side(rows_ref, ROW_BUP, 4)
    act, slope = gelu_pair(upward)
    gp_ref[...] = slope
    act = act.astype(BF)
    act_ref[...] = act
    branch = dot(act, wdown_ref[...]) + mods(ROW_BDOWN)
    f_ref[...] = branch
    stream = middle + mods(GATE2) * branch
    next_ref[...] = stream
    normed, _ = layer_norm(stream)
    hidden = modulated(normed, later, SCALE1, SHIFT1)
    qkv = dot(hidden, wa_ref[:, : 3 * D]) + side_by_side(rows_ref, ROW_BQKV, 3)
    qkv_ref[...] = qkv.astype(BF)


def ffn_back(
    mods, grad, branch_two, act, slope, normed, inverse, hidden, branch_one, att,
    wa_ref, wup_ref, wdown_ref, gdown_ref, gup_ref, gproj_ref, wide_ref, narrow_ref,
    dmid_ref, datt_ref,
):
    df = (mods(GATE2) * grad).astype(BF)
    narrow_ref[pl.ds(GATE2, 1), :] += col_sum(grad * branch_two)
    narrow_ref[pl.ds(7, 1), :] += col_sum(df.astype(F32))
    gdown_ref[...] += dot(act, df, TN)
    dact = dot(df, wdown_ref[...], NT)
    du = (dact * slope).astype(BF)
    wide_ref[pl.ds(0, 1), :] += col_sum(du.astype(F32))
    gup_ref[...] += dot(hidden, du, TN)
    dh = dot(du, wup_ref[...], NT)
    narrow_ref[pl.ds(SHIFT2, 1), :] += col_sum(dh)
    narrow_ref[pl.ds(SCALE2, 1), :] += col_sum(dh * normed)
    dmid = grad + norm_back(normed, inverse, dh * (1.0 + mods(SCALE2)))
    dmid_ref[...] = dmid
    da = (mods(GATE1) * dmid).astype(BF)
    narrow_ref[pl.ds(GATE1, 1), :] += col_sum(dmid * branch_one)
    narrow_ref[pl.ds(6, 1), :] += col_sum(da.astype(F32))
    gproj_ref[...] += dot(att, da, TN)
    datt_ref[...] = dot(da, wa_ref[:, 3 * D :], NT).astype(BF)


def turn_kernel(
    x_ref, att_ref, cot_ref, rows_ref, wa_ref, wup_ref, wdown_ref,
    out_ref, dmid_ref, datt_ref, gdown_ref, gup_ref, gproj_ref, wide_ref, narrow_ref,
):
    @pl.when(pl.program_id(0) == 0)
    def _():
        for ref in (gdown_ref, gup_ref, gproj_ref, wide_ref, narrow_ref):
            ref[...] = jnp.zeros_like(ref)

    mods = mod_reader(rows_ref, 1)
    shared = mod_reader(rows_ref, 0)
    att = att_ref[...]
    branch_one = dot(att, wa_ref[:, 3 * D :]) + shared(ROW_BPROJ)
    middle = x_ref[...] + mods(GATE1) * branch_one
    normed, inverse = layer_norm(middle)
    hidden = modulated(normed, mods, SCALE2, SHIFT2)
    upward = dot(hidden, wup_ref[...]) + side_by_side(rows_ref, ROW_BUP, 4)
    act, slope = gelu_pair(upward)
    act = act.astype(BF)
    branch_two = dot(act, wdown_ref[...]) + shared(ROW_BDOWN)
    out_ref[...] = middle + mods(GATE2) * branch_two
    ffn_back(
        mods, cot_ref[...].astype(F32), branch_two, act, slope, normed, inverse, hidden,
        branch_one, att, wa_ref, wup_ref, wdown_ref, gdown_ref, gup_ref, gproj_ref,
        wide_ref, narrow_ref, dmid_ref, datt_ref,
    )


def qkv_back(mods, stream, dmid, dqkv, wa_ref, gqkv_ref, narrow_ref, bias_ref):
    normed, inverse = layer_norm(stream)
    hidden = modulated(normed, mods, SCALE1, SHIFT1)
    bias_ref[pl.ds(0, 1), :] += col_sum(dqkv.astype(F32))
    gqkv_ref[...] += dot(hidden, dqkv, TN)
    dh = dot(dqkv, wa_ref[:, : 3 * D], NT)
    narrow_ref[pl.ds(SHIFT1, 1), :] += col_sum(dh)
    narrow_ref[pl.ds(SCALE1, 1), :] += col_sum(dh * normed)
    return dmid + norm_back(normed, inverse, dh * (1.0 + mods(SCALE1)))


def join_kernel(
    dq_ref, dk_ref, dv_ref, x1_ref, dmid1_ref, x0_ref, a_ref, gp_ref, act_ref, f_ref, att_ref,
    rows_ref, wa_ref, wup_ref, wdown_ref, gproj_in, gdown_in, gup_in,
    dmid_ref, datt_ref, gqkv_ref, gproj_ref, wide_ref, narrow1_ref, narrow_ref, bias_ref,
    up_blocks, down_blocks,
    gdown_sum, gup_sum, gdown_before, gup_before, sems,
):
    before = [
        pltpu.make_async_copy(gdown_in, gdown_before, sems.at[0]),
        pltpu.make_async_copy(gup_in, gup_before, sems.at[1]),
    ]

    @pl.when(pl.program_id(0) == 0)
    def _():
        for copy in before:
            copy.start()
        for ref in (gqkv_ref, wide_ref, narrow1_ref, narrow_ref, bias_ref, gdown_sum, gup_sum):
            ref[...] = jnp.zeros_like(ref)
        gproj_ref[...] = gproj_in[...]

    dqkv = jnp.concatenate([dq_ref[...], dk_ref[...], dv_ref[...]], axis=1)
    grad = qkv_back(
        mod_reader(rows_ref, 1), x1_ref[...], dmid1_ref[...], dqkv, wa_ref, gqkv_ref,
        narrow1_ref, bias_ref,
    )
    mods = mod_reader(rows_ref, 0)
    branch_one = a_ref[...]
    middle = x0_ref[...].astype(F32) + mods(GATE1) * branch_one
    normed, inverse = layer_norm(middle)
    hidden = modulated(normed, mods, SCALE2, SHIFT2)
    ffn_back(
        mods, grad, f_ref[...], act_ref[...], gp_ref[...], normed, inverse, hidden,
        branch_one, att_ref[...], wa_ref, wup_ref, wdown_ref, gdown_sum, gup_sum, gproj_ref,
        wide_ref, narrow_ref, dmid_ref, datt_ref,
    )

    @pl.when(pl.program_id(0) == pl.num_programs(0) - 1)
    def _():
        for copy in before:
            copy.wait()
        share = rows_ref[ROW_SHARE : ROW_SHARE + 1, :]
        for d in range(8):
            for g in range(4):
                rows, columns = (slice(SLAB * d, SLAB * (d + 1)), slice(PART * g, PART * (g + 1)))
                up_blocks[d, g] = ((gup_sum[rows, columns] + gup_before[rows, columns]) * share).astype(BF)
                first = SLAB * (4 * d + g)
                rows = slice(first, first + SLAB)
                down_blocks[d, g] = ((gdown_sum[rows, :] + gdown_before[rows, :]) * share).astype(BF)


def last_kernel(
    dq_ref, dk_ref, dv_ref, x_ref, dmid_ref, rows_ref, wa_ref, gqkv_in, gproj_in,
    wide1, narrow1, wide0, narrow1b, narrow0, bias1,
    dx_ref, vec_ref, qkv_blocks, gqkv_ref, narrow_ref, bias_ref,
):
    @pl.when(pl.program_id(0) == 0)
    def _():
        narrow_ref[...] = jnp.zeros_like(narrow_ref)
        bias_ref[...] = jnp.zeros_like(bias_ref)
        gqkv_ref[...] = gqkv_in[...]

    dqkv = jnp.concatenate([dq_ref[...], dk_ref[...], dv_ref[...]], axis=1)
    dx_ref[...] = qkv_back(
        mod_reader(rows_ref, 0), x_ref[...].astype(F32), dmid_ref[...], dqkv, wa_ref,
        gqkv_ref, narrow_ref, bias_ref,
    )

    @pl.when(pl.program_id(0) == pl.num_programs(0) - 1)
    def _():
        share = rows_ref[ROW_SHARE : ROW_SHARE + 1, :]
        for d in range(8):
            rows = slice(SLAB * d, SLAB * (d + 1))
            for g in range(3):
                qkv_blocks[d, g] = (gqkv_ref[rows, PART * g : PART * (g + 1)] * share).astype(BF)
            qkv_blocks[d, 3] = (gproj_in[rows, :] * share).astype(BF)

        def put(first, value):
            for j in range(value.shape[1] // 128):
                vec_ref[first + j : first + j + 1, :] = value[:, 128 * j : 128 * j + 128] * share[:, 0:128]

        qkv_bias = bias_ref[0:1, :] + bias1[0:1, :]
        put(0, qkv_bias[:, :D])
        put(3, qkv_bias[:, 2 * D :])
        put(6, narrow0[6:7, :] + narrow1[6:7, :])
        put(9, wide0[0:1, :] + wide1[0:1, :])
        put(21, narrow0[7:8, :] + narrow1[7:8, :])
        for r in range(6):
            put(24 + 3 * r, narrow0[r : r + 1, :] + narrow_ref[r : r + 1, :])
            put(42 + 3 * r, narrow1[r : r + 1, :] + narrow1b[r : r + 1, :])
        vec_ref[60:64, :] = jnp.zeros((4, 128), F32)


def rows_call(kernel, name, row_args, whole_args, row_outs, whole_outs, far_args=(), scratch=()):
    length = row_args[0].shape[0]
    row_spec = lambda width: pl.BlockSpec((ROWS, width), lambda i: (i, 0))
    fixed = lambda shape: (lambda i: (0,) * len(shape))
    whole_in = lambda shape: pl.BlockSpec(shape, fixed(shape), pipeline_mode=pl.Buffered(1))
    whole_out = lambda shape: pl.BlockSpec(shape, fixed(shape))
    return pl.pallas_call(
        kernel,
        grid=(length // ROWS,),
        in_specs=[row_spec(a.shape[1]) for a in row_args]
        + [whole_in(a.shape) for a in whole_args]
        + [pl.BlockSpec(memory_space=pl.ANY) for _ in far_args],
        out_specs=[row_spec(w) for w, _ in row_outs] + [whole_out(s) for s, _ in whole_outs],
        out_shape=[jax.ShapeDtypeStruct((length, w), t) for w, t in row_outs]
        + [jax.ShapeDtypeStruct(s, t) for s, t in whole_outs],
        scratch_shapes=list(scratch),
        name=name,
    )(*row_args, *whole_args, *far_args)


def head_lanes(rows):
    lane = lax.broadcasted_iota(jnp.int32, (rows, 2 * HEAD_DIM), 1)
    return (lane < HEAD_DIM, lane >= HEAD_DIM)


def turned_heads(rows_f32, out_ref):
    turned = jnp.transpose(rows_f32)
    row = lax.broadcasted_iota(jnp.int32, turned.shape, 0)
    out_ref[0] = jnp.where(row < HEAD_DIM, turned, 0.0).astype(BF)
    out_ref[1] = jnp.where(row >= HEAD_DIM, turned, 0.0).astype(BF)


score_scale = HEAD_DIM**-0.5


def attend_kernel(q_ref, k_ref, v_ref, o_ref, p_ref, vt_ref):
    @pl.when(pl.program_id(1) == 0)
    def _():
        turned_heads(v_ref[...].astype(F32), vt_ref)

    queries = q_ref[...] * BF(score_scale)
    mixed = None
    for half, lanes in enumerate(head_lanes(queries.shape[0])):
        scores = dot(k_ref[...], jnp.where(lanes, queries, BF(0)), NT)
        top = jnp.max(scores, axis=0, keepdims=True)
        weights = jnp.exp(scores - top)
        total = jnp.sum(weights, axis=0, keepdims=True)
        low = (weights * (1.0 / total)).astype(BF)
        p_ref[half] = low
        part = dot(vt_ref[half], low)
        mixed = part if mixed is None else mixed + part
    o_ref[...] = jnp.transpose(mixed).astype(BF)


def attend(qkv, block):
    length = qkv.shape[0]
    pairs = HEADS // 2
    return pl.pallas_call(
        attend_kernel,
        grid=(pairs, length // block),
        in_specs=[
            pl.BlockSpec((block, 128), lambda h, i: (i, h)),
            pl.BlockSpec((length, 128), lambda h, i: (0, pairs + h)),
            pl.BlockSpec((length, 128), lambda h, i: (0, 2 * pairs + h)),
        ],
        out_specs=[
            pl.BlockSpec((block, 128), lambda h, i: (i, h)),
            pl.BlockSpec((2, length, block), lambda h, i: (h, 0, i)),
        ],
        out_shape=[
            jax.ShapeDtypeStruct((length, D), BF),
            jax.ShapeDtypeStruct((HEADS, length, length), BF),
        ],
        scratch_shapes=[pltpu.VMEM((2, 128, length), BF)],
        name="attend",
    )(qkv, qkv, qkv)


def attend_back_kernel(
    q_ref, k_ref, v_ref, do_ref, p_ref, dq_ref, dk_ref, dv_ref, kt_ref, dk_sum, dv_sum
):
    block_id = pl.program_id(1)

    @pl.when(block_id == 0)
    def _():
        turned_heads(k_ref[...].astype(F32) * score_scale, kt_ref)
        dk_sum[...] = jnp.zeros_like(dk_sum)
        dv_sum[...] = jnp.zeros_like(dv_sum)

    queries = q_ref[...] * BF(score_scale)
    grads = do_ref[...]
    dq_turned = None
    for half, lanes in enumerate(head_lanes(queries.shape[0])):
        grad = jnp.where(lanes, grads, BF(0))
        query = jnp.where(lanes, queries, BF(0))
        low = p_ref[half]
        weight_grad = dot(v_ref[...], grad, NT)
        weights = low.astype(F32)
        delta = jnp.sum(weights * weight_grad, axis=0, keepdims=True)
        score_grad = (weights * (weight_grad - delta)).astype(BF)
        dk_sum[...] += dot(score_grad, query)
        dv_sum[...] += dot(low, grad)
        part = dot(kt_ref[half], score_grad)
        dq_turned = part if dq_turned is None else dq_turned + part
    dq_ref[...] = jnp.transpose(dq_turned).astype(BF)

    @pl.when(block_id == pl.num_programs(1) - 1)
    def _():
        dk_ref[...] = dk_sum[...].astype(BF)
        dv_ref[...] = dv_sum[...].astype(BF)


def attend_back(qkv, grads, weights, block):
    length = qkv.shape[0]
    pairs = HEADS // 2
    return pl.pallas_call(
        attend_back_kernel,
        grid=(pairs, length // block),
        in_specs=[
            pl.BlockSpec((block, 128), lambda h, i: (i, h)),
            pl.BlockSpec((length, 128), lambda h, i: (0, pairs + h)),
            pl.BlockSpec((length, 128), lambda h, i: (0, 2 * pairs + h)),
            pl.BlockSpec((block, 128), lambda h, i: (i, h)),
            pl.BlockSpec((2, length, block), lambda h, i: (h, 0, i)),
        ],
        out_specs=[
            pl.BlockSpec((block, 128), lambda h, i: (i, h)),
            pl.BlockSpec((length, 128), lambda h, i: (0, h)),
            pl.BlockSpec((length, 128), lambda h, i: (0, h)),
        ],
        out_shape=[jax.ShapeDtypeStruct((length, D), BF)] * 3,
        scratch_shapes=[
            pltpu.VMEM((2, 128, length), BF),
            pltpu.VMEM((length, 128), F32),
            pltpu.VMEM((length, 128), F32),
        ],
        name="attend_back",
    )(qkv, qkv, qkv, grads, weights)


MESH_ID = pl.DeviceIdType.MESH
GROUPS = 4
LAYERS = 4
UNITS = 3


class Place:
    def __init__(self):
        self.grp = lax.axis_index("grp")
        self.dp = lax.axis_index("dp")
        self.z = self.dp // 2
        self.core = self.dp % 2

    def sibling(self):
        return (self.grp, 2 * self.z + 1 - self.core)

    def along_grp(self, step):
        return (lax.rem(self.grp + step, GROUPS), self.dp)

    def along_z(self, step):
        return (self.grp, 2 * lax.rem(self.z + step, LAYERS) + self.core)

    def across(self, step):
        return (self.grp, 2 * lax.rem(self.z + step, LAYERS) + 1 - self.core)


def greet(peers):
    barrier = pltpu.get_barrier_semaphore()
    for peer in peers:
        pl.semaphore_signal(barrier, inc=1, device_id=peer, device_id_type=MESH_ID)
    return lambda: pl.semaphore_wait(barrier, len(peers))


def send(src, dst, send_sem, recv_sem, peer):
    copy = pltpu.make_async_remote_copy(
        src_ref=src, dst_ref=dst, send_sem=send_sem, recv_sem=recv_sem,
        device_id=peer, device_id_type=MESH_ID,
    )
    copy.start()
    return copy


def condition_rows(moments, intervals, lead_ref):
    shape = (8, D)
    row = lax.broadcasted_iota(jnp.int32, shape, 0)
    lane = lax.broadcasted_iota(jnp.int32, shape, 1)
    moment = jnp.zeros(shape, F32)
    chosen = jnp.zeros(shape, jnp.int32)
    for index, (value, interval) in enumerate(zip(moments, intervals)):
        moment = jnp.where(row == index, value.astype(F32), moment)
        chosen = jnp.where(row == index, interval, chosen)
    lead = jnp.zeros(shape, F32)
    for choice in range(INTERVALS):
        picked = jnp.broadcast_to(lead_ref[choice : choice + 1, :], shape)
        lead = jnp.where(chosen == choice, picked, lead)
    half_width = D // 2
    place = jnp.where(lane < half_width, lane, lane - half_width).astype(F32)
    angles = moment * jnp.exp(place * (-math.log(10000.0) / half_width))
    wave = jnp.where(lane < half_width, jnp.sin(angles), jnp.cos(angles))
    condition = lead + wave
    return (condition / (1.0 + jnp.exp(-condition))).astype(BF).astype(F32)


def part_of(unit, ref, grp, *owner):
    if unit == 2:
        return ref.at[(*owner, grp)]
    return ref.at[(*owner, slice(None), pl.ds(pl.multiple_of(PART * grp, 128), PART))]


def gather_kernel(
    start_ref, interval_ref, counts_ref, lead_ref, qkv_ref, proj_ref, up_ref, down_ref, ada_ref,
    bias_ref,
    wa_ref, wu_ref, wd_ref, rows_ref,
    slab_a, slab_u, slab_d, cond_t, part_own, part_sib, part_z, bias_slot, bias_full,
    z_send, z_recv, x_send, x_recv, s_send, s_recv, own_sem, m_send, m_recv,
):
    at = Place()
    steps = range(1, 4)
    ready = greet(
        [at.sibling()] + [at.along_grp(k) for k in steps] + [at.along_z(k) for k in steps]
    )
    slabs = (slab_a, slab_u, slab_d)
    wholes = (wa_ref, wu_ref, wd_ref)
    sends = []
    from_z = {}
    from_sib = {}

    def launch(unit):
        slab, whole = (slabs[unit], wholes[unit])
        for k in steps:
            copy = send(
                part_of(unit, slab, at.grp), part_of(unit, whole, at.grp, at.dp),
                z_send.at[unit, k - 1], z_recv.at[unit, k - 1], at.along_z(k),
            )
            from_z[unit, k] = copy
            sends.append(copy)
        copy = send(slab, whole.at[at.dp], s_send.at[unit, 0], s_recv.at[unit, 0], at.sibling())
        from_sib[unit, 0] = copy
        sends.append(copy)
        own = pltpu.make_async_copy(slab, whole.at[at.dp], own_sem.at[unit])
        own.start()
        return own

    for j in range(9):
        slab_a[:, 128 * j : 128 * j + 128] = qkv_ref[pl.ds(j, SLAB, stride=9), :].astype(BF)
    for j in range(3):
        slab_a[:, 128 * (9 + j) : 128 * (10 + j)] = proj_ref[pl.ds(j, SLAB, stride=3), :].astype(BF)
    ready()
    owns = [launch(0)]

    start = start_ref[at.grp]
    interval = interval_ref[at.grp]
    cond_t[...] = jnp.transpose(
        condition_rows([start + s for s in range(ROLLOUT)], [interval] * ROLLOUT, lead_ref)
    )
    own_cond = cond_t[pl.ds(pl.multiple_of(SLAB * at.dp, 8), SLAB), :]
    columns = [jnp.broadcast_to(own_cond[:, s : s + 1], (SLAB, 128)) for s in range(ROLLOUT)]
    for j in range(18):
        rows = ada_ref[pl.ds(j, SLAB, stride=18), :].astype(BF).astype(F32)
        for s in range(ROLLOUT):
            part_own[18 * s + j : 18 * s + j + 1, :] = col_sum(rows * columns[s])
    part_own[36:40, :] = jnp.zeros((4, 128), F32)
    lane = lax.broadcasted_iota(jnp.int32, (8, 128), 1)
    shift = lax.rem(32 * at.dp, 128)
    turned = pltpu.roll(bias_ref[...].astype(BF).astype(F32), shift, axis=1)
    above = pltpu.roll(turned, 1, axis=0)
    bias_slot[at.z, at.core] = jnp.where(lane >= shift, turned, above)
    part_copy = send(part_own, part_sib, m_send.at[0], m_recv.at[0], at.sibling())
    bias_copy = send(
        bias_slot.at[at.z, at.core], bias_slot.at[at.z, at.core], m_send.at[1], m_recv.at[1],
        at.sibling(),
    )
    sends += [part_copy, bias_copy]

    for j in range(12):
        slab_u[:, 128 * j : 128 * j + 128] = up_ref[pl.ds(j, SLAB, stride=12), :].astype(BF)
    owns.append(launch(1))
    for g in range(GROUPS):
        for j in range(3):
            slab_d[g, :, 128 * j : 128 * j + 128] = down_ref[
                pl.ds(3 * SLAB * g + j, SLAB, stride=3), :
            ].astype(BF)
    owns.append(launch(2))

    part_copy.wait_recv()
    bias_copy.wait_recv()
    part_z[at.z] = part_own[...] + part_sib[...]
    small = []
    for k in steps:
        small.append(
            send(part_z.at[at.z], part_z.at[at.z], m_send.at[1 + k], m_recv.at[1 + k], at.along_z(k))
        )
        small.append(
            send(
                bias_slot.at[at.z], bias_slot.at[at.z], m_send.at[4 + k], m_recv.at[4 + k],
                at.along_z(k),
            )
        )
    sends += small

    from_grp = {}
    for unit in range(UNITS):
        whole = wholes[unit]
        for k in steps:
            from_z[unit, k].wait_recv()
            owner = 2 * lax.rem(at.z + LAYERS - k, LAYERS) + at.core
            for m in steps:
                part = part_of(unit, whole, at.grp, owner)
                copy = send(
                    part, part, x_send.at[unit, k - 1, m - 1], x_recv.at[unit, k - 1, m - 1],
                    at.along_grp(m),
                )
                from_grp[unit, k, m] = copy
                sends.append(copy)

    for copy in small:
        copy.wait_recv()
    total = part_z[0] + part_z[1] + part_z[2] + part_z[3]
    bias_full[...] = jnp.zeros_like(bias_full)
    for d in range(2 * LAYERS):
        first = 672 * d // 128
        bias_full[first : first + 7, :] += bias_slot[d // 2, d % 2, 0:7, :]
    counts = [counts_ref[g].astype(F32) for g in range(GROUPS)]
    own_count = counts_ref[at.grp].astype(F32)
    share = jnp.full((1, D), GROUPS * own_count) / jnp.full((1, D), sum(counts[1:], counts[0]))

    def put(row, value):
        rows_ref[row : row + 1, :] = value

    def joined(first):
        return jnp.concatenate([bias_full[first + j : first + j + 1, :] for j in range(3)], axis=1)

    for s in range(ROLLOUT):
        for r in range(6):
            mod = jnp.concatenate(
                [total[18 * s + 3 * r + j : 18 * s + 3 * r + j + 1, :] for j in range(3)], axis=1
            )
            put(8 * s + r, mod + joined(24 + 3 * r))
        put(8 * s + 6, share)
        put(8 * s + 7, share)
    put(ROW_BQKV, joined(0))
    put(ROW_BQKV + 1, jnp.zeros((1, D), F32))
    put(ROW_BQKV + 2, joined(3))
    put(ROW_BPROJ, joined(6))
    for j in range(4):
        put(ROW_BUP + j, joined(9 + 3 * j))
    put(ROW_BDOWN, joined(21))
    rows_ref[25:32, :] = jnp.zeros((7, D), F32)

    for unit in range(UNITS):
        whole = wholes[unit]
        for k in steps:
            for m in steps:
                from_grp[unit, k, m].wait_recv()
            owner = 2 * lax.rem(at.z + LAYERS - k, LAYERS) + at.core
            copy = send(
                whole.at[owner], whole.at[owner], s_send.at[unit, k], s_recv.at[unit, k],
                at.sibling(),
            )
            from_sib[unit, k] = copy
            sends.append(copy)
    for copy in from_sib.values():
        copy.wait_recv()
    for own in owns:
        own.wait()
    for copy in sends:
        copy.wait_send()


def gather(start, interval, counts, lead, masters):
    qkv, proj, up, down, ada, bias = masters
    smem = pl.BlockSpec(memory_space=pltpu.SMEM)
    vmem = pl.BlockSpec(memory_space=pltpu.VMEM)
    hbm = pl.BlockSpec(memory_space=pl.ANY)
    dma = pltpu.SemaphoreType.DMA
    wa, wu, wd, rows = pl.pallas_call(
        gather_kernel,
        in_specs=[smem] * 3 + [vmem] * 7,
        out_specs=[hbm, hbm, hbm, vmem],
        out_shape=[
            jax.ShapeDtypeStruct((8, SLAB, FF), BF),
            jax.ShapeDtypeStruct((8, SLAB, FF), BF),
            jax.ShapeDtypeStruct((8, GROUPS, SLAB, PART), BF),
            jax.ShapeDtypeStruct((32, D), F32),
        ],
        scratch_shapes=[
            pltpu.VMEM((SLAB, FF), BF),
            pltpu.VMEM((SLAB, FF), BF),
            pltpu.VMEM((GROUPS, SLAB, PART), BF),
            pltpu.VMEM((D, 8), F32),
            pltpu.VMEM((40, 128), F32),
            pltpu.VMEM((40, 128), F32),
            pltpu.VMEM((LAYERS, 40, 128), F32),
            pltpu.VMEM((LAYERS, 2, 8, 128), F32),
            pltpu.VMEM((48, 128), F32),
            dma((UNITS, 3)), dma((UNITS, 3)), dma((UNITS, 3, 3)), dma((UNITS, 3, 3)),
            dma((UNITS, 4)), dma((UNITS, 4)), dma((UNITS,)), dma((8,)), dma((8,)),
        ],
        compiler_params=pltpu.CompilerParams(collective_id=0, has_side_effects=True),
        name="gather",
    )(
        start, interval, counts, lead, *(m.reshape(-1, 128) for m in (qkv, proj, up, down, ada)),
        jnp.pad(bias, (0, 1024 - bias.shape[0])).reshape(8, 128),
    )
    return (wa.reshape(D, FF), wu.reshape(D, FF), wd.reshape(FF, D), rows)


def reduce_kernel(
    start_ref, interval_ref, lead_ref, vec_ref, ga_ref, gu_ref, gd_ref,
    piece_ref, ada_ref, bias_ref, square_ref,
    own, got_s, sum_s, got_x, sum_x, got_z, pieces, cond_t,
    vec_s, vec_z, vec_g, square_own, square_d, square_g,
    own_sem, s_send, s_recv, x_send, x_recv, z_send, z_recv, a_send, a_recv,
    v_send, v_recv, q_send, q_recv,
):
    at = Place()
    steps = range(1, 4)
    ready = greet(
        [at.sibling()]
        + [at.along_grp(k) for k in steps]
        + [at.along_z(k) for k in steps]
        + [at.across(k) for k in steps]
    )
    grads = (ga_ref, gu_ref, gd_ref)
    sends = []
    owns = []
    for unit in range(UNITS):
        copy = pltpu.make_async_copy(grads[unit].at[:, at.core], own.at[unit], own_sem.at[unit])
        copy.start()
        owns.append(copy)
    ready()
    vec_copy = send(vec_ref, vec_s, v_send.at[0], v_recv.at[0], at.sibling())
    from_sib = [
        send(
            grads[unit].at[:, 1 - at.core], got_s.at[unit], s_send.at[unit], s_recv.at[unit],
            at.sibling(),
        )
        for unit in range(UNITS)
    ]
    sends += [vec_copy] + from_sib
    moments = [start_ref[g] + s for g in range(GROUPS) for s in range(ROLLOUT)]
    intervals = [interval_ref[g] for g in range(GROUPS) for s in range(ROLLOUT)]
    cond_t[...] = jnp.transpose(condition_rows(moments, intervals, lead_ref))

    vec_copy.wait_recv()
    vec_z[at.z] = vec_ref[...] + vec_s[...]
    vec_from_z = [
        send(vec_z.at[at.z], vec_z.at[at.z], v_send.at[k], v_recv.at[k], at.along_z(k))
        for k in steps
    ]
    sends += vec_from_z

    from_grp = {}
    for unit in range(UNITS):
        owns[unit].wait()
        from_sib[unit].wait_recv()

        def add_pair(z, carry):
            for g in range(GROUPS):
                sum_s[unit, z, g] = (
                    own[unit, z, g].astype(F32) + got_s[unit, z, g].astype(F32)
                ).astype(BF)
            return carry

        lax.fori_loop(0, LAYERS, add_pair, 0)
        for k in steps:
            peer = at.along_grp(k)
            copy = send(
                sum_s.at[unit, :, peer[0]], got_x.at[unit, k - 1], x_send.at[unit, k - 1],
                x_recv.at[unit, k - 1], peer,
            )
            from_grp[unit, k] = copy
            sends.append(copy)

    for copy in vec_from_z:
        copy.wait_recv()
    vec_g[at.grp] = vec_z[0] + vec_z[1] + vec_z[2] + vec_z[3]
    vec_from_grp = [
        send(vec_g.at[at.grp], vec_g.at[at.grp], v_send.at[3 + k], v_recv.at[3 + k], at.along_grp(k))
        for k in steps
    ]
    sends += vec_from_grp

    from_z = {}
    for unit in range(UNITS):
        for k in steps:
            from_grp[unit, k].wait_recv()

        def add_four(z, carry):
            value = sum_s[unit, z, at.grp].astype(F32)
            for k in range(3):
                value = value + got_x[unit, k, z].astype(F32)
            sum_x[unit, z] = value.astype(BF)
            return carry

        lax.fori_loop(0, LAYERS, add_four, 0)
        for k in steps:
            peer = at.along_z(k)
            copy = send(
                sum_x.at[unit, lax.rem(at.z + k, LAYERS)], got_z.at[unit, k - 1],
                z_send.at[unit, k - 1], z_recv.at[unit, k - 1], peer,
            )
            from_z[unit, k] = copy
            sends.append(copy)

    for copy in vec_from_grp:
        copy.wait_recv()
    own_cond = cond_t[pl.ds(pl.multiple_of(SLAB * at.dp, 8), SLAB), :]
    columns = [jnp.broadcast_to(own_cond[:, k : k + 1], (SLAB, 128)) for k in range(8)]

    def ada_tile(j, square):
        tile = jnp.zeros((SLAB, 128), F32)
        for g in range(GROUPS):
            for s in range(ROLLOUT):
                tile = tile + columns[ROLLOUT * g + s] * vec_g[g, pl.ds(24 + 18 * s + j, 1), :]
        ada_ref[pl.ds(j, SLAB, stride=18), :] = tile
        return square + col_sum(tile * tile)

    ada_square = lax.fori_loop(0, 18, ada_tile, jnp.zeros((1, 128), F32))
    vec_sum = vec_g[0] + vec_g[1] + vec_g[2] + vec_g[3]
    bias_ref[0:24, :] = vec_sum[0:24]
    bias_ref[24:42, :] = vec_sum[24:42] + vec_sum[42:60]
    bias_ref[42:48, :] = jnp.zeros((6, 128), F32)

    square = 0.25 * ada_square
    from_gather = []
    for unit in range(UNITS):
        for k in steps:
            from_z[unit, k].wait_recv()
        value = sum_x[unit, at.z].astype(F32)
        for k in range(3):
            value = value + got_z[unit, k].astype(F32)
        value = value.astype(BF)
        pieces[unit, at.grp] = value
        for k in steps:
            copy = send(
                pieces.at[unit, at.grp], pieces.at[unit, at.grp], a_send.at[unit, k - 1],
                a_recv.at[unit, k - 1], at.along_grp(k),
            )
            from_gather.append(copy)
            sends.append(copy)
        wide = value.astype(F32)
        wide = col_sum(wide * wide)
        square = square + wide[:, 0:128] + wide[:, 128:256] + wide[:, 256:384]

    square_d[at.dp] = jnp.broadcast_to(square, (8, 128))
    squares = [send(
        square_d.at[at.dp], square_d.at[at.dp], q_send.at[0], q_recv.at[0], at.sibling()
    )]
    for k in steps:
        for index, peer in ((k, at.along_z(k)), (3 + k, at.across(k))):
            squares.append(send(
                square_d.at[at.dp], square_d.at[at.dp], q_send.at[index], q_recv.at[index], peer
            ))
    for copy in squares:
        copy.wait_recv()
    total = square_d[0]
    for d in range(1, 2 * LAYERS):
        total = total + square_d[d]
    square_g[at.grp] = total
    final = [
        send(square_g.at[at.grp], square_g.at[at.grp], q_send.at[6 + k], q_recv.at[6 + k],
             at.along_grp(k))
        for k in steps
    ]
    sends += squares + final
    for copy in final:
        copy.wait_recv()
    bias_sum = bias_ref[...]
    bias_square = col_sum(bias_sum * bias_sum)
    total = square_g[0] + square_g[1] + square_g[2] + square_g[3] + bias_square
    square_ref[...] = jnp.broadcast_to(jnp.sum(total, axis=1, keepdims=True), (8, 128))

    for copy in from_gather:
        copy.wait_recv()
    piece_ref[...] = pieces[...]
    for copy in sends:
        copy.wait_send()


def reduce(start, interval, lead, vec, grads):
    smem = pl.BlockSpec(memory_space=pltpu.SMEM)
    vmem = pl.BlockSpec(memory_space=pltpu.VMEM)
    hbm = pl.BlockSpec(memory_space=pl.ANY)
    dma = pltpu.SemaphoreType.DMA
    slab = (LAYERS, GROUPS, SLAB, PART)
    piece = (SLAB, PART)
    return pl.pallas_call(
        reduce_kernel,
        in_specs=[smem, smem, vmem, vmem, hbm, hbm, hbm],
        out_specs=[vmem] * 4,
        out_shape=[
            jax.ShapeDtypeStruct((UNITS, GROUPS, *piece), BF),
            jax.ShapeDtypeStruct((18 * SLAB, 128), F32),
            jax.ShapeDtypeStruct((48, 128), F32),
            jax.ShapeDtypeStruct((8, 128), F32),
        ],
        scratch_shapes=[
            pltpu.VMEM((UNITS, *slab), BF),
            pltpu.VMEM((UNITS, *slab), BF),
            pltpu.VMEM((UNITS, *slab), BF),
            pltpu.VMEM((UNITS, 3, LAYERS, *piece), BF),
            pltpu.VMEM((UNITS, LAYERS, *piece), BF),
            pltpu.VMEM((UNITS, 3, *piece), BF),
            pltpu.VMEM((UNITS, GROUPS, *piece), BF),
            pltpu.VMEM((D, 8), F32),
            pltpu.VMEM((64, 128), F32),
            pltpu.VMEM((LAYERS, 64, 128), F32),
            pltpu.VMEM((GROUPS, 64, 128), F32),
            pltpu.VMEM((8, 128), F32),
            pltpu.VMEM((8, 8, 128), F32),
            pltpu.VMEM((GROUPS, 8, 128), F32),
            dma((UNITS,)), dma((UNITS,)), dma((UNITS,)),
            dma((UNITS, 3)), dma((UNITS, 3)), dma((UNITS, 3)), dma((UNITS, 3)),
            dma((UNITS, 3)), dma((UNITS, 3)), dma((7,)), dma((7,)), dma((10,)), dma((10,)),
        ],
        compiler_params=pltpu.CompilerParams(collective_id=1, has_side_effects=True),
        name="reduce",
    )(start, interval, lead, vec, *grads)


correction = 1.0 - 0.5**ADAM_STEP
grad_limit = math.sqrt(NPARAM)


def adam(master, first, second, clipped, decay):
    first_new = 0.5 * first + 0.5 * clipped
    second_new = 0.5 * second + 0.5 * clipped * clipped
    update = first_new / correction / (jnp.sqrt(second_new / correction) + adam_eps)
    return (master - learn_rate * (update + decay * master), first_new, second_new)


def adam_kernel(*refs):
    piece_ref, ada_ref, square_ref = refs[:3]
    masters, firsts, seconds = (refs[3:8], refs[8:13], refs[13:18])
    news, first_news, second_news, copies = (refs[18:23], refs[23:28], refs[28:33], refs[33:38])
    flats = refs[38:42]
    norm = jnp.sqrt(square_ref[0:1, :])
    clip = grad_limit / jnp.maximum(norm, grad_limit)
    qkv, proj, up, down = flats
    for g in range(3):
        for j in range(3):
            qkv[pl.ds(3 * g + j, SLAB, stride=9), :] = piece_ref[0, g, :, 128 * j : 128 * j + 128].astype(F32)
    for j in range(3):
        proj[pl.ds(j, SLAB, stride=3), :] = piece_ref[0, 3, :, 128 * j : 128 * j + 128].astype(F32)
    for g in range(GROUPS):
        for j in range(3):
            up[pl.ds(3 * g + j, SLAB, stride=12), :] = piece_ref[1, g, :, 128 * j : 128 * j + 128].astype(F32)
            down[pl.ds(3 * SLAB * g + j, SLAB, stride=3), :] = piece_ref[2, g, :, 128 * j : 128 * j + 128].astype(F32)
    for index, grad in enumerate((qkv, proj, up, down, ada_ref)):
        def chunk(i, carry):
            rows = pl.ds(pl.multiple_of(16 * i, 16), 16)
            new, first, second = adam(
                masters[index][rows, :], firsts[index][rows, :], seconds[index][rows, :],
                grad[rows, :] * clip, 0.1,
            )
            news[index][rows, :] = new
            first_news[index][rows, :] = first
            second_news[index][rows, :] = second
            copies[index][rows, :] = new.astype(BF)
            return carry

        lax.fori_loop(0, grad.shape[0] // 16, chunk, 0, unroll=3)


def update(pieces, ada, square, masters, firsts, seconds):
    flat = lambda arrays: [a.reshape(-1, 128) for a in arrays[:5]]
    masters, firsts, seconds = (flat(masters), flat(firsts), flat(seconds))
    vmem = pl.BlockSpec(memory_space=pltpu.VMEM)
    shapes = [m.shape for m in masters]
    outs = [jax.ShapeDtypeStruct(s, F32) for s in shapes] * 3
    outs += [jax.ShapeDtypeStruct(s, BF) for s in shapes]
    results = pl.pallas_call(
        adam_kernel,
        in_specs=[vmem] * 18,
        out_specs=[vmem] * 20,
        out_shape=outs,
        scratch_shapes=[pltpu.VMEM(s, F32) for s in shapes[:4]],
        name="adam",
    )(pieces, ada, square, *masters, *firsts, *seconds)
    results = [r.reshape(-1) for r in results]
    return (results[0:5], results[5:10], results[10:15], results[15:20])


def step_embedding(moment):
    half_width = D // 2
    freqs = jnp.exp(-math.log(10000.0) * jnp.arange(half_width, dtype=F32) / half_width)
    angles = moment[:, None] * freqs[None, :]
    return jnp.concatenate([jnp.sin(angles), jnp.cos(angles)], axis=1)


def all_conditions(group_interval, rollout_start, lead_table):
    chosen = group_interval[:, None] == jnp.arange(INTERVALS)[None, :]
    lead_rows = jnp.sum(jnp.where(chosen[:, :, None], lead_table[None], 0.0), axis=1)
    start = rollout_start.astype(F32)
    rows = [lead_rows + step_embedding(start + offset) for offset in range(ROLLOUT)]
    return jax.nn.silu(jnp.stack(rows, axis=1)).astype(BF)


def block_pass(inputs, cotangent, rows, wa, wup, wdown):
    block = inputs.shape[0]
    blocks = (8, 4, SLAB, PART)
    (qkv0,) = rows_call(first_kernel, "first", [inputs], [rows, wa], [(3 * D, BF)], [])
    att0, p0 = attend(qkv0, block)
    a0, gp0, act0, f0, x1, qkv1 = rows_call(
        middle_kernel, "middle", [inputs, att0], [rows, wa, wup, wdown],
        [(D, F32), (FF, F32), (FF, BF), (D, F32), (D, F32), (3 * D, BF)], [],
    )
    att1, p1 = attend(qkv1, block)
    result, dmid1, datt1, gdown, gup, gproj, wide1, narrow1 = rows_call(
        turn_kernel, "turn", [x1, att1, cotangent], [rows, wa, wup, wdown],
        [(D, F32), (D, F32), (D, BF)],
        [((FF, D), F32), ((D, FF), F32), ((D, D), F32), ((8, FF), F32), ((8, D), F32)],
    )
    dq, dk, dv = attend_back(qkv1, datt1, p1, block)
    dmid0, datt0, gqkv, gproj, wide0, narrow1b, narrow0, bias1, gup_blocks, gdown_blocks = rows_call(
        join_kernel, "join",
        [dq, dk, dv, x1, dmid1, inputs, a0, gp0, act0, f0, att0],
        [rows, wa, wup, wdown, gproj],
        [(D, F32), (D, BF)],
        [((D, 3 * D), F32), ((D, D), F32), ((8, FF), F32), ((8, D), F32), ((8, D), F32),
         ((8, 3 * D), F32), (blocks, BF), (blocks, BF)],
        [gdown, gup],
        [pltpu.VMEM((FF, D), F32), pltpu.VMEM((D, FF), F32), pltpu.VMEM((FF, D), F32),
         pltpu.VMEM((D, FF), F32), pltpu.SemaphoreType.DMA((2,))],
    )
    dq, dk, dv = attend_back(qkv0, datt0, p0, block)
    input_grad, vec, gqkv_blocks = rows_call(
        last_kernel, "last", [dq, dk, dv, inputs, dmid0],
        [rows, wa, gqkv, gproj, wide1, narrow1, wide0, narrow1b, narrow0, bias1],
        [(D, F32)], [((64, 128), F32), (blocks, BF)], (),
        [pltpu.VMEM((D, 3 * D), F32), pltpu.VMEM((8, D), F32), pltpu.VMEM((8, 3 * D), F32)],
    )
    return (result, input_grad, gqkv_blocks, gup_blocks, gdown_blocks, vec)


def plain_gather(group_interval, counts, rollout_start, lead_table, masters):
    low = [master.astype(BF) for master in masters]
    owner = lax.axis_index("dp")
    group_index = lax.axis_index("grp")
    own_rows = D // lax.axis_size("dp")
    counts = counts.astype(F32)
    share = lax.axis_size("grp") * counts / jnp.sum(counts)
    share = lax.dynamic_index_in_dim(share, group_index, keepdims=False)
    conditions = all_conditions(group_interval, rollout_start, lead_table)
    owner_columns = lax.dynamic_slice_in_dim(conditions, owner * own_rows, own_rows, axis=2)
    own_condition = lax.dynamic_index_in_dim(owner_columns, group_index, keepdims=False)
    modulation = lax.psum(dot(own_condition, low[4].reshape(own_rows, 6 * D)), "dp")
    qkv, proj, up, down, bias = [
        lax.all_gather(low[index], "dp", axis=0, tiled=True) for index in (0, 1, 2, 3, 5)
    ]
    bias = bias.astype(F32)
    modulation = modulation + bias[4 * D + FF :][None]
    share_rows = jnp.broadcast_to(share, (ROLLOUT, 2, D))
    mods = jnp.concatenate([modulation.reshape(ROLLOUT, 6, D), share_rows], axis=1).reshape(-1, D)
    rows = jnp.concatenate(
        [mods, bias[:D][None], jnp.zeros((1, D), F32), bias[D : 4 * D + FF].reshape(-1, D),
         jnp.zeros((7, D), F32)]
    )
    wa = jnp.concatenate([qkv.reshape(D, 3 * D), proj.reshape(D, D)], axis=1)
    return (wa, up.reshape(D, FF), down.reshape(FF, D), rows, owner_columns)


def plain_update(owner_columns, vec, blocks, masters, firsts, seconds):
    owner = lax.axis_index("dp")
    vec = vec.reshape(-1)
    split = 4 * D + FF
    dmod = vec[split : split + ROLLOUT * 6 * D].reshape(ROLLOUT, 6 * D)
    dmod_all = lax.all_gather(lax.psum(dmod, "dp"), "grp")
    bias_sum = lax.psum(vec[:split], ("grp", "dp"))
    bias_sum = jnp.concatenate([bias_sum, jnp.sum(dmod_all, axis=(0, 1))])
    bias_rows = masters[5].shape[0]
    bias_grad = lax.dynamic_slice_in_dim(bias_sum, owner * bias_rows, bias_rows)
    ada_grad = jnp.einsum(
        "gsr,gsc->rc", owner_columns.astype(F32), dmod_all, precision=lax.Precision.HIGHEST
    )
    flat_a, flat_up = [
        block.transpose(0, 2, 1, 3).reshape(D, FF) for block in blocks[:2]
    ]
    flat = [flat_a[:, : 3 * D], flat_a[:, 3 * D :], flat_up, blocks[2]]
    shares = []
    for grad in flat:
        summed = lax.psum(grad.reshape(-1), "grp").astype(F32)
        shares.append(lax.psum_scatter(summed, "dp", scatter_dimension=0, tiled=True))
    shares = shares + [ada_grad.reshape(-1), bias_grad]
    local_square = sum((jnp.sum(piece * piece) for piece in shares))
    grad_norm = jnp.sqrt(lax.psum(local_square, "dp"))
    clip = grad_limit / jnp.maximum(grad_norm, grad_limit)
    decays = [0.1, 0.1, 0.1, 0.1, 0.1, 0.0]
    results = [
        adam(master, first, second, grad * clip, decay)
        for master, first, second, grad, decay in zip(masters, firsts, seconds, shares, decays)
    ]
    news, first_news, second_news = zip(*results)
    return (grad_norm, *news, *first_news, *second_news, *(new.astype(BF) for new in news))


def per_device(
    inputs,
    cotangent,
    group_interval,
    sample_counts,
    rollout_start,
    lead_table,
    *state,
):
    masters, firsts, seconds = (state[0:6], state[6:12], state[12:18])
    owners = lax.axis_size("dp")
    fits = owners == 2 * LAYERS and lax.axis_size("grp") == GROUPS
    if fits:
        wa, wup, wdown, rows = gather(
            rollout_start, group_interval, sample_counts, lead_table, masters
        )
    else:
        wa, wup, wdown, rows, owner_columns = plain_gather(
            group_interval, sample_counts, rollout_start, lead_table, masters
        )
    result, input_grad, ga, gu, gd, vec = block_pass(inputs, cotangent, rows, wa, wup, wdown)
    if not fits:
        rest = plain_update(owner_columns, vec, (ga, gu, gd), masters, firsts, seconds)
        return (result, input_grad, *rest)
    pieces, ada_grad, bias_sum, square = reduce(
        rollout_start, group_interval, lead_table, vec,
        [grad.reshape(LAYERS, 2, GROUPS, SLAB, PART) for grad in (ga, gu, gd)],
    )
    news, first_news, second_news, copies = update(
        pieces, ada_grad, square, masters, firsts, seconds
    )
    grad_norm = jnp.sqrt(square[0, 0])
    clip = grad_limit / jnp.maximum(grad_norm, grad_limit)
    bias_rows = masters[5].shape[0]
    bias_grad = lax.dynamic_slice_in_dim(
        bias_sum.reshape(-1), lax.axis_index("dp") * bias_rows, bias_rows
    )
    new, first, second = adam(masters[5], firsts[5], seconds[5], bias_grad * clip, 0.0)
    return (
        result, input_grad, grad_norm, *news, new, *first_news, first, *second_news, second,
        *copies, new.astype(BF),
    )


def solution(mesh):
    rows = P(("grp", "dp"), None)
    return jax.shard_map(
        per_device,
        mesh=mesh,
        in_specs=(rows, rows, P(), P(), P(), P(), *[P("dp")] * 18),
        out_specs=(rows, rows, P(), *[P("dp")] * 24),
        check_vma=False,
    )
```

```python
import functools
import math

import jax
import jax.numpy as jnp
from jax import lax
from jax.experimental import pallas as pl
from jax.experimental.pallas import tpu as pltpu
from jax.sharding import PartitionSpec as P

D = 384
HEADS = 6
FF = 1536
ROLLOUT = 2
INTERVALS = 3
ADAM_STEP = 10
HEAD_DIM = 64
NPARAM = 2659584

norm_eps = 1e-06
learn_rate = 0.05
adam_eps = 1e-08

BF = jnp.bfloat16
F32 = jnp.float32
NN = (((1,), (0,)), ((), ()))
NT = (((1,), (1,)), ((), ()))
TN = (((0,), (0,)), ((), ()))

ROWS = 256
SLAB = 48
PART = 384
ROW_SHARE = 6
ROW_BQKV, ROW_BPROJ, ROW_BUP, ROW_BDOWN = 16, 19, 20, 24
SHIFT1, SCALE1, GATE1, SHIFT2, SCALE2, GATE2 = range(6)


def dot(left, right, dims=NN):
    return lax.dot_general(left, right, dims, preferred_element_type=F32)


def layer_norm(stream):
    centred = stream - jnp.mean(stream, axis=-1, keepdims=True)
    inverse = lax.rsqrt(jnp.mean(centred * centred, axis=-1, keepdims=True) + norm_eps)
    return (centred * inverse, inverse)


def norm_back(normed, inverse, grad_out):
    mean_grad = jnp.mean(grad_out, axis=-1, keepdims=True)
    mean_prod = jnp.mean(grad_out * normed, axis=-1, keepdims=True)
    return inverse * (grad_out - mean_grad - normed * mean_prod)


def col_sum(value):
    return jnp.sum(value, axis=0, keepdims=True)


def modulated(normed, mods, scale_row, shift_row):
    return (normed * (1.0 + mods(scale_row)) + mods(shift_row)).astype(BF)


def mod_reader(mod_ref, step):
    return lambda row: mod_ref[pl.ds(8 * step + row, 1), :]


def gelu_pair(value):
    cdf = 0.5 + 0.5 * lax.erf(value * (2.0**-0.5))
    density = jnp.exp(-0.5 * value * value) * (1.0 / math.sqrt(2.0 * math.pi))
    return (value * cdf, cdf + value * density)


def side_by_side(ref, first, count):
    return jnp.concatenate([ref[row : row + 1, :] for row in range(first, first + count)], axis=1)


def first_rows(x, rows_ref, wa_ref):
    normed, _ = layer_norm(x.astype(F32))
    hidden = modulated(normed, mod_reader(rows_ref, 0), SCALE1, SHIFT1)
    qkv = dot(hidden, wa_ref[:, : 3 * D]) + side_by_side(rows_ref, ROW_BQKV, 3)
    return qkv.astype(BF)


def middle_rows(
    x_ref, att_ref, rows_ref, wa_ref, wup_ref, wdown_ref,
    a_ref, gp_ref, act_ref, f_ref, next_ref, qkv_ref,
):
    mods = mod_reader(rows_ref, 0)
    later = mod_reader(rows_ref, 1)
    branch = dot(att_ref[...], wa_ref[:, 3 * D :]) + mods(ROW_BPROJ)
    a_ref[...] = branch
    middle = x_ref[...].astype(F32) + mods(GATE1) * branch
    normed, _ = layer_norm(middle)
    hidden = modulated(normed, mods, SCALE2, SHIFT2)
    upward = dot(hidden, wup_ref[...]) + side_by_side(rows_ref, ROW_BUP, 4)
    act, slope = gelu_pair(upward)
    gp_ref[...] = slope
    act = act.astype(BF)
    act_ref[...] = act
    branch = dot(act, wdown_ref[...]) + mods(ROW_BDOWN)
    f_ref[...] = branch
    stream = middle + mods(GATE2) * branch
    next_ref[...] = stream
    normed, _ = layer_norm(stream)
    hidden = modulated(normed, later, SCALE1, SHIFT1)
    qkv = dot(hidden, wa_ref[:, : 3 * D]) + side_by_side(rows_ref, ROW_BQKV, 3)
    qkv_ref[...] = qkv.astype(BF)


def ffn_back(
    mods, grad, branch_two, act, slope, normed, inverse, hidden, branch_one, att,
    wa_ref, wup_ref, wdown_ref, gdown_ref, gup_ref, gproj_ref, wide_ref, narrow_ref,
    dmid_ref, datt_ref,
):
    df = (mods(GATE2) * grad).astype(BF)
    narrow_ref[pl.ds(GATE2, 1), :] += col_sum(grad * branch_two)
    narrow_ref[pl.ds(7, 1), :] += col_sum(df.astype(F32))
    gdown_ref[...] += dot(act, df, TN)
    dact = dot(df, wdown_ref[...], NT)
    du = (dact * slope).astype(BF)
    wide_ref[pl.ds(0, 1), :] += col_sum(du.astype(F32))
    gup_ref[...] += dot(hidden, du, TN)
    dh = dot(du, wup_ref[...], NT)
    narrow_ref[pl.ds(SHIFT2, 1), :] += col_sum(dh)
    narrow_ref[pl.ds(SCALE2, 1), :] += col_sum(dh * normed)
    dmid = grad + norm_back(normed, inverse, dh * (1.0 + mods(SCALE2)))
    dmid_ref[...] = dmid
    da = (mods(GATE1) * dmid).astype(BF)
    narrow_ref[pl.ds(GATE1, 1), :] += col_sum(dmid * branch_one)
    narrow_ref[pl.ds(6, 1), :] += col_sum(da.astype(F32))
    gproj_ref[...] += dot(att, da, TN)
    datt_ref[...] = dot(da, wa_ref[:, 3 * D :], NT).astype(BF)


def turn_rows(
    x_ref, att_ref, cot_ref, rows_ref, wa_ref, wup_ref, wdown_ref,
    out_ref, dmid_ref, datt_ref, gdown_ref, gup_ref, gproj_ref, wide_ref, narrow_ref,
):
    mods = mod_reader(rows_ref, 1)
    shared = mod_reader(rows_ref, 0)
    att = att_ref[...]
    branch_one = dot(att, wa_ref[:, 3 * D :]) + shared(ROW_BPROJ)
    middle = x_ref[...] + mods(GATE1) * branch_one
    normed, inverse = layer_norm(middle)
    hidden = modulated(normed, mods, SCALE2, SHIFT2)
    upward = dot(hidden, wup_ref[...]) + side_by_side(rows_ref, ROW_BUP, 4)
    act, slope = gelu_pair(upward)
    act = act.astype(BF)
    branch_two = dot(act, wdown_ref[...]) + shared(ROW_BDOWN)
    out_ref[...] = middle + mods(GATE2) * branch_two
    ffn_back(
        mods, cot_ref[...].astype(F32), branch_two, act, slope, normed, inverse, hidden,
        branch_one, att, wa_ref, wup_ref, wdown_ref, gdown_ref, gup_ref, gproj_ref,
        wide_ref, narrow_ref, dmid_ref, datt_ref,
    )


def qkv_back(mods, stream, dmid, dqkv, wa_ref, gqkv_ref, narrow_ref, bias_ref):
    normed, inverse = layer_norm(stream)
    hidden = modulated(normed, mods, SCALE1, SHIFT1)
    bias_ref[pl.ds(0, 1), :] += col_sum(dqkv.astype(F32))
    gqkv_ref[...] += dot(hidden, dqkv, TN)
    dh = dot(dqkv, wa_ref[:, : 3 * D], NT)
    narrow_ref[pl.ds(SHIFT1, 1), :] += col_sum(dh)
    narrow_ref[pl.ds(SCALE1, 1), :] += col_sum(dh * normed)
    return dmid + norm_back(normed, inverse, dh * (1.0 + mods(SCALE1)))


def join_rows(
    dqkv_ref, x1_ref, x0_ref, a_ref, gp_ref, act_ref, f_ref, att_ref,
    rows_ref, wa_ref, wup_ref, wdown_ref,
    dmid_ref, datt_ref, gqkv_ref, gdown_ref, gup_ref, gproj_ref, wide_ref, narrow1_ref,
    narrow_ref, bias_ref,
):
    grad = qkv_back(
        mod_reader(rows_ref, 1), x1_ref[...], dmid_ref[...], dqkv_ref[...], wa_ref, gqkv_ref,
        narrow1_ref, bias_ref,
    )
    mods = mod_reader(rows_ref, 0)
    branch_one = a_ref[...]
    middle = x0_ref[...].astype(F32) + mods(GATE1) * branch_one
    normed, inverse = layer_norm(middle)
    hidden = modulated(normed, mods, SCALE2, SHIFT2)
    ffn_back(
        mods, grad, f_ref[...], act_ref[...], gp_ref[...], normed, inverse, hidden,
        branch_one, att_ref[...], wa_ref, wup_ref, wdown_ref, gdown_ref, gup_ref, gproj_ref,
        wide_ref, narrow_ref, dmid_ref, datt_ref,
    )


def head_lanes(rows):
    lane = lax.broadcasted_iota(jnp.int32, (rows, 2 * HEAD_DIM), 1)
    return (lane < HEAD_DIM, lane >= HEAD_DIM)


def turned_heads(rows_f32, out_ref):
    turned = jnp.transpose(rows_f32)
    row = lax.broadcasted_iota(jnp.int32, turned.shape, 0)
    out_ref[0] = jnp.where(row < HEAD_DIM, turned, 0.0).astype(BF)
    out_ref[1] = jnp.where(row >= HEAD_DIM, turned, 0.0).astype(BF)


score_scale = HEAD_DIM**-0.5


def attend_pair(q, k_ref, v, o_ref, p_ref, vt_ref):
    turned_heads(v.astype(F32), vt_ref)
    queries = q * BF(score_scale)
    mixed = None
    for half, lanes in enumerate(head_lanes(queries.shape[0])):
        scores = dot(k_ref[...], jnp.where(lanes, queries, BF(0)), NT)
        top = jnp.max(scores, axis=0, keepdims=True)
        weights = jnp.exp(scores - top)
        total = jnp.sum(weights, axis=0, keepdims=True)
        low = (weights * (1.0 / total)).astype(BF)
        p_ref[half] = low
        part = dot(vt_ref[half], low)
        mixed = part if mixed is None else mixed + part
    o_ref[...] = jnp.transpose(mixed).astype(BF)


def attend_back_pair(q, k, v_ref, grads, p_ref, dq_ref, dk_ref, dv_ref, kt_ref):
    turned_heads(k.astype(F32) * score_scale, kt_ref)
    queries = q * BF(score_scale)
    dq_turned, dk, dv = (None, None, None)
    for half, lanes in enumerate(head_lanes(queries.shape[0])):
        grad = jnp.where(lanes, grads, BF(0))
        query = jnp.where(lanes, queries, BF(0))
        low = p_ref[half]
        weight_grad = dot(v_ref[...], grad, NT)
        weights = low.astype(F32)
        delta = jnp.sum(weights * weight_grad, axis=0, keepdims=True)
        score_grad = (weights * (weight_grad - delta)).astype(BF)
        parts = (dot(kt_ref[half], score_grad), dot(score_grad, query), dot(low, grad))
        if half == 0:
            dq_turned, dk, dv = parts
        else:
            dq_turned, dk, dv = (dq_turned + parts[0], dk + parts[1], dv + parts[2])
    dq_ref[...] = jnp.transpose(dq_turned).astype(BF)
    dk_ref[...] = dk.astype(BF)
    dv_ref[...] = dv.astype(BF)


MESH_ID = pl.DeviceIdType.MESH
GROUPS = 4
LAYERS = 4
UNITS = 3


class Place:
    def __init__(self):
        self.grp = lax.axis_index("grp")
        self.dp = lax.axis_index("dp")
        self.z = self.dp // 2
        self.core = self.dp % 2

    def sibling(self):
        return (self.grp, 2 * self.z + 1 - self.core)

    def along_grp(self, step):
        return (lax.rem(self.grp + step, GROUPS), self.dp)

    def along_z(self, step):
        return (self.grp, 2 * lax.rem(self.z + step, LAYERS) + self.core)

    def across(self, step):
        return (self.grp, 2 * lax.rem(self.z + step, LAYERS) + 1 - self.core)


def greet(peers):
    barrier = pltpu.get_barrier_semaphore()
    for peer in peers:
        pl.semaphore_signal(barrier, inc=1, device_id=peer, device_id_type=MESH_ID)
    return lambda: pl.semaphore_wait(barrier, len(peers))


def send(src, dst, send_sem, recv_sem, peer):
    copy = pltpu.make_async_remote_copy(
        src_ref=src, dst_ref=dst, send_sem=send_sem, recv_sem=recv_sem,
        device_id=peer, device_id_type=MESH_ID,
    )
    copy.start()
    return copy


def condition_rows(moments, intervals, lead_ref):
    shape = (8, D)
    row = lax.broadcasted_iota(jnp.int32, shape, 0)
    lane = lax.broadcasted_iota(jnp.int32, shape, 1)
    moment = jnp.zeros(shape, F32)
    chosen = jnp.zeros(shape, jnp.int32)
    for index, (value, interval) in enumerate(zip(moments, intervals)):
        moment = jnp.where(row == index, value.astype(F32), moment)
        chosen = jnp.where(row == index, interval, chosen)
    lead = jnp.zeros(shape, F32)
    for choice in range(INTERVALS):
        picked = jnp.broadcast_to(lead_ref[choice : choice + 1, :], shape)
        lead = jnp.where(chosen == choice, picked, lead)
    half_width = D // 2
    place = jnp.where(lane < half_width, lane, lane - half_width).astype(F32)
    angles = moment * jnp.exp(place * (-math.log(10000.0) / half_width))
    wave = jnp.where(lane < half_width, jnp.sin(angles), jnp.cos(angles))
    condition = lead + wave
    return (condition / (1.0 + jnp.exp(-condition))).astype(BF).astype(F32)


def part_of(unit, ref, grp, *owner):
    if unit == 2:
        return ref.at[(*owner, grp)]
    return ref.at[(*owner, slice(None), pl.ds(pl.multiple_of(PART * grp, 128), PART))]


def gather_kernel(
    start_ref, interval_ref, counts_ref, lead_ref, qkv_ref, proj_ref, up_ref, down_ref, ada_ref,
    bias_ref,
    wa_ref, wu_ref, wd_ref, rows_ref,
    slab_a, slab_u, slab_d, cond_t, part_own, part_sib, part_z, bias_slot, bias_full,
    z_send, z_recv, x_send, x_recv, s_send, s_recv, own_sem, m_send, m_recv,
):
    at = Place()
    steps = range(1, 4)
    ready = greet(
        [at.sibling()] + [at.along_grp(k) for k in steps] + [at.along_z(k) for k in steps]
    )
    slabs = (slab_a, slab_u, slab_d)
    wholes = (wa_ref, wu_ref, wd_ref)
    sends = []
    from_z = {}
    from_sib = {}

    def launch(unit):
        slab, whole = (slabs[unit], wholes[unit])
        for k in steps:
            copy = send(
                part_of(unit, slab, at.grp), part_of(unit, whole, at.grp, at.dp),
                z_send.at[unit, k - 1], z_recv.at[unit, k - 1], at.along_z(k),
            )
            from_z[unit, k] = copy
            sends.append(copy)
        copy = send(slab, whole.at[at.dp], s_send.at[unit, 0], s_recv.at[unit, 0], at.sibling())
        from_sib[unit, 0] = copy
        sends.append(copy)
        own = pltpu.make_async_copy(slab, whole.at[at.dp], own_sem.at[unit])
        own.start()
        return own

    for j in range(9):
        slab_a[:, 128 * j : 128 * j + 128] = qkv_ref[pl.ds(j, SLAB, stride=9), :].astype(BF)
    for j in range(3):
        slab_a[:, 128 * (9 + j) : 128 * (10 + j)] = proj_ref[pl.ds(j, SLAB, stride=3), :].astype(BF)
    ready()
    owns = [launch(0)]

    start = start_ref[at.grp]
    interval = interval_ref[at.grp]
    cond_t[...] = jnp.transpose(
        condition_rows([start + s for s in range(ROLLOUT)], [interval] * ROLLOUT, lead_ref)
    )
    own_cond = cond_t[pl.ds(pl.multiple_of(SLAB * at.dp, 8), SLAB), :]
    columns = [jnp.broadcast_to(own_cond[:, s : s + 1], (SLAB, 128)) for s in range(ROLLOUT)]
    for j in range(18):
        rows = ada_ref[pl.ds(j, SLAB, stride=18), :].astype(BF).astype(F32)
        for s in range(ROLLOUT):
            part_own[18 * s + j : 18 * s + j + 1, :] = col_sum(rows * columns[s])
    part_own[36:40, :] = jnp.zeros((4, 128), F32)
    lane = lax.broadcasted_iota(jnp.int32, (8, 128), 1)
    shift = lax.rem(32 * at.dp, 128)
    turned = pltpu.roll(bias_ref[...].astype(BF).astype(F32), shift, axis=1)
    above = pltpu.roll(turned, 1, axis=0)
    bias_slot[at.z, at.core] = jnp.where(lane >= shift, turned, above)
    part_copy = send(part_own, part_sib, m_send.at[0], m_recv.at[0], at.sibling())
    bias_copy = send(
        bias_slot.at[at.z, at.core], bias_slot.at[at.z, at.core], m_send.at[1], m_recv.at[1],
        at.sibling(),
    )
    sends += [part_copy, bias_copy]

    for j in range(12):
        slab_u[:, 128 * j : 128 * j + 128] = up_ref[pl.ds(j, SLAB, stride=12), :].astype(BF)
    owns.append(launch(1))
    for g in range(GROUPS):
        for j in range(3):
            slab_d[g, :, 128 * j : 128 * j + 128] = down_ref[
                pl.ds(3 * SLAB * g + j, SLAB, stride=3), :
            ].astype(BF)
    owns.append(launch(2))

    part_copy.wait_recv()
    bias_copy.wait_recv()
    part_z[at.z] = part_own[...] + part_sib[...]
    small = []
    for k in steps:
        small.append(
            send(part_z.at[at.z], part_z.at[at.z], m_send.at[1 + k], m_recv.at[1 + k], at.along_z(k))
        )
        small.append(
            send(
                bias_slot.at[at.z], bias_slot.at[at.z], m_send.at[4 + k], m_recv.at[4 + k],
                at.along_z(k),
            )
        )
    sends += small

    from_grp = {}
    for unit in range(UNITS):
        whole = wholes[unit]
        for k in steps:
            from_z[unit, k].wait_recv()
            owner = 2 * lax.rem(at.z + LAYERS - k, LAYERS) + at.core
            for m in steps:
                part = part_of(unit, whole, at.grp, owner)
                copy = send(
                    part, part, x_send.at[unit, k - 1, m - 1], x_recv.at[unit, k - 1, m - 1],
                    at.along_grp(m),
                )
                from_grp[unit, k, m] = copy
                sends.append(copy)

    for copy in small:
        copy.wait_recv()
    total = part_z[0] + part_z[1] + part_z[2] + part_z[3]
    bias_full[...] = jnp.zeros_like(bias_full)
    for d in range(2 * LAYERS):
        first = 672 * d // 128
        bias_full[first : first + 7, :] += bias_slot[d // 2, d % 2, 0:7, :]
    counts = [counts_ref[g].astype(F32) for g in range(GROUPS)]
    own_count = counts_ref[at.grp].astype(F32)
    share = jnp.full((1, D), GROUPS * own_count) / jnp.full((1, D), sum(counts[1:], counts[0]))

    def put(row, value):
        rows_ref[row : row + 1, :] = value

    def joined(first):
        return jnp.concatenate([bias_full[first + j : first + j + 1, :] for j in range(3)], axis=1)

    for s in range(ROLLOUT):
        for r in range(6):
            mod = jnp.concatenate(
                [total[18 * s + 3 * r + j : 18 * s + 3 * r + j + 1, :] for j in range(3)], axis=1
            )
            put(8 * s + r, mod + joined(24 + 3 * r))
        put(8 * s + 6, share)
        put(8 * s + 7, share)
    put(ROW_BQKV, joined(0))
    put(ROW_BQKV + 1, jnp.zeros((1, D), F32))
    put(ROW_BQKV + 2, joined(3))
    put(ROW_BPROJ, joined(6))
    for j in range(4):
        put(ROW_BUP + j, joined(9 + 3 * j))
    put(ROW_BDOWN, joined(21))
    rows_ref[25:32, :] = jnp.zeros((7, D), F32)

    for unit in range(UNITS):
        whole = wholes[unit]
        for k in steps:
            for m in steps:
                from_grp[unit, k, m].wait_recv()
            owner = 2 * lax.rem(at.z + LAYERS - k, LAYERS) + at.core
            copy = send(
                whole.at[owner], whole.at[owner], s_send.at[unit, k], s_recv.at[unit, k],
                at.sibling(),
            )
            from_sib[unit, k] = copy
            sends.append(copy)
    for copy in from_sib.values():
        copy.wait_recv()
    for own in owns:
        own.wait()
    for copy in sends:
        copy.wait_send()


def gather(start, interval, counts, lead, masters):
    qkv, proj, up, down, ada, bias = masters
    smem = pl.BlockSpec(memory_space=pltpu.SMEM)
    vmem = pl.BlockSpec(memory_space=pltpu.VMEM)
    hbm = pl.BlockSpec(memory_space=pl.ANY)
    dma = pltpu.SemaphoreType.DMA
    wa, wu, wd, rows = pl.pallas_call(
        gather_kernel,
        in_specs=[smem] * 3 + [vmem] * 7,
        out_specs=[hbm, hbm, hbm, vmem],
        out_shape=[
            jax.ShapeDtypeStruct((8, SLAB, FF), BF),
            jax.ShapeDtypeStruct((8, SLAB, FF), BF),
            jax.ShapeDtypeStruct((8, GROUPS, SLAB, PART), BF),
            jax.ShapeDtypeStruct((32, D), F32),
        ],
        scratch_shapes=[
            pltpu.VMEM((SLAB, FF), BF),
            pltpu.VMEM((SLAB, FF), BF),
            pltpu.VMEM((GROUPS, SLAB, PART), BF),
            pltpu.VMEM((D, 8), F32),
            pltpu.VMEM((40, 128), F32),
            pltpu.VMEM((40, 128), F32),
            pltpu.VMEM((LAYERS, 40, 128), F32),
            pltpu.VMEM((LAYERS, 2, 8, 128), F32),
            pltpu.VMEM((48, 128), F32),
            dma((UNITS, 3)), dma((UNITS, 3)), dma((UNITS, 3, 3)), dma((UNITS, 3, 3)),
            dma((UNITS, 4)), dma((UNITS, 4)), dma((UNITS,)), dma((8,)), dma((8,)),
        ],
        compiler_params=pltpu.CompilerParams(collective_id=0, has_side_effects=True),
        name="gather",
    )(
        start, interval, counts, lead, *(m.reshape(-1, 128) for m in (qkv, proj, up, down, ada)),
        jnp.pad(bias, (0, 1024 - bias.shape[0])).reshape(8, 128),
    )
    return (wa.reshape(D, FF), wu.reshape(D, FF), wd.reshape(FF, D), rows)


def reduce_kernel(
    start_ref, interval_ref, lead_ref, vec_ref, ga_ref, gu_ref, gd_ref,
    piece_ref, ada_ref, bias_ref, square_ref,
    own, got_s, sum_s, got_x, sum_x, got_z, pieces, cond_t,
    vec_s, vec_z, vec_g, square_own, square_d, square_g,
    own_sem, s_send, s_recv, x_send, x_recv, z_send, z_recv, a_send, a_recv,
    v_send, v_recv, q_send, q_recv,
):
    at = Place()
    steps = range(1, 4)
    ready = greet(
        [at.sibling()]
        + [at.along_grp(k) for k in steps]
        + [at.along_z(k) for k in steps]
        + [at.across(k) for k in steps]
    )
    grads = (ga_ref, gu_ref, gd_ref)
    sends = []
    owns = []
    for unit in range(UNITS):
        copy = pltpu.make_async_copy(grads[unit].at[:, at.core], own.at[unit], own_sem.at[unit])
        copy.start()
        owns.append(copy)
    ready()
    vec_copy = send(vec_ref, vec_s, v_send.at[0], v_recv.at[0], at.sibling())
    from_sib = [
        send(
            grads[unit].at[:, 1 - at.core], got_s.at[unit], s_send.at[unit], s_recv.at[unit],
            at.sibling(),
        )
        for unit in range(UNITS)
    ]
    sends += [vec_copy] + from_sib
    moments = [start_ref[g] + s for g in range(GROUPS) for s in range(ROLLOUT)]
    intervals = [interval_ref[g] for g in range(GROUPS) for s in range(ROLLOUT)]
    cond_t[...] = jnp.transpose(condition_rows(moments, intervals, lead_ref))

    vec_copy.wait_recv()
    vec_z[at.z] = vec_ref[...] + vec_s[...]
    vec_from_z = [
        send(vec_z.at[at.z], vec_z.at[at.z], v_send.at[k], v_recv.at[k], at.along_z(k))
        for k in steps
    ]
    sends += vec_from_z

    from_grp = {}
    for unit in range(UNITS):
        owns[unit].wait()
        from_sib[unit].wait_recv()

        def add_pair(z, carry):
            for g in range(GROUPS):
                sum_s[unit, z, g] = (
                    own[unit, z, g].astype(F32) + got_s[unit, z, g].astype(F32)
                ).astype(BF)
            return carry

        lax.fori_loop(0, LAYERS, add_pair, 0)
        for k in steps:
            peer = at.along_grp(k)
            copy = send(
                sum_s.at[unit, :, peer[0]], got_x.at[unit, k - 1], x_send.at[unit, k - 1],
                x_recv.at[unit, k - 1], peer,
            )
            from_grp[unit, k] = copy
            sends.append(copy)

    for copy in vec_from_z:
        copy.wait_recv()
    vec_g[at.grp] = vec_z[0] + vec_z[1] + vec_z[2] + vec_z[3]
    vec_from_grp = [
        send(vec_g.at[at.grp], vec_g.at[at.grp], v_send.at[3 + k], v_recv.at[3 + k], at.along_grp(k))
        for k in steps
    ]
    sends += vec_from_grp

    from_z = {}
    for unit in range(UNITS):
        for k in steps:
            from_grp[unit, k].wait_recv()

        def add_four(z, carry):
            value = sum_s[unit, z, at.grp].astype(F32)
            for k in range(3):
                value = value + got_x[unit, k, z].astype(F32)
            sum_x[unit, z] = value.astype(BF)
            return carry

        lax.fori_loop(0, LAYERS, add_four, 0)
        for k in steps:
            peer = at.along_z(k)
            copy = send(
                sum_x.at[unit, lax.rem(at.z + k, LAYERS)], got_z.at[unit, k - 1],
                z_send.at[unit, k - 1], z_recv.at[unit, k - 1], peer,
            )
            from_z[unit, k] = copy
            sends.append(copy)

    for copy in vec_from_grp:
        copy.wait_recv()
    own_cond = cond_t[pl.ds(pl.multiple_of(SLAB * at.dp, 8), SLAB), :]
    columns = [jnp.broadcast_to(own_cond[:, k : k + 1], (SLAB, 128)) for k in range(8)]

    def ada_tile(j, square):
        tile = jnp.zeros((SLAB, 128), F32)
        for g in range(GROUPS):
            for s in range(ROLLOUT):
                tile = tile + columns[ROLLOUT * g + s] * vec_g[g, pl.ds(24 + 18 * s + j, 1), :]
        ada_ref[pl.ds(j, SLAB, stride=18), :] = tile
        return square + col_sum(tile * tile)

    ada_square = lax.fori_loop(0, 18, ada_tile, jnp.zeros((1, 128), F32))
    vec_sum = vec_g[0] + vec_g[1] + vec_g[2] + vec_g[3]
    bias_ref[0:24, :] = vec_sum[0:24]
    bias_ref[24:42, :] = vec_sum[24:42] + vec_sum[42:60]
    bias_ref[42:48, :] = jnp.zeros((6, 128), F32)

    square = 0.25 * ada_square
    from_gather = []
    for unit in range(UNITS):
        for k in steps:
            from_z[unit, k].wait_recv()
        value = sum_x[unit, at.z].astype(F32)
        for k in range(3):
            value = value + got_z[unit, k].astype(F32)
        value = value.astype(BF)
        pieces[unit, at.grp] = value
        for k in steps:
            copy = send(
                pieces.at[unit, at.grp], pieces.at[unit, at.grp], a_send.at[unit, k - 1],
                a_recv.at[unit, k - 1], at.along_grp(k),
            )
            from_gather.append(copy)
            sends.append(copy)
        wide = value.astype(F32)
        wide = col_sum(wide * wide)
        square = square + wide[:, 0:128] + wide[:, 128:256] + wide[:, 256:384]

    square_d[at.dp] = jnp.broadcast_to(square, (8, 128))
    squares = [send(
        square_d.at[at.dp], square_d.at[at.dp], q_send.at[0], q_recv.at[0], at.sibling()
    )]
    for k in steps:
        for index, peer in ((k, at.along_z(k)), (3 + k, at.across(k))):
            squares.append(send(
                square_d.at[at.dp], square_d.at[at.dp], q_send.at[index], q_recv.at[index], peer
            ))
    for copy in squares:
        copy.wait_recv()
    total = square_d[0]
    for d in range(1, 2 * LAYERS):
        total = total + square_d[d]
    square_g[at.grp] = total
    final = [
        send(square_g.at[at.grp], square_g.at[at.grp], q_send.at[6 + k], q_recv.at[6 + k],
             at.along_grp(k))
        for k in steps
    ]
    sends += squares + final
    for copy in final:
        copy.wait_recv()
    bias_sum = bias_ref[...]
    bias_square = col_sum(bias_sum * bias_sum)
    total = square_g[0] + square_g[1] + square_g[2] + square_g[3] + bias_square
    square_ref[...] = jnp.broadcast_to(jnp.sum(total, axis=1, keepdims=True), (8, 128))

    for copy in from_gather:
        copy.wait_recv()
    piece_ref[...] = pieces[...]
    for copy in sends:
        copy.wait_send()


def reduce(start, interval, lead, vec, grads):
    smem = pl.BlockSpec(memory_space=pltpu.SMEM)
    vmem = pl.BlockSpec(memory_space=pltpu.VMEM)
    hbm = pl.BlockSpec(memory_space=pl.ANY)
    dma = pltpu.SemaphoreType.DMA
    slab = (LAYERS, GROUPS, SLAB, PART)
    piece = (SLAB, PART)
    return pl.pallas_call(
        reduce_kernel,
        in_specs=[smem, smem, vmem, vmem, hbm, hbm, hbm],
        out_specs=[vmem] * 4,
        out_shape=[
            jax.ShapeDtypeStruct((UNITS, GROUPS, *piece), BF),
            jax.ShapeDtypeStruct((18 * SLAB, 128), F32),
            jax.ShapeDtypeStruct((48, 128), F32),
            jax.ShapeDtypeStruct((8, 128), F32),
        ],
        scratch_shapes=[
            pltpu.VMEM((UNITS, *slab), BF),
            pltpu.VMEM((UNITS, *slab), BF),
            pltpu.VMEM((UNITS, *slab), BF),
            pltpu.VMEM((UNITS, 3, LAYERS, *piece), BF),
            pltpu.VMEM((UNITS, LAYERS, *piece), BF),
            pltpu.VMEM((UNITS, 3, *piece), BF),
            pltpu.VMEM((UNITS, GROUPS, *piece), BF),
            pltpu.VMEM((D, 8), F32),
            pltpu.VMEM((64, 128), F32),
            pltpu.VMEM((LAYERS, 64, 128), F32),
            pltpu.VMEM((GROUPS, 64, 128), F32),
            pltpu.VMEM((8, 128), F32),
            pltpu.VMEM((8, 8, 128), F32),
            pltpu.VMEM((GROUPS, 8, 128), F32),
            dma((UNITS,)), dma((UNITS,)), dma((UNITS,)),
            dma((UNITS, 3)), dma((UNITS, 3)), dma((UNITS, 3)), dma((UNITS, 3)),
            dma((UNITS, 3)), dma((UNITS, 3)), dma((7,)), dma((7,)), dma((10,)), dma((10,)),
        ],
        compiler_params=pltpu.CompilerParams(collective_id=1, has_side_effects=True),
        name="reduce",
    )(start, interval, lead, vec, *grads)


correction = 1.0 - 0.5**ADAM_STEP
grad_limit = math.sqrt(NPARAM)


def adam(master, first, second, clipped, decay):
    first_new = 0.5 * first + 0.5 * clipped
    second_new = 0.5 * second + 0.5 * clipped * clipped
    update = first_new / correction / (jnp.sqrt(second_new / correction) + adam_eps)
    return (master - learn_rate * (update + decay * master), first_new, second_new)


def adam_kernel(*refs):
    piece_ref, ada_ref, square_ref = refs[:3]
    masters, firsts, seconds = (refs[3:8], refs[8:13], refs[13:18])
    news, first_news, second_news, copies = (refs[18:23], refs[23:28], refs[28:33], refs[33:38])
    flats = refs[38:42]
    norm = jnp.sqrt(square_ref[0:1, :])
    clip = grad_limit / jnp.maximum(norm, grad_limit)
    qkv, proj, up, down = flats
    for g in range(3):
        for j in range(3):
            qkv[pl.ds(3 * g + j, SLAB, stride=9), :] = piece_ref[0, g, :, 128 * j : 128 * j + 128].astype(F32)
    for j in range(3):
        proj[pl.ds(j, SLAB, stride=3), :] = piece_ref[0, 3, :, 128 * j : 128 * j + 128].astype(F32)
    for g in range(GROUPS):
        for j in range(3):
            up[pl.ds(3 * g + j, SLAB, stride=12), :] = piece_ref[1, g, :, 128 * j : 128 * j + 128].astype(F32)
            down[pl.ds(3 * SLAB * g + j, SLAB, stride=3), :] = piece_ref[2, g, :, 128 * j : 128 * j + 128].astype(F32)
    for index, grad in enumerate((qkv, proj, up, down, ada_ref)):
        def chunk(i, carry):
            rows = pl.ds(pl.multiple_of(16 * i, 16), 16)
            new, first, second = adam(
                masters[index][rows, :], firsts[index][rows, :], seconds[index][rows, :],
                grad[rows, :] * clip, 0.1,
            )
            news[index][rows, :] = new
            first_news[index][rows, :] = first
            second_news[index][rows, :] = second
            copies[index][rows, :] = new.astype(BF)
            return carry

        lax.fori_loop(0, grad.shape[0] // 16, chunk, 0, unroll=3)


def update(pieces, ada, square, masters, firsts, seconds):
    flat = lambda arrays: [a.reshape(-1, 128) for a in arrays[:5]]
    masters, firsts, seconds = (flat(masters), flat(firsts), flat(seconds))
    vmem = pl.BlockSpec(memory_space=pltpu.VMEM)
    shapes = [m.shape for m in masters]
    outs = [jax.ShapeDtypeStruct(s, F32) for s in shapes] * 3
    outs += [jax.ShapeDtypeStruct(s, BF) for s in shapes]
    results = pl.pallas_call(
        adam_kernel,
        in_specs=[vmem] * 18,
        out_specs=[vmem] * 20,
        out_shape=outs,
        scratch_shapes=[pltpu.VMEM(s, F32) for s in shapes[:4]],
        name="adam",
    )(pieces, ada, square, *masters, *firsts, *seconds)
    results = [r.reshape(-1) for r in results]
    return (results[0:5], results[5:10], results[10:15], results[15:20])


def block_kernel(
    x_ref, rows_ref, wa_far, wup_far, wdown_far, cot_far,
    y_far, dx_far, ga_far, gu_far, gd_far, vec_ref, p_far,
    wa_ref, wup_ref, wdown_ref, cot_ref, qkv0, qkv1, p_ref, att0, att1, a_ref, f_ref, x1_ref,
    dmid_ref, y_ref, gp_ref, act_ref, datt_ref, dqkv_ref, gqkv, gproj, gup, gdown, turned_ref,
    wide, narrow0, narrow1, bias, blocks, in_sems, p_sems, out_sems,
):
    def copy(src, dst, sem):
        made = pltpu.make_async_copy(src, dst, sem)
        made.start()
        return made

    length = x_ref.shape[0]
    get_wa = copy(wa_far, wa_ref, in_sems.at[0])
    later = [
        copy(wup_far, wup_ref, in_sems.at[1]),
        copy(wdown_far, wdown_ref, in_sems.at[2]),
        copy(cot_far, cot_ref, in_sems.at[3]),
    ]

    def over_rows(body):
        def step(i, carry):
            body(pl.ds(pl.multiple_of(i * ROWS, ROWS), ROWS))
            return carry

        lax.fori_loop(0, length // ROWS, step, 0)

    def columns(h, offset=0):
        return pl.ds(pl.multiple_of(offset + 128 * h, 128), 128)

    def over_pairs(body):
        def step(h, carry):
            body(h)
            return carry

        lax.fori_loop(0, HEADS // 2, step, 0)

    pairs = HEADS // 2

    def save(step, h):
        slot = lax.rem(h, 2)
        return pltpu.make_async_copy(
            p_ref.at[slot], p_far.at[step, pl.ds(2 * h, 2)], p_sems.at[slot]
        )

    def fetch(step, h):
        slot = lax.rem(h, 2)
        return pltpu.make_async_copy(
            p_far.at[step, pl.ds(2 * h, 2)], p_ref.at[slot], p_sems.at[slot]
        )

    def attend(step, qkv, att):
        def body(h):
            @pl.when(h >= 2)
            def _():
                save(step, h - 2).wait()

            attend_pair(
                qkv[:, columns(h)], qkv.at[:, columns(h, D)], qkv[:, columns(h, 2 * D)],
                att.at[:, columns(h)], p_ref.at[lax.rem(h, 2)], turned_ref,
            )
            save(step, h).start()

        over_pairs(body)

    def finish_saves(step):
        for h in range(pairs - 2, pairs):
            save(step, h).wait()

    def attend_back(step, qkv):
        def body(h):
            fetch(step, h).wait()
            attend_back_pair(
                qkv[:, columns(h)], qkv[:, columns(h, D)], qkv.at[:, columns(h, 2 * D)],
                datt_ref[:, columns(h)], p_ref.at[lax.rem(h, 2)],
                dqkv_ref.at[:, columns(h)], dqkv_ref.at[:, columns(h, D)],
                dqkv_ref.at[:, columns(h, 2 * D)], turned_ref,
            )

            @pl.when(h + 2 < pairs)
            def _():
                fetch(step, h + 2).start()

        over_pairs(body)

    get_wa.wait()

    def first(rows):
        qkv0[rows, :] = first_rows(x_ref[rows, :], rows_ref, wa_ref)

    over_rows(first)

    attend(0, qkv0, att0)
    for made in later:
        made.wait()

    def middle(rows):
        middle_rows(
            x_ref.at[rows], att0.at[rows], rows_ref, wa_ref, wup_ref, wdown_ref,
            a_ref.at[rows], gp_ref.at[rows], act_ref.at[rows], f_ref.at[rows], x1_ref.at[rows],
            qkv1.at[rows],
        )

    over_rows(middle)
    finish_saves(0)
    attend(1, qkv1, att1)

    for ref in (gqkv, gproj, gup, gdown, wide, narrow0, narrow1, bias):
        ref[...] = jnp.zeros_like(ref)

    def turn(rows):
        turn_rows(
            x1_ref.at[rows], att1.at[rows], cot_ref.at[rows], rows_ref, wa_ref, wup_ref,
            wdown_ref, y_ref.at[rows], dmid_ref.at[rows], datt_ref.at[rows], gdown, gup, gproj,
            wide, narrow1,
        )

    finish_saves(1)
    for h in range(2):
        fetch(1, h).start()
    over_rows(turn)
    put_y = copy(y_ref, y_far, out_sems.at[0])
    attend_back(1, qkv1)
    for h in range(2):
        fetch(0, h).start()

    def join(rows):
        join_rows(
            dqkv_ref.at[rows], x1_ref.at[rows], x_ref.at[rows], a_ref.at[rows], gp_ref.at[rows],
            act_ref.at[rows], f_ref.at[rows], att0.at[rows], rows_ref, wa_ref, wup_ref, wdown_ref,
            dmid_ref.at[rows], datt_ref.at[rows], gqkv, gdown, gup, gproj, wide, narrow1, narrow0,
            bias,
        )

    over_rows(join)
    share = rows_ref[ROW_SHARE : ROW_SHARE + 1, :]
    for d in range(8):
        rows = slice(SLAB * d, SLAB * (d + 1))
        blocks[0, d, 3] = (gproj[rows, :] * share).astype(BF)
        for g in range(4):
            blocks[1, d, g] = (gup[rows, PART * g : PART * (g + 1)] * share).astype(BF)
            first_row = SLAB * (4 * d + g)
            blocks[2, d, g] = (gdown[first_row : first_row + SLAB, :] * share).astype(BF)
    puts = [copy(blocks.at[1], gu_far, out_sems.at[1]), copy(blocks.at[2], gd_far, out_sems.at[2])]
    attend_back(0, qkv0)

    def last(rows):
        dmid_ref[rows, :] = qkv_back(
            mod_reader(rows_ref, 0), x_ref[rows, :].astype(F32), dmid_ref[rows, :],
            dqkv_ref[rows, :], wa_ref, gqkv, narrow0, bias,
        )

    over_rows(last)
    put_dx = copy(dmid_ref, dx_far, out_sems.at[3])
    for d in range(8):
        rows = slice(SLAB * d, SLAB * (d + 1))
        for g in range(3):
            blocks[0, d, g] = (gqkv[rows, PART * g : PART * (g + 1)] * share).astype(BF)
    puts.append(copy(blocks.at[0], ga_far, out_sems.at[4]))

    def put(first_row, value):
        for j in range(value.shape[1] // 128):
            vec_ref[first_row + j : first_row + j + 1, :] = (
                value[:, 128 * j : 128 * j + 128] * share[:, 0:128]
            )

    put(0, bias[0:1, :D])
    put(3, bias[0:1, 2 * D :])
    put(6, narrow0[6:7, :] + narrow1[6:7, :])
    put(9, wide[0:1, :])
    put(21, narrow0[7:8, :] + narrow1[7:8, :])
    for r in range(6):
        put(24 + 3 * r, narrow0[r : r + 1, :])
        put(42 + 3 * r, narrow1[r : r + 1, :])
    vec_ref[60:64, :] = jnp.zeros((4, 128), F32)
    for made in puts + [put_y, put_dx]:
        made.wait()


def block_pass(inputs, cotangent, rows, wa, wup, wdown):
    length = inputs.shape[0]
    vmem = pl.BlockSpec(memory_space=pltpu.VMEM)
    hbm = pl.BlockSpec(memory_space=pl.ANY)
    blocks = (8, 4, SLAB, PART)
    weights = (ROLLOUT, HEADS, length, length)
    y, dx, ga, gu, gd, vec, _ = pl.pallas_call(
        block_kernel,
        in_specs=[vmem, vmem, hbm, hbm, hbm, hbm],
        out_specs=[hbm, hbm, hbm, hbm, hbm, vmem, hbm],
        out_shape=[
            jax.ShapeDtypeStruct((length, D), F32),
            jax.ShapeDtypeStruct((length, D), F32),
            jax.ShapeDtypeStruct(blocks, BF),
            jax.ShapeDtypeStruct(blocks, BF),
            jax.ShapeDtypeStruct(blocks, BF),
            jax.ShapeDtypeStruct((64, 128), F32),
            jax.ShapeDtypeStruct(weights, BF),
        ],
        scratch_shapes=[
            pltpu.VMEM((D, FF), BF),
            pltpu.VMEM((D, FF), BF),
            pltpu.VMEM((FF, D), BF),
            pltpu.VMEM((length, D), BF),
            pltpu.VMEM((length, 3 * D), BF),
            pltpu.VMEM((length, 3 * D), BF),
            pltpu.VMEM((2, 2, length, length), BF),
            pltpu.VMEM((length, D), BF),
            pltpu.VMEM((length, D), BF),
            *[pltpu.VMEM((length, D), F32)] * 5,
            pltpu.VMEM((length, FF), F32),
            pltpu.VMEM((length, FF), BF),
            pltpu.VMEM((length, D), BF),
            pltpu.VMEM((length, 3 * D), BF),
            pltpu.VMEM((D, 3 * D), F32),
            pltpu.VMEM((D, D), F32),
            pltpu.VMEM((D, FF), F32),
            pltpu.VMEM((FF, D), F32),
            pltpu.VMEM((2, 128, length), BF),
            pltpu.VMEM((8, FF), F32),
            pltpu.VMEM((8, D), F32),
            pltpu.VMEM((8, D), F32),
            pltpu.VMEM((8, 3 * D), F32),
            pltpu.VMEM((UNITS, *blocks), BF),
            pltpu.SemaphoreType.DMA((4,)),
            pltpu.SemaphoreType.DMA((2,)),
            pltpu.SemaphoreType.DMA((5,)),
        ],
        compiler_params=pltpu.CompilerParams(vmem_limit_bytes=67043328),
        name="block",
    )(inputs, rows, wa, wup, wdown, cotangent)
    return (y, dx, ga, gu, gd, vec)


def step_embedding(moment):
    half_width = D // 2
    freqs = jnp.exp(-math.log(10000.0) * jnp.arange(half_width, dtype=F32) / half_width)
    angles = moment[:, None] * freqs[None, :]
    return jnp.concatenate([jnp.sin(angles), jnp.cos(angles)], axis=1)


def all_conditions(group_interval, rollout_start, lead_table):
    chosen = group_interval[:, None] == jnp.arange(INTERVALS)[None, :]
    lead_rows = jnp.sum(jnp.where(chosen[:, :, None], lead_table[None], 0.0), axis=1)
    start = rollout_start.astype(F32)
    rows = [lead_rows + step_embedding(start + offset) for offset in range(ROLLOUT)]
    return jax.nn.silu(jnp.stack(rows, axis=1)).astype(BF)


def plain_gather(group_interval, counts, rollout_start, lead_table, masters):
    low = [master.astype(BF) for master in masters]
    owner = lax.axis_index("dp")
    group_index = lax.axis_index("grp")
    own_rows = D // lax.axis_size("dp")
    counts = counts.astype(F32)
    share = lax.axis_size("grp") * counts / jnp.sum(counts)
    share = lax.dynamic_index_in_dim(share, group_index, keepdims=False)
    conditions = all_conditions(group_interval, rollout_start, lead_table)
    owner_columns = lax.dynamic_slice_in_dim(conditions, owner * own_rows, own_rows, axis=2)
    own_condition = lax.dynamic_index_in_dim(owner_columns, group_index, keepdims=False)
    modulation = lax.psum(dot(own_condition, low[4].reshape(own_rows, 6 * D)), "dp")
    qkv, proj, up, down, bias = [
        lax.all_gather(low[index], "dp", axis=0, tiled=True) for index in (0, 1, 2, 3, 5)
    ]
    bias = bias.astype(F32)
    modulation = modulation + bias[4 * D + FF :][None]
    share_rows = jnp.broadcast_to(share, (ROLLOUT, 2, D))
    mods = jnp.concatenate([modulation.reshape(ROLLOUT, 6, D), share_rows], axis=1).reshape(-1, D)
    rows = jnp.concatenate(
        [mods, bias[:D][None], jnp.zeros((1, D), F32), bias[D : 4 * D + FF].reshape(-1, D),
         jnp.zeros((7, D), F32)]
    )
    wa = jnp.concatenate([qkv.reshape(D, 3 * D), proj.reshape(D, D)], axis=1)
    return (wa, up.reshape(D, FF), down.reshape(FF, D), rows, owner_columns)


def plain_update(owner_columns, vec, blocks, masters, firsts, seconds):
    owner = lax.axis_index("dp")
    vec = vec.reshape(-1)
    split = 4 * D + FF
    dmod = vec[split : split + ROLLOUT * 6 * D].reshape(ROLLOUT, 6 * D)
    dmod_all = lax.all_gather(lax.psum(dmod, "dp"), "grp")
    bias_sum = lax.psum(vec[:split], ("grp", "dp"))
    bias_sum = jnp.concatenate([bias_sum, jnp.sum(dmod_all, axis=(0, 1))])
    bias_rows = masters[5].shape[0]
    bias_grad = lax.dynamic_slice_in_dim(bias_sum, owner * bias_rows, bias_rows)
    ada_grad = jnp.einsum(
        "gsr,gsc->rc", owner_columns.astype(F32), dmod_all, precision=lax.Precision.HIGHEST
    )
    flat_a, flat_up = [
        block.transpose(0, 2, 1, 3).reshape(D, FF) for block in blocks[:2]
    ]
    flat = [flat_a[:, : 3 * D], flat_a[:, 3 * D :], flat_up, blocks[2]]
    shares = []
    for grad in flat:
        summed = lax.psum(grad.reshape(-1), "grp").astype(F32)
        shares.append(lax.psum_scatter(summed, "dp", scatter_dimension=0, tiled=True))
    shares = shares + [ada_grad.reshape(-1), bias_grad]
    local_square = sum((jnp.sum(piece * piece) for piece in shares))
    grad_norm = jnp.sqrt(lax.psum(local_square, "dp"))
    clip = grad_limit / jnp.maximum(grad_norm, grad_limit)
    decays = [0.1, 0.1, 0.1, 0.1, 0.1, 0.0]
    results = [
        adam(master, first, second, grad * clip, decay)
        for master, first, second, grad, decay in zip(masters, firsts, seconds, shares, decays)
    ]
    news, first_news, second_news = zip(*results)
    return (grad_norm, *news, *first_news, *second_news, *(new.astype(BF) for new in news))


def per_device(
    inputs,
    cotangent,
    group_interval,
    sample_counts,
    rollout_start,
    lead_table,
    *state,
):
    masters, firsts, seconds = (state[0:6], state[6:12], state[12:18])
    owners = lax.axis_size("dp")
    fits = owners == 2 * LAYERS and lax.axis_size("grp") == GROUPS
    if fits:
        wa, wup, wdown, rows = gather(
            rollout_start, group_interval, sample_counts, lead_table, masters
        )
    else:
        wa, wup, wdown, rows, owner_columns = plain_gather(
            group_interval, sample_counts, rollout_start, lead_table, masters
        )
    result, input_grad, ga, gu, gd, vec = block_pass(inputs, cotangent, rows, wa, wup, wdown)
    if not fits:
        rest = plain_update(owner_columns, vec, (ga, gu, gd), masters, firsts, seconds)
        return (result, input_grad, *rest)
    pieces, ada_grad, bias_sum, square = reduce(
        rollout_start, group_interval, lead_table, vec,
        [grad.reshape(LAYERS, 2, GROUPS, SLAB, PART) for grad in (ga, gu, gd)],
    )
    news, first_news, second_news, copies = update(
        pieces, ada_grad, square, masters, firsts, seconds
    )
    grad_norm = jnp.sqrt(square[0, 0])
    clip = grad_limit / jnp.maximum(grad_norm, grad_limit)
    bias_rows = masters[5].shape[0]
    bias_grad = lax.dynamic_slice_in_dim(
        bias_sum.reshape(-1), lax.axis_index("dp") * bias_rows, bias_rows
    )
    new, first, second = adam(masters[5], firsts[5], seconds[5], bias_grad * clip, 0.0)
    return (
        result, input_grad, grad_norm, *news, new, *first_news, first, *second_news, second,
        *copies, new.astype(BF),
    )


def solution(mesh):
    rows = P(("grp", "dp"), None)
    return jax.shard_map(
        per_device,
        mesh=mesh,
        in_specs=(rows, rows, P(), P(), P(), P(), *[P("dp")] * 18),
        out_specs=(rows, rows, P(), *[P("dp")] * 24),
        check_vma=False,
    )
```

```python
import functools
import math

import jax
import jax.numpy as jnp
from jax import lax
from jax.experimental import pallas as pl
from jax.experimental.pallas import tpu as pltpu
from jax.sharding import PartitionSpec as P

D = 384
HEADS = 6
FF = 1536
ROLLOUT = 2
INTERVALS = 3
ADAM_STEP = 10
HEAD_DIM = 64
NPARAM = 2659584

norm_eps = 1e-06
learn_rate = 0.05
adam_eps = 1e-08

BF = jnp.bfloat16
F32 = jnp.float32
NN = (((1,), (0,)), ((), ()))
NT = (((1,), (1,)), ((), ()))
TN = (((0,), (0,)), ((), ()))

ROWS = 256
SLAB = 48
PART = 384
ROW_SHARE = 6
ROW_BQKV, ROW_BPROJ, ROW_BUP, ROW_BDOWN = 16, 19, 20, 24
SHIFT1, SCALE1, GATE1, SHIFT2, SCALE2, GATE2 = range(6)


def dot(left, right, dims=NN):
    return lax.dot_general(left, right, dims, preferred_element_type=F32)


def layer_norm(stream):
    centred = stream - jnp.mean(stream, axis=-1, keepdims=True)
    inverse = lax.rsqrt(jnp.mean(centred * centred, axis=-1, keepdims=True) + norm_eps)
    return (centred * inverse, inverse)


def norm_back(normed, inverse, grad_out):
    mean_grad = jnp.mean(grad_out, axis=-1, keepdims=True)
    mean_prod = jnp.mean(grad_out * normed, axis=-1, keepdims=True)
    return inverse * (grad_out - mean_grad - normed * mean_prod)


def col_sum(value):
    return jnp.sum(value, axis=0, keepdims=True)


def modulated(normed, mods, scale_row, shift_row):
    return (normed * (1.0 + mods(scale_row)) + mods(shift_row)).astype(BF)


def mod_reader(mod_ref, step):
    return lambda row: mod_ref[pl.ds(8 * step + row, 1), :]


def gelu_pair(value):
    cdf = 0.5 + 0.5 * lax.erf(value * (2.0**-0.5))
    density = jnp.exp(-0.5 * value * value) * (1.0 / math.sqrt(2.0 * math.pi))
    return (value * cdf, cdf + value * density)


def side_by_side(ref, first, count):
    return jnp.concatenate([ref[row : row + 1, :] for row in range(first, first + count)], axis=1)


def first_rows(x, rows_ref, wa_ref):
    normed, _ = layer_norm(x.astype(F32))
    hidden = modulated(normed, mod_reader(rows_ref, 0), SCALE1, SHIFT1)
    qkv = dot(hidden, wa_ref[:, : 3 * D]) + side_by_side(rows_ref, ROW_BQKV, 3)
    return qkv.astype(BF)


def middle_rows(
    x_ref, att_ref, rows_ref, wa_ref, wup_ref, wdown_ref,
    a_refs, gp_ref, act_refs, f_ref, next_ref, qkv_ref,
):
    mods = mod_reader(rows_ref, 0)
    later = mod_reader(rows_ref, 1)
    branch = dot(att_ref[...], wa_ref[:, 3 * D :]) + mods(ROW_BPROJ)
    for part, ref in enumerate(a_refs):
        ref[...] = branch[:, 128 * part : 128 * (part + 1)]
    middle = x_ref[...].astype(F32) + mods(GATE1) * branch
    normed, _ = layer_norm(middle)
    hidden = modulated(normed, mods, SCALE2, SHIFT2)
    upward = dot(hidden, wup_ref[...]) + side_by_side(rows_ref, ROW_BUP, 4)
    act, slope = gelu_pair(upward)
    gp_ref[...] = slope
    act = act.astype(BF)
    for part, ref in enumerate(act_refs):
        ref[...] = act[:, PART * part : PART * (part + 1)]
    branch = dot(act, wdown_ref[...]) + mods(ROW_BDOWN)
    f_ref[...] = branch
    stream = middle + mods(GATE2) * branch
    next_ref[...] = stream
    normed, _ = layer_norm(stream)
    hidden = modulated(normed, later, SCALE1, SHIFT1)
    qkv = dot(hidden, wa_ref[:, : 3 * D]) + side_by_side(rows_ref, ROW_BQKV, 3)
    qkv_ref[...] = qkv.astype(BF)


def ffn_back(
    mods, grad, branch_two, act, slope, normed, inverse, hidden, branch_one, att,
    wa_ref, wup_ref, wdown_ref, gdown_ref, gup_ref, gproj_ref, wide_ref, narrow_ref,
    dmid_ref, datt_ref,
):
    df = (mods(GATE2) * grad).astype(BF)
    narrow_ref[pl.ds(GATE2, 1), :] += col_sum(grad * branch_two)
    narrow_ref[pl.ds(7, 1), :] += col_sum(df.astype(F32))
    gdown_ref[...] += dot(act, df, TN)
    dact = dot(df, wdown_ref[...], NT)
    du = (dact * slope).astype(BF)
    wide_ref[pl.ds(0, 1), :] += col_sum(du.astype(F32))
    gup_ref[...] += dot(hidden, du, TN)
    dh = dot(du, wup_ref[...], NT)
    narrow_ref[pl.ds(SHIFT2, 1), :] += col_sum(dh)
    narrow_ref[pl.ds(SCALE2, 1), :] += col_sum(dh * normed)
    dmid = grad + norm_back(normed, inverse, dh * (1.0 + mods(SCALE2)))
    dmid_ref[...] = dmid
    da = (mods(GATE1) * dmid).astype(BF)
    narrow_ref[pl.ds(GATE1, 1), :] += col_sum(dmid * branch_one)
    narrow_ref[pl.ds(6, 1), :] += col_sum(da.astype(F32))
    gproj_ref[...] += dot(att, da, TN)
    datt_ref[...] = dot(da, wa_ref[:, 3 * D :], NT).astype(BF)


def turn_rows(
    x_ref, att_ref, cot_ref, rows_ref, wa_ref, wup_ref, wdown_ref,
    out_ref, dmid_ref, datt_ref, gdown_ref, gup_ref, gproj_ref, wide_ref, narrow_ref,
):
    mods = mod_reader(rows_ref, 1)
    shared = mod_reader(rows_ref, 0)
    att = att_ref[...]
    branch_one = dot(att, wa_ref[:, 3 * D :]) + shared(ROW_BPROJ)
    middle = x_ref[...] + mods(GATE1) * branch_one
    normed, inverse = layer_norm(middle)
    hidden = modulated(normed, mods, SCALE2, SHIFT2)
    upward = dot(hidden, wup_ref[...]) + side_by_side(rows_ref, ROW_BUP, 4)
    act, slope = gelu_pair(upward)
    act = act.astype(BF)
    branch_two = dot(act, wdown_ref[...]) + shared(ROW_BDOWN)
    out_ref[...] = middle + mods(GATE2) * branch_two
    ffn_back(
        mods, cot_ref[...].astype(F32), branch_two, act, slope, normed, inverse, hidden,
        branch_one, att, wa_ref, wup_ref, wdown_ref, gdown_ref, gup_ref, gproj_ref,
        wide_ref, narrow_ref, dmid_ref, datt_ref,
    )


def qkv_back(mods, stream, dmid, dqkv, wa_ref, gqkv_ref, narrow_ref, bias_ref):
    normed, inverse = layer_norm(stream)
    hidden = modulated(normed, mods, SCALE1, SHIFT1)
    bias_ref[pl.ds(0, 1), :] += col_sum(dqkv.astype(F32))
    gqkv_ref[...] += dot(hidden, dqkv, TN)
    dh = dot(dqkv, wa_ref[:, : 3 * D], NT)
    narrow_ref[pl.ds(SHIFT1, 1), :] += col_sum(dh)
    narrow_ref[pl.ds(SCALE1, 1), :] += col_sum(dh * normed)
    return dmid + norm_back(normed, inverse, dh * (1.0 + mods(SCALE1)))


def join_rows(
    dqkv_ref, x1_ref, x0_ref, a_refs, gp_ref, act_refs, f_ref, att_ref,
    rows_ref, wa_ref, wup_ref, wdown_ref,
    dmid_ref, datt_ref, gqkv_ref, gdown_ref, gup_ref, gproj_ref, wide_ref, narrow1_ref,
    narrow_ref, bias_ref,
):
    grad = qkv_back(
        mod_reader(rows_ref, 1), x1_ref[...], dmid_ref[...], dqkv_ref[...], wa_ref, gqkv_ref,
        narrow1_ref, bias_ref,
    )
    mods = mod_reader(rows_ref, 0)
    branch_one = jnp.concatenate([ref[...] for ref in a_refs], axis=1)
    middle = x0_ref[...].astype(F32) + mods(GATE1) * branch_one
    normed, inverse = layer_norm(middle)
    hidden = modulated(normed, mods, SCALE2, SHIFT2)
    ffn_back(
        mods, grad, f_ref[...], jnp.concatenate([ref[...] for ref in act_refs], axis=1), gp_ref[...], normed, inverse, hidden,
        branch_one, att_ref[...], wa_ref, wup_ref, wdown_ref, gdown_ref, gup_ref, gproj_ref,
        wide_ref, narrow_ref, dmid_ref, datt_ref,
    )


def head_lanes(rows):
    lane = lax.broadcasted_iota(jnp.int32, (rows, 2 * HEAD_DIM), 1)
    return (lane < HEAD_DIM, lane >= HEAD_DIM)


def turned_heads(rows_f32, out_ref):
    turned = jnp.transpose(rows_f32)
    row = lax.broadcasted_iota(jnp.int32, turned.shape, 0)
    out_ref[0] = jnp.where(row < HEAD_DIM, turned, 0.0).astype(BF)
    out_ref[1] = jnp.where(row >= HEAD_DIM, turned, 0.0).astype(BF)


score_scale = HEAD_DIM**-0.5


def attend_pair(q, k_ref, v, o_ref, p_ref, vt_ref):
    turned_heads(v.astype(F32), vt_ref)
    queries = q * BF(score_scale)
    mixed = None
    for half, lanes in enumerate(head_lanes(queries.shape[0])):
        scores = dot(k_ref[...], jnp.where(lanes, queries, BF(0)), NT)
        top = jnp.max(scores, axis=0, keepdims=True)
        weights = jnp.exp(scores - top)
        total = jnp.sum(weights, axis=0, keepdims=True)
        low = (weights * (1.0 / total)).astype(BF)
        p_ref[half] = low
        part = dot(vt_ref[half], low)
        mixed = part if mixed is None else mixed + part
    o_ref[...] = jnp.transpose(mixed).astype(BF)


def attend_back_pair(q, k, v_ref, grads, p_ref, dq_ref, dk_ref, dv_ref, kt_ref):
    turned_heads(k.astype(F32) * score_scale, kt_ref)
    queries = q * BF(score_scale)
    dq_turned, dk, dv = (None, None, None)
    for half, lanes in enumerate(head_lanes(queries.shape[0])):
        grad = jnp.where(lanes, grads, BF(0))
        query = jnp.where(lanes, queries, BF(0))
        low = p_ref[half]
        weight_grad = dot(v_ref[...], grad, NT)
        weights = low.astype(F32)
        delta = jnp.sum(weights * weight_grad, axis=0, keepdims=True)
        score_grad = (weights * (weight_grad - delta)).astype(BF)
        parts = (dot(kt_ref[half], score_grad), dot(score_grad, query), dot(low, grad))
        if half == 0:
            dq_turned, dk, dv = parts
        else:
            dq_turned, dk, dv = (dq_turned + parts[0], dk + parts[1], dv + parts[2])
    dq_ref[...] = jnp.transpose(dq_turned).astype(BF)
    dk_ref[...] = dk.astype(BF)
    dv_ref[...] = dv.astype(BF)


MESH_ID = pl.DeviceIdType.MESH
GROUPS = 4
LAYERS = 4
UNITS = 3
HALF = 768


class Place:
    def __init__(self):
        self.grp = lax.axis_index("grp")
        self.dp = lax.axis_index("dp")
        self.z = self.dp // 2
        self.core = self.dp % 2

    def sibling(self):
        return (self.grp, 2 * self.z + 1 - self.core)

    def along_grp(self, step):
        return (lax.rem(self.grp + step, GROUPS), self.dp)

    def along_z(self, step):
        return (self.grp, 2 * lax.rem(self.z + step, LAYERS) + self.core)

    def across(self, step):
        return (self.grp, 2 * lax.rem(self.z + step, LAYERS) + 1 - self.core)


def greet(peers):
    barrier = pltpu.get_barrier_semaphore()
    for peer in peers:
        pl.semaphore_signal(barrier, inc=1, device_id=peer, device_id_type=MESH_ID)
    return lambda: pl.semaphore_wait(barrier, len(peers))


def remote(src, dst, sems, index, peer):
    send_sem, recv_sem = sems
    return pltpu.make_async_remote_copy(
        src_ref=src, dst_ref=dst, send_sem=send_sem.at[index], recv_sem=recv_sem.at[index],
        device_id=peer, device_id_type=MESH_ID,
    )


def condition_rows(moments, intervals, lead_ref):
    shape = (8, D)
    row = lax.broadcasted_iota(jnp.int32, shape, 0)
    lane = lax.broadcasted_iota(jnp.int32, shape, 1)
    moment = jnp.zeros(shape, F32)
    chosen = jnp.zeros(shape, jnp.int32)
    for index, (value, interval) in enumerate(zip(moments, intervals)):
        moment = jnp.where(row == index, value.astype(F32), moment)
        chosen = jnp.where(row == index, interval, chosen)
    lead = jnp.zeros(shape, F32)
    for choice in range(INTERVALS):
        picked = jnp.broadcast_to(lead_ref[choice : choice + 1, :], shape)
        lead = jnp.where(chosen == choice, picked, lead)
    half_width = D // 2
    place = jnp.where(lane < half_width, lane, lane - half_width).astype(F32)
    angles = moment * jnp.exp(place * (-math.log(10000.0) / half_width))
    wave = jnp.where(lane < half_width, jnp.sin(angles), jnp.cos(angles))
    condition = lead + wave
    return (condition / (1.0 + jnp.exp(-condition))).astype(BF).astype(F32)


def span(start, size):
    return pl.ds(pl.multiple_of(start, SLAB), size)


def local(src, dst, sem):
    made = pltpu.make_async_copy(src, dst, sem)
    made.start()
    return made


class Alone:
    def __init__(self, refs):
        self.refs = refs

    def begin(self):
        r = self.refs
        sems = r.in_sems
        first = [local(r.wa_far, r.wa, sems.at[0]), local(r.rows_far, r.rows, sems.at[3])]
        self.later = [local(r.wup_far, r.wup, sems.at[1]), local(r.wdown_far, r.wdown, sems.at[2])]
        for made in first:
            made.wait()

    def after_first(self):
        pass

    def after_attend_pair(self, h):
        pass

    def before_middle(self):
        for made in self.later:
            made.wait()

    def after_join(self):
        fill_blocks(self.refs, (1, 2))

    def after_back_pair(self, h):
        pass

    def after_last(self):
        r = self.refs
        fill_blocks(r, (0,))
        fill_vec(r)
        puts = [local(r.blocks, r.blocks_far, r.in_sems.at[0]), local(r.vec, r.vec_far, r.in_sems.at[1])]
        for made in puts:
            made.wait()


def fill_blocks(refs, units):
    share = refs.rows[ROW_SHARE : ROW_SHARE + 1, :]
    for d in range(8):
        own = slice(SLAB * d, SLAB * (d + 1))
        for g in range(4):
            columns = slice(PART * g, PART * (g + 1))
            first = HALF * (d % 2) + 4 * SLAB * g + SLAB * (d // 2)
            there = slice(first, first + SLAB)
            for unit in units:
                if unit == 0:
                    value = refs.gqkv[own, columns] if g < 3 else refs.gproj[own, :]
                elif unit == 1:
                    value = refs.gup[own, columns]
                else:
                    value = refs.gdown[SLAB * (4 * d + g) : SLAB * (4 * d + g + 1), :]
                refs.blocks[unit, there, :] = (value * share).astype(BF)


def fill_vec(refs):
    share = refs.rows[ROW_SHARE : ROW_SHARE + 1, :]

    def put(first_row, value):
        for j in range(value.shape[1] // 128):
            refs.vec[first_row + j : first_row + j + 1, :] = (
                value[:, 128 * j : 128 * j + 128] * share[:, 0:128]
            )

    bias, wide, narrow0, narrow1 = (refs.bias, refs.wide, refs.narrow0, refs.narrow1)
    put(0, bias[0:1, :D])
    put(3, bias[0:1, 2 * D :])
    put(6, narrow0[6:7, :] + narrow1[6:7, :])
    put(9, wide[0:1, :])
    put(21, narrow0[7:8, :] + narrow1[7:8, :])
    for r in range(6):
        put(24 + 3 * r, narrow0[r : r + 1, :])
        put(42 + 3 * r, narrow1[r : r + 1, :])
    refs.vec[60:64, :] = jnp.zeros((4, 128), F32)


class Together:
    steps = range(1, 4)

    def __init__(self, refs):
        self.refs = refs
        self.at = Place()

    def start(self, copy):
        copy.start()


    def whole(self, unit):
        return (self.refs.wa, self.refs.wup, self.refs.wdown)[unit]

    def part(self, unit, owner, grp):
        if unit == 2:
            return self.whole(2).at[span(4 * SLAB * owner + SLAB * grp, SLAB), :]
        return self.whole(unit).at[
            span(SLAB * owner, SLAB), pl.ds(pl.multiple_of(PART * grp, 128), PART)
        ]

    def slab(self, unit, owner):
        if unit == 2:
            return self.whole(2).at[span(4 * SLAB * owner, 4 * SLAB), :]
        return self.whole(unit).at[span(SLAB * owner, SLAB), :]

    def owner(self, k):
        return 2 * lax.rem(self.at.z + LAYERS - k, LAYERS) + self.at.core

    def gather_z(self, unit, k):
        own = self.part(unit, self.at.dp, self.at.grp)
        return remote(own, own, self.refs.gz, (unit, k - 1), self.at.along_z(k))

    def gather_grp(self, unit, k, m):
        part = self.part(unit, self.owner(k), self.at.grp)
        return remote(part, part, self.refs.gx, (unit, k - 1, m - 1), self.at.along_grp(m))

    def gather_sibling(self, unit, k):
        slab = self.slab(unit, self.owner(k) if k else self.at.dp)
        return remote(slab, slab, self.refs.gs, (unit, k), self.at.sibling())

    def launch(self, unit):
        for k in self.steps:
            self.start(self.gather_z(unit, k))
        self.start(self.gather_sibling(unit, 0))

    def forward_grp(self, unit):
        for k in self.steps:
            self.gather_z(unit, k).wait_recv()
            for m in self.steps:
                self.start(self.gather_grp(unit, k, m))

    def forward_sibling(self, unit):
        for k in self.steps:
            for m in self.steps:
                self.gather_grp(unit, k, m).wait_recv()
            self.start(self.gather_sibling(unit, k))

    def finish_sibling(self, unit):
        for k in range(4):
            self.gather_sibling(unit, k).wait_recv()

    def small(self, index):
        r, at = (self.refs, self.at)
        if index == 0:
            return remote(r.part_own, r.part_sib, r.gm, 0, at.sibling())
        if index == 1:
            own = r.bias_slot.at[at.z, at.core]
            return remote(own, own, r.gm, 1, at.sibling())
        if index < 5:
            own = r.part_z.at[at.z]
            return remote(own, own, r.gm, index, at.along_z(index - 1))
        own = r.bias_slot.at[at.z]
        return remote(own, own, r.gm, index, at.along_z(index - 4))

    def begin(self):
        r, at, steps = (self.refs, self.at, self.steps)
        stage = {
            "qkv": r.a.at[0:432], "proj": r.a.at[432:576], "ada": r.a.at[1728:2592],
            "up": r.a.at[576:1152], "down": r.a.at[1152:1728],
        }
        loads = {
            name: local(r.masters[name], stage[name], r.in_sems.at[index])
            for index, name in enumerate(stage)
        }
        ready = greet(
            [at.sibling()]
            + [at.along_grp(k) for k in steps]
            + [at.along_z(k) for k in steps]
            + [at.across(k) for k in steps]
        )

        def fill(unit, source, count, offset, first=0):
            for j in range(count):
                value = source[pl.ds(first + j, SLAB, stride=count), :].astype(BF)
                where = offset + 128 * j
                if unit == 2:
                    rows = span(4 * SLAB * at.dp + offset, SLAB)
                    where = 128 * j
                else:
                    rows = span(SLAB * at.dp, SLAB)
                self.whole(unit)[rows, where : where + 128] = value

        loads["qkv"].wait()
        fill(0, stage["qkv"], 9, 0)
        loads["proj"].wait()
        fill(0, stage["proj"], 3, 3 * D)
        ready()
        self.launch(0)

        moment, interval = (r.start[at.grp], r.interval[at.grp])
        r.cond_t[...] = jnp.transpose(
            condition_rows([moment + s for s in range(ROLLOUT)], [interval] * ROLLOUT, r.lead)
        )
        own_cond = r.cond_t[span(SLAB * at.dp, SLAB), :]
        columns = [jnp.broadcast_to(own_cond[:, s : s + 1], (SLAB, 128)) for s in range(ROLLOUT)]
        loads["ada"].wait()
        for j in range(18):
            rows = stage["ada"][pl.ds(j, SLAB, stride=18), :].astype(BF).astype(F32)
            for s in range(ROLLOUT):
                r.part_own[18 * s + j : 18 * s + j + 1, :] = col_sum(rows * columns[s])
        r.part_own[36:40, :] = jnp.zeros((4, 128), F32)
        lane = lax.broadcasted_iota(jnp.int32, (8, 128), 1)
        shift = lax.rem(32 * at.dp, 128)
        turned = pltpu.roll(r.bias_own[...].astype(BF).astype(F32), shift, axis=1)
        above = pltpu.roll(turned, 1, axis=0)
        r.bias_slot[at.z, at.core] = jnp.where(lane >= shift, turned, above)
        self.start(self.small(0))
        self.start(self.small(1))

        loads["up"].wait()
        fill(1, stage["up"], 12, 0)
        loads["down"].wait()
        for g in range(GROUPS):
            fill(2, stage["down"], 3, SLAB * g, 3 * SLAB * g)

        self.small(0).wait_recv()
        self.small(1).wait_recv()
        r.part_z[at.z] = r.part_own[...] + r.part_sib[...]
        for index in range(2, 8):
            self.start(self.small(index))
        self.forward_grp(0)
        self.launch(1)
        self.launch(2)

        for index in range(2, 8):
            self.small(index).wait_recv()
        total = r.part_z[0] + r.part_z[1] + r.part_z[2] + r.part_z[3]
        r.bias_full[...] = jnp.zeros_like(r.bias_full)
        for d in range(2 * LAYERS):
            first = 672 * d // 128
            r.bias_full[first : first + 7, :] += r.bias_slot[d // 2, d % 2, 0:7, :]
        counts = [r.counts[g].astype(F32) for g in range(GROUPS)]
        own_count = r.counts[at.grp].astype(F32)
        share = jnp.full((1, D), GROUPS * own_count) / jnp.full((1, D), sum(counts[1:], counts[0]))

        def put(row, value):
            r.rows[row : row + 1, :] = value

        def joined(first):
            return jnp.concatenate(
                [r.bias_full[first + j : first + j + 1, :] for j in range(3)], axis=1
            )

        for s in range(ROLLOUT):
            for row in range(6):
                first = 18 * s + 3 * row
                mod = jnp.concatenate([total[first + j : first + j + 1, :] for j in range(3)], axis=1)
                put(8 * s + row, mod + joined(24 + 3 * row))
            put(8 * s + 6, share)
            put(8 * s + 7, share)
        put(ROW_BQKV, joined(0))
        put(ROW_BQKV + 1, jnp.zeros((1, D), F32))
        put(ROW_BQKV + 2, joined(3))
        put(ROW_BPROJ, joined(6))
        for j in range(4):
            put(ROW_BUP + j, joined(9 + 3 * j))
        put(ROW_BDOWN, joined(21))
        r.rows[25:32, :] = jnp.zeros((7, D), F32)
        self.forward_sibling(0)
        self.finish_sibling(0)

    def after_first(self):
        self.forward_grp(1)
        self.forward_grp(2)

    def after_attend_pair(self, h):
        @pl.when(h == 1)
        def _():
            self.forward_sibling(1)

    def before_middle(self):
        self.forward_sibling(2)
        self.finish_sibling(1)
        self.finish_sibling(2)


    def got(self, unit, name, k=1):
        first = {"sib": 0, "grp": HALF, "z": HALF + 12 * SLAB, "piece": HALF + 15 * SLAB}[name]
        first += {"sib": 0, "grp": 4 * SLAB, "z": SLAB, "piece": 0}[name] * (k - 1)
        size = {"sib": HALF, "grp": 4 * SLAB, "z": SLAB, "piece": 4 * SLAB}[name]
        if unit == 0:
            if name in ("sib", "piece"):
                first = 0 if name == "sib" else HALF
                return self.refs.att0.at[first : first + size]
            first += 2 * 35 * SLAB - HALF
        else:
            first += 35 * SLAB * (unit - 1)
        return self.refs.act.at[first : first + size]

    def mine(self, unit):
        return self.refs.blocks.at[unit, span(HALF * self.at.core, HALF), :]

    def sum_sibling(self, unit):
        src = self.refs.blocks.at[unit, span(HALF * (1 - self.at.core), HALF), :]
        return remote(src, self.got(unit, "sib"), self.refs.rs, unit, self.at.sibling())

    def sum_grp(self, unit, k):
        peer = self.at.along_grp(k)
        src = self.mine(unit).at[span(4 * SLAB * peer[0], 4 * SLAB), :]
        return remote(src, self.got(unit, "grp", k), self.refs.rx, (unit, k - 1), peer)

    def sum_z(self, unit, k):
        there = lax.rem(self.at.z + k, LAYERS)
        src = self.mine(unit).at[span(4 * SLAB * self.at.grp + SLAB * there, SLAB), :]
        return remote(src, self.got(unit, "z", k), self.refs.rz, (unit, k - 1), self.at.along_z(k))

    def share_piece(self, unit, k):
        own = self.got(unit, "piece").at[span(SLAB * self.at.grp, SLAB), :]
        return remote(own, own, self.refs.ra, (unit, k - 1), self.at.along_grp(k))

    def add_sibling(self, unit):
        self.sum_sibling(unit).wait_recv()
        mine, got = (self.mine(unit), self.got(unit, "sib"))

        def add(i, carry):
            rows = span(SLAB * i, SLAB)
            mine[rows, :] = (mine[rows, :].astype(F32) + got[rows, :].astype(F32)).astype(BF)
            return carry

        lax.fori_loop(0, 16, add, 0)
        for k in self.steps:
            self.start(self.sum_grp(unit, k))

    def add_grp(self, unit):
        for k in self.steps:
            self.sum_grp(unit, k).wait_recv()
        mine = self.mine(unit).at[span(4 * SLAB * self.at.grp, 4 * SLAB), :]

        def add(i, carry):
            rows = span(SLAB * i, SLAB)
            value = mine[rows, :].astype(F32)
            for k in self.steps:
                value = value + self.got(unit, "grp", k)[rows, :].astype(F32)
            mine[rows, :] = value.astype(BF)
            return carry

        lax.fori_loop(0, 4, add, 0)
        for k in self.steps:
            self.start(self.sum_z(unit, k))

    def add_z(self, unit):
        for k in self.steps:
            self.sum_z(unit, k).wait_recv()
        mine = self.mine(unit).at[span(4 * SLAB * self.at.grp + SLAB * self.at.z, SLAB), :]
        value = mine[...].astype(F32)
        for k in self.steps:
            value = value + self.got(unit, "z", k)[...].astype(F32)
        value = value.astype(BF)
        self.got(unit, "piece")[span(SLAB * self.at.grp, SLAB), :] = value
        for k in self.steps:
            self.start(self.share_piece(unit, k))
        value = value.astype(F32)
        squares = col_sum(value * value)
        return squares[:, 0:128] + squares[:, 128:256] + squares[:, 256:384]

    def after_join(self):
        r, at = (self.refs, self.at)
        for peer in (
            [at.sibling()]
            + [at.along_grp(k) for k in self.steps]
            + [at.along_z(k) for k in self.steps]
        ):
            pl.semaphore_signal(r.joined, inc=1, device_id=peer, device_id_type=MESH_ID)
        fill_blocks(r, (1, 2))
        pl.semaphore_wait(r.joined, 7)
        self.start(self.sum_sibling(1))
        self.start(self.sum_sibling(2))

    def after_back_pair(self, h):
        @pl.when(h == 0)
        def _():
            self.add_sibling(1)
            self.add_sibling(2)

    def small_sum(self, index):
        r, at = (self.refs, self.at)
        if index == 0:
            return remote(r.vec, r.vec_sib, r.rv, 0, at.sibling())
        if index < 4:
            own = r.vec_z.at[at.z]
            return remote(own, own, r.rv, index, at.along_z(index))
        own = r.vec_g.at[at.grp]
        return remote(own, own, r.rv, index, at.along_grp(index - 3))

    def square_sum(self, index):
        r, at = (self.refs, self.at)
        if index < 7:
            peer = at.sibling()
            if index > 0:
                peer = at.along_z(index) if index < 4 else at.across(index - 3)
            own = r.square_d.at[at.dp]
        else:
            peer = at.along_grp(index - 6)
            own = r.square_g.at[at.grp]
        return remote(own, own, r.rq, index, peer)

    def after_last(self):
        r, at, steps = (self.refs, self.at, self.steps)
        fill_blocks(r, (0,))
        self.start(self.sum_sibling(0))
        fill_vec(r)
        self.start(self.small_sum(0))
        self.add_grp(1)
        moments = [r.start[g] + s for g in range(GROUPS) for s in range(ROLLOUT)]
        intervals = [r.interval[g] for g in range(GROUPS) for s in range(ROLLOUT)]
        r.cond_t[...] = jnp.transpose(condition_rows(moments, intervals, r.lead))
        self.small_sum(0).wait_recv()
        r.vec_z[at.z] = r.vec[...] + r.vec_sib[...]
        for index in steps:
            self.start(self.small_sum(index))
        self.add_sibling(0)
        self.add_grp(2)
        square = self.add_z(1)
        for index in steps:
            self.small_sum(index).wait_recv()
        r.vec_g[at.grp] = r.vec_z[0] + r.vec_z[1] + r.vec_z[2] + r.vec_z[3]
        for index in steps:
            self.start(self.small_sum(3 + index))
        square = square + self.add_z(2)
        self.add_grp(0)

        for index in steps:
            self.small_sum(3 + index).wait_recv()
        own_cond = r.cond_t[span(SLAB * at.dp, SLAB), :]
        columns = [jnp.broadcast_to(own_cond[:, k : k + 1], (SLAB, 128)) for k in range(8)]
        ada = r.a.at[0:864]

        def ada_tile(j, total):
            tile = jnp.zeros((SLAB, 128), F32)
            for g in range(GROUPS):
                for s in range(ROLLOUT):
                    row = r.vec_g[g, pl.ds(24 + 18 * s + j, 1), :]
                    tile = tile + columns[ROLLOUT * g + s] * row
            ada[pl.ds(j, SLAB, stride=18), :] = tile
            return total + col_sum(tile * tile)

        ada_square = lax.fori_loop(0, 18, ada_tile, jnp.zeros((1, 128), F32))
        puts = [local(ada, r.ada_far, r.in_sems.at[0])]
        vec_sum = r.vec_g[0] + r.vec_g[1] + r.vec_g[2] + r.vec_g[3]
        r.bias_out[0:24, :] = vec_sum[0:24]
        r.bias_out[24:42, :] = vec_sum[24:42] + vec_sum[42:60]
        r.bias_out[42:48, :] = jnp.zeros((6, 128), F32)

        square = square + 0.25 * ada_square + self.add_z(0)
        r.square_d[at.dp] = jnp.broadcast_to(square, (8, 128))
        for index in range(7):
            self.start(self.square_sum(index))
        for index in range(7):
            self.square_sum(index).wait_recv()
        total = r.square_d[0]
        for d in range(1, 2 * LAYERS):
            total = total + r.square_d[d]
        r.square_g[at.grp] = total
        for index in range(7, 10):
            self.start(self.square_sum(index))
        for unit in (1, 2, 0):
            for k in steps:
                self.share_piece(unit, k).wait_recv()
            puts.append(local(self.got(unit, "piece"), r.pieces_far.at[unit], r.in_sems.at[1 + unit]))
        for index in range(7, 10):
            self.square_sum(index).wait_recv()
        bias_sum = r.bias_out[...]
        total = r.square_g[0] + r.square_g[1] + r.square_g[2] + r.square_g[3]
        total = total + col_sum(bias_sum * bias_sum)
        r.square_out[...] = jnp.broadcast_to(jnp.sum(total, axis=1, keepdims=True), (8, 128))
        for made in puts:
            made.wait()
        self.drain()

    def drain(self):
        for unit in range(UNITS):
            for k in self.steps:
                self.gather_z(unit, k).wait_send()
                for m in self.steps:
                    self.gather_grp(unit, k, m).wait_send()
                self.sum_grp(unit, k).wait_send()
                self.sum_z(unit, k).wait_send()
                self.share_piece(unit, k).wait_send()
            for k in range(4):
                self.gather_sibling(unit, k).wait_send()
            self.sum_sibling(unit).wait_send()
        for index in range(8):
            self.small(index).wait_send()
        for index in range(7):
            self.small_sum(index).wait_send()
        for index in range(10):
            self.square_sum(index).wait_send()


correction = 1.0 - 0.5**ADAM_STEP
grad_limit = math.sqrt(NPARAM)


def adam(master, first, second, clipped, decay):
    first_new = 0.5 * first + 0.5 * clipped
    second_new = 0.5 * second + 0.5 * clipped * clipped
    update = first_new / correction / (jnp.sqrt(second_new / correction) + adam_eps)
    return (master - learn_rate * (update + decay * master), first_new, second_new)


def adam_kernel(*refs):
    piece_ref, ada_ref, square_ref = refs[:3]
    masters, firsts, seconds = (refs[3:8], refs[8:13], refs[13:18])
    news, first_news, second_news, copies = (refs[18:23], refs[23:28], refs[28:33], refs[33:38])
    flats = refs[38:42]
    norm = jnp.sqrt(square_ref[0:1, :])
    clip = grad_limit / jnp.maximum(norm, grad_limit)
    qkv, proj, up, down = flats
    for g in range(3):
        for j in range(3):
            qkv[pl.ds(3 * g + j, SLAB, stride=9), :] = piece_ref[0, SLAB * g : SLAB * (g + 1), 128 * j : 128 * j + 128].astype(F32)
    for j in range(3):
        proj[pl.ds(j, SLAB, stride=3), :] = piece_ref[0, 3 * SLAB :, 128 * j : 128 * j + 128].astype(F32)
    for g in range(GROUPS):
        for j in range(3):
            up[pl.ds(3 * g + j, SLAB, stride=12), :] = piece_ref[1, SLAB * g : SLAB * (g + 1), 128 * j : 128 * j + 128].astype(F32)
            down[pl.ds(3 * SLAB * g + j, SLAB, stride=3), :] = piece_ref[2, SLAB * g : SLAB * (g + 1), 128 * j : 128 * j + 128].astype(F32)
    for index, grad in enumerate((qkv, proj, up, down, ada_ref)):
        def chunk(i, carry):
            rows = pl.ds(pl.multiple_of(16 * i, 16), 16)
            new, first, second = adam(
                masters[index][rows, :], firsts[index][rows, :], seconds[index][rows, :],
                grad[rows, :] * clip, 0.1,
            )
            news[index][rows, :] = new
            first_news[index][rows, :] = first
            second_news[index][rows, :] = second
            copies[index][rows, :] = new.astype(BF)
            return carry

        lax.fori_loop(0, grad.shape[0] // 16, chunk, 0, unroll=3)


def update(pieces, ada, square, masters, firsts, seconds):
    flat = lambda arrays: [a.reshape(-1, 128) for a in arrays[:5]]
    masters, firsts, seconds = (flat(masters), flat(firsts), flat(seconds))
    vmem = pl.BlockSpec(memory_space=pltpu.VMEM)
    shapes = [m.shape for m in masters]
    outs = [jax.ShapeDtypeStruct(s, F32) for s in shapes] * 3
    outs += [jax.ShapeDtypeStruct(s, BF) for s in shapes]
    results = pl.pallas_call(
        adam_kernel,
        in_specs=[vmem] * 18,
        out_specs=[vmem] * 20,
        out_shape=outs,
        scratch_shapes=[pltpu.VMEM(s, F32) for s in shapes[:4]],
        name="adam",
    )(pieces, ada, square, *masters, *firsts, *seconds)
    results = [r.reshape(-1) for r in results]
    return (results[0:5], results[5:10], results[10:15], results[15:20])


class Refs:
    def __init__(self, names, refs):
        for name, ref in zip(names, refs, strict=True):
            setattr(self, name, ref)


MASTERS = ("qkv", "proj", "up", "down", "ada")


def block_kernel(names, hooked, *refs):
    r = Refs(names, refs)
    if hooked is Together:
        r.masters = {name: getattr(r, "far_" + name) for name in MASTERS}
        for name in ("gz", "gx", "gs", "gm", "rs", "rx", "rz", "ra", "rv", "rq"):
            setattr(r, name, (getattr(r, name + "_out"), getattr(r, name + "_in")))
    hooks = hooked(r)
    length = r.x.shape[0]
    pairs = HEADS // 2
    get_cot = local(r.cot_far, r.cot, r.out_sems.at[2])

    def over_rows(body):
        def step(i, carry):
            body(pl.ds(pl.multiple_of(i * ROWS, ROWS), ROWS))
            return carry

        lax.fori_loop(0, length // ROWS, step, 0)

    def columns(h, offset=0):
        return pl.ds(pl.multiple_of(offset + 128 * h, 128), 128)

    def over_pairs(body):
        def step(h, carry):
            body(h)
            return carry

        lax.fori_loop(0, pairs, step, 0)

    def act_refs(rows):
        first = rows.start
        return [
            r.act.at[pl.ds(pl.multiple_of(length * part + first, ROWS), ROWS)] for part in range(4)
        ]

    def a_refs(rows):
        first = rows.start
        return [
            r.a.at[pl.ds(pl.multiple_of(length * part + first, ROWS), ROWS)] for part in range(3)
        ]

    def save(step, h):
        slot = lax.rem(h, 2)
        return pltpu.make_async_copy(
            r.p.at[slot], r.p_far.at[step, pl.ds(2 * h, 2)], r.p_sems.at[slot]
        )

    def fetch(step, h):
        slot = lax.rem(h, 2)
        return pltpu.make_async_copy(
            r.p_far.at[step, pl.ds(2 * h, 2)], r.p.at[slot], r.p_sems.at[slot]
        )

    def attend(step, qkv, att, after):
        def body(h):
            @pl.when(h >= 2)
            def _():
                save(step, h - 2).wait()

            attend_pair(
                qkv[:, columns(h)], qkv.at[:, columns(h, D)], qkv[:, columns(h, 2 * D)],
                att.at[:, columns(h)], r.p.at[lax.rem(h, 2)], r.turned,
            )
            save(step, h).start()
            after(h)

        over_pairs(body)

    def finish_saves(step):
        for h in range(pairs - 2, pairs):
            save(step, h).wait()

    def attend_back(step, qkv, after):
        def body(h):
            fetch(step, h).wait()
            attend_back_pair(
                qkv[:, columns(h)], qkv[:, columns(h, D)], qkv.at[:, columns(h, 2 * D)],
                r.datt[:, columns(h)], r.p.at[lax.rem(h, 2)],
                r.dqkv.at[:, columns(h)], r.dqkv.at[:, columns(h, D)],
                r.dqkv.at[:, columns(h, 2 * D)], r.turned,
            )

            @pl.when(h + 2 < pairs)
            def _():
                fetch(step, h + 2).start()

            after(h)

        over_pairs(body)

    nothing = lambda h: None
    hooks.begin()

    def first(rows):
        r.qkv0[rows, :] = first_rows(r.x[rows, :], r.rows, r.wa)

    over_rows(first)
    hooks.after_first()
    attend(0, r.qkv0, r.att0, hooks.after_attend_pair)
    hooks.before_middle()

    def middle(rows):
        middle_rows(
            r.x.at[rows], r.att0.at[rows], r.rows, r.wa, r.wup, r.wdown,
            a_refs(rows), r.gp.at[rows], act_refs(rows), r.f.at[rows], r.x1.at[rows],
            r.qkv1.at[rows],
        )

    over_rows(middle)
    finish_saves(0)
    attend(1, r.qkv1, r.att1, nothing)

    for ref in (r.gqkv, r.gproj, r.gup, r.gdown, r.wide, r.narrow0, r.narrow1, r.bias):
        ref[...] = jnp.zeros_like(ref)

    def turn(rows):
        turn_rows(
            r.x1.at[rows], r.att1.at[rows], r.cot.at[rows], r.rows, r.wa, r.wup,
            r.wdown, r.y.at[rows], r.dmid.at[rows], r.datt.at[rows], r.gdown, r.gup, r.gproj,
            r.wide, r.narrow1,
        )

    finish_saves(1)
    for h in range(2):
        fetch(1, h).start()
    get_cot.wait()
    over_rows(turn)
    put_y = local(r.y, r.y_far, r.out_sems.at[0])
    attend_back(1, r.qkv1, nothing)
    for h in range(2):
        fetch(0, h).start()

    def join(rows):
        join_rows(
            r.dqkv.at[rows], r.x1.at[rows], r.x.at[rows], a_refs(rows), r.gp.at[rows],
            act_refs(rows), r.f.at[rows], r.att0.at[rows], r.rows, r.wa, r.wup, r.wdown,
            r.dmid.at[rows], r.datt.at[rows], r.gqkv, r.gdown, r.gup, r.gproj, r.wide, r.narrow1,
            r.narrow0, r.bias,
        )

    over_rows(join)
    hooks.after_join()
    attend_back(0, r.qkv0, hooks.after_back_pair)

    def last(rows):
        r.dmid[rows, :] = qkv_back(
            mod_reader(r.rows, 0), r.x[rows, :].astype(F32), r.dmid[rows, :],
            r.dqkv[rows, :], r.wa, r.gqkv, r.narrow0, r.bias,
        )

    over_rows(last)
    put_dx = local(r.dmid, r.dx_far, r.out_sems.at[1])
    hooks.after_last()
    put_y.wait()
    put_dx.wait()


def block_call(hooked, inputs, cotangent, extra_in, extra_out, extra_scratch, params):
    length = inputs.shape[0]
    vmem, hbm, dma = (pltpu.VMEM, pl.ANY, pltpu.SemaphoreType.DMA)
    weights = (ROLLOUT, HEADS, length, length)
    ins = [("x", inputs, vmem), ("cot_far", cotangent, hbm), *extra_in]
    outs = [
        ("y_far", (length, D), F32, hbm), ("dx_far", (length, D), F32, hbm),
        ("p_far", weights, BF, hbm), *extra_out,
    ]
    scratch = [
        ("wa", vmem((D, FF), BF)), ("wup", vmem((D, FF), BF)), ("wdown", vmem((FF, D), BF)),
        ("cot", vmem((length, D), BF)), ("qkv0", vmem((length, 3 * D), BF)),
        ("qkv1", vmem((length, 3 * D), BF)), ("p", vmem((2, 2, length, length), BF)),
        ("att0", vmem((length, D), BF)), ("att1", vmem((length, D), BF)),
        *[(name, vmem((length, D), F32)) for name in ("f", "x1", "dmid", "y")], ("a", vmem((3 * length, 128), F32)),
        ("gp", vmem((length, FF), F32)), ("act", vmem((4 * length, D), BF)),
        ("datt", vmem((length, D), BF)), ("dqkv", vmem((length, 3 * D), BF)),
        ("gqkv", vmem((D, 3 * D), F32)), ("gproj", vmem((D, D), F32)),
        ("gup", vmem((D, FF), F32)), ("gdown", vmem((FF, D), F32)),
        ("turned", vmem((2, 128, length), BF)), ("wide", vmem((8, FF), F32)),
        ("narrow0", vmem((8, D), F32)), ("narrow1", vmem((8, D), F32)),
        ("bias", vmem((8, 3 * D), F32)), ("blocks", vmem((UNITS, 2 * HALF, PART), BF)),
        ("rows", vmem((32, D), F32)), ("vec", vmem((64, 128), F32)),
        ("in_sems", dma((5,))), ("p_sems", dma((2,))), ("out_sems", dma((3,))),
        *extra_scratch,
    ]
    names = [item[0] for item in (*ins, *outs, *scratch)]
    return pl.pallas_call(
        functools.partial(block_kernel, names, hooked),
        in_specs=[pl.BlockSpec(memory_space=space) for _, _, space in ins],
        out_specs=[pl.BlockSpec(memory_space=space) for *_, space in outs],
        out_shape=[jax.ShapeDtypeStruct(shape, kind) for _, shape, kind, _ in outs],
        scratch_shapes=[kind for _, kind in scratch],
        compiler_params=pltpu.CompilerParams(vmem_limit_bytes=67043328, **params),
        name="block",
    )(*(array for _, array, _ in ins))


def block_alone(inputs, cotangent, rows, wa, wup, wdown):
    hbm = pl.ANY
    y, dx, _, blocks, vec = block_call(
        Alone, inputs, cotangent,
        [("rows_far", rows, hbm), ("wa_far", wa, hbm), ("wup_far", wup, hbm), ("wdown_far", wdown, hbm)],
        [("blocks_far", (UNITS, 2 * HALF, PART), BF, hbm), ("vec_far", (64, 128), F32, hbm)],
        [], {},
    )
    return (y, dx, blocks, vec)


def block_together(inputs, cotangent, start, interval, counts, lead, masters):
    vmem, hbm, smem, dma = (pltpu.VMEM, pl.ANY, pltpu.SMEM, pltpu.SemaphoreType.DMA)
    qkv, proj, up, down, ada, bias = masters
    far = [
        ("far_" + name, array.reshape(-1, 128), hbm)
        for name, array in zip(MASTERS, (qkv, proj, up, down, ada))
    ]
    bias = jnp.pad(bias, (0, 1024 - bias.shape[0])).reshape(8, 128)
    pairs_of = [
        ("gz", (UNITS, 3)), ("gx", (UNITS, 3, 3)), ("gs", (UNITS, 4)), ("gm", (8,)),
        ("rs", (UNITS,)), ("rx", (UNITS, 3)), ("rz", (UNITS, 3)), ("ra", (UNITS, 3)),
        ("rv", (7,)), ("rq", (10,)),
    ]
    y, dx, _, pieces, ada_grad, bias_sum, square = block_call(
        Together, inputs, cotangent,
        [("start", start, smem), ("interval", interval, smem), ("counts", counts, smem),
         ("lead", lead, vmem), ("bias_own", bias, vmem), *far],
        [("pieces_far", (UNITS, 4 * SLAB, PART), BF, hbm), ("ada_far", (18 * SLAB, 128), F32, hbm),
         ("bias_out", (48, 128), F32, vmem), ("square_out", (8, 128), F32, vmem)],
        [("cond_t", vmem((D, 8), F32)), ("part_own", vmem((40, 128), F32)),
         ("part_sib", vmem((40, 128), F32)), ("part_z", vmem((LAYERS, 40, 128), F32)),
         ("bias_slot", vmem((LAYERS, 2, 8, 128), F32)), ("bias_full", vmem((48, 128), F32)),
         ("vec_sib", vmem((64, 128), F32)), ("vec_z", vmem((LAYERS, 64, 128), F32)),
         ("vec_g", vmem((GROUPS, 64, 128), F32)), ("square_d", vmem((8, 8, 128), F32)),
         ("square_g", vmem((GROUPS, 8, 128), F32)), ("joined", pltpu.SemaphoreType.REGULAR),
         *[(name + end, dma(shape)) for name, shape in pairs_of for end in ("_out", "_in")]],
        dict(collective_id=0, has_side_effects=True),
    )
    return (y, dx, pieces, ada_grad, bias_sum, square)


def step_embedding(moment):
    half_width = D // 2
    freqs = jnp.exp(-math.log(10000.0) * jnp.arange(half_width, dtype=F32) / half_width)
    angles = moment[:, None] * freqs[None, :]
    return jnp.concatenate([jnp.sin(angles), jnp.cos(angles)], axis=1)


def all_conditions(group_interval, rollout_start, lead_table):
    chosen = group_interval[:, None] == jnp.arange(INTERVALS)[None, :]
    lead_rows = jnp.sum(jnp.where(chosen[:, :, None], lead_table[None], 0.0), axis=1)
    start = rollout_start.astype(F32)
    rows = [lead_rows + step_embedding(start + offset) for offset in range(ROLLOUT)]
    return jax.nn.silu(jnp.stack(rows, axis=1)).astype(BF)


def plain_gather(group_interval, counts, rollout_start, lead_table, masters):
    low = [master.astype(BF) for master in masters]
    owner = lax.axis_index("dp")
    group_index = lax.axis_index("grp")
    own_rows = D // lax.axis_size("dp")
    counts = counts.astype(F32)
    share = lax.axis_size("grp") * counts / jnp.sum(counts)
    share = lax.dynamic_index_in_dim(share, group_index, keepdims=False)
    conditions = all_conditions(group_interval, rollout_start, lead_table)
    owner_columns = lax.dynamic_slice_in_dim(conditions, owner * own_rows, own_rows, axis=2)
    own_condition = lax.dynamic_index_in_dim(owner_columns, group_index, keepdims=False)
    modulation = lax.psum(dot(own_condition, low[4].reshape(own_rows, 6 * D)), "dp")
    qkv, proj, up, down, bias = [
        lax.all_gather(low[index], "dp", axis=0, tiled=True) for index in (0, 1, 2, 3, 5)
    ]
    bias = bias.astype(F32)
    modulation = modulation + bias[4 * D + FF :][None]
    share_rows = jnp.broadcast_to(share, (ROLLOUT, 2, D))
    mods = jnp.concatenate([modulation.reshape(ROLLOUT, 6, D), share_rows], axis=1).reshape(-1, D)
    rows = jnp.concatenate(
        [mods, bias[:D][None], jnp.zeros((1, D), F32), bias[D : 4 * D + FF].reshape(-1, D),
         jnp.zeros((7, D), F32)]
    )
    wa = jnp.concatenate([qkv.reshape(D, 3 * D), proj.reshape(D, D)], axis=1)
    return (wa, up.reshape(D, FF), down.reshape(FF, D), rows, owner_columns)


def plain_update(owner_columns, vec, blocks, masters, firsts, seconds):
    owner = lax.axis_index("dp")
    vec = vec.reshape(-1)
    split = 4 * D + FF
    dmod = vec[split : split + ROLLOUT * 6 * D].reshape(ROLLOUT, 6 * D)
    dmod_all = lax.all_gather(lax.psum(dmod, "dp"), "grp")
    bias_sum = lax.psum(vec[:split], ("grp", "dp"))
    bias_sum = jnp.concatenate([bias_sum, jnp.sum(dmod_all, axis=(0, 1))])
    bias_rows = masters[5].shape[0]
    bias_grad = lax.dynamic_slice_in_dim(bias_sum, owner * bias_rows, bias_rows)
    ada_grad = jnp.einsum(
        "gsr,gsc->rc", owner_columns.astype(F32), dmod_all, precision=lax.Precision.HIGHEST
    )
    blocks = blocks.reshape(UNITS, 2, 4, LAYERS, SLAB, PART)
    flat_a, flat_up = [blocks[u].transpose(2, 0, 3, 1, 4).reshape(D, FF) for u in (0, 1)]
    flat_down = blocks[2].transpose(2, 0, 1, 3, 4)
    flat = [flat_a[:, : 3 * D], flat_a[:, 3 * D :], flat_up, flat_down]
    shares = []
    for grad in flat:
        summed = lax.psum(grad.reshape(-1), "grp").astype(F32)
        shares.append(lax.psum_scatter(summed, "dp", scatter_dimension=0, tiled=True))
    shares = shares + [ada_grad.reshape(-1), bias_grad]
    local_square = sum((jnp.sum(piece * piece) for piece in shares))
    grad_norm = jnp.sqrt(lax.psum(local_square, "dp"))
    clip = grad_limit / jnp.maximum(grad_norm, grad_limit)
    decays = [0.1, 0.1, 0.1, 0.1, 0.1, 0.0]
    results = [
        adam(master, first, second, grad * clip, decay)
        for master, first, second, grad, decay in zip(masters, firsts, seconds, shares, decays)
    ]
    news, first_news, second_news = zip(*results)
    return (grad_norm, *news, *first_news, *second_news, *(new.astype(BF) for new in news))


def per_device(
    inputs,
    cotangent,
    group_interval,
    sample_counts,
    rollout_start,
    lead_table,
    *state,
):
    masters, firsts, seconds = (state[0:6], state[6:12], state[12:18])
    fits = (
        lax.axis_size("dp") == 2 * LAYERS
        and lax.axis_size("grp") == GROUPS
        and inputs.shape[0] == 1024
    )
    if not fits:
        wa, wup, wdown, rows, owner_columns = plain_gather(
            group_interval, sample_counts, rollout_start, lead_table, masters
        )
        result, input_grad, blocks, vec = block_alone(inputs, cotangent, rows, wa, wup, wdown)
        rest = plain_update(owner_columns, vec, blocks, masters, firsts, seconds)
        return (result, input_grad, *rest)
    result, input_grad, pieces, ada_grad, bias_sum, square = block_together(
        inputs, cotangent, rollout_start, group_interval, sample_counts, lead_table, masters
    )
    news, first_news, second_news, copies = update(
        pieces, ada_grad, square, masters, firsts, seconds
    )
    grad_norm = jnp.sqrt(square[0, 0])
    clip = grad_limit / jnp.maximum(grad_norm, grad_limit)
    bias_rows = masters[5].shape[0]
    bias_grad = lax.dynamic_slice_in_dim(
        bias_sum.reshape(-1), lax.axis_index("dp") * bias_rows, bias_rows
    )
    new, first, second = adam(masters[5], firsts[5], seconds[5], bias_grad * clip, 0.0)
    return (
        result, input_grad, grad_norm, *news, new, *first_news, first, *second_news, second,
        *copies, new.astype(BF),
    )


def solution(mesh):
    rows = P(("grp", "dp"), None)
    return jax.shard_map(
        per_device,
        mesh=mesh,
        in_specs=(rows, rows, P(), P(), P(), P(), *[P("dp")] * 18),
        out_specs=(rows, rows, P(), *[P("dp")] * 24),
        check_vma=False,
    )
```

```python
import functools
import math

import jax
import jax.numpy as jnp
from jax import lax
from jax.experimental import pallas as pl
from jax.experimental.pallas import tpu as pltpu
from jax.sharding import PartitionSpec as P

D = 384
HEADS = 6
FF = 1536
ROLLOUT = 2
INTERVALS = 3
ADAM_STEP = 10
HEAD_DIM = 64
NPARAM = 2659584

norm_eps = 1e-06
learn_rate = 0.05
adam_eps = 1e-08

BF = jnp.bfloat16
F32 = jnp.float32
NN = (((1,), (0,)), ((), ()))
NT = (((1,), (1,)), ((), ()))
TN = (((0,), (0,)), ((), ()))

ROWS = 256
SLAB = 48
PART = 384
ROW_SHARE = 6
ROW_BQKV, ROW_BPROJ, ROW_BUP, ROW_BDOWN = 16, 19, 20, 24
SHIFT1, SCALE1, GATE1, SHIFT2, SCALE2, GATE2 = range(6)


def dot(left, right, dims=NN):
    return lax.dot_general(left, right, dims, preferred_element_type=F32)


def layer_norm(stream):
    centred = stream - jnp.mean(stream, axis=-1, keepdims=True)
    inverse = lax.rsqrt(jnp.mean(centred * centred, axis=-1, keepdims=True) + norm_eps)
    return (centred * inverse, inverse)


def norm_back(normed, inverse, grad_out):
    mean_grad = jnp.mean(grad_out, axis=-1, keepdims=True)
    mean_prod = jnp.mean(grad_out * normed, axis=-1, keepdims=True)
    return inverse * (grad_out - mean_grad - normed * mean_prod)


def col_sum(value):
    return jnp.sum(value, axis=0, keepdims=True)


def modulated(normed, mods, scale_row, shift_row):
    return (normed * (1.0 + mods(scale_row)) + mods(shift_row)).astype(BF)


def mod_reader(mod_ref, step):
    return lambda row: mod_ref[pl.ds(8 * step + row, 1), :]


def gelu_pair(value):
    cdf = 0.5 + 0.5 * lax.erf(value * (2.0**-0.5))
    density = jnp.exp(-0.5 * value * value) * (1.0 / math.sqrt(2.0 * math.pi))
    return (value * cdf, cdf + value * density)


def side_by_side(ref, first, count):
    return jnp.concatenate([ref[row : row + 1, :] for row in range(first, first + count)], axis=1)


def first_rows(x, rows_ref, wa_ref):
    normed, _ = layer_norm(x.astype(F32))
    hidden = modulated(normed, mod_reader(rows_ref, 0), SCALE1, SHIFT1)
    qkv = dot(hidden, wa_ref[:, : 3 * D]) + side_by_side(rows_ref, ROW_BQKV, 3)
    return qkv.astype(BF)


def middle_rows(
    x_ref, att_ref, rows_ref, wa_ref, wup_ref, wdown_ref,
    a_refs, gp_ref, act_refs, f_ref, next_ref, qkv_ref,
):
    mods = mod_reader(rows_ref, 0)
    later = mod_reader(rows_ref, 1)
    branch = dot(att_ref[...], wa_ref[:, 3 * D :]) + mods(ROW_BPROJ)
    for part, ref in enumerate(a_refs):
        ref[...] = branch[:, 128 * part : 128 * (part + 1)]
    middle = x_ref[...].astype(F32) + mods(GATE1) * branch
    normed, _ = layer_norm(middle)
    hidden = modulated(normed, mods, SCALE2, SHIFT2)
    upward = dot(hidden, wup_ref[...]) + side_by_side(rows_ref, ROW_BUP, 4)
    act, slope = gelu_pair(upward)
    gp_ref[...] = slope
    act = act.astype(BF)
    for part, ref in enumerate(act_refs):
        ref[...] = act[:, PART * part : PART * (part + 1)]
    branch = dot(act, wdown_ref[...]) + mods(ROW_BDOWN)
    f_ref[...] = branch
    stream = middle + mods(GATE2) * branch
    next_ref[...] = stream
    normed, _ = layer_norm(stream)
    hidden = modulated(normed, later, SCALE1, SHIFT1)
    qkv = dot(hidden, wa_ref[:, : 3 * D]) + side_by_side(rows_ref, ROW_BQKV, 3)
    qkv_ref[...] = qkv.astype(BF)


def ffn_back(
    mods, grad, branch_two, act, slope, normed, inverse, hidden, branch_one, att,
    wa_ref, wup_ref, wdown_ref, gdown_ref, gup_ref, gproj_ref, wide_ref, narrow_ref,
    dmid_ref, datt_ref,
):
    df = (mods(GATE2) * grad).astype(BF)
    narrow_ref[pl.ds(GATE2, 1), :] += col_sum(grad * branch_two)
    narrow_ref[pl.ds(7, 1), :] += col_sum(df.astype(F32))
    gdown_ref[...] += dot(act, df, TN)
    dact = dot(df, wdown_ref[...], NT)
    du = (dact * slope).astype(BF)
    wide_ref[pl.ds(0, 1), :] += col_sum(du.astype(F32))
    gup_ref[...] += dot(hidden, du, TN)
    dh = dot(du, wup_ref[...], NT)
    narrow_ref[pl.ds(SHIFT2, 1), :] += col_sum(dh)
    narrow_ref[pl.ds(SCALE2, 1), :] += col_sum(dh * normed)
    dmid = grad + norm_back(normed, inverse, dh * (1.0 + mods(SCALE2)))
    dmid_ref[...] = dmid
    da = (mods(GATE1) * dmid).astype(BF)
    narrow_ref[pl.ds(GATE1, 1), :] += col_sum(dmid * branch_one)
    narrow_ref[pl.ds(6, 1), :] += col_sum(da.astype(F32))
    gproj_ref[...] += dot(att, da, TN)
    datt_ref[...] = dot(da, wa_ref[:, 3 * D :], NT).astype(BF)


def turn_rows(
    x_ref, att_ref, cot_ref, rows_ref, wa_ref, wup_ref, wdown_ref,
    out_ref, dmid_ref, datt_ref, gdown_ref, gup_ref, gproj_ref, wide_ref, narrow_ref,
):
    mods = mod_reader(rows_ref, 1)
    shared = mod_reader(rows_ref, 0)
    att = att_ref[...]
    branch_one = dot(att, wa_ref[:, 3 * D :]) + shared(ROW_BPROJ)
    middle = x_ref[...] + mods(GATE1) * branch_one
    normed, inverse = layer_norm(middle)
    hidden = modulated(normed, mods, SCALE2, SHIFT2)
    upward = dot(hidden, wup_ref[...]) + side_by_side(rows_ref, ROW_BUP, 4)
    act, slope = gelu_pair(upward)
    act = act.astype(BF)
    branch_two = dot(act, wdown_ref[...]) + shared(ROW_BDOWN)
    out_ref[...] = middle + mods(GATE2) * branch_two
    ffn_back(
        mods, cot_ref[...].astype(F32), branch_two, act, slope, normed, inverse, hidden,
        branch_one, att, wa_ref, wup_ref, wdown_ref, gdown_ref, gup_ref, gproj_ref,
        wide_ref, narrow_ref, dmid_ref, datt_ref,
    )


def qkv_back(mods, stream, dmid, dqkv, wa_ref, gqkv_ref, narrow_ref, bias_ref):
    normed, inverse = layer_norm(stream)
    hidden = modulated(normed, mods, SCALE1, SHIFT1)
    bias_ref[pl.ds(0, 1), :] += col_sum(dqkv.astype(F32))
    gqkv_ref[...] += dot(hidden, dqkv, TN)
    dh = dot(dqkv, wa_ref[:, : 3 * D], NT)
    narrow_ref[pl.ds(SHIFT1, 1), :] += col_sum(dh)
    narrow_ref[pl.ds(SCALE1, 1), :] += col_sum(dh * normed)
    return dmid + norm_back(normed, inverse, dh * (1.0 + mods(SCALE1)))


def join_rows(
    dqkv_ref, x1_ref, x0_ref, a_refs, gp_ref, act_refs, f_ref, att_ref,
    rows_ref, wa_ref, wup_ref, wdown_ref,
    dmid_ref, datt_ref, gqkv_ref, gdown_ref, gup_ref, gproj_ref, wide_ref, narrow1_ref,
    narrow_ref, bias_ref,
):
    grad = qkv_back(
        mod_reader(rows_ref, 1), x1_ref[...], dmid_ref[...], dqkv_ref[...], wa_ref, gqkv_ref,
        narrow1_ref, bias_ref,
    )
    mods = mod_reader(rows_ref, 0)
    branch_one = jnp.concatenate([ref[...] for ref in a_refs], axis=1)
    middle = x0_ref[...].astype(F32) + mods(GATE1) * branch_one
    normed, inverse = layer_norm(middle)
    hidden = modulated(normed, mods, SCALE2, SHIFT2)
    ffn_back(
        mods, grad, f_ref[...], jnp.concatenate([ref[...] for ref in act_refs], axis=1), gp_ref[...], normed, inverse, hidden,
        branch_one, att_ref[...], wa_ref, wup_ref, wdown_ref, gdown_ref, gup_ref, gproj_ref,
        wide_ref, narrow_ref, dmid_ref, datt_ref,
    )


def head_lanes(rows):
    lane = lax.broadcasted_iota(jnp.int32, (rows, 2 * HEAD_DIM), 1)
    return (lane < HEAD_DIM, lane >= HEAD_DIM)


def turned_heads(rows_f32, out_ref):
    turned = jnp.transpose(rows_f32)
    row = lax.broadcasted_iota(jnp.int32, turned.shape, 0)
    out_ref[0] = jnp.where(row < HEAD_DIM, turned, 0.0).astype(BF)
    out_ref[1] = jnp.where(row >= HEAD_DIM, turned, 0.0).astype(BF)


score_scale = HEAD_DIM**-0.5


def attend_pair(q, k_ref, v, o_ref, p_ref, vt_ref):
    turned_heads(v.astype(F32), vt_ref)
    queries = q * BF(score_scale)
    mixed = None
    for half, lanes in enumerate(head_lanes(queries.shape[0])):
        scores = dot(k_ref[...], jnp.where(lanes, queries, BF(0)), NT)
        top = jnp.max(scores, axis=0, keepdims=True)
        weights = jnp.exp(scores - top)
        total = jnp.sum(weights, axis=0, keepdims=True)
        low = (weights * (1.0 / total)).astype(BF)
        p_ref[half] = low
        part = dot(vt_ref[half], low)
        mixed = part if mixed is None else mixed + part
    o_ref[...] = jnp.transpose(mixed).astype(BF)


def attend_back_pair(q, k, v_ref, grads, p_ref, dq_ref, dk_ref, dv_ref, kt_ref):
    turned_heads(k.astype(F32) * score_scale, kt_ref)
    queries = q * BF(score_scale)
    dq_turned, dk, dv = (None, None, None)
    for half, lanes in enumerate(head_lanes(queries.shape[0])):
        grad = jnp.where(lanes, grads, BF(0))
        query = jnp.where(lanes, queries, BF(0))
        low = p_ref[half]
        weight_grad = dot(v_ref[...], grad, NT)
        weights = low.astype(F32)
        delta = jnp.sum(weights * weight_grad, axis=0, keepdims=True)
        score_grad = (weights * (weight_grad - delta)).astype(BF)
        parts = (dot(kt_ref[half], score_grad), dot(score_grad, query), dot(low, grad))
        if half == 0:
            dq_turned, dk, dv = parts
        else:
            dq_turned, dk, dv = (dq_turned + parts[0], dk + parts[1], dv + parts[2])
    dq_ref[...] = jnp.transpose(dq_turned).astype(BF)
    dk_ref[...] = dk.astype(BF)
    dv_ref[...] = dv.astype(BF)


class Refs:
    def __init__(self, names, refs):
        for name, ref in zip(names, refs, strict=True):
            setattr(self, name, ref)

MESH_ID = pl.DeviceIdType.MESH
GROUPS = 4
LAYERS = 4
UNITS = 3
HALF = 768


class Place:
    def __init__(self):
        self.grp = lax.axis_index("grp")
        self.dp = lax.axis_index("dp")
        self.z = self.dp // 2
        self.core = self.dp % 2

    def sibling(self):
        return (self.grp, 2 * self.z + 1 - self.core)

    def along_grp(self, step):
        return (lax.rem(self.grp + step, GROUPS), self.dp)

    def along_z(self, step):
        return (self.grp, 2 * lax.rem(self.z + step, LAYERS) + self.core)

    def across(self, step):
        return (self.grp, 2 * lax.rem(self.z + step, LAYERS) + 1 - self.core)


def greet(peers):
    barrier = pltpu.get_barrier_semaphore()
    for peer in peers:
        pl.semaphore_signal(barrier, inc=1, device_id=peer, device_id_type=MESH_ID)
    return lambda: pl.semaphore_wait(barrier, len(peers))


def remote(src, dst, sems, index, peer):
    send_sem, recv_sem = sems
    return pltpu.make_async_remote_copy(
        src_ref=src, dst_ref=dst, send_sem=send_sem.at[index], recv_sem=recv_sem.at[index],
        device_id=peer, device_id_type=MESH_ID,
    )


def condition_rows(moments, intervals, lead_ref):
    shape = (8, D)
    row = lax.broadcasted_iota(jnp.int32, shape, 0)
    lane = lax.broadcasted_iota(jnp.int32, shape, 1)
    moment = jnp.zeros(shape, F32)
    chosen = jnp.zeros(shape, jnp.int32)
    for index, (value, interval) in enumerate(zip(moments, intervals)):
        moment = jnp.where(row == index, value.astype(F32), moment)
        chosen = jnp.where(row == index, interval, chosen)
    lead = jnp.zeros(shape, F32)
    for choice in range(INTERVALS):
        picked = jnp.broadcast_to(lead_ref[choice : choice + 1, :], shape)
        lead = jnp.where(chosen == choice, picked, lead)
    half_width = D // 2
    place = jnp.where(lane < half_width, lane, lane - half_width).astype(F32)
    angles = moment * jnp.exp(place * (-math.log(10000.0) / half_width))
    wave = jnp.where(lane < half_width, jnp.sin(angles), jnp.cos(angles))
    condition = lead + wave
    return (condition / (1.0 + jnp.exp(-condition))).astype(BF).astype(F32)


def span(start, size):
    return pl.ds(pl.multiple_of(start, SLAB), size)


def local(src, dst, sem):
    made = pltpu.make_async_copy(src, dst, sem)
    made.start()
    return made


class Alone:
    def __init__(self, refs):
        self.refs = refs

    def begin(self):
        r = self.refs
        sems = r.in_sems
        first = [local(r.wa_far, r.wa, sems.at[0]), local(r.rows_far, r.rows, sems.at[3])]
        self.later = [local(r.wup_far, r.wup, sems.at[1]), local(r.wdown_far, r.wdown, sems.at[2])]
        for made in first:
            made.wait()

    def after_first(self):
        pass

    def after_attend_pair(self, h):
        pass

    def before_middle(self):
        for made in self.later:
            made.wait()

    def after_join(self):
        fill_blocks(self.refs, (1, 2))

    def after_back_pair(self, h):
        pass

    def after_last(self):
        r = self.refs
        fill_blocks(r, (0,))
        fill_vec(r)
        puts = [local(r.blocks, r.blocks_far, r.in_sems.at[0]), local(r.vec, r.vec_far, r.in_sems.at[1])]
        for made in puts:
            made.wait()


def fill_blocks(refs, units):
    share = refs.rows[ROW_SHARE : ROW_SHARE + 1, :]
    for d in range(8):
        own = slice(SLAB * d, SLAB * (d + 1))
        for g in range(4):
            columns = slice(PART * g, PART * (g + 1))
            first = HALF * (d % 2) + 4 * SLAB * g + SLAB * (d // 2)
            there = slice(first, first + SLAB)
            for unit in units:
                if unit == 0:
                    value = refs.gqkv[own, columns] if g < 3 else refs.gproj[own, :]
                elif unit == 1:
                    value = refs.gup[own, columns]
                else:
                    value = refs.gdown[SLAB * (4 * d + g) : SLAB * (4 * d + g + 1), :]
                refs.blocks[unit, there, :] = (value * share).astype(BF)


def fill_vec(refs):
    share = refs.rows[ROW_SHARE : ROW_SHARE + 1, :]

    def put(first_row, value):
        for j in range(value.shape[1] // 128):
            refs.vec[first_row + j : first_row + j + 1, :] = (
                value[:, 128 * j : 128 * j + 128] * share[:, 0:128]
            )

    bias, wide, narrow0, narrow1 = (refs.bias, refs.wide, refs.narrow0, refs.narrow1)
    put(0, bias[0:1, :D])
    put(3, bias[0:1, 2 * D :])
    put(6, narrow0[6:7, :] + narrow1[6:7, :])
    put(9, wide[0:1, :])
    put(21, narrow0[7:8, :] + narrow1[7:8, :])
    for r in range(6):
        put(24 + 3 * r, narrow0[r : r + 1, :])
        put(42 + 3 * r, narrow1[r : r + 1, :])
    refs.vec[60:64, :] = jnp.zeros((4, 128), F32)


class Together:
    steps = range(1, 4)

    def __init__(self, refs):
        self.refs = refs
        self.at = Place()

    def start(self, copy):
        copy.start()


    def whole(self, unit):
        return (self.refs.wa, self.refs.wup, self.refs.wdown)[unit]

    def part(self, unit, owner, grp):
        if unit == 2:
            return self.whole(2).at[span(4 * SLAB * owner + SLAB * grp, SLAB), :]
        return self.whole(unit).at[
            span(SLAB * owner, SLAB), pl.ds(pl.multiple_of(PART * grp, 128), PART)
        ]

    def slab(self, unit, owner):
        if unit == 2:
            return self.whole(2).at[span(4 * SLAB * owner, 4 * SLAB), :]
        return self.whole(unit).at[span(SLAB * owner, SLAB), :]

    def owner(self, k):
        return 2 * lax.rem(self.at.z + LAYERS - k, LAYERS) + self.at.core

    def gather_z(self, unit, k):
        own = self.part(unit, self.at.dp, self.at.grp)
        return remote(own, own, self.refs.gz, (unit, k - 1), self.at.along_z(k))

    def gather_grp(self, unit, k, m):
        part = self.part(unit, self.owner(k), self.at.grp)
        return remote(part, part, self.refs.gx, (unit, k - 1, m - 1), self.at.along_grp(m))

    def gather_sibling(self, unit, k):
        slab = self.slab(unit, self.owner(k) if k else self.at.dp)
        return remote(slab, slab, self.refs.gs, (unit, k), self.at.sibling())

    def launch(self, unit):
        for k in self.steps:
            self.start(self.gather_z(unit, k))
        self.start(self.gather_sibling(unit, 0))

    def forward_grp(self, unit):
        for k in self.steps:
            self.gather_z(unit, k).wait_recv()
            for m in self.steps:
                self.start(self.gather_grp(unit, k, m))

    def forward_sibling(self, unit):
        for k in self.steps:
            for m in self.steps:
                self.gather_grp(unit, k, m).wait_recv()
            self.start(self.gather_sibling(unit, k))

    def finish_sibling(self, unit):
        for k in range(4):
            self.gather_sibling(unit, k).wait_recv()

    def small(self, index):
        r, at = (self.refs, self.at)
        if index == 0:
            return remote(r.part_own, r.part_sib, r.gm, 0, at.sibling())
        if index == 1:
            own = r.bias_slot.at[at.z, at.core]
            return remote(own, own, r.gm, 1, at.sibling())
        if index < 5:
            own = r.part_z.at[at.z]
            return remote(own, own, r.gm, index, at.along_z(index - 1))
        own = r.bias_slot.at[at.z]
        return remote(own, own, r.gm, index, at.along_z(index - 4))

    def begin(self):
        r, at, steps = (self.refs, self.at, self.steps)
        stage = {
            "qkv": r.a.at[0:432], "proj": r.a.at[432:576], "ada": r.a.at[1728:2592],
            "up": r.a.at[576:1152], "down": r.a.at[1152:1728],
        }
        loads = {
            name: local(r.masters[name], stage[name], r.in_sems.at[index])
            for index, name in enumerate(stage)
        }
        ready = greet(
            [at.sibling()]
            + [at.along_grp(k) for k in steps]
            + [at.along_z(k) for k in steps]
            + [at.across(k) for k in steps]
        )

        def fill(unit, source, count, offset, first=0):
            for j in range(count):
                value = source[pl.ds(first + j, SLAB, stride=count), :].astype(BF)
                where = offset + 128 * j
                if unit == 2:
                    rows = span(4 * SLAB * at.dp + offset, SLAB)
                    where = 128 * j
                else:
                    rows = span(SLAB * at.dp, SLAB)
                self.whole(unit)[rows, where : where + 128] = value

        loads["qkv"].wait()
        fill(0, stage["qkv"], 9, 0)
        loads["proj"].wait()
        fill(0, stage["proj"], 3, 3 * D)
        ready()
        self.launch(0)

        moment, interval = (r.start[at.grp], r.interval[at.grp])
        r.cond_t[...] = jnp.transpose(
            condition_rows([moment + s for s in range(ROLLOUT)], [interval] * ROLLOUT, r.lead)
        )
        own_cond = r.cond_t[span(SLAB * at.dp, SLAB), :]
        columns = [jnp.broadcast_to(own_cond[:, s : s + 1], (SLAB, 128)) for s in range(ROLLOUT)]
        loads["ada"].wait()
        for j in range(18):
            rows = stage["ada"][pl.ds(j, SLAB, stride=18), :].astype(BF).astype(F32)
            for s in range(ROLLOUT):
                r.part_own[18 * s + j : 18 * s + j + 1, :] = col_sum(rows * columns[s])
        r.part_own[36:40, :] = jnp.zeros((4, 128), F32)
        r.bias_own[...] = jnp.zeros((8, 128), F32)
        for i in range(6):
            size = 128 if i < 5 else 32
            r.bias_own[i : i + 1, 0:size] = r.bias_flat[pl.ds(128 * i, size)].reshape(1, size)
        lane = lax.broadcasted_iota(jnp.int32, (8, 128), 1)
        shift = lax.rem(32 * at.dp, 128)
        turned = pltpu.roll(r.bias_own[...].astype(BF).astype(F32), shift, axis=1)
        above = pltpu.roll(turned, 1, axis=0)
        r.bias_slot[at.z, at.core] = jnp.where(lane >= shift, turned, above)
        self.start(self.small(0))
        self.start(self.small(1))

        loads["up"].wait()
        fill(1, stage["up"], 12, 0)
        loads["down"].wait()
        for g in range(GROUPS):
            fill(2, stage["down"], 3, SLAB * g, 3 * SLAB * g)

        self.small(0).wait_recv()
        self.small(1).wait_recv()
        r.part_z[at.z] = r.part_own[...] + r.part_sib[...]
        for index in range(2, 8):
            self.start(self.small(index))
        self.forward_grp(0)
        self.launch(1)
        self.launch(2)

        for index in range(2, 8):
            self.small(index).wait_recv()
        total = r.part_z[0] + r.part_z[1] + r.part_z[2] + r.part_z[3]
        r.bias_full[...] = jnp.zeros_like(r.bias_full)
        for d in range(2 * LAYERS):
            first = 672 * d // 128
            r.bias_full[first : first + 7, :] += r.bias_slot[d // 2, d % 2, 0:7, :]
        counts = [r.counts[g].astype(F32) for g in range(GROUPS)]
        own_count = r.counts[at.grp].astype(F32)
        share = jnp.full((1, D), GROUPS * own_count) / jnp.full((1, D), sum(counts[1:], counts[0]))

        def put(row, value):
            r.rows[row : row + 1, :] = value

        def joined(first):
            return jnp.concatenate(
                [r.bias_full[first + j : first + j + 1, :] for j in range(3)], axis=1
            )

        for s in range(ROLLOUT):
            for row in range(6):
                first = 18 * s + 3 * row
                mod = jnp.concatenate([total[first + j : first + j + 1, :] for j in range(3)], axis=1)
                put(8 * s + row, mod + joined(24 + 3 * row))
            put(8 * s + 6, share)
            put(8 * s + 7, share)
        put(ROW_BQKV, joined(0))
        put(ROW_BQKV + 1, jnp.zeros((1, D), F32))
        put(ROW_BQKV + 2, joined(3))
        put(ROW_BPROJ, joined(6))
        for j in range(4):
            put(ROW_BUP + j, joined(9 + 3 * j))
        put(ROW_BDOWN, joined(21))
        r.rows[25:32, :] = jnp.zeros((7, D), F32)
        self.forward_sibling(0)
        self.finish_sibling(0)

    def after_first(self):
        self.forward_grp(1)
        self.forward_grp(2)

    def after_attend_pair(self, h):
        @pl.when(h == 1)
        def _():
            self.forward_sibling(1)

    def before_middle(self):
        self.forward_sibling(2)
        self.finish_sibling(1)
        self.finish_sibling(2)


    def got(self, unit, name, k=1):
        first = {"sib": 0, "grp": HALF, "z": HALF + 12 * SLAB, "piece": HALF + 15 * SLAB}[name]
        first += {"sib": 0, "grp": 4 * SLAB, "z": SLAB, "piece": 0}[name] * (k - 1)
        size = {"sib": HALF, "grp": 4 * SLAB, "z": SLAB, "piece": 4 * SLAB}[name]
        if unit == 0:
            if name in ("sib", "piece"):
                first = 0 if name == "sib" else HALF
                return self.refs.att0.at[first : first + size]
            first += 2 * 35 * SLAB - HALF
        else:
            first += 35 * SLAB * (unit - 1)
        return self.refs.act.at[first : first + size]

    def mine(self, unit):
        return self.refs.blocks.at[unit, span(HALF * self.at.core, HALF), :]

    def sum_sibling(self, unit):
        src = self.refs.blocks.at[unit, span(HALF * (1 - self.at.core), HALF), :]
        return remote(src, self.got(unit, "sib"), self.refs.rs, unit, self.at.sibling())

    def sum_grp(self, unit, k):
        peer = self.at.along_grp(k)
        src = self.mine(unit).at[span(4 * SLAB * peer[0], 4 * SLAB), :]
        return remote(src, self.got(unit, "grp", k), self.refs.rx, (unit, k - 1), peer)

    def sum_z(self, unit, k):
        there = lax.rem(self.at.z + k, LAYERS)
        src = self.mine(unit).at[span(4 * SLAB * self.at.grp + SLAB * there, SLAB), :]
        return remote(src, self.got(unit, "z", k), self.refs.rz, (unit, k - 1), self.at.along_z(k))

    def share_piece(self, unit, k):
        own = self.got(unit, "piece").at[span(SLAB * self.at.grp, SLAB), :]
        return remote(own, own, self.refs.ra, (unit, k - 1), self.at.along_grp(k))

    def add_sibling(self, unit):
        self.sum_sibling(unit).wait_recv()
        mine, got = (self.mine(unit), self.got(unit, "sib"))

        def add(i, carry):
            rows = span(SLAB * i, SLAB)
            mine[rows, :] = (mine[rows, :].astype(F32) + got[rows, :].astype(F32)).astype(BF)
            return carry

        lax.fori_loop(0, 16, add, 0)
        for k in self.steps:
            self.start(self.sum_grp(unit, k))

    def add_grp(self, unit):
        for k in self.steps:
            self.sum_grp(unit, k).wait_recv()
        mine = self.mine(unit).at[span(4 * SLAB * self.at.grp, 4 * SLAB), :]

        def add(i, carry):
            rows = span(SLAB * i, SLAB)
            value = mine[rows, :].astype(F32)
            for k in self.steps:
                value = value + self.got(unit, "grp", k)[rows, :].astype(F32)
            mine[rows, :] = value.astype(BF)
            return carry

        lax.fori_loop(0, 4, add, 0)
        for k in self.steps:
            self.start(self.sum_z(unit, k))

    def add_z(self, unit):
        for k in self.steps:
            self.sum_z(unit, k).wait_recv()
        mine = self.mine(unit).at[span(4 * SLAB * self.at.grp + SLAB * self.at.z, SLAB), :]
        value = mine[...].astype(F32)
        for k in self.steps:
            value = value + self.got(unit, "z", k)[...].astype(F32)
        value = value.astype(BF)
        self.got(unit, "piece")[span(SLAB * self.at.grp, SLAB), :] = value
        for k in self.steps:
            self.start(self.share_piece(unit, k))
        value = value.astype(F32)
        squares = col_sum(value * value)
        return squares[:, 0:128] + squares[:, 128:256] + squares[:, 256:384]

    def after_join(self):
        r, at = (self.refs, self.at)
        for peer in (
            [at.sibling()]
            + [at.along_grp(k) for k in self.steps]
            + [at.along_z(k) for k in self.steps]
        ):
            pl.semaphore_signal(r.joined, inc=1, device_id=peer, device_id_type=MESH_ID)
        fill_blocks(r, (1, 2))
        pl.semaphore_wait(r.joined, 7)
        self.start(self.sum_sibling(1))
        self.start(self.sum_sibling(2))

    def after_back_pair(self, h):
        @pl.when(h == 0)
        def _():
            self.add_sibling(1)
            self.add_sibling(2)

    def small_sum(self, index):
        r, at = (self.refs, self.at)
        if index == 0:
            return remote(r.vec, r.vec_sib, r.rv, 0, at.sibling())
        if index < 4:
            own = r.vec_z.at[at.z]
            return remote(own, own, r.rv, index, at.along_z(index))
        own = r.vec_g.at[at.grp]
        return remote(own, own, r.rv, index, at.along_grp(index - 3))

    def square_sum(self, index):
        r, at = (self.refs, self.at)
        if index < 7:
            peer = at.sibling()
            if index > 0:
                peer = at.along_z(index) if index < 4 else at.across(index - 3)
            own = r.square_d.at[at.dp]
        else:
            peer = at.along_grp(index - 6)
            own = r.square_g.at[at.grp]
        return remote(own, own, r.rq, index, peer)

    def after_last(self):
        r, at, steps = (self.refs, self.at, self.steps)
        fill_blocks(r, (0,))
        self.start(self.sum_sibling(0))
        fill_vec(r)
        self.start(self.small_sum(0))
        self.add_grp(1)
        moments = [r.start[g] + s for g in range(GROUPS) for s in range(ROLLOUT)]
        intervals = [r.interval[g] for g in range(GROUPS) for s in range(ROLLOUT)]
        r.cond_t[...] = jnp.transpose(condition_rows(moments, intervals, r.lead))
        self.small_sum(0).wait_recv()
        r.vec_z[at.z] = r.vec[...] + r.vec_sib[...]
        for index in steps:
            self.start(self.small_sum(index))
        self.add_sibling(0)
        self.add_grp(2)
        square = self.add_z(1)
        for index in steps:
            self.small_sum(index).wait_recv()
        r.vec_g[at.grp] = r.vec_z[0] + r.vec_z[1] + r.vec_z[2] + r.vec_z[3]
        for index in steps:
            self.start(self.small_sum(3 + index))
        square = square + self.add_z(2)
        self.add_grp(0)

        for index in steps:
            self.small_sum(3 + index).wait_recv()
        own_cond = r.cond_t[span(SLAB * at.dp, SLAB), :]
        columns = [jnp.broadcast_to(own_cond[:, k : k + 1], (SLAB, 128)) for k in range(8)]
        ada = r.a.at[0:864]

        def ada_tile(j, total):
            tile = jnp.zeros((SLAB, 128), F32)
            for g in range(GROUPS):
                for s in range(ROLLOUT):
                    row = r.vec_g[g, pl.ds(24 + 18 * s + j, 1), :]
                    tile = tile + columns[ROLLOUT * g + s] * row
            ada[pl.ds(j, SLAB, stride=18), :] = tile
            return total + col_sum(tile * tile)

        ada_square = lax.fori_loop(0, 18, ada_tile, jnp.zeros((1, 128), F32))
        puts = [local(ada, r.ada_far, r.in_sems.at[0])]
        vec_sum = r.vec_g[0] + r.vec_g[1] + r.vec_g[2] + r.vec_g[3]
        r.bias_out[0:24, :] = vec_sum[0:24]
        r.bias_out[24:42, :] = vec_sum[24:42] + vec_sum[42:60]
        r.bias_out[42:48, :] = jnp.zeros((6, 128), F32)

        square = square + 0.25 * ada_square + self.add_z(0)
        r.square_d[at.dp] = jnp.broadcast_to(square, (8, 128))
        for index in range(7):
            self.start(self.square_sum(index))
        for index in range(7):
            self.square_sum(index).wait_recv()
        total = r.square_d[0]
        for d in range(1, 2 * LAYERS):
            total = total + r.square_d[d]
        r.square_g[at.grp] = total
        for index in range(7, 10):
            self.start(self.square_sum(index))
        for unit in (1, 2, 0):
            for k in steps:
                self.share_piece(unit, k).wait_recv()
            puts.append(local(self.got(unit, "piece"), r.pieces_far.at[unit], r.in_sems.at[1 + unit]))
        for index in range(7, 10):
            self.square_sum(index).wait_recv()
        bias_sum = r.bias_out[...]
        total = r.square_g[0] + r.square_g[1] + r.square_g[2] + r.square_g[3]
        total = total + col_sum(bias_sum * bias_sum)
        r.square_out[...] = jnp.broadcast_to(jnp.sum(total, axis=1, keepdims=True), (8, 128))
        for made in puts:
            made.wait()
        self.drain()

    def drain(self):
        for unit in range(UNITS):
            for k in self.steps:
                self.gather_z(unit, k).wait_send()
                for m in self.steps:
                    self.gather_grp(unit, k, m).wait_send()
                self.sum_grp(unit, k).wait_send()
                self.sum_z(unit, k).wait_send()
                self.share_piece(unit, k).wait_send()
            for k in range(4):
                self.gather_sibling(unit, k).wait_send()
            self.sum_sibling(unit).wait_send()
        for index in range(8):
            self.small(index).wait_send()
        for index in range(7):
            self.small_sum(index).wait_send()
        for index in range(10):
            self.square_sum(index).wait_send()


correction = 1.0 - 0.5**ADAM_STEP
grad_limit = math.sqrt(NPARAM)


def adam(master, first, second, clipped, decay):
    first_new = 0.5 * first + 0.5 * clipped
    second_new = 0.5 * second + 0.5 * clipped * clipped
    update = first_new / correction / (jnp.sqrt(second_new / correction) + adam_eps)
    return (master - learn_rate * (update + decay * master), first_new, second_new)


STATE = ("qkv", "proj", "up", "down", "ada")


def finish_kernel(names, *refs):
    r = Refs(names, refs)
    loads = {
        name: local(getattr(r, name + "_far"), getattr(r, name), r.in_sems.at[index])
        for index, name in enumerate(("pieces", "grad_ada"))
    }
    for index, name in enumerate(STATE):
        for kind in range(3):
            loads[name, kind] = local(
                getattr(r, f"{name}_in{kind}"), getattr(r, f"{name}_{kind}"),
                r.in_sems.at[2 + 3 * index + kind],
            )
    streams = [
        local(getattr(r, name + "_in"), getattr(r, name), r.stream_sems.at[index])
        for index, name in enumerate(("y", "dx"))
    ]
    norm = jnp.sqrt(r.square[...])
    r.norm[0, 0] = jnp.max(norm)
    clip = grad_limit / jnp.maximum(norm, grad_limit)
    row_clip = clip[0:1, :]

    owner = lax.axis_index("dp")
    lane = lax.broadcasted_iota(jnp.int32, (1, 128), 1)
    first = 672 * owner // 128
    shift = lax.rem(32 * owner, 128)
    back = lax.rem(128 - shift, 128)
    for i in range(6):
        size = 128 if i < 5 else 32
        here = pltpu.roll(r.bias_sum[pl.ds(first + i, 1), :], back, axis=1)
        there = pltpu.roll(r.bias_sum[pl.ds(first + i + 1, 1), :], back, axis=1)
        grad = jnp.where(lane < 128 - shift, here, there) * row_clip
        place = pl.ds(128 * i, size)
        state = [getattr(r, f"bias_in{kind}")[place].reshape(1, size) for kind in range(3)]
        new, first_new, second_new = adam(*state, grad[:, :size], 0.0)
        r.bias_out0[place] = new.reshape(size)
        r.bias_out1[place] = first_new.reshape(size)
        r.bias_out2[place] = second_new.reshape(size)
        r.bias_out3[place] = new.reshape(size).astype(BF)

    loads["pieces"].wait()
    piece = r.pieces
    for g in range(3):
        for j in range(3):
            r.grad_qkv[pl.ds(3 * g + j, SLAB, stride=9), :] = piece[
                0, SLAB * g : SLAB * (g + 1), 128 * j : 128 * j + 128
            ].astype(F32)
    for j in range(3):
        columns = slice(128 * j, 128 * j + 128)
        r.grad_proj[pl.ds(j, SLAB, stride=3), :] = piece[0, 3 * SLAB :, columns].astype(F32)
    for g in range(GROUPS):
        rows = slice(SLAB * g, SLAB * (g + 1))
        for j in range(3):
            columns = slice(128 * j, 128 * j + 128)
            r.grad_up[pl.ds(3 * g + j, SLAB, stride=12), :] = piece[1, rows, columns].astype(F32)
            r.grad_down[pl.ds(3 * SLAB * g + j, SLAB, stride=3), :] = piece[2, rows, columns].astype(F32)

    stores = []
    for index, name in enumerate(STATE):
        for kind in range(3):
            loads[name, kind].wait()
        if name == "ada":
            loads["grad_ada"].wait()
        grad, low = (getattr(r, "grad_" + name), getattr(r, name + "_low"))
        state = [getattr(r, f"{name}_{kind}") for kind in range(3)]

        def chunk(i, carry):
            rows = pl.ds(pl.multiple_of(16 * i, 16), 16)
            new, first_new, second_new = adam(
                *(ref[rows, :] for ref in state), grad[rows, :] * row_clip, 0.1
            )
            for ref, value in zip(state, (new, first_new, second_new)):
                ref[rows, :] = value
            low[rows, :] = new.astype(BF)
            return carry

        lax.fori_loop(0, grad.shape[0] // 16, chunk, 0, unroll=3)
        for kind, ref in enumerate((*state, low)):
            stores.append(local(ref, getattr(r, f"{name}_out{kind}"), r.out_sems.at[4 * index + kind]))
        if index < 2:
            name = ("y", "dx")[index]
            streams[index].wait()
            stores.append(local(getattr(r, name), getattr(r, name + "_out"), r.stream_sems.at[index]))
    for made in stores:
        made.wait()


def finish(y, dx, pieces, ada, bias_sum, square, masters, firsts, seconds):
    vmem, hbm, dma = (pltpu.VMEM, pl.ANY, pltpu.SemaphoreType.DMA)
    state = list(zip(masters, firsts, seconds))
    shapes = {name: (arrays[0].size // 128, 128) for name, arrays in zip(STATE, state)}
    ins = [
        ("square", square, vmem), ("bias_sum", bias_sum, vmem), ("pieces_far", pieces, hbm),
        ("grad_ada_far", ada, hbm), ("y_in", y, hbm), ("dx_in", dx, hbm),
        *[(f"bias_in{kind}", array, vmem) for kind, array in enumerate(state[5])],
        *[
            (f"{name}_in{kind}", array.reshape(-1, 128), hbm)
            for name, arrays in zip(STATE, state)
            for kind, array in enumerate(arrays)
        ],
    ]
    outs = [("norm", (1, 1), F32, pltpu.SMEM), ("y_out", y.shape, F32, hbm), ("dx_out", dx.shape, F32, hbm)]
    for kind in range(4):
        dtype = F32 if kind < 3 else BF
        outs += [(f"{name}_out{kind}", shapes[name], dtype, hbm) for name in STATE]
        outs.append((f"bias_out{kind}", state[5][0].shape, dtype, vmem))
    scratch = [
        ("pieces", vmem(pieces.shape, BF)), ("y", vmem(y.shape, F32)), ("dx", vmem(dx.shape, F32)),
        *[(f"{name}_{kind}", vmem(shapes[name], F32)) for name in STATE for kind in range(3)],
        *[(f"{name}_low", vmem(shapes[name], BF)) for name in STATE],
        *[(f"grad_{name}", vmem(shapes[name], F32)) for name in STATE],
        ("in_sems", dma((17,))), ("stream_sems", dma((2,))), ("out_sems", dma((20,))),
    ]
    names = [item[0] for item in (*ins, *outs, *scratch)]
    norm, y, dx, *rest = pl.pallas_call(
        functools.partial(finish_kernel, names),
        in_specs=[pl.BlockSpec(memory_space=space) for *_, space in ins],
        out_specs=[pl.BlockSpec(memory_space=space) for *_, space in outs],
        out_shape=[jax.ShapeDtypeStruct(shape, kind) for _, shape, kind, _ in outs],
        scratch_shapes=[kind for _, kind in scratch],
        name="finish",
    )(*(array for _, array, _ in ins))
    return (y, dx, norm.reshape(()), *(array.reshape(-1) for array in rest))


MASTERS = ("qkv", "proj", "up", "down", "ada")


def block_kernel(names, hooked, *refs):
    r = Refs(names, refs)
    if hooked is Together:
        r.masters = {name: getattr(r, "far_" + name) for name in MASTERS}
        for name in ("gz", "gx", "gs", "gm", "rs", "rx", "rz", "ra", "rv", "rq"):
            setattr(r, name, (getattr(r, name + "_out"), getattr(r, name + "_in")))
    hooks = hooked(r)
    length = r.x.shape[0]
    pairs = HEADS // 2
    get_cot = local(r.cot_far, r.cot, r.out_sems.at[2])

    def over_rows(body):
        def step(i, carry):
            body(pl.ds(pl.multiple_of(i * ROWS, ROWS), ROWS))
            return carry

        lax.fori_loop(0, length // ROWS, step, 0)

    def columns(h, offset=0):
        return pl.ds(pl.multiple_of(offset + 128 * h, 128), 128)

    def over_pairs(body):
        def step(h, carry):
            body(h)
            return carry

        lax.fori_loop(0, pairs, step, 0)

    def act_refs(rows):
        first = rows.start
        return [
            r.act.at[pl.ds(pl.multiple_of(length * part + first, ROWS), ROWS)] for part in range(4)
        ]

    def a_refs(rows):
        first = rows.start
        return [
            r.a.at[pl.ds(pl.multiple_of(length * part + first, ROWS), ROWS)] for part in range(3)
        ]

    def save(step, h):
        slot = lax.rem(h, 2)
        return pltpu.make_async_copy(
            r.p.at[slot], r.p_far.at[step, pl.ds(2 * h, 2)], r.p_sems.at[slot]
        )

    def fetch(step, h):
        slot = lax.rem(h, 2)
        return pltpu.make_async_copy(
            r.p_far.at[step, pl.ds(2 * h, 2)], r.p.at[slot], r.p_sems.at[slot]
        )

    def attend(step, qkv, att, after):
        def body(h):
            @pl.when(h >= 2)
            def _():
                save(step, h - 2).wait()

            attend_pair(
                qkv[:, columns(h)], qkv.at[:, columns(h, D)], qkv[:, columns(h, 2 * D)],
                att.at[:, columns(h)], r.p.at[lax.rem(h, 2)], r.turned,
            )
            save(step, h).start()
            after(h)

        over_pairs(body)

    def finish_saves(step):
        for h in range(pairs - 2, pairs):
            save(step, h).wait()

    def attend_back(step, qkv, after):
        def body(h):
            fetch(step, h).wait()
            attend_back_pair(
                qkv[:, columns(h)], qkv[:, columns(h, D)], qkv.at[:, columns(h, 2 * D)],
                r.datt[:, columns(h)], r.p.at[lax.rem(h, 2)],
                r.dqkv.at[:, columns(h)], r.dqkv.at[:, columns(h, D)],
                r.dqkv.at[:, columns(h, 2 * D)], r.turned,
            )

            @pl.when(h + 2 < pairs)
            def _():
                fetch(step, h + 2).start()

            after(h)

        over_pairs(body)

    nothing = lambda h: None
    hooks.begin()

    def first(rows):
        r.qkv0[rows, :] = first_rows(r.x[rows, :], r.rows, r.wa)

    over_rows(first)
    hooks.after_first()
    attend(0, r.qkv0, r.att0, hooks.after_attend_pair)
    hooks.before_middle()

    def middle(rows):
        middle_rows(
            r.x.at[rows], r.att0.at[rows], r.rows, r.wa, r.wup, r.wdown,
            a_refs(rows), r.gp.at[rows], act_refs(rows), r.f.at[rows], r.x1.at[rows],
            r.qkv1.at[rows],
        )

    over_rows(middle)
    finish_saves(0)
    attend(1, r.qkv1, r.att1, nothing)

    for ref in (r.gqkv, r.gproj, r.gup, r.gdown, r.wide, r.narrow0, r.narrow1, r.bias):
        ref[...] = jnp.zeros_like(ref)

    def turn(rows):
        turn_rows(
            r.x1.at[rows], r.att1.at[rows], r.cot.at[rows], r.rows, r.wa, r.wup,
            r.wdown, r.y.at[rows], r.dmid.at[rows], r.datt.at[rows], r.gdown, r.gup, r.gproj,
            r.wide, r.narrow1,
        )

    finish_saves(1)
    for h in range(2):
        fetch(1, h).start()
    get_cot.wait()
    over_rows(turn)
    put_y = local(r.y, r.y_far, r.out_sems.at[0])
    attend_back(1, r.qkv1, nothing)
    for h in range(2):
        fetch(0, h).start()

    def join(rows):
        join_rows(
            r.dqkv.at[rows], r.x1.at[rows], r.x.at[rows], a_refs(rows), r.gp.at[rows],
            act_refs(rows), r.f.at[rows], r.att0.at[rows], r.rows, r.wa, r.wup, r.wdown,
            r.dmid.at[rows], r.datt.at[rows], r.gqkv, r.gdown, r.gup, r.gproj, r.wide, r.narrow1,
            r.narrow0, r.bias,
        )

    over_rows(join)
    hooks.after_join()
    attend_back(0, r.qkv0, hooks.after_back_pair)

    def last(rows):
        r.dmid[rows, :] = qkv_back(
            mod_reader(r.rows, 0), r.x[rows, :].astype(F32), r.dmid[rows, :],
            r.dqkv[rows, :], r.wa, r.gqkv, r.narrow0, r.bias,
        )

    over_rows(last)
    put_dx = local(r.dmid, r.dx_far, r.out_sems.at[1])
    hooks.after_last()
    put_y.wait()
    put_dx.wait()


def block_call(hooked, inputs, cotangent, extra_in, extra_out, extra_scratch, params):
    length = inputs.shape[0]
    vmem, hbm, dma = (pltpu.VMEM, pl.ANY, pltpu.SemaphoreType.DMA)
    weights = (ROLLOUT, HEADS, length, length)
    ins = [("x", inputs, vmem), ("cot_far", cotangent, hbm), *extra_in]
    outs = [
        ("y_far", (length, D), F32, hbm), ("dx_far", (length, D), F32, hbm),
        ("p_far", weights, BF, hbm), *extra_out,
    ]
    scratch = [
        ("wa", vmem((D, FF), BF)), ("wup", vmem((D, FF), BF)), ("wdown", vmem((FF, D), BF)),
        ("cot", vmem((length, D), BF)), ("qkv0", vmem((length, 3 * D), BF)),
        ("qkv1", vmem((length, 3 * D), BF)), ("p", vmem((2, 2, length, length), BF)),
        ("att0", vmem((length, D), BF)), ("att1", vmem((length, D), BF)),
        *[(name, vmem((length, D), F32)) for name in ("f", "x1", "dmid", "y")], ("a", vmem((3 * length, 128), F32)),
        ("gp", vmem((length, FF), F32)), ("act", vmem((4 * length, D), BF)),
        ("datt", vmem((length, D), BF)), ("dqkv", vmem((length, 3 * D), BF)),
        ("gqkv", vmem((D, 3 * D), F32)), ("gproj", vmem((D, D), F32)),
        ("gup", vmem((D, FF), F32)), ("gdown", vmem((FF, D), F32)),
        ("turned", vmem((2, 128, length), BF)), ("wide", vmem((8, FF), F32)),
        ("narrow0", vmem((8, D), F32)), ("narrow1", vmem((8, D), F32)),
        ("bias", vmem((8, 3 * D), F32)), ("blocks", vmem((UNITS, 2 * HALF, PART), BF)),
        ("rows", vmem((32, D), F32)), ("vec", vmem((64, 128), F32)),
        ("in_sems", dma((5,))), ("p_sems", dma((2,))), ("out_sems", dma((3,))),
        *extra_scratch,
    ]
    names = [item[0] for item in (*ins, *outs, *scratch)]
    return pl.pallas_call(
        functools.partial(block_kernel, names, hooked),
        in_specs=[pl.BlockSpec(memory_space=space) for _, _, space in ins],
        out_specs=[pl.BlockSpec(memory_space=space) for *_, space in outs],
        out_shape=[jax.ShapeDtypeStruct(shape, kind) for _, shape, kind, _ in outs],
        scratch_shapes=[kind for _, kind in scratch],
        compiler_params=pltpu.CompilerParams(vmem_limit_bytes=67043328, **params),
        name="block",
    )(*(array for _, array, _ in ins))


def block_alone(inputs, cotangent, rows, wa, wup, wdown):
    hbm = pl.ANY
    y, dx, _, blocks, vec = block_call(
        Alone, inputs, cotangent,
        [("rows_far", rows, hbm), ("wa_far", wa, hbm), ("wup_far", wup, hbm), ("wdown_far", wdown, hbm)],
        [("blocks_far", (UNITS, 2 * HALF, PART), BF, hbm), ("vec_far", (64, 128), F32, hbm)],
        [], {},
    )
    return (y, dx, blocks, vec)


def block_together(inputs, cotangent, start, interval, counts, lead, masters):
    vmem, hbm, smem, dma = (pltpu.VMEM, pl.ANY, pltpu.SMEM, pltpu.SemaphoreType.DMA)
    qkv, proj, up, down, ada, bias = masters
    far = [
        ("far_" + name, array.reshape(-1, 128), hbm)
        for name, array in zip(MASTERS, (qkv, proj, up, down, ada))
    ]
    pairs_of = [
        ("gz", (UNITS, 3)), ("gx", (UNITS, 3, 3)), ("gs", (UNITS, 4)), ("gm", (8,)),
        ("rs", (UNITS,)), ("rx", (UNITS, 3)), ("rz", (UNITS, 3)), ("ra", (UNITS, 3)),
        ("rv", (7,)), ("rq", (10,)),
    ]
    y, dx, _, pieces, ada_grad, bias_sum, square = block_call(
        Together, inputs, cotangent,
        [("start", start, smem), ("interval", interval, smem), ("counts", counts, smem),
         ("lead", lead, vmem), ("bias_flat", bias, vmem), *far],
        [("pieces_far", (UNITS, 4 * SLAB, PART), BF, hbm), ("ada_far", (18 * SLAB, 128), F32, hbm),
         ("bias_out", (48, 128), F32, vmem), ("square_out", (8, 128), F32, vmem)],
        [("cond_t", vmem((D, 8), F32)), ("part_own", vmem((40, 128), F32)),
         ("part_sib", vmem((40, 128), F32)), ("part_z", vmem((LAYERS, 40, 128), F32)),
         ("bias_own", vmem((8, 128), F32)), ("bias_slot", vmem((LAYERS, 2, 8, 128), F32)), ("bias_full", vmem((48, 128), F32)),
         ("vec_sib", vmem((64, 128), F32)), ("vec_z", vmem((LAYERS, 64, 128), F32)),
         ("vec_g", vmem((GROUPS, 64, 128), F32)), ("square_d", vmem((8, 8, 128), F32)),
         ("square_g", vmem((GROUPS, 8, 128), F32)), ("joined", pltpu.SemaphoreType.REGULAR),
         *[(name + end, dma(shape)) for name, shape in pairs_of for end in ("_out", "_in")]],
        dict(collective_id=0, has_side_effects=True),
    )
    return (y, dx, pieces, ada_grad, bias_sum, square)


def step_embedding(moment):
    half_width = D // 2
    freqs = jnp.exp(-math.log(10000.0) * jnp.arange(half_width, dtype=F32) / half_width)
    angles = moment[:, None] * freqs[None, :]
    return jnp.concatenate([jnp.sin(angles), jnp.cos(angles)], axis=1)


def all_conditions(group_interval, rollout_start, lead_table):
    chosen = group_interval[:, None] == jnp.arange(INTERVALS)[None, :]
    lead_rows = jnp.sum(jnp.where(chosen[:, :, None], lead_table[None], 0.0), axis=1)
    start = rollout_start.astype(F32)
    rows = [lead_rows + step_embedding(start + offset) for offset in range(ROLLOUT)]
    return jax.nn.silu(jnp.stack(rows, axis=1)).astype(BF)


def plain_gather(group_interval, counts, rollout_start, lead_table, masters):
    low = [master.astype(BF) for master in masters]
    owner = lax.axis_index("dp")
    group_index = lax.axis_index("grp")
    own_rows = D // lax.axis_size("dp")
    counts = counts.astype(F32)
    share = lax.axis_size("grp") * counts / jnp.sum(counts)
    share = lax.dynamic_index_in_dim(share, group_index, keepdims=False)
    conditions = all_conditions(group_interval, rollout_start, lead_table)
    owner_columns = lax.dynamic_slice_in_dim(conditions, owner * own_rows, own_rows, axis=2)
    own_condition = lax.dynamic_index_in_dim(owner_columns, group_index, keepdims=False)
    modulation = lax.psum(dot(own_condition, low[4].reshape(own_rows, 6 * D)), "dp")
    qkv, proj, up, down, bias = [
        lax.all_gather(low[index], "dp", axis=0, tiled=True) for index in (0, 1, 2, 3, 5)
    ]
    bias = bias.astype(F32)
    modulation = modulation + bias[4 * D + FF :][None]
    share_rows = jnp.broadcast_to(share, (ROLLOUT, 2, D))
    mods = jnp.concatenate([modulation.reshape(ROLLOUT, 6, D), share_rows], axis=1).reshape(-1, D)
    rows = jnp.concatenate(
        [mods, bias[:D][None], jnp.zeros((1, D), F32), bias[D : 4 * D + FF].reshape(-1, D),
         jnp.zeros((7, D), F32)]
    )
    wa = jnp.concatenate([qkv.reshape(D, 3 * D), proj.reshape(D, D)], axis=1)
    return (wa, up.reshape(D, FF), down.reshape(FF, D), rows, owner_columns)


def plain_update(owner_columns, vec, blocks, masters, firsts, seconds):
    owner = lax.axis_index("dp")
    vec = vec.reshape(-1)
    split = 4 * D + FF
    dmod = vec[split : split + ROLLOUT * 6 * D].reshape(ROLLOUT, 6 * D)
    dmod_all = lax.all_gather(lax.psum(dmod, "dp"), "grp")
    bias_sum = lax.psum(vec[:split], ("grp", "dp"))
    bias_sum = jnp.concatenate([bias_sum, jnp.sum(dmod_all, axis=(0, 1))])
    bias_rows = masters[5].shape[0]
    bias_grad = lax.dynamic_slice_in_dim(bias_sum, owner * bias_rows, bias_rows)
    ada_grad = jnp.einsum(
        "gsr,gsc->rc", owner_columns.astype(F32), dmod_all, precision=lax.Precision.HIGHEST
    )
    blocks = blocks.reshape(UNITS, 2, 4, LAYERS, SLAB, PART)
    flat_a, flat_up = [blocks[u].transpose(2, 0, 3, 1, 4).reshape(D, FF) for u in (0, 1)]
    flat_down = blocks[2].transpose(2, 0, 1, 3, 4)
    flat = [flat_a[:, : 3 * D], flat_a[:, 3 * D :], flat_up, flat_down]
    shares = []
    for grad in flat:
        summed = lax.psum(grad.reshape(-1), "grp").astype(F32)
        shares.append(lax.psum_scatter(summed, "dp", scatter_dimension=0, tiled=True))
    shares = shares + [ada_grad.reshape(-1), bias_grad]
    local_square = sum((jnp.sum(piece * piece) for piece in shares))
    grad_norm = jnp.sqrt(lax.psum(local_square, "dp"))
    clip = grad_limit / jnp.maximum(grad_norm, grad_limit)
    decays = [0.1, 0.1, 0.1, 0.1, 0.1, 0.0]
    results = [
        adam(master, first, second, grad * clip, decay)
        for master, first, second, grad, decay in zip(masters, firsts, seconds, shares, decays)
    ]
    news, first_news, second_news = zip(*results)
    return (grad_norm, *news, *first_news, *second_news, *(new.astype(BF) for new in news))


def per_device(
    inputs,
    cotangent,
    group_interval,
    sample_counts,
    rollout_start,
    lead_table,
    *state,
):
    masters, firsts, seconds = (state[0:6], state[6:12], state[12:18])
    fits = (
        lax.axis_size("dp") == 2 * LAYERS
        and lax.axis_size("grp") == GROUPS
        and inputs.shape[0] == 1024
    )
    if not fits:
        wa, wup, wdown, rows, owner_columns = plain_gather(
            group_interval, sample_counts, rollout_start, lead_table, masters
        )
        result, input_grad, blocks, vec = block_alone(inputs, cotangent, rows, wa, wup, wdown)
        rest = plain_update(owner_columns, vec, blocks, masters, firsts, seconds)
        return (result, input_grad, *rest)
    result, input_grad, pieces, ada_grad, bias_sum, square = block_together(
        inputs, cotangent, rollout_start, group_interval, sample_counts, lead_table, masters
    )
    return finish(
        result, input_grad, pieces, ada_grad, bias_sum, square, masters, firsts, seconds
    )


def solution(mesh):
    rows = P(("grp", "dp"), None)
    return jax.shard_map(
        per_device,
        mesh=mesh,
        in_specs=(rows, rows, P(), P(), P(), P(), *[P("dp")] * 18),
        out_specs=(rows, rows, P(), *[P("dp")] * 24),
        check_vma=False,
    )
```

```python
import functools
import math

import jax
import jax.numpy as jnp
from jax import lax
from jax.experimental import pallas as pl
from jax.experimental.pallas import tpu as pltpu
from jax.sharding import PartitionSpec as P

D = 384
HEADS = 6
FF = 1536
ROLLOUT = 2
INTERVALS = 3
ADAM_STEP = 10
HEAD_DIM = 64
NPARAM = 2659584

norm_eps = 1e-06
learn_rate = 0.05
adam_eps = 1e-08

BF = jnp.bfloat16
F32 = jnp.float32
NN = (((1,), (0,)), ((), ()))
NT = (((1,), (1,)), ((), ()))
TN = (((0,), (0,)), ((), ()))

ROWS = 256
SLAB = 48
PART = 384
ROW_SHARE = 6
ROW_BQKV, ROW_BPROJ, ROW_BUP, ROW_BDOWN = 16, 19, 20, 24
SHIFT1, SCALE1, GATE1, SHIFT2, SCALE2, GATE2 = range(6)


def dot(left, right, dims=NN):
    return lax.dot_general(left, right, dims, preferred_element_type=F32)


def layer_norm(stream):
    centred = stream - jnp.mean(stream, axis=-1, keepdims=True)
    inverse = lax.rsqrt(jnp.mean(centred * centred, axis=-1, keepdims=True) + norm_eps)
    return (centred * inverse, inverse)


def norm_back(normed, inverse, grad_out):
    mean_grad = jnp.mean(grad_out, axis=-1, keepdims=True)
    mean_prod = jnp.mean(grad_out * normed, axis=-1, keepdims=True)
    return inverse * (grad_out - mean_grad - normed * mean_prod)


def col_sum(value):
    return jnp.sum(value, axis=0, keepdims=True)


def modulated(normed, mods, scale_row, shift_row):
    return (normed * (1.0 + mods(scale_row)) + mods(shift_row)).astype(BF)


def mod_reader(mod_ref, step):
    return lambda row: mod_ref[pl.ds(8 * step + row, 1), :]


def gelu_pair(value):
    cdf = 0.5 + 0.5 * lax.erf(value * (2.0**-0.5))
    density = jnp.exp(-0.5 * value * value) * (1.0 / math.sqrt(2.0 * math.pi))
    return (value * cdf, cdf + value * density)


def side_by_side(ref, first, count):
    return jnp.concatenate([ref[row : row + 1, :] for row in range(first, first + count)], axis=1)


def first_rows(x, rows_ref, wa_ref):
    normed, _ = layer_norm(x.astype(F32))
    hidden = modulated(normed, mod_reader(rows_ref, 0), SCALE1, SHIFT1)
    qkv = dot(hidden, wa_ref[:, : 3 * D]) + side_by_side(rows_ref, ROW_BQKV, 3)
    return qkv.astype(BF)


def middle_rows(
    x_ref, att_ref, rows_ref, wa_ref, wup_ref, wdown_ref,
    a_refs, gp_ref, act_refs, f_ref, next_ref, qkv_ref,
):
    mods = mod_reader(rows_ref, 0)
    later = mod_reader(rows_ref, 1)
    branch = dot(att_ref[...], wa_ref[:, 3 * D :]) + mods(ROW_BPROJ)
    for part, ref in enumerate(a_refs):
        ref[...] = branch[:, 128 * part : 128 * (part + 1)]
    middle = x_ref[...].astype(F32) + mods(GATE1) * branch
    normed, _ = layer_norm(middle)
    hidden = modulated(normed, mods, SCALE2, SHIFT2)
    upward = dot(hidden, wup_ref[...]) + side_by_side(rows_ref, ROW_BUP, 4)
    act, slope = gelu_pair(upward)
    gp_ref[...] = slope
    act = act.astype(BF)
    for part, ref in enumerate(act_refs):
        ref[...] = act[:, PART * part : PART * (part + 1)]
    branch = dot(act, wdown_ref[...]) + mods(ROW_BDOWN)
    f_ref[...] = branch
    stream = middle + mods(GATE2) * branch
    next_ref[...] = stream
    normed, _ = layer_norm(stream)
    hidden = modulated(normed, later, SCALE1, SHIFT1)
    qkv = dot(hidden, wa_ref[:, : 3 * D]) + side_by_side(rows_ref, ROW_BQKV, 3)
    qkv_ref[...] = qkv.astype(BF)


def ffn_back(
    mods, grad, branch_two, act, slope, hidden, wdown_ref, gdown_ref, gup_ref, wide_ref, narrow_ref
):
    df = (mods(GATE2) * grad).astype(BF)
    narrow_ref[pl.ds(GATE2, 1), :] += col_sum(grad * branch_two)
    narrow_ref[pl.ds(7, 1), :] += col_sum(df.astype(F32))
    gdown_ref[...] += dot(act, df, TN)
    dact = dot(df, wdown_ref[...], NT)
    du = (dact * slope).astype(BF)
    wide_ref[pl.ds(0, 1), :] += col_sum(du.astype(F32))
    gup_ref[...] += dot(hidden, du, TN)
    return du


def middle_back(
    mods, grad, du, normed, inverse, branch_one, att, wa_ref, wup_ref, gproj_ref, narrow_ref,
    dmid_ref, datt_ref,
):
    dh = dot(du, wup_ref[...], NT)
    narrow_ref[pl.ds(SHIFT2, 1), :] += col_sum(dh)
    narrow_ref[pl.ds(SCALE2, 1), :] += col_sum(dh * normed)
    dmid = grad + norm_back(normed, inverse, dh * (1.0 + mods(SCALE2)))
    dmid_ref[...] = dmid
    da = (mods(GATE1) * dmid).astype(BF)
    narrow_ref[pl.ds(GATE1, 1), :] += col_sum(dmid * branch_one)
    narrow_ref[pl.ds(6, 1), :] += col_sum(da.astype(F32))
    gproj_ref[...] += dot(att, da, TN)
    datt_ref[...] = dot(da, wa_ref[:, 3 * D :], NT).astype(BF)


def turn_rows(
    x_ref, att_ref, cot_ref, rows_ref, wa_ref, wup_ref, wdown_ref,
    out_ref, dmid_ref, datt_ref, gdown_ref, gup_ref, gproj_ref, wide_ref, narrow_ref,
):
    mods = mod_reader(rows_ref, 1)
    shared = mod_reader(rows_ref, 0)
    att = att_ref[...]
    branch_one = dot(att, wa_ref[:, 3 * D :]) + shared(ROW_BPROJ)
    middle = x_ref[...] + mods(GATE1) * branch_one
    normed, inverse = layer_norm(middle)
    hidden = modulated(normed, mods, SCALE2, SHIFT2)
    upward = dot(hidden, wup_ref[...]) + side_by_side(rows_ref, ROW_BUP, 4)
    act, slope = gelu_pair(upward)
    act = act.astype(BF)
    branch_two = dot(act, wdown_ref[...]) + shared(ROW_BDOWN)
    out_ref[...] = middle + mods(GATE2) * branch_two
    grad = cot_ref[...].astype(F32)
    du = ffn_back(
        mods, grad, branch_two, act, slope, hidden, wdown_ref, gdown_ref, gup_ref, wide_ref, narrow_ref
    )
    middle_back(
        mods, grad, du, normed, inverse, branch_one, att, wa_ref, wup_ref, gproj_ref, narrow_ref,
        dmid_ref, datt_ref,
    )


def qkv_back(mods, stream, dmid, dqkv, wa_ref, narrow_ref, bias_ref, gqkv_ref=None):
    normed, inverse = layer_norm(stream)
    bias_ref[pl.ds(0, 1), :] += col_sum(dqkv.astype(F32))
    if gqkv_ref is not None:
        gqkv_ref[...] += dot(modulated(normed, mods, SCALE1, SHIFT1), dqkv, TN)
    dh = dot(dqkv, wa_ref[:, : 3 * D], NT)
    narrow_ref[pl.ds(SHIFT1, 1), :] += col_sum(dh)
    narrow_ref[pl.ds(SCALE1, 1), :] += col_sum(dh * normed)
    return dmid + norm_back(normed, inverse, dh * (1.0 + mods(SCALE1)))


def middle_again(mods, x_ref, a_refs):
    branch_one = jnp.concatenate([ref[...] for ref in a_refs], axis=1)
    normed, inverse = layer_norm(x_ref[...].astype(F32) + mods(GATE1) * branch_one)
    return (branch_one, normed, inverse)


def join_rows(
    dqkv_ref, x1_ref, x0_ref, a_refs, gp_ref, act_refs, f_ref, rows_ref, wa_ref, wdown_ref,
    hidden_ref, dmid_ref, gqkv_ref, gdown_ref, gup_ref, wide_ref, narrow1_ref, narrow_ref, bias_ref,
):
    grad = qkv_back(
        mod_reader(rows_ref, 1), x1_ref[...], dmid_ref[...], dqkv_ref[...], wa_ref,
        narrow1_ref, bias_ref, gqkv_ref,
    )
    dmid_ref[...] = grad
    mods = mod_reader(rows_ref, 0)
    normed, _ = layer_norm(x0_ref[...].astype(F32))
    hidden_ref[...] = modulated(normed, mods, SCALE1, SHIFT1)
    _, normed, _ = middle_again(mods, x0_ref, a_refs)
    act = jnp.concatenate([ref[...] for ref in act_refs], axis=1)
    du = ffn_back(
        mods, grad, f_ref[...], act, gp_ref[...], modulated(normed, mods, SCALE2, SHIFT2),
        wdown_ref, gdown_ref, gup_ref, wide_ref, narrow_ref,
    )
    for part, ref in enumerate(act_refs):
        ref[...] = du[:, PART * part : PART * (part + 1)]


def join_middle_rows(
    x0_ref, a_refs, du_refs, att_ref, rows_ref, wa_ref, wup_ref,
    dmid_ref, datt_ref, gproj_ref, narrow_ref,
):
    mods = mod_reader(rows_ref, 0)
    branch_one, normed, inverse = middle_again(mods, x0_ref, a_refs)
    du = jnp.concatenate([ref[...] for ref in du_refs], axis=1)
    middle_back(
        mods, dmid_ref[...], du, normed, inverse, branch_one, att_ref[...], wa_ref, wup_ref,
        gproj_ref, narrow_ref, dmid_ref, datt_ref,
    )


def head_lanes(rows):
    lane = lax.broadcasted_iota(jnp.int32, (rows, 2 * HEAD_DIM), 1)
    return (lane < HEAD_DIM, lane >= HEAD_DIM)


def turned_heads(rows_f32, out_ref):
    turned = jnp.transpose(rows_f32)
    row = lax.broadcasted_iota(jnp.int32, turned.shape, 0)
    out_ref[0] = jnp.where(row < HEAD_DIM, turned, 0.0).astype(BF)
    out_ref[1] = jnp.where(row >= HEAD_DIM, turned, 0.0).astype(BF)


score_scale = HEAD_DIM**-0.5


def attend_pair(q, k_ref, v, o_ref, p_ref, vt_ref):
    turned_heads(v.astype(F32), vt_ref)
    queries = q * BF(score_scale)
    mixed = None
    for half, lanes in enumerate(head_lanes(queries.shape[0])):
        scores = dot(k_ref[...], jnp.where(lanes, queries, BF(0)), NT)
        top = jnp.max(scores, axis=0, keepdims=True)
        weights = jnp.exp(scores - top)
        total = jnp.sum(weights, axis=0, keepdims=True)
        low = (weights * (1.0 / total)).astype(BF)
        p_ref[half] = low
        part = dot(vt_ref[half], low)
        mixed = part if mixed is None else mixed + part
    o_ref[...] = jnp.transpose(mixed).astype(BF)


def attend_back_pair(q, k, v_ref, grads, p_ref, dq_ref, dk_ref, dv_ref, kt_ref, between):
    turned_heads(k.astype(F32) * score_scale, kt_ref)
    queries = q * BF(score_scale)
    own_lanes = head_lanes(queries.shape[0])
    for half, lanes in enumerate(own_lanes):
        grad = jnp.where(lanes, grads, BF(0))
        query = jnp.where(lanes, queries, BF(0))
        low = p_ref[half]
        weight_grad = dot(v_ref[...], grad, NT)
        weights = low.astype(F32)
        delta = jnp.sum(weights * weight_grad, axis=0, keepdims=True)
        score_grad = (weights * (weight_grad - delta)).astype(BF)
        news = (
            jnp.transpose(dot(kt_ref[half], score_grad)), dot(score_grad, query), dot(low, grad)
        )
        for ref, new in zip((dq_ref, dk_ref, dv_ref), news):
            new = new.astype(BF)
            ref[...] = new if half == 0 else jnp.where(lanes, new, ref[...])
        if half == 0 and between is not None:
            between()


class Refs:
    def __init__(self, names, refs):
        for name, ref in zip(names, refs, strict=True):
            setattr(self, name, ref)

MESH_ID = pl.DeviceIdType.MESH
GROUPS = 4
LAYERS = 4
UNITS = 3
HALF = 768


class Place:
    def __init__(self):
        self.grp = lax.axis_index("grp")
        self.dp = lax.axis_index("dp")
        self.z = self.dp // 2
        self.core = self.dp % 2

    def sibling(self):
        return (self.grp, 2 * self.z + 1 - self.core)

    def along_grp(self, step):
        return (lax.rem(self.grp + step, GROUPS), self.dp)

    def along_z(self, step):
        return (self.grp, 2 * lax.rem(self.z + step, LAYERS) + self.core)

    def across(self, step):
        return (self.grp, 2 * lax.rem(self.z + step, LAYERS) + 1 - self.core)


def greet(peers):
    barrier = pltpu.get_barrier_semaphore()
    for peer in peers:
        pl.semaphore_signal(barrier, inc=1, device_id=peer, device_id_type=MESH_ID)
    return lambda: pl.semaphore_wait(barrier, len(peers))


def remote(src, dst, sems, index, peer):
    send_sem, recv_sem = sems
    return pltpu.make_async_remote_copy(
        src_ref=src, dst_ref=dst, send_sem=send_sem.at[index], recv_sem=recv_sem.at[index],
        device_id=peer, device_id_type=MESH_ID,
    )


def condition_rows(moments, intervals, lead_ref):
    shape = (8, D)
    row = lax.broadcasted_iota(jnp.int32, shape, 0)
    lane = lax.broadcasted_iota(jnp.int32, shape, 1)
    moment = jnp.zeros(shape, F32)
    chosen = jnp.zeros(shape, jnp.int32)
    for index, (value, interval) in enumerate(zip(moments, intervals)):
        moment = jnp.where(row == index, value.astype(F32), moment)
        chosen = jnp.where(row == index, interval, chosen)
    lead = jnp.zeros(shape, F32)
    for choice in range(INTERVALS):
        picked = jnp.broadcast_to(lead_ref[choice : choice + 1, :], shape)
        lead = jnp.where(chosen == choice, picked, lead)
    half_width = D // 2
    place = jnp.where(lane < half_width, lane, lane - half_width).astype(F32)
    angles = moment * jnp.exp(place * (-math.log(10000.0) / half_width))
    wave = jnp.where(lane < half_width, jnp.sin(angles), jnp.cos(angles))
    condition = lead + wave
    return (condition / (1.0 + jnp.exp(-condition))).astype(BF).astype(F32)


def span(start, size):
    return pl.ds(pl.multiple_of(start, SLAB), size)


def local(src, dst, sem):
    made = pltpu.make_async_copy(src, dst, sem)
    made.start()
    return made


class Alone:
    def __init__(self, refs):
        self.refs = refs

    def begin(self):
        r = self.refs
        sems = r.in_sems
        first = [local(r.wa_far, r.wa, sems.at[0]), local(r.rows_far, r.rows, sems.at[3])]
        self.later = [local(r.wup_far, r.wup, sems.at[1]), local(r.wdown_far, r.wdown, sems.at[2])]
        for made in first:
            made.wait()

    def after_first(self):
        pass

    def after_attend_pair(self, h):
        pass

    def before_middle(self):
        for made in self.later:
            made.wait()

    def before_join(self):
        pass

    def amid_join(self):
        fill_blocks(self.refs)

    def after_join(self):
        pass

    def amid_back_pair(self, h):
        pass

    def after_back_pair(self, h):
        fill_pair(self.refs, h)

    def after_last_rows(self, i):
        pass

    def after_last(self):
        r = self.refs
        fill_vec(r)
        fill_late(r, r.late)
        r.vec[0:6, :] = r.late[0:6, :]
        r.vec[VEC_STEP : VEC_STEP + 6, :] = r.late[6:12, :]
        puts = [local(r.blocks, r.blocks_far, r.in_sems.at[0]), local(r.vec, r.vec_far, r.in_sems.at[1])]
        for made in puts:
            made.wait()


def block_rows(owner, part):
    first = HALF * (owner % 2) + 4 * SLAB * part + SLAB * (owner // 2)
    return slice(first, first + SLAB)


def fill_blocks(refs):
    share = refs.rows[ROW_SHARE : ROW_SHARE + 1, :]
    for d in range(8):
        own = slice(SLAB * d, SLAB * (d + 1))
        for g in range(4):
            up = refs.gup[own, PART * g : PART * (g + 1)]
            down = refs.gdown[SLAB * (4 * d + g) : SLAB * (4 * d + g + 1), :]
            refs.blocks[1, block_rows(d, g), :] = (up * share).astype(BF)
            refs.blocks[2, block_rows(d, g), :] = (down * share).astype(BF)


def fill_pair(refs, h):
    share = refs.rows[ROW_SHARE : ROW_SHARE + 1, 0:128]
    columns = [pl.ds(pl.multiple_of(D * g + 128 * h, 128), 128) for g in range(3)]
    grads = jnp.concatenate([refs.dqkv[:, column] for column in columns], axis=1)
    value = dot(refs.att1[...], grads, TN)
    for d in range(8):
        own = slice(SLAB * d, SLAB * (d + 1))
        for g in range(3):
            part = value[own, 128 * g : 128 * (g + 1)] + refs.gqkv[own, columns[g]]
            refs.blocks[0, block_rows(d, g), columns[0]] = (part * share).astype(BF)
        part = refs.gproj[own, columns[0]]
        refs.blocks[0, block_rows(d, 3), columns[0]] = (part * share).astype(BF)


VEC = 72
VEC_STEP = 24


def fill_vec(refs):
    share = refs.rows[ROW_SHARE : ROW_SHARE + 1, 0:128]

    def put(first_row, value):
        for j in range(value.shape[1] // 128):
            refs.vec[first_row + j : first_row + j + 1, :] = value[:, 128 * j : 128 * j + 128] * share

    refs.vec[...] = jnp.zeros_like(refs.vec)
    wide, narrow0, narrow1 = (refs.wide, refs.narrow0, refs.narrow1)
    put(6, narrow0[6:7, :] + narrow1[6:7, :])
    put(9, wide[0:1, :])
    put(21, narrow0[7:8, :] + narrow1[7:8, :])
    for r in range(6):
        if r > 1:
            put(VEC_STEP + 3 * r, narrow0[r : r + 1, :])
        put(2 * VEC_STEP + 3 * r, narrow1[r : r + 1, :])


def fill_late(refs, late_ref):
    share = refs.rows[ROW_SHARE : ROW_SHARE + 1, 0:128]
    rest = (refs.bias[0:1, :D], refs.bias[0:1, 2 * D :], refs.narrow0[0:1, :], refs.narrow0[1:2, :])
    for index, value in enumerate(rest):
        for j in range(3):
            row = 3 * index + j
            late_ref[row : row + 1, :] = value[:, 128 * j : 128 * j + 128] * share
    late_ref[12:16, :] = jnp.zeros((4, 128), F32)


class Together:
    steps = range(1, 4)

    def __init__(self, refs):
        self.refs = refs
        self.at = Place()

    def start(self, copy):
        copy.start()


    def whole(self, unit):
        return (self.refs.wa, self.refs.wup, self.refs.wdown)[unit]

    def part(self, unit, owner, grp):
        if unit == 2:
            return self.whole(2).at[span(4 * SLAB * owner + SLAB * grp, SLAB), :]
        return self.whole(unit).at[
            span(SLAB * owner, SLAB), pl.ds(pl.multiple_of(PART * grp, 128), PART)
        ]

    def slab(self, unit, owner):
        if unit == 2:
            return self.whole(2).at[span(4 * SLAB * owner, 4 * SLAB), :]
        return self.whole(unit).at[span(SLAB * owner, SLAB), :]

    def owner(self, k):
        return 2 * lax.rem(self.at.z + LAYERS - k, LAYERS) + self.at.core

    def gather_z(self, unit, k):
        own = self.part(unit, self.at.dp, self.at.grp)
        return remote(own, own, self.refs.gz, (unit, k - 1), self.at.along_z(k))

    def gather_grp(self, unit, k, m):
        part = self.part(unit, self.owner(k), self.at.grp)
        return remote(part, part, self.refs.gx, (unit, k - 1, m - 1), self.at.along_grp(m))

    def gather_sibling(self, unit, k):
        slab = self.slab(unit, self.owner(k) if k else self.at.dp)
        return remote(slab, slab, self.refs.gs, (unit, k), self.at.sibling())

    def launch(self, unit):
        for k in self.steps:
            self.start(self.gather_z(unit, k))
        self.start(self.gather_sibling(unit, 0))

    def forward_grp(self, unit):
        for k in self.steps:
            self.gather_z(unit, k).wait_recv()
            for m in self.steps:
                self.start(self.gather_grp(unit, k, m))

    def forward_sibling(self, unit):
        for k in self.steps:
            for m in self.steps:
                self.gather_grp(unit, k, m).wait_recv()
            self.start(self.gather_sibling(unit, k))

    def finish_sibling(self, unit):
        for k in range(4):
            self.gather_sibling(unit, k).wait_recv()

    def small(self, index):
        r, at = (self.refs, self.at)
        if index == 0:
            return remote(r.part_own, r.part_sib, r.gm, 0, at.sibling())
        if index == 1:
            own = r.bias_slot.at[at.z, at.core]
            return remote(own, own, r.gm, 1, at.sibling())
        if index < 5:
            own = r.part_z.at[at.z]
            return remote(own, own, r.gm, index, at.along_z(index - 1))
        own = r.bias_slot.at[at.z]
        return remote(own, own, r.gm, index, at.along_z(index - 4))

    def begin(self):
        r, at, steps = (self.refs, self.at, self.steps)
        stage = {
            "qkv": r.a.at[0:432], "proj": r.a.at[432:576], "ada": r.a.at[1728:2592],
            "up": r.a.at[576:1152], "down": r.a.at[1152:1728],
        }
        loads = {
            name: local(r.masters[name], stage[name], r.in_sems.at[index])
            for index, name in enumerate(stage)
        }
        ready = greet([self.everywhere(step) for step in range(1, 8 * LAYERS)])

        def fill(unit, source, count, offset, first=0):
            for j in range(count):
                value = source[pl.ds(first + j, SLAB, stride=count), :].astype(BF)
                where = offset + 128 * j
                if unit == 2:
                    rows = span(4 * SLAB * at.dp + offset, SLAB)
                    where = 128 * j
                else:
                    rows = span(SLAB * at.dp, SLAB)
                self.whole(unit)[rows, where : where + 128] = value

        loads["qkv"].wait()
        fill(0, stage["qkv"], 9, 0)
        loads["proj"].wait()
        fill(0, stage["proj"], 3, 3 * D)
        ready()
        self.launch(0)

        moment, interval = (r.start[at.grp], r.interval[at.grp])
        r.cond_t[...] = jnp.transpose(
            condition_rows([moment + s for s in range(ROLLOUT)], [interval] * ROLLOUT, r.lead)
        )
        own_cond = r.cond_t[span(SLAB * at.dp, SLAB), :]
        columns = [jnp.broadcast_to(own_cond[:, s : s + 1], (SLAB, 128)) for s in range(ROLLOUT)]
        loads["ada"].wait()
        for j in range(18):
            rows = stage["ada"][pl.ds(j, SLAB, stride=18), :].astype(BF).astype(F32)
            for s in range(ROLLOUT):
                r.part_own[18 * s + j : 18 * s + j + 1, :] = col_sum(rows * columns[s])
        r.part_own[36:40, :] = jnp.zeros((4, 128), F32)
        r.bias_own[...] = jnp.zeros((8, 128), F32)
        for i in range(6):
            size = 128 if i < 5 else 32
            r.bias_own[i : i + 1, 0:size] = r.bias_flat[pl.ds(128 * i, size)].reshape(1, size)
        lane = lax.broadcasted_iota(jnp.int32, (8, 128), 1)
        shift = lax.rem(32 * at.dp, 128)
        turned = pltpu.roll(r.bias_own[...].astype(BF).astype(F32), shift, axis=1)
        above = pltpu.roll(turned, 1, axis=0)
        r.bias_slot[at.z, at.core] = jnp.where(lane >= shift, turned, above)
        self.start(self.small(0))
        self.start(self.small(1))

        loads["up"].wait()
        fill(1, stage["up"], 12, 0)
        loads["down"].wait()
        for g in range(GROUPS):
            fill(2, stage["down"], 3, SLAB * g, 3 * SLAB * g)

        self.small(0).wait_recv()
        self.small(1).wait_recv()
        r.part_z[at.z] = r.part_own[...] + r.part_sib[...]
        for index in range(2, 8):
            self.start(self.small(index))
        self.forward_grp(0)
        self.launch(1)
        self.launch(2)

        for index in range(2, 8):
            self.small(index).wait_recv()
        total = r.part_z[0] + r.part_z[1] + r.part_z[2] + r.part_z[3]
        r.bias_full[...] = jnp.zeros_like(r.bias_full)
        for d in range(2 * LAYERS):
            first = 672 * d // 128
            r.bias_full[first : first + 7, :] += r.bias_slot[d // 2, d % 2, 0:7, :]
        counts = [r.counts[g].astype(F32) for g in range(GROUPS)]
        own_count = r.counts[at.grp].astype(F32)
        share = jnp.full((1, D), GROUPS * own_count) / jnp.full((1, D), sum(counts[1:], counts[0]))

        def put(row, value):
            r.rows[row : row + 1, :] = value

        def joined(first):
            return jnp.concatenate(
                [r.bias_full[first + j : first + j + 1, :] for j in range(3)], axis=1
            )

        for s in range(ROLLOUT):
            for row in range(6):
                first = 18 * s + 3 * row
                mod = jnp.concatenate([total[first + j : first + j + 1, :] for j in range(3)], axis=1)
                put(8 * s + row, mod + joined(24 + 3 * row))
            put(8 * s + 6, share)
            put(8 * s + 7, share)
        put(ROW_BQKV, joined(0))
        put(ROW_BQKV + 1, jnp.zeros((1, D), F32))
        put(ROW_BQKV + 2, joined(3))
        put(ROW_BPROJ, joined(6))
        for j in range(4):
            put(ROW_BUP + j, joined(9 + 3 * j))
        put(ROW_BDOWN, joined(21))
        r.rows[25:32, :] = jnp.zeros((7, D), F32)
        self.forward_sibling(0)
        self.finish_sibling(0)

    def after_first(self):
        self.forward_grp(1)

    def after_attend_pair(self, h):
        @pl.when(h == 0)
        def _():
            self.forward_grp(2)

        @pl.when(h == 1)
        def _():
            self.forward_sibling(1)

    def before_middle(self):
        self.forward_sibling(2)
        self.finish_sibling(1)
        self.finish_sibling(2)


    x_first = {3: True, 4: False}

    def columns(self, unit):
        return pl.ds(128 * unit, 128) if unit < 3 else slice(None)

    def got(self, unit, name):
        first = {"sib": 0, "piece": HALF, "grp": 0, "one": 0, "two": 8 * SLAB, "z": 12 * SLAB}[name]
        size = {"sib": HALF, "piece": 4 * SLAB, "grp": 12 * SLAB, "one": 8 * SLAB, "two": 4 * SLAB, "z": 3 * SLAB}[name]
        r, rows = (self.refs, slice(first, first + size))
        if unit < 3:
            return (r.att0 if name in ("sib", "piece") else r.act).at[rows, self.columns(unit)]
        if name in ("sib", "piece"):
            third = 0 if unit == 3 else 1
            return r.qkv1.at[rows, D * third : D * (third + 1)]
        return r.cot.at[rows] if unit == 3 else r.qkv1.at[rows, 2 * D : 3 * D]

    def half(self, unit, core):
        block = max(unit - 2, 0)
        return self.refs.blocks.at[block, span(HALF * core, HALF), self.columns(unit)]

    def parts(self, unit, part, count=1):
        return self.half(unit, self.at.core).at[span(4 * SLAB * part, 4 * SLAB * count), :]

    def sum_sibling(self, unit):
        src = self.half(unit, 1 - self.at.core)
        return remote(src, self.got(unit, "sib"), self.refs.rs, unit, self.at.sibling())

    def grp_peer(self, along_x):
        x, y = (self.at.grp % 2, self.at.grp // 2)
        grp = 2 * y + 1 - x if along_x else 2 * (1 - y) + x
        return (grp, self.at.dp)

    def stage_parts(self, unit, own):
        x, y = (self.at.grp % 2, self.at.grp // 2)
        if self.x_first[unit]:
            return [2 * j + (x if own else 1 - x) for j in range(2)]
        return [2 * (y if own else 1 - y) + j for j in range(2)]

    def sum_one(self, unit, j):
        src = self.parts(unit, self.stage_parts(unit, False)[j])
        dst = self.got(unit, "one").at[4 * SLAB * j : 4 * SLAB * (j + 1)]
        return remote(src, dst, self.refs.rx, (unit, j), self.grp_peer(self.x_first[unit]))

    def sum_two(self, unit):
        peer = self.grp_peer(not self.x_first[unit])
        return remote(self.parts(unit, peer[0]), self.got(unit, "two"), self.refs.rx, (unit, 2), peer)

    def sum_grp(self, unit, k):
        peer = self.at.along_grp(k)
        first = 4 * SLAB * (k - 1)
        dst = self.got(unit, "grp").at[first : first + 4 * SLAB]
        return remote(self.parts(unit, peer[0]), dst, self.refs.rx, (unit, k - 1), peer)

    def own_part(self, unit):
        return self.parts(unit, self.at.grp)

    def sum_z(self, unit, k):
        there = lax.rem(self.at.z + k, LAYERS)
        src = self.own_part(unit).at[span(SLAB * there, SLAB), :]
        dst = self.got(unit, "z").at[SLAB * (k - 1) : SLAB * k]
        return remote(src, dst, self.refs.rz, (unit, k - 1), self.at.along_z(k))

    def share_piece(self, unit, k):
        own = self.got(unit, "piece").at[span(SLAB * self.at.grp, SLAB), :]
        return remote(own, own, self.refs.ra, (unit, k - 1), self.at.along_grp(k))

    def add(self, mine, got, count):
        def step(i, carry):
            rows = span(SLAB * i, SLAB)
            mine[rows, :] = (mine[rows, :].astype(F32) + got[rows, :].astype(F32)).astype(BF)
            return carry

        lax.fori_loop(0, count, step, 0)

    def add_sibling(self, unit):
        self.sum_sibling(unit).wait_recv()
        self.add(self.half(unit, self.at.core), self.got(unit, "sib"), 16)
        if unit < 3:
            for k in self.steps:
                self.start(self.sum_grp(unit, k))
        else:
            for j in range(2):
                self.start(self.sum_one(unit, j))

    def add_grp(self, unit):
        for k in self.steps:
            self.sum_grp(unit, k).wait_recv()
        mine, got = (self.own_part(unit), self.got(unit, "grp"))

        def step(i, carry):
            rows = span(SLAB * i, SLAB)
            value = mine[rows, :].astype(F32)
            for k in self.steps:
                value = value + got[span(SLAB * (i + 4 * (k - 1)), SLAB), :].astype(F32)
            mine[rows, :] = value.astype(BF)
            return carry

        lax.fori_loop(0, 4, step, 0)
        for k in self.steps:
            self.start(self.sum_z(unit, k))

    def add_one(self, unit):
        for j in range(2):
            self.sum_one(unit, j).wait_recv()
            got = self.got(unit, "one").at[4 * SLAB * j : 4 * SLAB * (j + 1)]
            self.add(self.parts(unit, self.stage_parts(unit, True)[j]), got, 4)
        self.start(self.sum_two(unit))

    def add_two(self, unit):
        self.sum_two(unit).wait_recv()
        self.add(self.own_part(unit), self.got(unit, "two"), 4)
        for k in self.steps:
            self.start(self.sum_z(unit, k))

    def add_z(self, unit):
        for k in self.steps:
            self.sum_z(unit, k).wait_recv()
        value = self.own_part(unit)[span(SLAB * self.at.z, SLAB), :].astype(F32)
        for k in self.steps:
            value = value + self.got(unit, "z")[SLAB * (k - 1) : SLAB * k, :].astype(F32)
        value = value.astype(BF)
        self.got(unit, "piece")[span(SLAB * self.at.grp, SLAB), :] = value
        for k in self.steps:
            self.start(self.share_piece(unit, k))
        value = value.astype(F32)
        squares = col_sum(value * value)
        if unit < 3:
            return squares
        return squares[:, 0:128] + squares[:, 128:256] + squares[:, 256:384]

    def tell(self, sem):
        at = self.at
        for peer in (
            [at.sibling()]
            + [at.along_grp(k) for k in self.steps]
            + [at.along_z(k) for k in self.steps]
        ):
            pl.semaphore_signal(sem, inc=1, device_id=peer, device_id_type=MESH_ID)

    def before_join(self):
        self.tell(self.refs.turned_back)

    def amid_join(self):
        fill_blocks(self.refs)
        pl.semaphore_wait(self.refs.turned_back, 7)
        self.start(self.sum_sibling(3))
        self.start(self.sum_sibling(4))

    def after_join(self):
        r = self.refs
        self.tell(r.joined)
        self.add_sibling(3)
        self.add_sibling(4)
        fill_vec(r)
        self.start(self.small_sum(0))

    def amid_back_pair(self, h):
        r, at = (self.refs, self.at)

        @pl.when(h == 0)
        def _():
            self.small_sum(0).wait_recv()
            r.vec_z[at.z] = r.vec[...] + r.vec_sib[...]
            for index in self.steps:
                self.start(self.small_sum(index))

        @pl.when(h == 1)
        def _():
            self.add_one(3)
            self.add_one(4)
            self.add_sibling(0)
            for index in self.steps:
                self.small_sum(index).wait_recv()
            r.vec_g[at.grp] = r.vec_z[0] + r.vec_z[1] + r.vec_z[2] + r.vec_z[3]
            for index in self.steps:
                self.start(self.small_sum(3 + index))

        @pl.when(h == 2)
        def _():
            self.add_two(3)
            self.add_two(4)
            self.add_sibling(1)
            self.add_grp(0)

    def after_back_pair(self, h):
        r = self.refs
        fill_pair(r, h)

        @pl.when(h == 0)
        def _():
            pl.semaphore_wait(r.joined, 7)
            self.start(self.sum_sibling(0))

        @pl.when(h == 1)
        def _():
            self.start(self.sum_sibling(1))

        @pl.when(h == 2)
        def _():
            self.start(self.sum_sibling(2))

    def after_last_rows(self, i):
        @pl.when(i == 0)
        def _():
            self.add_sibling(2)

        @pl.when(i == 2)
        def _():
            self.add_grp(1)

    def small_sum(self, index):
        r, at = (self.refs, self.at)
        if index == 0:
            return remote(r.vec, r.vec_sib, r.rv, 0, at.sibling())
        if index < 4:
            own = r.vec_z.at[at.z]
            return remote(own, own, r.rv, index, at.along_z(index))
        own = r.vec_g.at[at.grp]
        return remote(own, own, r.rv, index, at.along_grp(index - 3))

    def across_dp(self, index):
        at = self.at
        if index == 0:
            return at.sibling()
        return at.along_z(index) if index < 4 else at.across(index - 3)

    def everywhere(self, step):
        device = lax.rem(2 * LAYERS * self.at.grp + self.at.dp + step, 8 * LAYERS)
        return (device // (2 * LAYERS), lax.rem(device, 2 * LAYERS))

    def square_sum(self, step):
        own = self.refs.squares.at[2 * LAYERS * self.at.grp + self.at.dp]
        return remote(own, own, self.refs.rq, step, self.everywhere(step))

    def late_sum(self, index):
        r, at = (self.refs, self.at)
        if index < 7:
            own = r.late_d.at[at.dp]
            return remote(own, own, r.rl, index, self.across_dp(index))
        own = r.late_g.at[at.grp]
        return remote(own, own, r.rl, index, at.along_grp(index - 6))

    def ada_square(self):
        r = self.refs
        left = r.cond_out[...]
        right = [
            r.vec_out[g, VEC_STEP * (s + 1) : VEC_STEP * (s + 2), :]
            for g in range(GROUPS)
            for s in range(ROLLOUT)
        ]
        total = jnp.zeros((VEC_STEP, 128), F32)
        for step, weight in ((0, 1.0), (1, 2.0), (2, 2.0), (3, 2.0), (4, 1.0)):
            moved = left if step == 0 else pltpu.roll(left, step, axis=0)
            products = jnp.sum(left * moved, axis=1, keepdims=True) * weight
            for k in range(8):
                total = total + products[k : k + 1, :] * (right[k] * right[(k - step) % 8])
        return col_sum(total)

    def after_last(self):
        r, at, steps = (self.refs, self.at, self.steps)
        fill_late(r, r.late_d.at[at.dp])
        for index in range(7):
            self.start(self.late_sum(index))
        moments = [r.start[g] + s for g in range(GROUPS) for s in range(ROLLOUT)]
        intervals = [r.interval[g] for g in range(GROUPS) for s in range(ROLLOUT)]
        r.cond_out[...] = condition_rows(moments, intervals, r.lead)
        self.add_grp(2)
        for index in range(7):
            self.late_sum(index).wait_recv()
        total = r.late_d[0]
        for d in range(1, 2 * LAYERS):
            total = total + r.late_d[d]
        r.late_g[at.grp] = total
        for index in range(7, 10):
            self.start(self.late_sum(index))
        square = self.add_z(0) + self.add_z(3) + self.add_z(4) + self.add_z(1)
        for index in steps:
            self.small_sum(3 + index).wait_recv()
        for index in range(7, 10):
            self.late_sum(index).wait_recv()
        vec = r.vec_out
        vec[...] = r.vec_g[...]
        for g in range(GROUPS):
            vec[g, 0:6, :] = r.late_g[g, 0:6, :]
            vec[g, VEC_STEP : VEC_STEP + 6, :] = r.late_g[g, 6:12, :]
        vec_sum = vec[0] + vec[1] + vec[2] + vec[3]
        r.bias_out[0:24, :] = vec_sum[0:24]
        r.bias_out[24:48, :] = vec_sum[24:48] + vec_sum[48:72]
        ada_square = self.ada_square()
        square = square + self.add_z(2)
        own = 2 * LAYERS * at.grp + at.dp
        r.squares[own] = square
        for k in range(1, 8 * LAYERS):
            self.start(self.square_sum(k))
        for unit in range(5):
            for k in steps:
                self.share_piece(unit, k).wait_recv()
        whole = [r.att0.at[HALF : HALF + 4 * SLAB], self.got(3, "piece"), self.got(4, "piece")]
        puts = [
            local(whole[unit], r.pieces_far.at[unit], r.in_sems.at[1 + unit])
            for unit in range(UNITS)
        ]
        bias_sum = r.bias_out[...]
        total = col_sum(bias_sum * bias_sum) + ada_square
        for k in range(1, 8 * LAYERS):
            self.square_sum(k).wait_recv()
        for device in range(8 * LAYERS):
            total = total + r.squares[device]
        r.square_out[...] = jnp.broadcast_to(jnp.sum(total, axis=1, keepdims=True), (8, 128))
        for made in puts:
            made.wait()
        self.drain()

    def drain(self):
        for unit in range(UNITS):
            for k in self.steps:
                self.gather_z(unit, k).wait_send()
                for m in self.steps:
                    self.gather_grp(unit, k, m).wait_send()
            for k in range(4):
                self.gather_sibling(unit, k).wait_send()
        for unit in range(5):
            self.sum_sibling(unit).wait_send()
            if unit < 3:
                for k in self.steps:
                    self.sum_grp(unit, k).wait_send()
            else:
                self.sum_one(unit, 0).wait_send()
                self.sum_one(unit, 1).wait_send()
                self.sum_two(unit).wait_send()
            for k in self.steps:
                self.sum_z(unit, k).wait_send()
                self.share_piece(unit, k).wait_send()
        for index in range(8):
            self.small(index).wait_send()
        for index in range(7):
            self.small_sum(index).wait_send()
        for index in range(10):
            self.late_sum(index).wait_send()
        for step in range(1, 8 * LAYERS):
            self.square_sum(step).wait_send()


correction = 1.0 - 0.5**ADAM_STEP
grad_limit = math.sqrt(NPARAM)


def adam(master, first, second, clipped, decay):
    first_new = 0.5 * first + 0.5 * clipped
    second_new = 0.5 * second + 0.5 * clipped * clipped
    update = first_new / correction / (jnp.sqrt(second_new / correction) + adam_eps)
    return (master - learn_rate * (update + decay * master), first_new, second_new)


STATE = ("qkv", "proj", "up", "down", "ada")


def finish_kernel(names, *refs):
    r = Refs(names, refs)
    loads = {"pieces": local(r.pieces_far, r.pieces, r.in_sems.at[0])}
    for index, name in enumerate(STATE):
        for kind in range(3):
            loads[name, kind] = local(
                getattr(r, f"{name}_in{kind}"), getattr(r, f"{name}_{kind}"),
                r.in_sems.at[1 + 3 * index + kind],
            )
    streams = [
        local(getattr(r, name + "_in"), getattr(r, name), r.stream_sems.at[index])
        for index, name in enumerate(("y", "dx"))
    ]
    norm = jnp.sqrt(r.square[...])
    r.norm[0, 0] = jnp.max(norm)
    clip = grad_limit / jnp.maximum(norm, grad_limit)
    row_clip = clip[0:1, :]

    owner = lax.axis_index("dp")
    lane = lax.broadcasted_iota(jnp.int32, (1, 128), 1)
    first = 672 * owner // 128
    shift = lax.rem(32 * owner, 128)
    back = lax.rem(128 - shift, 128)
    for i in range(6):
        size = 128 if i < 5 else 32
        here = pltpu.roll(r.bias_sum[pl.ds(first + i, 1), :], back, axis=1)
        there = pltpu.roll(r.bias_sum[pl.ds(first + i + 1, 1), :], back, axis=1)
        grad = jnp.where(lane < 128 - shift, here, there) * row_clip
        place = pl.ds(128 * i, size)
        state = [getattr(r, f"bias_in{kind}")[place].reshape(1, size) for kind in range(3)]
        new, first_new, second_new = adam(*state, grad[:, :size], 0.0)
        r.bias_out0[place] = new.reshape(size)
        r.bias_out1[place] = first_new.reshape(size)
        r.bias_out2[place] = second_new.reshape(size)
        r.bias_out3[place] = new.reshape(size).astype(BF)

    r.cond_t[...] = jnp.transpose(r.cond[...])
    own_cond = r.cond_t[pl.ds(pl.multiple_of(SLAB * owner, SLAB), SLAB), :]
    columns = [jnp.broadcast_to(own_cond[:, k : k + 1], (SLAB, 128)) for k in range(8)]

    def ada_tile(j, carry):
        tile = jnp.zeros((SLAB, 128), F32)
        for k in range(8):
            row = r.vec[k // ROLLOUT, pl.ds(VEC_STEP * (k % ROLLOUT + 1) + j, 1), :]
            tile = tile + columns[k] * row
        r.grad_ada[pl.ds(j, SLAB, stride=18), :] = tile
        return carry

    lax.fori_loop(0, 18, ada_tile, 0)

    loads["pieces"].wait()
    piece = r.pieces
    for g in range(3):
        for j in range(3):
            r.grad_qkv[pl.ds(3 * g + j, SLAB, stride=9), :] = piece[
                0, SLAB * g : SLAB * (g + 1), 128 * j : 128 * j + 128
            ].astype(F32)
    for j in range(3):
        columns = slice(128 * j, 128 * j + 128)
        r.grad_proj[pl.ds(j, SLAB, stride=3), :] = piece[0, 3 * SLAB :, columns].astype(F32)
    for g in range(GROUPS):
        rows = slice(SLAB * g, SLAB * (g + 1))
        for j in range(3):
            columns = slice(128 * j, 128 * j + 128)
            r.grad_up[pl.ds(3 * g + j, SLAB, stride=12), :] = piece[1, rows, columns].astype(F32)
            r.grad_down[pl.ds(3 * SLAB * g + j, SLAB, stride=3), :] = piece[2, rows, columns].astype(F32)

    stores = []
    for index, name in enumerate(STATE):
        for kind in range(3):
            loads[name, kind].wait()
        grad, low = (getattr(r, "grad_" + name), getattr(r, name + "_low"))
        state = [getattr(r, f"{name}_{kind}") for kind in range(3)]

        def chunk(i, carry):
            rows = pl.ds(pl.multiple_of(16 * i, 16), 16)
            new, first_new, second_new = adam(
                *(ref[rows, :] for ref in state), grad[rows, :] * row_clip, 0.1
            )
            for ref, value in zip(state, (new, first_new, second_new)):
                ref[rows, :] = value
            low[rows, :] = new.astype(BF)
            return carry

        lax.fori_loop(0, grad.shape[0] // 16, chunk, 0, unroll=3)
        for kind, ref in enumerate((*state, low)):
            stores.append(local(ref, getattr(r, f"{name}_out{kind}"), r.out_sems.at[4 * index + kind]))
        if index < 2:
            name = ("y", "dx")[index]
            streams[index].wait()
            stores.append(local(getattr(r, name), getattr(r, name + "_out"), r.stream_sems.at[index]))
    for made in stores:
        made.wait()


def finish(y, dx, pieces, vec, cond, bias_sum, square, masters, firsts, seconds):
    vmem, hbm, dma = (pltpu.VMEM, pl.ANY, pltpu.SemaphoreType.DMA)
    state = list(zip(masters, firsts, seconds))
    shapes = {name: (arrays[0].size // 128, 128) for name, arrays in zip(STATE, state)}
    ins = [
        ("square", square, vmem), ("bias_sum", bias_sum, vmem), ("pieces_far", pieces, hbm),
        ("vec", vec, vmem), ("cond", cond, vmem), ("y_in", y, hbm), ("dx_in", dx, hbm),
        *[(f"bias_in{kind}", array, vmem) for kind, array in enumerate(state[5])],
        *[
            (f"{name}_in{kind}", array.reshape(-1, 128), hbm)
            for name, arrays in zip(STATE, state)
            for kind, array in enumerate(arrays)
        ],
    ]
    outs = [("norm", (1, 1), F32, pltpu.SMEM), ("y_out", y.shape, F32, hbm), ("dx_out", dx.shape, F32, hbm)]
    for kind in range(4):
        dtype = F32 if kind < 3 else BF
        outs += [(f"{name}_out{kind}", shapes[name], dtype, hbm) for name in STATE]
        outs.append((f"bias_out{kind}", state[5][0].shape, dtype, vmem))
    scratch = [
        ("pieces", vmem(pieces.shape, BF)), ("y", vmem(y.shape, F32)), ("dx", vmem(dx.shape, F32)),
        *[(f"{name}_{kind}", vmem(shapes[name], F32)) for name in STATE for kind in range(3)],
        *[(f"{name}_low", vmem(shapes[name], BF)) for name in STATE],
        *[(f"grad_{name}", vmem(shapes[name], F32)) for name in STATE],
        ("cond_t", vmem((D, 8), F32)), ("in_sems", dma((16,))), ("stream_sems", dma((2,))), ("out_sems", dma((20,))),
    ]
    names = [item[0] for item in (*ins, *outs, *scratch)]
    norm, y, dx, *rest = pl.pallas_call(
        functools.partial(finish_kernel, names),
        in_specs=[pl.BlockSpec(memory_space=space) for *_, space in ins],
        out_specs=[pl.BlockSpec(memory_space=space) for *_, space in outs],
        out_shape=[jax.ShapeDtypeStruct(shape, kind) for _, shape, kind, _ in outs],
        scratch_shapes=[kind for _, kind in scratch],
        name="finish",
    )(*(array for _, array, _ in ins))
    return (y, dx, norm.reshape(()), *(array.reshape(-1) for array in rest))


MASTERS = ("qkv", "proj", "up", "down", "ada")


def block_kernel(names, hooked, *refs):
    r = Refs(names, refs)
    if hooked is Together:
        r.masters = {name: getattr(r, "far_" + name) for name in MASTERS}
        for name in ("gz", "gx", "gs", "gm", "rs", "rx", "rz", "ra", "rv", "rq", "rl"):
            setattr(r, name, (getattr(r, name + "_out"), getattr(r, name + "_in")))
    hooks = hooked(r)
    length = r.x.shape[0]
    pairs = HEADS // 2
    get_cot = local(r.cot_far, r.cot, r.out_sems.at[2])

    def over_rows(body, after=None):
        def step(i, carry):
            body(pl.ds(pl.multiple_of(i * ROWS, ROWS), ROWS))
            if after is not None:
                after(i)
            return carry

        lax.fori_loop(0, length // ROWS, step, 0)

    def columns(h, offset=0):
        return pl.ds(pl.multiple_of(offset + 128 * h, 128), 128)

    def over_pairs(body):
        def step(h, carry):
            body(h)
            return carry

        lax.fori_loop(0, pairs, step, 0)

    def act_refs(rows):
        first = rows.start
        return [
            r.act.at[pl.ds(pl.multiple_of(length * part + first, ROWS), ROWS)] for part in range(4)
        ]

    def a_refs(rows):
        first = rows.start
        return [
            r.a.at[pl.ds(pl.multiple_of(length * part + first, ROWS), ROWS)] for part in range(3)
        ]

    def save(step, h):
        slot = lax.rem(h, 2)
        return pltpu.make_async_copy(
            r.p.at[slot], r.p_far.at[step, pl.ds(2 * h, 2)], r.p_sems.at[slot]
        )

    def fetch(step, h):
        slot = lax.rem(h, 2)
        return pltpu.make_async_copy(
            r.p_far.at[step, pl.ds(2 * h, 2)], r.p.at[slot], r.p_sems.at[slot]
        )

    def attend(step, qkv, att, after):
        def body(h):
            @pl.when(h >= 2)
            def _():
                save(step, h - 2).wait()

            attend_pair(
                qkv[:, columns(h)], qkv.at[:, columns(h, D)], qkv[:, columns(h, 2 * D)],
                att.at[:, columns(h)], r.p.at[lax.rem(h, 2)], r.turned,
            )
            save(step, h).start()
            after(h)

        over_pairs(body)

    def finish_saves(step):
        for h in range(pairs - 2, pairs):
            save(step, h).wait()

    def attend_back(step, qkv, between, after):
        def body(h):
            fetch(step, h).wait()
            attend_back_pair(
                qkv[:, columns(h)], qkv[:, columns(h, D)], qkv.at[:, columns(h, 2 * D)],
                r.datt[:, columns(h)], r.p.at[lax.rem(h, 2)],
                r.dqkv.at[:, columns(h)], r.dqkv.at[:, columns(h, D)],
                r.dqkv.at[:, columns(h, 2 * D)], r.turned,
                None if between is None else lambda: between(h),
            )

            @pl.when(h + 2 < pairs)
            def _():
                fetch(step, h + 2).start()

            after(h)

        over_pairs(body)

    nothing = lambda h: None
    hooks.begin()

    def first(rows):
        r.qkv0[rows, :] = first_rows(r.x[rows, :], r.rows, r.wa)

    over_rows(first)
    hooks.after_first()
    attend(0, r.qkv0, r.att0, hooks.after_attend_pair)
    hooks.before_middle()

    def middle(rows):
        middle_rows(
            r.x.at[rows], r.att0.at[rows], r.rows, r.wa, r.wup, r.wdown,
            a_refs(rows), r.gp.at[rows], act_refs(rows), r.f.at[rows], r.x1.at[rows],
            r.qkv1.at[rows],
        )

    over_rows(middle)
    finish_saves(0)
    attend(1, r.qkv1, r.att1, nothing)

    for ref in (r.gqkv, r.gproj, r.gup, r.gdown, r.wide, r.narrow0, r.narrow1, r.bias):
        ref[...] = jnp.zeros_like(ref)

    def turn(rows):
        turn_rows(
            r.x1.at[rows], r.att1.at[rows], r.cot.at[rows], r.rows, r.wa, r.wup,
            r.wdown, r.y.at[rows], r.dmid.at[rows], r.datt.at[rows], r.gdown, r.gup, r.gproj,
            r.wide, r.narrow1,
        )

    finish_saves(1)
    for h in range(2):
        fetch(1, h).start()
    get_cot.wait()
    over_rows(turn)
    put_y = local(r.y, r.y_far, r.out_sems.at[0])
    attend_back(1, r.qkv1, None, nothing)
    for h in range(2):
        fetch(0, h).start()

    def join(rows):
        join_rows(
            r.dqkv.at[rows], r.x1.at[rows], r.x.at[rows], a_refs(rows), r.gp.at[rows],
            act_refs(rows), r.f.at[rows], r.rows, r.wa, r.wdown, r.att1.at[rows],
            r.dmid.at[rows], r.gqkv, r.gdown, r.gup, r.wide, r.narrow1, r.narrow0, r.bias,
        )

    def join_middle(rows):
        join_middle_rows(
            r.x.at[rows], a_refs(rows), act_refs(rows), r.att0.at[rows], r.rows, r.wa, r.wup,
            r.dmid.at[rows], r.datt.at[rows], r.gproj, r.narrow0,
        )

    hooks.before_join()
    over_rows(join)
    hooks.amid_join()
    over_rows(join_middle)
    hooks.after_join()
    attend_back(0, r.qkv0, hooks.amid_back_pair, hooks.after_back_pair)

    def last(rows):
        r.dmid[rows, :] = qkv_back(
            mod_reader(r.rows, 0), r.x[rows, :].astype(F32), r.dmid[rows, :],
            r.dqkv[rows, :], r.wa, r.narrow0, r.bias,
        )

    over_rows(last, hooks.after_last_rows)
    put_dx = local(r.dmid, r.dx_far, r.out_sems.at[1])
    hooks.after_last()
    put_y.wait()
    put_dx.wait()


def block_call(hooked, inputs, cotangent, extra_in, extra_out, extra_scratch, params):
    length = inputs.shape[0]
    vmem, hbm, dma = (pltpu.VMEM, pl.ANY, pltpu.SemaphoreType.DMA)
    weights = (ROLLOUT, HEADS, length, length)
    ins = [("x", inputs, vmem), ("cot_far", cotangent, hbm), *extra_in]
    outs = [
        ("y_far", (length, D), F32, hbm), ("dx_far", (length, D), F32, hbm),
        ("p_far", weights, BF, hbm), *extra_out,
    ]
    scratch = [
        ("wa", vmem((D, FF), BF)), ("wup", vmem((D, FF), BF)), ("wdown", vmem((FF, D), BF)),
        ("cot", vmem((length, D), BF)), ("qkv0", vmem((length, 3 * D), BF)),
        ("qkv1", vmem((length, 3 * D), BF)), ("p", vmem((2, 2, length, length), BF)),
        ("att0", vmem((length, D), BF)), ("att1", vmem((length, D), BF)),
        *[(name, vmem((length, D), F32)) for name in ("f", "x1", "dmid", "y")], ("a", vmem((3 * length, 128), F32)),
        ("gp", vmem((length, FF), F32)), ("act", vmem((4 * length, D), BF)),
        ("datt", vmem((length, D), BF)), ("dqkv", vmem((length, 3 * D), BF)),
        ("gqkv", vmem((D, 3 * D), F32)), ("gproj", vmem((D, D), F32)),
        ("gup", vmem((D, FF), F32)), ("gdown", vmem((FF, D), F32)),
        ("turned", vmem((2, 128, length), BF)), ("wide", vmem((8, FF), F32)),
        ("narrow0", vmem((8, D), F32)), ("narrow1", vmem((8, D), F32)),
        ("bias", vmem((8, 3 * D), F32)), ("blocks", vmem((UNITS, 2 * HALF, PART), BF)),
        ("rows", vmem((32, D), F32)), ("vec", vmem((VEC, 128), F32)), ("late", vmem((16, 128), F32)),
        ("in_sems", dma((5,))), ("p_sems", dma((2,))), ("out_sems", dma((3,))),
        *extra_scratch,
    ]
    names = [item[0] for item in (*ins, *outs, *scratch)]
    return pl.pallas_call(
        functools.partial(block_kernel, names, hooked),
        in_specs=[pl.BlockSpec(memory_space=space) for _, _, space in ins],
        out_specs=[pl.BlockSpec(memory_space=space) for *_, space in outs],
        out_shape=[jax.ShapeDtypeStruct(shape, kind) for _, shape, kind, _ in outs],
        scratch_shapes=[kind for _, kind in scratch],
        compiler_params=pltpu.CompilerParams(vmem_limit_bytes=67043328, **params),
        name="block",
    )(*(array for _, array, _ in ins))


def block_alone(inputs, cotangent, rows, wa, wup, wdown):
    hbm = pl.ANY
    y, dx, _, blocks, vec = block_call(
        Alone, inputs, cotangent,
        [("rows_far", rows, hbm), ("wa_far", wa, hbm), ("wup_far", wup, hbm), ("wdown_far", wdown, hbm)],
        [("blocks_far", (UNITS, 2 * HALF, PART), BF, hbm), ("vec_far", (VEC, 128), F32, hbm)],
        [], {},
    )
    return (y, dx, blocks, vec)


def block_together(inputs, cotangent, start, interval, counts, lead, masters):
    vmem, hbm, smem, dma = (pltpu.VMEM, pl.ANY, pltpu.SMEM, pltpu.SemaphoreType.DMA)
    qkv, proj, up, down, ada, bias = masters
    far = [
        ("far_" + name, array.reshape(-1, 128), hbm)
        for name, array in zip(MASTERS, (qkv, proj, up, down, ada))
    ]
    pairs_of = [
        ("gz", (UNITS, 3)), ("gx", (UNITS, 3, 3)), ("gs", (UNITS, 4)), ("gm", (8,)),
        ("rs", (5,)), ("rx", (5, 3)), ("rz", (5, 3)), ("ra", (5, 3)),
        ("rv", (7,)), ("rq", (8 * LAYERS,)), ("rl", (10,)),
    ]
    y, dx, _, pieces, vec, cond, bias_sum, square = block_call(
        Together, inputs, cotangent,
        [("start", start, smem), ("interval", interval, smem), ("counts", counts, smem),
         ("lead", lead, vmem), ("bias_flat", bias, vmem), *far],
        [("pieces_far", (UNITS, 4 * SLAB, PART), BF, hbm), ("vec_out", (GROUPS, VEC, 128), F32, vmem), ("cond_out", (8, D), F32, vmem),
         ("bias_out", (48, 128), F32, vmem), ("square_out", (8, 128), F32, vmem)],
        [("cond_t", vmem((D, 8), F32)), ("part_own", vmem((40, 128), F32)),
         ("part_sib", vmem((40, 128), F32)), ("part_z", vmem((LAYERS, 40, 128), F32)),
         ("bias_own", vmem((8, 128), F32)), ("bias_slot", vmem((LAYERS, 2, 8, 128), F32)), ("bias_full", vmem((48, 128), F32)),
         ("vec_sib", vmem((VEC, 128), F32)), ("vec_z", vmem((LAYERS, VEC, 128), F32)),
         ("vec_g", vmem((GROUPS, VEC, 128), F32)), ("late_d", vmem((8, 16, 128), F32)),
         ("late_g", vmem((GROUPS, 16, 128), F32)), ("squares", vmem((8 * LAYERS, 1, 128), F32)), ("joined", pltpu.SemaphoreType.REGULAR), ("turned_back", pltpu.SemaphoreType.REGULAR),
         *[(name + end, dma(shape)) for name, shape in pairs_of for end in ("_out", "_in")]],
        dict(collective_id=0, has_side_effects=True),
    )
    return (y, dx, pieces, vec, cond, bias_sum, square)


def step_embedding(moment):
    half_width = D // 2
    freqs = jnp.exp(-math.log(10000.0) * jnp.arange(half_width, dtype=F32) / half_width)
    angles = moment[:, None] * freqs[None, :]
    return jnp.concatenate([jnp.sin(angles), jnp.cos(angles)], axis=1)


def all_conditions(group_interval, rollout_start, lead_table):
    chosen = group_interval[:, None] == jnp.arange(INTERVALS)[None, :]
    lead_rows = jnp.sum(jnp.where(chosen[:, :, None], lead_table[None], 0.0), axis=1)
    start = rollout_start.astype(F32)
    rows = [lead_rows + step_embedding(start + offset) for offset in range(ROLLOUT)]
    return jax.nn.silu(jnp.stack(rows, axis=1)).astype(BF)


def plain_gather(group_interval, counts, rollout_start, lead_table, masters):
    low = [master.astype(BF) for master in masters]
    owner = lax.axis_index("dp")
    group_index = lax.axis_index("grp")
    own_rows = D // lax.axis_size("dp")
    counts = counts.astype(F32)
    share = lax.axis_size("grp") * counts / jnp.sum(counts)
    share = lax.dynamic_index_in_dim(share, group_index, keepdims=False)
    conditions = all_conditions(group_interval, rollout_start, lead_table)
    owner_columns = lax.dynamic_slice_in_dim(conditions, owner * own_rows, own_rows, axis=2)
    own_condition = lax.dynamic_index_in_dim(owner_columns, group_index, keepdims=False)
    modulation = lax.psum(dot(own_condition, low[4].reshape(own_rows, 6 * D)), "dp")
    qkv, proj, up, down, bias = [
        lax.all_gather(low[index], "dp", axis=0, tiled=True) for index in (0, 1, 2, 3, 5)
    ]
    bias = bias.astype(F32)
    modulation = modulation + bias[4 * D + FF :][None]
    share_rows = jnp.broadcast_to(share, (ROLLOUT, 2, D))
    mods = jnp.concatenate([modulation.reshape(ROLLOUT, 6, D), share_rows], axis=1).reshape(-1, D)
    rows = jnp.concatenate(
        [mods, bias[:D][None], jnp.zeros((1, D), F32), bias[D : 4 * D + FF].reshape(-1, D),
         jnp.zeros((7, D), F32)]
    )
    wa = jnp.concatenate([qkv.reshape(D, 3 * D), proj.reshape(D, D)], axis=1)
    return (wa, up.reshape(D, FF), down.reshape(FF, D), rows, owner_columns)


def plain_update(owner_columns, vec, blocks, masters, firsts, seconds):
    owner = lax.axis_index("dp")
    vec = vec.reshape(-1)
    split = 4 * D + FF
    dmod = vec[split:].reshape(ROLLOUT, VEC_STEP * 128)[:, : 6 * D]
    dmod_all = lax.all_gather(lax.psum(dmod, "dp"), "grp")
    bias_sum = lax.psum(vec[:split], ("grp", "dp"))
    bias_sum = jnp.concatenate([bias_sum, jnp.sum(dmod_all, axis=(0, 1))])
    bias_rows = masters[5].shape[0]
    bias_grad = lax.dynamic_slice_in_dim(bias_sum, owner * bias_rows, bias_rows)
    ada_grad = jnp.einsum(
        "gsr,gsc->rc", owner_columns.astype(F32), dmod_all, precision=lax.Precision.HIGHEST
    )
    blocks = blocks.reshape(UNITS, 2, 4, LAYERS, SLAB, PART)
    flat_a, flat_up = [blocks[u].transpose(2, 0, 3, 1, 4).reshape(D, FF) for u in (0, 1)]
    flat_down = blocks[2].transpose(2, 0, 1, 3, 4)
    flat = [flat_a[:, : 3 * D], flat_a[:, 3 * D :], flat_up, flat_down]
    shares = []
    for grad in flat:
        summed = lax.psum(grad.reshape(-1), "grp").astype(F32)
        shares.append(lax.psum_scatter(summed, "dp", scatter_dimension=0, tiled=True))
    shares = shares + [ada_grad.reshape(-1), bias_grad]
    local_square = sum((jnp.sum(piece * piece) for piece in shares))
    grad_norm = jnp.sqrt(lax.psum(local_square, "dp"))
    clip = grad_limit / jnp.maximum(grad_norm, grad_limit)
    decays = [0.1, 0.1, 0.1, 0.1, 0.1, 0.0]
    results = [
        adam(master, first, second, grad * clip, decay)
        for master, first, second, grad, decay in zip(masters, firsts, seconds, shares, decays)
    ]
    news, first_news, second_news = zip(*results)
    return (grad_norm, *news, *first_news, *second_news, *(new.astype(BF) for new in news))


def per_device(
    inputs,
    cotangent,
    group_interval,
    sample_counts,
    rollout_start,
    lead_table,
    *state,
):
    masters, firsts, seconds = (state[0:6], state[6:12], state[12:18])
    fits = (
        lax.axis_size("dp") == 2 * LAYERS
        and lax.axis_size("grp") == GROUPS
        and inputs.shape[0] == 1024
    )
    if not fits:
        wa, wup, wdown, rows, owner_columns = plain_gather(
            group_interval, sample_counts, rollout_start, lead_table, masters
        )
        result, input_grad, blocks, vec = block_alone(inputs, cotangent, rows, wa, wup, wdown)
        rest = plain_update(owner_columns, vec, blocks, masters, firsts, seconds)
        return (result, input_grad, *rest)
    result, input_grad, pieces, vec, cond, bias_sum, square = block_together(
        inputs, cotangent, rollout_start, group_interval, sample_counts, lead_table, masters
    )
    return finish(
        result, input_grad, pieces, vec, cond, bias_sum, square, masters, firsts, seconds
    )


def solution(mesh):
    rows = P(("grp", "dp"), None)
    return jax.shard_map(
        per_device,
        mesh=mesh,
        in_specs=(rows, rows, P(), P(), P(), P(), *[P("dp")] * 18),
        out_specs=(rows, rows, P(), *[P("dp")] * 24),
        check_vma=False,
    )
```

```python
import functools
import math

import jax
import jax.numpy as jnp
from jax import lax
from jax.experimental import pallas as pl
from jax.experimental.pallas import tpu as pltpu
from jax.sharding import PartitionSpec as P

D = 384
HEADS = 6
FF = 1536
ROLLOUT = 2
INTERVALS = 3
ADAM_STEP = 10
HEAD_DIM = 64
NPARAM = 2659584

norm_eps = 1e-06
learn_rate = 0.05
adam_eps = 1e-08

BF = jnp.bfloat16
F32 = jnp.float32
NN = (((1,), (0,)), ((), ()))
NT = (((1,), (1,)), ((), ()))
TN = (((0,), (0,)), ((), ()))

ROWS = 256
SLAB = 48
PART = 384
ROW_SHARE = 6
ROW_BQKV, ROW_BPROJ, ROW_BUP, ROW_BDOWN = 16, 19, 20, 24
SHIFT1, SCALE1, GATE1, SHIFT2, SCALE2, GATE2 = range(6)


def dot(left, right, dims=NN):
    return lax.dot_general(left, right, dims, preferred_element_type=F32)


def layer_norm(stream):
    centred = stream - jnp.mean(stream, axis=-1, keepdims=True)
    inverse = lax.rsqrt(jnp.mean(centred * centred, axis=-1, keepdims=True) + norm_eps)
    return (centred * inverse, inverse)


def norm_back(normed, inverse, grad_out):
    mean_grad = jnp.mean(grad_out, axis=-1, keepdims=True)
    mean_prod = jnp.mean(grad_out * normed, axis=-1, keepdims=True)
    return inverse * (grad_out - mean_grad - normed * mean_prod)


def col_sum(value):
    return jnp.sum(value, axis=0, keepdims=True)


def modulated(normed, mods, scale_row, shift_row):
    return (normed * (1.0 + mods(scale_row)) + mods(shift_row)).astype(BF)


def mod_reader(mod_ref, step):
    return lambda row: mod_ref[pl.ds(8 * step + row, 1), :]


def gelu_pair(value):
    cdf = 0.5 + 0.5 * lax.erf(value * (2.0**-0.5))
    density = jnp.exp(-0.5 * value * value) * (1.0 / math.sqrt(2.0 * math.pi))
    return (value * cdf, cdf + value * density)


def side_by_side(ref, first, count):
    return jnp.concatenate([ref[row : row + 1, :] for row in range(first, first + count)], axis=1)


def first_rows(x, rows_ref, wa_ref):
    normed, _ = layer_norm(x.astype(F32))
    hidden = modulated(normed, mod_reader(rows_ref, 0), SCALE1, SHIFT1)
    qkv = dot(hidden, wa_ref[:, : 3 * D]) + side_by_side(rows_ref, ROW_BQKV, 3)
    return qkv.astype(BF)


def middle_rows(
    x_ref, att_ref, rows_ref, wa_ref, wup_ref, wdown_ref,
    a_refs, gp_ref, act_refs, f_ref, next_ref, qkv_ref,
):
    mods = mod_reader(rows_ref, 0)
    later = mod_reader(rows_ref, 1)
    branch = dot(att_ref[...], wa_ref[:, 3 * D :]) + mods(ROW_BPROJ)
    for part, ref in enumerate(a_refs):
        ref[...] = branch[:, 128 * part : 128 * (part + 1)]
    middle = x_ref[...].astype(F32) + mods(GATE1) * branch
    normed, _ = layer_norm(middle)
    hidden = modulated(normed, mods, SCALE2, SHIFT2)
    upward = dot(hidden, wup_ref[...]) + side_by_side(rows_ref, ROW_BUP, 4)
    act, slope = gelu_pair(upward)
    gp_ref[...] = slope
    act = act.astype(BF)
    for part, ref in enumerate(act_refs):
        ref[...] = act[:, PART * part : PART * (part + 1)]
    branch = dot(act, wdown_ref[...]) + mods(ROW_BDOWN)
    f_ref[...] = branch
    stream = middle + mods(GATE2) * branch
    next_ref[...] = stream
    normed, _ = layer_norm(stream)
    hidden = modulated(normed, later, SCALE1, SHIFT1)
    qkv = dot(hidden, wa_ref[:, : 3 * D]) + side_by_side(rows_ref, ROW_BQKV, 3)
    qkv_ref[...] = qkv.astype(BF)


def ffn_back(
    mods, grad, branch_two, act, slope, hidden, wdown_ref, gdown_ref, gup_ref, wide_ref, narrow_ref
):
    df = (mods(GATE2) * grad).astype(BF)
    narrow_ref[pl.ds(GATE2, 1), :] += col_sum(grad * branch_two)
    narrow_ref[pl.ds(7, 1), :] += col_sum(df.astype(F32))
    gdown_ref[...] += dot(act, df, TN)
    dact = dot(df, wdown_ref[...], NT)
    du = (dact * slope).astype(BF)
    wide_ref[pl.ds(0, 1), :] += col_sum(du.astype(F32))
    gup_ref[...] += dot(hidden, du, TN)
    return du


def middle_back(
    mods, grad, du, normed, inverse, branch_one, att, wa_ref, wup_ref, gproj_ref, narrow_ref,
    dmid_ref, datt_ref,
):
    dh = dot(du, wup_ref[...], NT)
    narrow_ref[pl.ds(SHIFT2, 1), :] += col_sum(dh)
    narrow_ref[pl.ds(SCALE2, 1), :] += col_sum(dh * normed)
    dmid = grad + norm_back(normed, inverse, dh * (1.0 + mods(SCALE2)))
    dmid_ref[...] = dmid
    da = (mods(GATE1) * dmid).astype(BF)
    narrow_ref[pl.ds(GATE1, 1), :] += col_sum(dmid * branch_one)
    narrow_ref[pl.ds(6, 1), :] += col_sum(da.astype(F32))
    gproj_ref[...] += dot(att, da, TN)
    datt_ref[...] = dot(da, wa_ref[:, 3 * D :], NT).astype(BF)


def turn_rows(
    x_ref, att_ref, cot_ref, rows_ref, wa_ref, wup_ref, wdown_ref,
    out_ref, dmid_ref, datt_ref, gdown_ref, gup_ref, gproj_ref, wide_ref, narrow_ref,
):
    mods = mod_reader(rows_ref, 1)
    shared = mod_reader(rows_ref, 0)
    att = att_ref[...]
    branch_one = dot(att, wa_ref[:, 3 * D :]) + shared(ROW_BPROJ)
    middle = x_ref[...] + mods(GATE1) * branch_one
    normed, inverse = layer_norm(middle)
    hidden = modulated(normed, mods, SCALE2, SHIFT2)
    upward = dot(hidden, wup_ref[...]) + side_by_side(rows_ref, ROW_BUP, 4)
    act, slope = gelu_pair(upward)
    act = act.astype(BF)
    branch_two = dot(act, wdown_ref[...]) + shared(ROW_BDOWN)
    out_ref[...] = middle + mods(GATE2) * branch_two
    grad = cot_ref[...].astype(F32)
    du = ffn_back(
        mods, grad, branch_two, act, slope, hidden, wdown_ref, gdown_ref, gup_ref, wide_ref, narrow_ref
    )
    middle_back(
        mods, grad, du, normed, inverse, branch_one, att, wa_ref, wup_ref, gproj_ref, narrow_ref,
        dmid_ref, datt_ref,
    )


def qkv_back(mods, stream, dmid, dqkv, wa_ref, narrow_ref, bias_ref, gqkv_ref=None):
    normed, inverse = layer_norm(stream)
    bias_ref[pl.ds(0, 1), :] += col_sum(dqkv.astype(F32))
    if gqkv_ref is not None:
        gqkv_ref[...] += dot(modulated(normed, mods, SCALE1, SHIFT1), dqkv, TN)
    dh = dot(dqkv, wa_ref[:, : 3 * D], NT)
    narrow_ref[pl.ds(SHIFT1, 1), :] += col_sum(dh)
    narrow_ref[pl.ds(SCALE1, 1), :] += col_sum(dh * normed)
    return dmid + norm_back(normed, inverse, dh * (1.0 + mods(SCALE1)))


def middle_again(mods, x_ref, a_refs):
    branch_one = jnp.concatenate([ref[...] for ref in a_refs], axis=1)
    normed, inverse = layer_norm(x_ref[...].astype(F32) + mods(GATE1) * branch_one)
    return (branch_one, normed, inverse)


def join_rows(
    dqkv_ref, x1_ref, x0_ref, a_refs, gp_ref, act_refs, f_ref, rows_ref, wa_ref, wdown_ref,
    hidden_ref, dmid_ref, gqkv_ref, gdown_ref, gup_ref, wide_ref, narrow1_ref, narrow_ref, bias_ref,
):
    grad = qkv_back(
        mod_reader(rows_ref, 1), x1_ref[...], dmid_ref[...], dqkv_ref[...], wa_ref,
        narrow1_ref, bias_ref, gqkv_ref,
    )
    dmid_ref[...] = grad
    mods = mod_reader(rows_ref, 0)
    normed, _ = layer_norm(x0_ref[...].astype(F32))
    hidden_ref[...] = modulated(normed, mods, SCALE1, SHIFT1)
    _, normed, _ = middle_again(mods, x0_ref, a_refs)
    act = jnp.concatenate([ref[...] for ref in act_refs], axis=1)
    du = ffn_back(
        mods, grad, f_ref[...], act, gp_ref[...], modulated(normed, mods, SCALE2, SHIFT2),
        wdown_ref, gdown_ref, gup_ref, wide_ref, narrow_ref,
    )
    for part, ref in enumerate(act_refs):
        ref[...] = du[:, PART * part : PART * (part + 1)]


def join_middle_rows(
    x0_ref, a_refs, du_refs, att_ref, rows_ref, wa_ref, wup_ref,
    dmid_ref, datt_ref, gproj_ref, narrow_ref,
):
    mods = mod_reader(rows_ref, 0)
    branch_one, normed, inverse = middle_again(mods, x0_ref, a_refs)
    du = jnp.concatenate([ref[...] for ref in du_refs], axis=1)
    middle_back(
        mods, dmid_ref[...], du, normed, inverse, branch_one, att_ref[...], wa_ref, wup_ref,
        gproj_ref, narrow_ref, dmid_ref, datt_ref,
    )


def head_lanes(rows):
    lane = lax.broadcasted_iota(jnp.int32, (rows, 2 * HEAD_DIM), 1)
    return (lane < HEAD_DIM, lane >= HEAD_DIM)


def turned_heads(rows_f32, out_ref):
    turned = jnp.transpose(rows_f32)
    row = lax.broadcasted_iota(jnp.int32, turned.shape, 0)
    out_ref[0] = jnp.where(row < HEAD_DIM, turned, 0.0).astype(BF)
    out_ref[1] = jnp.where(row >= HEAD_DIM, turned, 0.0).astype(BF)


score_scale = HEAD_DIM**-0.5


def attend_pair(q, k_ref, v, o_ref, p_ref, vt_ref):
    turned_heads(v.astype(F32), vt_ref)
    queries = q * BF(score_scale)
    mixed = None
    for half, lanes in enumerate(head_lanes(queries.shape[0])):
        scores = dot(k_ref[...], jnp.where(lanes, queries, BF(0)), NT)
        top = jnp.max(scores, axis=0, keepdims=True)
        weights = jnp.exp(scores - top)
        total = jnp.sum(weights, axis=0, keepdims=True)
        low = (weights * (1.0 / total)).astype(BF)
        p_ref[half] = low
        part = dot(vt_ref[half], low)
        mixed = part if mixed is None else mixed + part
    o_ref[...] = jnp.transpose(mixed).astype(BF)


def attend_back_pair(q, k, v_ref, grads, p_ref, dq_ref, dk_ref, dv_ref, kt_ref, between):
    turned_heads(k.astype(F32) * score_scale, kt_ref)
    queries = q * BF(score_scale)
    own_lanes = head_lanes(queries.shape[0])
    for half, lanes in enumerate(own_lanes):
        grad = jnp.where(lanes, grads, BF(0))
        query = jnp.where(lanes, queries, BF(0))
        low = p_ref[half]
        weight_grad = dot(v_ref[...], grad, NT)
        weights = low.astype(F32)
        delta = jnp.sum(weights * weight_grad, axis=0, keepdims=True)
        score_grad = (weights * (weight_grad - delta)).astype(BF)
        news = (
            jnp.transpose(dot(kt_ref[half], score_grad)), dot(score_grad, query), dot(low, grad)
        )
        for ref, new in zip((dq_ref, dk_ref, dv_ref), news):
            new = new.astype(BF)
            ref[...] = new if half == 0 else jnp.where(lanes, new, ref[...])
        if half == 0 and between is not None:
            between()


class Refs:
    def __init__(self, names, refs):
        for name, ref in zip(names, refs, strict=True):
            setattr(self, name, ref)

MESH_ID = pl.DeviceIdType.MESH
GROUPS = 4
LAYERS = 4
UNITS = 3
HALF = 768


class Place:
    def __init__(self):
        self.grp = lax.axis_index("grp")
        self.dp = lax.axis_index("dp")
        self.z = self.dp // 2
        self.core = self.dp % 2

    def sibling(self):
        return (self.grp, 2 * self.z + 1 - self.core)

    def along_grp(self, step):
        return (lax.rem(self.grp + step, GROUPS), self.dp)

    def along_z(self, step):
        return (self.grp, 2 * lax.rem(self.z + step, LAYERS) + self.core)

    def across(self, step):
        return (self.grp, 2 * lax.rem(self.z + step, LAYERS) + 1 - self.core)


def greet(peers):
    barrier = pltpu.get_barrier_semaphore()
    for peer in peers:
        pl.semaphore_signal(barrier, inc=1, device_id=peer, device_id_type=MESH_ID)
    return lambda: pl.semaphore_wait(barrier, len(peers))


def remote(src, dst, sems, index, peer):
    send_sem, recv_sem = sems
    return pltpu.make_async_remote_copy(
        src_ref=src, dst_ref=dst, send_sem=send_sem.at[index], recv_sem=recv_sem.at[index],
        device_id=peer, device_id_type=MESH_ID,
    )


def condition_rows(moments, intervals, lead_ref):
    shape = (8, D)
    row = lax.broadcasted_iota(jnp.int32, shape, 0)
    lane = lax.broadcasted_iota(jnp.int32, shape, 1)
    moment = jnp.zeros(shape, F32)
    chosen = jnp.zeros(shape, jnp.int32)
    for index, (value, interval) in enumerate(zip(moments, intervals)):
        moment = jnp.where(row == index, value.astype(F32), moment)
        chosen = jnp.where(row == index, interval, chosen)
    lead = jnp.zeros(shape, F32)
    for choice in range(INTERVALS):
        picked = jnp.broadcast_to(lead_ref[choice : choice + 1, :], shape)
        lead = jnp.where(chosen == choice, picked, lead)
    half_width = D // 2
    place = jnp.where(lane < half_width, lane, lane - half_width).astype(F32)
    angles = moment * jnp.exp(place * (-math.log(10000.0) / half_width))
    wave = jnp.where(lane < half_width, jnp.sin(angles), jnp.cos(angles))
    condition = lead + wave
    return (condition / (1.0 + jnp.exp(-condition))).astype(BF).astype(F32)


def span(start, size):
    return pl.ds(pl.multiple_of(start, SLAB), size)


def local(src, dst, sem):
    made = pltpu.make_async_copy(src, dst, sem)
    made.start()
    return made


class Alone:
    def __init__(self, refs):
        self.refs = refs

    def begin(self):
        r = self.refs
        sems = r.in_sems
        first = [local(r.wa_far, r.wa, sems.at[0]), local(r.rows_far, r.rows, sems.at[3])]
        self.later = [local(r.wup_far, r.wup, sems.at[1]), local(r.wdown_far, r.wdown, sems.at[2])]
        for made in first:
            made.wait()

    def after_first(self):
        pass

    def after_attend_pair(self, h):
        pass

    def before_middle(self):
        for made in self.later:
            made.wait()

    def before_join(self):
        pass

    def amid_join(self):
        fill_blocks(self.refs)

    def after_join(self):
        pass

    def amid_back_pair(self, h):
        pass

    def after_back_pair(self, h):
        fill_pair(self.refs, h)

    def after_last_rows(self, i):
        pass

    def after_last(self):
        r = self.refs
        fill_vec(r)
        fill_late(r, r.late)
        r.vec[0:6, :] = r.late[0:6, :]
        r.vec[VEC_STEP : VEC_STEP + 6, :] = r.late[6:12, :]
        puts = [local(r.blocks, r.blocks_far, r.in_sems.at[0]), local(r.vec, r.vec_far, r.in_sems.at[1])]
        for made in puts:
            made.wait()


def block_rows(owner, part):
    first = HALF * (owner % 2) + 4 * SLAB * part + SLAB * (owner // 2)
    return slice(first, first + SLAB)


def fill_blocks(refs):
    share = refs.rows[ROW_SHARE : ROW_SHARE + 1, :]

    def owner(d, carry):
        for g in range(4):
            there = span(HALF * (d % 2) + 4 * SLAB * g + SLAB * (d // 2), SLAB)
            up = refs.gup[span(SLAB * d, SLAB), PART * g : PART * (g + 1)]
            down = refs.gdown[span(SLAB * (4 * d + g), SLAB), :]
            refs.blocks[1, there, :] = (up * share).astype(BF)
            refs.blocks[2, there, :] = (down * share).astype(BF)
        return carry

    lax.fori_loop(0, 8, owner, 0)


def fill_pair(refs, h):
    share = refs.rows[ROW_SHARE : ROW_SHARE + 1, 0:128]
    columns = [pl.ds(pl.multiple_of(D * g + 128 * h, 128), 128) for g in range(3)]
    grads = jnp.concatenate([refs.dqkv[:, column] for column in columns], axis=1)
    value = dot(refs.att1[...], grads, TN)
    for d in range(8):
        own = slice(SLAB * d, SLAB * (d + 1))
        for g in range(3):
            part = value[own, 128 * g : 128 * (g + 1)] + refs.gqkv[own, columns[g]]
            refs.blocks[0, block_rows(d, g), columns[0]] = (part * share).astype(BF)
        part = refs.gproj[own, columns[0]]
        refs.blocks[0, block_rows(d, 3), columns[0]] = (part * share).astype(BF)


VEC = 72
VEC_STEP = 24


def fill_vec(refs):
    share = refs.rows[ROW_SHARE : ROW_SHARE + 1, 0:128]

    def put(first_row, value):
        for j in range(value.shape[1] // 128):
            refs.vec[first_row + j : first_row + j + 1, :] = value[:, 128 * j : 128 * j + 128] * share

    refs.vec[...] = jnp.zeros_like(refs.vec)
    wide, narrow0, narrow1 = (refs.wide, refs.narrow0, refs.narrow1)
    put(6, narrow0[6:7, :] + narrow1[6:7, :])
    put(9, wide[0:1, :])
    put(21, narrow0[7:8, :] + narrow1[7:8, :])
    for r in range(6):
        if r > 1:
            put(VEC_STEP + 3 * r, narrow0[r : r + 1, :])
        put(2 * VEC_STEP + 3 * r, narrow1[r : r + 1, :])


def fill_late(refs, late_ref):
    share = refs.rows[ROW_SHARE : ROW_SHARE + 1, 0:128]
    rest = (refs.bias[0:1, :D], refs.bias[0:1, 2 * D :], refs.narrow0[0:1, :], refs.narrow0[1:2, :])
    for index, value in enumerate(rest):
        for j in range(3):
            row = 3 * index + j
            late_ref[row : row + 1, :] = value[:, 128 * j : 128 * j + 128] * share
    late_ref[12:16, :] = jnp.zeros((4, 128), F32)


class Together:
    steps = range(1, 4)

    def __init__(self, refs):
        self.refs = refs
        self.at = Place()

    def start(self, copy):
        copy.start()


    def whole(self, unit):
        return (self.refs.wa, self.refs.wup, self.refs.wdown)[unit]

    def part(self, unit, owner, grp):
        if unit == 2:
            return self.whole(2).at[span(4 * SLAB * owner + SLAB * grp, SLAB), :]
        return self.whole(unit).at[
            span(SLAB * owner, SLAB), pl.ds(pl.multiple_of(PART * grp, 128), PART)
        ]

    def slab(self, unit, owner):
        if unit == 2:
            return self.whole(2).at[span(4 * SLAB * owner, 4 * SLAB), :]
        return self.whole(unit).at[span(SLAB * owner, SLAB), :]

    def owner(self, k):
        return 2 * lax.rem(self.at.z + LAYERS - k, LAYERS) + self.at.core

    def gather_z(self, unit, k):
        own = self.part(unit, self.at.dp, self.at.grp)
        return remote(own, own, self.refs.gz, (unit, k - 1), self.at.along_z(k))

    def gather_grp(self, unit, k, m):
        part = self.part(unit, self.owner(k), self.at.grp)
        return remote(part, part, self.refs.gx, (unit, k - 1, m - 1), self.at.along_grp(m))

    def gather_sibling(self, unit, k):
        slab = self.slab(unit, self.owner(k) if k else self.at.dp)
        return remote(slab, slab, self.refs.gs, (unit, k), self.at.sibling())

    def launch(self, unit):
        for k in self.steps:
            self.start(self.gather_z(unit, k))
        self.start(self.gather_sibling(unit, 0))

    def forward_grp(self, unit):
        for k in self.steps:
            self.gather_z(unit, k).wait_recv()
            for m in self.steps:
                self.start(self.gather_grp(unit, k, m))

    def forward_sibling(self, unit):
        for k in self.steps:
            for m in self.steps:
                self.gather_grp(unit, k, m).wait_recv()
            self.start(self.gather_sibling(unit, k))

    def finish_sibling(self, unit):
        for k in range(4):
            self.gather_sibling(unit, k).wait_recv()

    def small(self, index):
        r, at = (self.refs, self.at)
        if index == 0:
            return remote(r.part_own, r.part_sib, r.gm, 0, at.sibling())
        if index == 1:
            own = r.bias_slot.at[at.z, at.core]
            return remote(own, own, r.gm, 1, at.sibling())
        if index < 5:
            own = r.part_z.at[at.z]
            return remote(own, own, r.gm, index, at.along_z(index - 1))
        own = r.bias_slot.at[at.z]
        return remote(own, own, r.gm, index, at.along_z(index - 4))

    def begin(self):
        r, at, steps = (self.refs, self.at, self.steps)
        stage = {
            "qkv": r.a.at[0:432], "proj": r.a.at[432:576], "ada": r.a.at[1728:2592],
            "up": r.a.at[576:1152], "down": r.a.at[1152:1728],
        }
        loads = {
            name: local(r.masters[name], stage[name], r.in_sems.at[index])
            for index, name in enumerate(stage)
        }
        ready = greet([self.everywhere(step) for step in range(1, 8 * LAYERS)])

        def fill(unit, source, count, offset, first=0):
            for j in range(count):
                value = source[pl.ds(first + j, SLAB, stride=count), :].astype(BF)
                where = offset + 128 * j
                if unit == 2:
                    rows = span(4 * SLAB * at.dp + offset, SLAB)
                    where = 128 * j
                else:
                    rows = span(SLAB * at.dp, SLAB)
                self.whole(unit)[rows, where : where + 128] = value

        loads["qkv"].wait()
        fill(0, stage["qkv"], 9, 0)
        loads["proj"].wait()
        fill(0, stage["proj"], 3, 3 * D)
        ready()
        self.launch(0)

        moment, interval = (r.start[at.grp], r.interval[at.grp])
        r.cond_t[...] = jnp.transpose(
            condition_rows([moment + s for s in range(ROLLOUT)], [interval] * ROLLOUT, r.lead)
        )
        own_cond = r.cond_t[span(SLAB * at.dp, SLAB), :]
        columns = [jnp.broadcast_to(own_cond[:, s : s + 1], (SLAB, 128)) for s in range(ROLLOUT)]
        loads["ada"].wait()
        for j in range(18):
            rows = stage["ada"][pl.ds(j, SLAB, stride=18), :].astype(BF).astype(F32)
            for s in range(ROLLOUT):
                r.part_own[18 * s + j : 18 * s + j + 1, :] = col_sum(rows * columns[s])
        r.part_own[36:40, :] = jnp.zeros((4, 128), F32)
        r.bias_own[...] = jnp.zeros((8, 128), F32)
        for i in range(6):
            size = 128 if i < 5 else 32
            r.bias_own[i : i + 1, 0:size] = r.bias_flat[pl.ds(128 * i, size)].reshape(1, size)
        lane = lax.broadcasted_iota(jnp.int32, (8, 128), 1)
        shift = lax.rem(32 * at.dp, 128)
        turned = pltpu.roll(r.bias_own[...].astype(BF).astype(F32), shift, axis=1)
        above = pltpu.roll(turned, 1, axis=0)
        r.bias_slot[at.z, at.core] = jnp.where(lane >= shift, turned, above)
        self.start(self.small(0))
        self.start(self.small(1))

        loads["up"].wait()
        fill(1, stage["up"], 12, 0)
        loads["down"].wait()
        for g in range(GROUPS):
            fill(2, stage["down"], 3, SLAB * g, 3 * SLAB * g)

        self.small(0).wait_recv()
        self.small(1).wait_recv()
        r.part_z[at.z] = r.part_own[...] + r.part_sib[...]
        for index in range(2, 8):
            self.start(self.small(index))
        self.forward_grp(0)
        self.launch(1)
        self.launch(2)

        for index in range(2, 8):
            self.small(index).wait_recv()
        total = r.part_z[0] + r.part_z[1] + r.part_z[2] + r.part_z[3]
        r.bias_full[...] = jnp.zeros_like(r.bias_full)
        for d in range(2 * LAYERS):
            first = 672 * d // 128
            r.bias_full[first : first + 7, :] += r.bias_slot[d // 2, d % 2, 0:7, :]
        counts = [r.counts[g].astype(F32) for g in range(GROUPS)]
        own_count = r.counts[at.grp].astype(F32)
        share = jnp.full((1, D), GROUPS * own_count) / jnp.full((1, D), sum(counts[1:], counts[0]))

        def put(row, value):
            r.rows[row : row + 1, :] = value

        def joined(first):
            return jnp.concatenate(
                [r.bias_full[first + j : first + j + 1, :] for j in range(3)], axis=1
            )

        for s in range(ROLLOUT):
            for row in range(6):
                first = 18 * s + 3 * row
                mod = jnp.concatenate([total[first + j : first + j + 1, :] for j in range(3)], axis=1)
                put(8 * s + row, mod + joined(24 + 3 * row))
            put(8 * s + 6, share)
            put(8 * s + 7, share)
        put(ROW_BQKV, joined(0))
        put(ROW_BQKV + 1, jnp.zeros((1, D), F32))
        put(ROW_BQKV + 2, joined(3))
        put(ROW_BPROJ, joined(6))
        for j in range(4):
            put(ROW_BUP + j, joined(9 + 3 * j))
        put(ROW_BDOWN, joined(21))
        r.rows[25:32, :] = jnp.zeros((7, D), F32)
        self.forward_sibling(0)
        self.finish_sibling(0)

    def after_first(self):
        self.forward_grp(1)

    def after_attend_pair(self, h):
        @pl.when(h == 0)
        def _():
            self.forward_grp(2)

        @pl.when(h == 1)
        def _():
            self.forward_sibling(1)

    def before_middle(self):
        self.forward_sibling(2)
        self.finish_sibling(1)
        self.finish_sibling(2)


    x_first = {3: True, 4: False}

    def columns(self, unit):
        return pl.ds(128 * unit, 128) if unit < 3 else slice(None)

    def got(self, unit, name):
        first = {"sib": 0, "piece": HALF, "grp": 0, "one": 0, "two": 8 * SLAB, "z": 12 * SLAB}[name]
        size = {"sib": HALF, "piece": 4 * SLAB, "grp": 12 * SLAB, "one": 8 * SLAB, "two": 4 * SLAB, "z": 3 * SLAB}[name]
        r, rows = (self.refs, slice(first, first + size))
        if unit < 3:
            return (r.att0 if name in ("sib", "piece") else r.act).at[rows, self.columns(unit)]
        if name in ("sib", "piece"):
            third = 0 if unit == 3 else 1
            return r.qkv1.at[rows, D * third : D * (third + 1)]
        return r.cot.at[rows] if unit == 3 else r.qkv1.at[rows, 2 * D : 3 * D]

    def half(self, unit, core):
        block = max(unit - 2, 0)
        return self.refs.blocks.at[block, span(HALF * core, HALF), self.columns(unit)]

    def parts(self, unit, part, count=1):
        return self.half(unit, self.at.core).at[span(4 * SLAB * part, 4 * SLAB * count), :]

    def sum_sibling(self, unit):
        src = self.half(unit, 1 - self.at.core)
        return remote(src, self.got(unit, "sib"), self.refs.rs, unit, self.at.sibling())

    def grp_peer(self, along_x):
        x, y = (self.at.grp % 2, self.at.grp // 2)
        grp = 2 * y + 1 - x if along_x else 2 * (1 - y) + x
        return (grp, self.at.dp)

    def stage_parts(self, unit, own):
        x, y = (self.at.grp % 2, self.at.grp // 2)
        if self.x_first[unit]:
            return [2 * j + (x if own else 1 - x) for j in range(2)]
        return [2 * (y if own else 1 - y) + j for j in range(2)]

    def sum_one(self, unit, j):
        src = self.parts(unit, self.stage_parts(unit, False)[j])
        dst = self.got(unit, "one").at[4 * SLAB * j : 4 * SLAB * (j + 1)]
        return remote(src, dst, self.refs.rx, (unit, j), self.grp_peer(self.x_first[unit]))

    def sum_two(self, unit):
        peer = self.grp_peer(not self.x_first[unit])
        return remote(self.parts(unit, peer[0]), self.got(unit, "two"), self.refs.rx, (unit, 2), peer)

    def sum_grp(self, unit, k):
        peer = self.at.along_grp(k)
        first = 4 * SLAB * (k - 1)
        dst = self.got(unit, "grp").at[first : first + 4 * SLAB]
        return remote(self.parts(unit, peer[0]), dst, self.refs.rx, (unit, k - 1), peer)

    def own_part(self, unit):
        return self.parts(unit, self.at.grp)

    def sum_z(self, unit, k):
        there = lax.rem(self.at.z + k, LAYERS)
        src = self.own_part(unit).at[span(SLAB * there, SLAB), :]
        dst = self.got(unit, "z").at[SLAB * (k - 1) : SLAB * k]
        return remote(src, dst, self.refs.rz, (unit, k - 1), self.at.along_z(k))

    def share_piece(self, unit, k):
        own = self.got(unit, "piece").at[span(SLAB * self.at.grp, SLAB), :]
        return remote(own, own, self.refs.ra, (unit, k - 1), self.at.along_grp(k))

    def add(self, mine, got, count):
        def step(i, carry):
            rows = span(SLAB * i, SLAB)
            mine[rows, :] = (mine[rows, :].astype(F32) + got[rows, :].astype(F32)).astype(BF)
            return carry

        lax.fori_loop(0, count, step, 0)

    def add_sibling(self, unit):
        self.sum_sibling(unit).wait_recv()
        self.add(self.half(unit, self.at.core), self.got(unit, "sib"), 16)
        if unit < 3:
            for k in self.steps:
                self.start(self.sum_grp(unit, k))
        else:
            for j in range(2):
                self.start(self.sum_one(unit, j))

    def add_grp(self, unit):
        for k in self.steps:
            self.sum_grp(unit, k).wait_recv()
        mine, got = (self.own_part(unit), self.got(unit, "grp"))

        def step(i, carry):
            rows = span(SLAB * i, SLAB)
            value = mine[rows, :].astype(F32)
            for k in self.steps:
                value = value + got[span(SLAB * (i + 4 * (k - 1)), SLAB), :].astype(F32)
            mine[rows, :] = value.astype(BF)
            return carry

        lax.fori_loop(0, 4, step, 0)
        for k in self.steps:
            self.start(self.sum_z(unit, k))

    def add_one(self, unit):
        for j in range(2):
            self.sum_one(unit, j).wait_recv()
            got = self.got(unit, "one").at[4 * SLAB * j : 4 * SLAB * (j + 1)]
            self.add(self.parts(unit, self.stage_parts(unit, True)[j]), got, 4)
        self.start(self.sum_two(unit))

    def add_two(self, unit):
        self.sum_two(unit).wait_recv()
        self.add(self.own_part(unit), self.got(unit, "two"), 4)
        for k in self.steps:
            self.start(self.sum_z(unit, k))

    def add_z(self, unit):
        for k in self.steps:
            self.sum_z(unit, k).wait_recv()
        value = self.own_part(unit)[span(SLAB * self.at.z, SLAB), :].astype(F32)
        for k in self.steps:
            value = value + self.got(unit, "z")[SLAB * (k - 1) : SLAB * k, :].astype(F32)
        value = value.astype(BF)
        self.got(unit, "piece")[span(SLAB * self.at.grp, SLAB), :] = value
        for k in self.steps:
            self.start(self.share_piece(unit, k))
        value = value.astype(F32)
        squares = col_sum(value * value)
        if unit < 3:
            return squares
        return squares[:, 0:128] + squares[:, 128:256] + squares[:, 256:384]

    def tell(self, sem):
        at = self.at
        for peer in (
            [at.sibling()]
            + [at.along_grp(k) for k in self.steps]
            + [at.along_z(k) for k in self.steps]
        ):
            pl.semaphore_signal(sem, inc=1, device_id=peer, device_id_type=MESH_ID)

    def before_join(self):
        self.tell(self.refs.turned_back)

    def amid_join(self):
        fill_blocks(self.refs)
        pl.semaphore_wait(self.refs.turned_back, 7)
        self.start(self.sum_sibling(3))
        self.start(self.sum_sibling(4))

    def after_join(self):
        r = self.refs
        self.tell(r.joined)
        self.add_sibling(3)
        self.add_sibling(4)
        fill_vec(r)
        self.start(self.small_sum(0))

    def amid_back_pair(self, h):
        r, at = (self.refs, self.at)

        @pl.when(h == 0)
        def _():
            self.small_sum(0).wait_recv()
            r.vec_z[at.z] = r.vec[...] + r.vec_sib[...]
            for index in self.steps:
                self.start(self.small_sum(index))

        @pl.when(h == 1)
        def _():
            self.add_one(3)
            self.add_one(4)
            self.add_sibling(0)
            for index in self.steps:
                self.small_sum(index).wait_recv()
            r.vec_g[at.grp] = r.vec_z[0] + r.vec_z[1] + r.vec_z[2] + r.vec_z[3]
            for index in self.steps:
                self.start(self.small_sum(3 + index))

        @pl.when(h == 2)
        def _():
            self.add_two(3)
            self.add_two(4)
            self.add_sibling(1)
            self.add_grp(0)

    def after_back_pair(self, h):
        r = self.refs
        fill_pair(r, h)

        @pl.when(h == 0)
        def _():
            pl.semaphore_wait(r.joined, 7)
            self.start(self.sum_sibling(0))

        @pl.when(h == 1)
        def _():
            self.start(self.sum_sibling(1))

        @pl.when(h == 2)
        def _():
            self.start(self.sum_sibling(2))

    def after_last_rows(self, i):
        @pl.when(i == 0)
        def _():
            self.add_sibling(2)

        @pl.when(i == 2)
        def _():
            self.add_grp(1)

    def small_sum(self, index):
        r, at = (self.refs, self.at)
        if index == 0:
            return remote(r.vec, r.vec_sib, r.rv, 0, at.sibling())
        if index < 4:
            own = r.vec_z.at[at.z]
            return remote(own, own, r.rv, index, at.along_z(index))
        own = r.vec_g.at[at.grp]
        return remote(own, own, r.rv, index, at.along_grp(index - 3))

    def across_dp(self, index):
        at = self.at
        if index == 0:
            return at.sibling()
        return at.along_z(index) if index < 4 else at.across(index - 3)

    def everywhere(self, step):
        device = lax.rem(2 * LAYERS * self.at.grp + self.at.dp + step, 8 * LAYERS)
        return (device // (2 * LAYERS), lax.rem(device, 2 * LAYERS))

    def square_sum(self, step):
        own = self.refs.squares.at[2 * LAYERS * self.at.grp + self.at.dp]
        return remote(own, own, self.refs.rq, step, self.everywhere(step))

    def late_sum(self, index):
        r, at = (self.refs, self.at)
        if index < 7:
            own = r.late_d.at[at.dp]
            return remote(own, own, r.rl, index, self.across_dp(index))
        own = r.late_g.at[at.grp]
        return remote(own, own, r.rl, index, at.along_grp(index - 6))

    def ada_square(self):
        r = self.refs
        left = r.cond[...]
        right = [
            r.vec_sum[g, VEC_STEP * (s + 1) : VEC_STEP * (s + 2), :]
            for g in range(GROUPS)
            for s in range(ROLLOUT)
        ]
        total = jnp.zeros((VEC_STEP, 128), F32)
        for step, weight in ((0, 1.0), (1, 2.0), (2, 2.0), (3, 2.0), (4, 1.0)):
            moved = left if step == 0 else pltpu.roll(left, step, axis=0)
            products = jnp.sum(left * moved, axis=1, keepdims=True) * weight
            for k in range(8):
                total = total + products[k : k + 1, :] * (right[k] * right[(k - step) % 8])
        return col_sum(total)

    def after_last(self):
        r, at, steps = (self.refs, self.at, self.steps)
        fill_late(r, r.late_d.at[at.dp])
        for index in range(7):
            self.start(self.late_sum(index))
        moments = [r.start[g] + s for g in range(GROUPS) for s in range(ROLLOUT)]
        intervals = [r.interval[g] for g in range(GROUPS) for s in range(ROLLOUT)]
        r.cond[...] = condition_rows(moments, intervals, r.lead)
        self.add_grp(2)
        for index in range(7):
            self.late_sum(index).wait_recv()
        total = r.late_d[0]
        for d in range(1, 2 * LAYERS):
            total = total + r.late_d[d]
        r.late_g[at.grp] = total
        for index in range(7, 10):
            self.start(self.late_sum(index))
        square = self.add_z(0) + self.add_z(3) + self.add_z(4) + self.add_z(1)
        for index in steps:
            self.small_sum(3 + index).wait_recv()
        for index in range(7, 10):
            self.late_sum(index).wait_recv()
        vec = r.vec_sum
        vec[...] = r.vec_g[...]
        for g in range(GROUPS):
            vec[g, 0:6, :] = r.late_g[g, 0:6, :]
            vec[g, VEC_STEP : VEC_STEP + 6, :] = r.late_g[g, 6:12, :]
        vec_sum = vec[0] + vec[1] + vec[2] + vec[3]
        r.bias_out[0:24, :] = vec_sum[0:24]
        r.bias_out[24:48, :] = vec_sum[24:48] + vec_sum[48:72]
        ada_square = self.ada_square()
        square = square + self.add_z(2)
        own = 2 * LAYERS * at.grp + at.dp
        r.squares[own] = square
        for k in range(1, 8 * LAYERS):
            self.start(self.square_sum(k))

        r.cond_t[...] = jnp.transpose(r.cond[...])
        own_cond = r.cond_t[span(SLAB * at.dp, SLAB), :]
        columns = [jnp.broadcast_to(own_cond[:, k : k + 1], (SLAB, 128)) for k in range(8)]
        ada = r.a.at[0 : 18 * SLAB]

        def ada_tile(j, carry):
            tile = jnp.zeros((SLAB, 128), F32)
            for k in range(8):
                row = vec[k // ROLLOUT, pl.ds(VEC_STEP * (k % ROLLOUT + 1) + j, 1), :]
                tile = tile + columns[k] * row
            ada[pl.ds(j, SLAB, stride=18), :] = tile
            return carry

        lax.fori_loop(0, 18, ada_tile, 0)
        for unit in range(5):
            for k in steps:
                self.share_piece(unit, k).wait_recv()
        whole = [r.att0.at[HALF : HALF + 4 * SLAB], self.got(3, "piece"), self.got(4, "piece")]
        puts = [local(ada, r.ada_far, r.in_sems.at[0])]
        puts += [
            local(whole[unit], r.pieces_far.at[unit], r.in_sems.at[1 + unit])
            for unit in range(UNITS)
        ]
        bias_sum = r.bias_out[...]
        total = col_sum(bias_sum * bias_sum) + ada_square
        for k in range(1, 8 * LAYERS):
            self.square_sum(k).wait_recv()
        for device in range(8 * LAYERS):
            total = total + r.squares[device]
        r.square_out[...] = jnp.broadcast_to(jnp.sum(total, axis=1, keepdims=True), (8, 128))
        for made in puts:
            made.wait()
        self.drain()

    def drain(self):
        for unit in range(UNITS):
            for k in self.steps:
                self.gather_z(unit, k).wait_send()
                for m in self.steps:
                    self.gather_grp(unit, k, m).wait_send()
            for k in range(4):
                self.gather_sibling(unit, k).wait_send()
        for unit in range(5):
            self.sum_sibling(unit).wait_send()
            if unit < 3:
                for k in self.steps:
                    self.sum_grp(unit, k).wait_send()
            else:
                self.sum_one(unit, 0).wait_send()
                self.sum_one(unit, 1).wait_send()
                self.sum_two(unit).wait_send()
            for k in self.steps:
                self.sum_z(unit, k).wait_send()
                self.share_piece(unit, k).wait_send()
        for index in range(8):
            self.small(index).wait_send()
        for index in range(7):
            self.small_sum(index).wait_send()
        for index in range(10):
            self.late_sum(index).wait_send()
        for step in range(1, 8 * LAYERS):
            self.square_sum(step).wait_send()


correction = 1.0 - 0.5**ADAM_STEP
grad_limit = math.sqrt(NPARAM)


def adam(master, first, second, clipped, decay):
    first_new = 0.5 * first + 0.5 * clipped
    second_new = 0.5 * second + 0.5 * clipped * clipped
    update = first_new / correction / (jnp.sqrt(second_new / correction) + adam_eps)
    return (master - learn_rate * (update + decay * master), first_new, second_new)


CHUNK = 48
STATE = ("qkv", "proj", "up", "down", "ada")


def finish_kernel(names, *refs):
    r = Refs(names, refs)
    loads = {
        "pieces": local(r.pieces_far, r.pieces, r.in_sems.at[0]),
        "grad": local(r.grad_ada_far, r.grad_ada, r.in_sems.at[16]),
    }
    for index, name in enumerate(STATE):
        for kind in range(3):
            loads[name, kind] = local(
                getattr(r, f"{name}_in{kind}"), getattr(r, f"{name}_{kind}"),
                r.in_sems.at[1 + 3 * index + kind],
            )
    streams = [
        local(getattr(r, name + "_in"), getattr(r, name), r.stream_sems.at[index])
        for index, name in enumerate(("y", "dx"))
    ]
    norm = jnp.sqrt(r.square[...])
    r.norm[0, 0] = jnp.max(norm)
    clip = grad_limit / jnp.maximum(norm, grad_limit)
    row_clip = clip[0:1, :]

    loads["pieces"].wait()
    piece = r.pieces

    def unpack(name):
        for j in range(3):
            columns = slice(128 * j, 128 * j + 128)
            if name == "proj":
                r.grad_proj[pl.ds(j, SLAB, stride=3), :] = piece[0, 3 * SLAB :, columns].astype(F32)
            for g in range(GROUPS):
                rows = slice(SLAB * g, SLAB * (g + 1))
                if name == "qkv" and g < 3:
                    r.grad_qkv[pl.ds(3 * g + j, SLAB, stride=9), :] = piece[0, rows, columns].astype(F32)
                if name == "up":
                    r.grad_up[pl.ds(3 * g + j, SLAB, stride=12), :] = piece[1, rows, columns].astype(F32)
                if name == "down":
                    r.grad_down[pl.ds(3 * SLAB * g + j, SLAB, stride=3), :] = piece[2, rows, columns].astype(F32)

    stores = []
    for index, name in enumerate(STATE):
        for kind in range(3):
            loads[name, kind].wait()
        if name == "ada":
            loads["grad"].wait()
        unpack(name)
        grad, low = (getattr(r, "grad_" + name), getattr(r, name + "_low"))
        state = [getattr(r, f"{name}_{kind}") for kind in range(3)]

        def chunk(i, carry):
            rows = pl.ds(pl.multiple_of(CHUNK * i, 16), CHUNK)
            new, first_new, second_new = adam(
                *(ref[rows, :] for ref in state), grad[rows, :] * row_clip, 0.1
            )
            for ref, value in zip(state, (new, first_new, second_new)):
                ref[rows, :] = value
            low[rows, :] = new.astype(BF)
            return carry

        lax.fori_loop(0, grad.shape[0] // CHUNK, chunk, 0)
        for kind, ref in enumerate((*state, low)):
            stores.append(local(ref, getattr(r, f"{name}_out{kind}"), r.out_sems.at[4 * index + kind]))
        if index < 2:
            name = ("y", "dx")[index]
            streams[index].wait()
            stores.append(local(getattr(r, name), getattr(r, name + "_out"), r.stream_sems.at[index]))
    owner = lax.axis_index("dp")
    lane = lax.broadcasted_iota(jnp.int32, (1, 128), 1)
    first = 672 * owner // 128
    shift = lax.rem(32 * owner, 128)
    back = lax.rem(128 - shift, 128)
    for i in range(6):
        size = 128 if i < 5 else 32
        here = pltpu.roll(r.bias_sum[pl.ds(first + i, 1), :], back, axis=1)
        there = pltpu.roll(r.bias_sum[pl.ds(first + i + 1, 1), :], back, axis=1)
        grad = jnp.where(lane < 128 - shift, here, there) * row_clip
        place = pl.ds(128 * i, size)
        state = [getattr(r, f"bias_in{kind}")[place].reshape(1, size) for kind in range(3)]
        new, first_new, second_new = adam(*state, grad[:, :size], 0.0)
        r.bias_out0[place] = new.reshape(size)
        r.bias_out1[place] = first_new.reshape(size)
        r.bias_out2[place] = second_new.reshape(size)
        r.bias_out3[place] = new.reshape(size).astype(BF)

    for made in stores:
        made.wait()


def finish(y, dx, pieces, ada, bias_sum, square, masters, firsts, seconds):
    vmem, hbm, dma = (pltpu.VMEM, pl.ANY, pltpu.SemaphoreType.DMA)
    state = list(zip(masters, firsts, seconds))
    shapes = {name: (arrays[0].size // 128, 128) for name, arrays in zip(STATE, state)}
    ins = [
        ("square", square, vmem), ("bias_sum", bias_sum, vmem), ("pieces_far", pieces, hbm),
        ("grad_ada_far", ada, hbm), ("y_in", y, hbm), ("dx_in", dx, hbm),
        *[(f"bias_in{kind}", array, vmem) for kind, array in enumerate(state[5])],
        *[
            (f"{name}_in{kind}", array.reshape(-1, 128), hbm)
            for name, arrays in zip(STATE, state)
            for kind, array in enumerate(arrays)
        ],
    ]
    outs = [("norm", (1, 1), F32, pltpu.SMEM), ("y_out", y.shape, F32, hbm), ("dx_out", dx.shape, F32, hbm)]
    for kind in range(4):
        dtype = F32 if kind < 3 else BF
        outs += [(f"{name}_out{kind}", shapes[name], dtype, hbm) for name in STATE]
        outs.append((f"bias_out{kind}", state[5][0].shape, dtype, vmem))
    scratch = [
        ("pieces", vmem(pieces.shape, BF)), ("y", vmem(y.shape, F32)), ("dx", vmem(dx.shape, F32)),
        *[(f"{name}_{kind}", vmem(shapes[name], F32)) for name in STATE for kind in range(3)],
        *[(f"{name}_low", vmem(shapes[name], BF)) for name in STATE],
        *[(f"grad_{name}", vmem(shapes[name], F32)) for name in STATE],
        ("in_sems", dma((17,))), ("stream_sems", dma((2,))), ("out_sems", dma((20,))),
    ]
    names = [item[0] for item in (*ins, *outs, *scratch)]
    norm, y, dx, *rest = pl.pallas_call(
        functools.partial(finish_kernel, names),
        in_specs=[pl.BlockSpec(memory_space=space) for *_, space in ins],
        out_specs=[pl.BlockSpec(memory_space=space) for *_, space in outs],
        out_shape=[jax.ShapeDtypeStruct(shape, kind) for _, shape, kind, _ in outs],
        scratch_shapes=[kind for _, kind in scratch],
        name="finish",
    )(*(array for _, array, _ in ins))
    return (y, dx, norm.reshape(()), *(array.reshape(-1) for array in rest))


MASTERS = ("qkv", "proj", "up", "down", "ada")


def block_kernel(names, hooked, *refs):
    r = Refs(names, refs)
    if hooked is Together:
        r.masters = {name: getattr(r, "far_" + name) for name in MASTERS}
        for name in ("gz", "gx", "gs", "gm", "rs", "rx", "rz", "ra", "rv", "rq", "rl"):
            setattr(r, name, (getattr(r, name + "_out"), getattr(r, name + "_in")))
    hooks = hooked(r)
    length = r.x.shape[0]
    pairs = HEADS // 2
    get_cot = local(r.cot_far, r.cot, r.out_sems.at[2])

    def over_rows(body, after=None, size=ROWS):
        def step(i, carry):
            body(pl.ds(pl.multiple_of(i * size, size), size))
            if after is not None:
                after(i)
            return carry

        lax.fori_loop(0, length // size, step, 0)

    def columns(h, offset=0):
        return pl.ds(pl.multiple_of(offset + 128 * h, 128), 128)

    def over_pairs(body):
        def step(h, carry):
            body(h)
            return carry

        lax.fori_loop(0, pairs, step, 0)

    def act_refs(rows):
        first = rows.start
        return [
            r.act.at[pl.ds(pl.multiple_of(length * part + first, ROWS), rows.size)]
            for part in range(4)
        ]

    def a_refs(rows):
        first = rows.start
        return [
            r.a.at[pl.ds(pl.multiple_of(length * part + first, ROWS), rows.size)]
            for part in range(3)
        ]

    def save(step, h):
        slot = lax.rem(h, 2)
        return pltpu.make_async_copy(
            r.p.at[slot], r.p_far.at[step, pl.ds(2 * h, 2)], r.p_sems.at[slot]
        )

    def fetch(step, h):
        slot = lax.rem(h, 2)
        return pltpu.make_async_copy(
            r.p_far.at[step, pl.ds(2 * h, 2)], r.p.at[slot], r.p_sems.at[slot]
        )

    def attend(step, qkv, att, after):
        def body(h):
            @pl.when(h >= 2)
            def _():
                save(step, h - 2).wait()

            attend_pair(
                qkv[:, columns(h)], qkv.at[:, columns(h, D)], qkv[:, columns(h, 2 * D)],
                att.at[:, columns(h)], r.p.at[lax.rem(h, 2)], r.turned,
            )
            save(step, h).start()
            after(h)

        over_pairs(body)

    def finish_saves(step):
        for h in range(pairs - 2, pairs):
            save(step, h).wait()

    def attend_back(step, qkv, between, after):
        def body(h):
            fetch(step, h).wait()
            attend_back_pair(
                qkv[:, columns(h)], qkv[:, columns(h, D)], qkv.at[:, columns(h, 2 * D)],
                r.datt[:, columns(h)], r.p.at[lax.rem(h, 2)],
                r.dqkv.at[:, columns(h)], r.dqkv.at[:, columns(h, D)],
                r.dqkv.at[:, columns(h, 2 * D)], r.turned,
                None if between is None else lambda: between(h),
            )

            @pl.when(h + 2 < pairs)
            def _():
                fetch(step, h + 2).start()

            after(h)

        over_pairs(body)

    nothing = lambda h: None
    hooks.begin()

    def first(rows):
        r.qkv0[rows, :] = first_rows(r.x[rows, :], r.rows, r.wa)

    over_rows(first)
    hooks.after_first()
    attend(0, r.qkv0, r.att0, hooks.after_attend_pair)
    hooks.before_middle()

    def middle(rows):
        middle_rows(
            r.x.at[rows], r.att0.at[rows], r.rows, r.wa, r.wup, r.wdown,
            a_refs(rows), r.gp.at[rows], act_refs(rows), r.f.at[rows], r.x1.at[rows],
            r.qkv1.at[rows],
        )

    over_rows(middle, size=2 * ROWS)
    finish_saves(0)
    attend(1, r.qkv1, r.att1, nothing)

    def clear(i, carry):
        for ref in (r.gqkv, r.gproj, r.gup, r.gdown):
            size = ref.shape[0] // 8
            ref[span(i * size, size), :] = jnp.zeros((size, ref.shape[1]), F32)
        return carry

    lax.fori_loop(0, 8, clear, 0)
    for ref in (r.wide, r.narrow0, r.narrow1, r.bias):
        ref[...] = jnp.zeros_like(ref)

    def turn(rows):
        turn_rows(
            r.x1.at[rows], r.att1.at[rows], r.cot.at[rows], r.rows, r.wa, r.wup,
            r.wdown, r.y.at[rows], r.dmid.at[rows], r.datt.at[rows], r.gdown, r.gup, r.gproj,
            r.wide, r.narrow1,
        )

    finish_saves(1)
    for h in range(2):
        fetch(1, h).start()
    get_cot.wait()
    over_rows(turn, size=2 * ROWS)
    put_y = local(r.y, r.y_far, r.out_sems.at[0])
    attend_back(1, r.qkv1, None, nothing)
    for h in range(2):
        fetch(0, h).start()

    def join(rows):
        join_rows(
            r.dqkv.at[rows], r.x1.at[rows], r.x.at[rows], a_refs(rows), r.gp.at[rows],
            act_refs(rows), r.f.at[rows], r.rows, r.wa, r.wdown, r.att1.at[rows],
            r.dmid.at[rows], r.gqkv, r.gdown, r.gup, r.wide, r.narrow1, r.narrow0, r.bias,
        )

    def join_middle(rows):
        join_middle_rows(
            r.x.at[rows], a_refs(rows), act_refs(rows), r.att0.at[rows], r.rows, r.wa, r.wup,
            r.dmid.at[rows], r.datt.at[rows], r.gproj, r.narrow0,
        )

    hooks.before_join()
    over_rows(join)
    hooks.amid_join()
    over_rows(join_middle, size=2 * ROWS)
    hooks.after_join()
    attend_back(0, r.qkv0, hooks.amid_back_pair, hooks.after_back_pair)

    def last(rows):
        r.dmid[rows, :] = qkv_back(
            mod_reader(r.rows, 0), r.x[rows, :].astype(F32), r.dmid[rows, :],
            r.dqkv[rows, :], r.wa, r.narrow0, r.bias,
        )

    over_rows(last, hooks.after_last_rows)
    put_dx = local(r.dmid, r.dx_far, r.out_sems.at[1])
    hooks.after_last()
    put_y.wait()
    put_dx.wait()


def block_call(hooked, inputs, cotangent, extra_in, extra_out, extra_scratch, params):
    length = inputs.shape[0]
    vmem, hbm, dma = (pltpu.VMEM, pl.ANY, pltpu.SemaphoreType.DMA)
    weights = (ROLLOUT, HEADS, length, length)
    ins = [("x", inputs, vmem), ("cot_far", cotangent, hbm), *extra_in]
    outs = [
        ("y_far", (length, D), F32, hbm), ("dx_far", (length, D), F32, hbm),
        ("p_far", weights, BF, hbm), *extra_out,
    ]
    scratch = [
        ("wa", vmem((D, FF), BF)), ("wup", vmem((D, FF), BF)), ("wdown", vmem((FF, D), BF)),
        ("cot", vmem((length, D), BF)), ("qkv0", vmem((length, 3 * D), BF)),
        ("qkv1", vmem((length, 3 * D), BF)), ("p", vmem((2, 2, length, length), BF)),
        ("att0", vmem((length, D), BF)), ("att1", vmem((length, D), BF)),
        *[(name, vmem((length, D), F32)) for name in ("f", "x1", "dmid", "y")], ("a", vmem((3 * length, 128), F32)),
        ("gp", vmem((length, FF), F32)), ("act", vmem((4 * length, D), BF)),
        ("datt", vmem((length, D), BF)), ("dqkv", vmem((length, 3 * D), BF)),
        ("gqkv", vmem((D, 3 * D), F32)), ("gproj", vmem((D, D), F32)),
        ("gup", vmem((D, FF), F32)), ("gdown", vmem((FF, D), F32)),
        ("turned", vmem((2, 128, length), BF)), ("wide", vmem((8, FF), F32)),
        ("narrow0", vmem((8, D), F32)), ("narrow1", vmem((8, D), F32)),
        ("bias", vmem((8, 3 * D), F32)), ("blocks", vmem((UNITS, 2 * HALF, PART), BF)),
        ("rows", vmem((32, D), F32)), ("vec", vmem((VEC, 128), F32)), ("late", vmem((16, 128), F32)),
        ("in_sems", dma((5,))), ("p_sems", dma((2,))), ("out_sems", dma((3,))),
        *extra_scratch,
    ]
    names = [item[0] for item in (*ins, *outs, *scratch)]
    return pl.pallas_call(
        functools.partial(block_kernel, names, hooked),
        in_specs=[pl.BlockSpec(memory_space=space) for _, _, space in ins],
        out_specs=[pl.BlockSpec(memory_space=space) for *_, space in outs],
        out_shape=[jax.ShapeDtypeStruct(shape, kind) for _, shape, kind, _ in outs],
        scratch_shapes=[kind for _, kind in scratch],
        compiler_params=pltpu.CompilerParams(vmem_limit_bytes=67043328, **params),
        name="block",
    )(*(array for _, array, _ in ins))


def block_alone(inputs, cotangent, rows, wa, wup, wdown):
    hbm = pl.ANY
    y, dx, _, blocks, vec = block_call(
        Alone, inputs, cotangent,
        [("rows_far", rows, hbm), ("wa_far", wa, hbm), ("wup_far", wup, hbm), ("wdown_far", wdown, hbm)],
        [("blocks_far", (UNITS, 2 * HALF, PART), BF, hbm), ("vec_far", (VEC, 128), F32, hbm)],
        [], {},
    )
    return (y, dx, blocks, vec)


def block_together(inputs, cotangent, start, interval, counts, lead, masters):
    vmem, hbm, smem, dma = (pltpu.VMEM, pl.ANY, pltpu.SMEM, pltpu.SemaphoreType.DMA)
    qkv, proj, up, down, ada, bias = masters
    far = [
        ("far_" + name, array.reshape(-1, 128), hbm)
        for name, array in zip(MASTERS, (qkv, proj, up, down, ada))
    ]
    pairs_of = [
        ("gz", (UNITS, 3)), ("gx", (UNITS, 3, 3)), ("gs", (UNITS, 4)), ("gm", (8,)),
        ("rs", (5,)), ("rx", (5, 3)), ("rz", (5, 3)), ("ra", (5, 3)),
        ("rv", (7,)), ("rq", (8 * LAYERS,)), ("rl", (10,)),
    ]
    y, dx, _, pieces, ada_grad, bias_sum, square = block_call(
        Together, inputs, cotangent,
        [("start", start, smem), ("interval", interval, smem), ("counts", counts, smem),
         ("lead", lead, vmem), ("bias_flat", bias, vmem), *far],
        [("pieces_far", (UNITS, 4 * SLAB, PART), BF, hbm), ("ada_far", (18 * SLAB, 128), F32, hbm),
         ("bias_out", (48, 128), F32, vmem), ("square_out", (8, 128), F32, vmem)],
        [("cond_t", vmem((D, 8), F32)), ("part_own", vmem((40, 128), F32)),
         ("part_sib", vmem((40, 128), F32)), ("part_z", vmem((LAYERS, 40, 128), F32)),
         ("bias_own", vmem((8, 128), F32)), ("bias_slot", vmem((LAYERS, 2, 8, 128), F32)), ("bias_full", vmem((48, 128), F32)),
         ("vec_sib", vmem((VEC, 128), F32)), ("vec_z", vmem((LAYERS, VEC, 128), F32)),
         ("vec_g", vmem((GROUPS, VEC, 128), F32)), ("late_d", vmem((8, 16, 128), F32)),
         ("vec_sum", vmem((GROUPS, VEC, 128), F32)), ("cond", vmem((8, D), F32)),
         ("late_g", vmem((GROUPS, 16, 128), F32)), ("squares", vmem((8 * LAYERS, 1, 128), F32)), ("joined", pltpu.SemaphoreType.REGULAR), ("turned_back", pltpu.SemaphoreType.REGULAR),
         *[(name + end, dma(shape)) for name, shape in pairs_of for end in ("_out", "_in")]],
        dict(collective_id=0, has_side_effects=True),
    )
    return (y, dx, pieces, ada_grad, bias_sum, square)


def step_embedding(moment):
    half_width = D // 2
    freqs = jnp.exp(-math.log(10000.0) * jnp.arange(half_width, dtype=F32) / half_width)
    angles = moment[:, None] * freqs[None, :]
    return jnp.concatenate([jnp.sin(angles), jnp.cos(angles)], axis=1)


def all_conditions(group_interval, rollout_start, lead_table):
    chosen = group_interval[:, None] == jnp.arange(INTERVALS)[None, :]
    lead_rows = jnp.sum(jnp.where(chosen[:, :, None], lead_table[None], 0.0), axis=1)
    start = rollout_start.astype(F32)
    rows = [lead_rows + step_embedding(start + offset) for offset in range(ROLLOUT)]
    return jax.nn.silu(jnp.stack(rows, axis=1)).astype(BF)


def plain_gather(group_interval, counts, rollout_start, lead_table, masters):
    low = [master.astype(BF) for master in masters]
    owner = lax.axis_index("dp")
    group_index = lax.axis_index("grp")
    own_rows = D // lax.axis_size("dp")
    counts = counts.astype(F32)
    share = lax.axis_size("grp") * counts / jnp.sum(counts)
    share = lax.dynamic_index_in_dim(share, group_index, keepdims=False)
    conditions = all_conditions(group_interval, rollout_start, lead_table)
    owner_columns = lax.dynamic_slice_in_dim(conditions, owner * own_rows, own_rows, axis=2)
    own_condition = lax.dynamic_index_in_dim(owner_columns, group_index, keepdims=False)
    modulation = lax.psum(dot(own_condition, low[4].reshape(own_rows, 6 * D)), "dp")
    qkv, proj, up, down, bias = [
        lax.all_gather(low[index], "dp", axis=0, tiled=True) for index in (0, 1, 2, 3, 5)
    ]
    bias = bias.astype(F32)
    modulation = modulation + bias[4 * D + FF :][None]
    share_rows = jnp.broadcast_to(share, (ROLLOUT, 2, D))
    mods = jnp.concatenate([modulation.reshape(ROLLOUT, 6, D), share_rows], axis=1).reshape(-1, D)
    rows = jnp.concatenate(
        [mods, bias[:D][None], jnp.zeros((1, D), F32), bias[D : 4 * D + FF].reshape(-1, D),
         jnp.zeros((7, D), F32)]
    )
    wa = jnp.concatenate([qkv.reshape(D, 3 * D), proj.reshape(D, D)], axis=1)
    return (wa, up.reshape(D, FF), down.reshape(FF, D), rows, owner_columns)


def plain_update(owner_columns, vec, blocks, masters, firsts, seconds):
    owner = lax.axis_index("dp")
    vec = vec.reshape(-1)
    split = 4 * D + FF
    dmod = vec[split:].reshape(ROLLOUT, VEC_STEP * 128)[:, : 6 * D]
    dmod_all = lax.all_gather(lax.psum(dmod, "dp"), "grp")
    bias_sum = lax.psum(vec[:split], ("grp", "dp"))
    bias_sum = jnp.concatenate([bias_sum, jnp.sum(dmod_all, axis=(0, 1))])
    bias_rows = masters[5].shape[0]
    bias_grad = lax.dynamic_slice_in_dim(bias_sum, owner * bias_rows, bias_rows)
    ada_grad = jnp.einsum(
        "gsr,gsc->rc", owner_columns.astype(F32), dmod_all, precision=lax.Precision.HIGHEST
    )
    blocks = blocks.reshape(UNITS, 2, 4, LAYERS, SLAB, PART)
    flat_a, flat_up = [blocks[u].transpose(2, 0, 3, 1, 4).reshape(D, FF) for u in (0, 1)]
    flat_down = blocks[2].transpose(2, 0, 1, 3, 4)
    flat = [flat_a[:, : 3 * D], flat_a[:, 3 * D :], flat_up, flat_down]
    shares = []
    for grad in flat:
        summed = lax.psum(grad.reshape(-1), "grp").astype(F32)
        shares.append(lax.psum_scatter(summed, "dp", scatter_dimension=0, tiled=True))
    shares = shares + [ada_grad.reshape(-1), bias_grad]
    local_square = sum((jnp.sum(piece * piece) for piece in shares))
    grad_norm = jnp.sqrt(lax.psum(local_square, "dp"))
    clip = grad_limit / jnp.maximum(grad_norm, grad_limit)
    decays = [0.1, 0.1, 0.1, 0.1, 0.1, 0.0]
    results = [
        adam(master, first, second, grad * clip, decay)
        for master, first, second, grad, decay in zip(masters, firsts, seconds, shares, decays)
    ]
    news, first_news, second_news = zip(*results)
    return (grad_norm, *news, *first_news, *second_news, *(new.astype(BF) for new in news))


def per_device(
    inputs,
    cotangent,
    group_interval,
    sample_counts,
    rollout_start,
    lead_table,
    *state,
):
    masters, firsts, seconds = (state[0:6], state[6:12], state[12:18])
    fits = (
        lax.axis_size("dp") == 2 * LAYERS
        and lax.axis_size("grp") == GROUPS
        and inputs.shape[0] == 1024
    )
    if not fits:
        wa, wup, wdown, rows, owner_columns = plain_gather(
            group_interval, sample_counts, rollout_start, lead_table, masters
        )
        result, input_grad, blocks, vec = block_alone(inputs, cotangent, rows, wa, wup, wdown)
        rest = plain_update(owner_columns, vec, blocks, masters, firsts, seconds)
        return (result, input_grad, *rest)
    result, input_grad, pieces, ada_grad, bias_sum, square = block_together(
        inputs, cotangent, rollout_start, group_interval, sample_counts, lead_table, masters
    )
    return finish(
        result, input_grad, pieces, ada_grad, bias_sum, square, masters, firsts, seconds
    )


def solution(mesh):
    rows = P(("grp", "dp"), None)
    return jax.shard_map(
        per_device,
        mesh=mesh,
        in_specs=(rows, rows, P(), P(), P(), P(), *[P("dp")] * 18),
        out_specs=(rows, rows, P(), *[P("dp")] * 24),
        check_vma=False,
    )
```

```python
import functools
import math

import jax
import jax.numpy as jnp
from jax import lax
from jax.experimental import pallas as pl
from jax.experimental.pallas import tpu as pltpu
from jax.sharding import PartitionSpec as P

D = 384
HEADS = 6
FF = 1536
ROLLOUT = 2
INTERVALS = 3
ADAM_STEP = 10
HEAD_DIM = 64
NPARAM = 2659584

norm_eps = 1e-06
learn_rate = 0.05
adam_eps = 1e-08

BF = jnp.bfloat16
F32 = jnp.float32
NN = (((1,), (0,)), ((), ()))
NT = (((1,), (1,)), ((), ()))
TN = (((0,), (0,)), ((), ()))

ROWS = 256
SLAB = 48
PART = 384
ROW_SHARE = 6
ROW_BQKV, ROW_BPROJ, ROW_BUP, ROW_BDOWN = 16, 19, 20, 24
SHIFT1, SCALE1, GATE1, SHIFT2, SCALE2, GATE2 = range(6)


def dot(left, right, dims=NN):
    return lax.dot_general(left, right, dims, preferred_element_type=F32)


def layer_norm(stream):
    centred = stream - jnp.mean(stream, axis=-1, keepdims=True)
    inverse = lax.rsqrt(jnp.mean(centred * centred, axis=-1, keepdims=True) + norm_eps)
    return (centred * inverse, inverse)


def norm_back(normed, inverse, grad_out):
    mean_grad = jnp.mean(grad_out, axis=-1, keepdims=True)
    mean_prod = jnp.mean(grad_out * normed, axis=-1, keepdims=True)
    return inverse * (grad_out - mean_grad - normed * mean_prod)


def col_sum(value):
    return jnp.sum(value, axis=0, keepdims=True)


def modulated(normed, mods, scale_row, shift_row):
    return (normed * (1.0 + mods(scale_row)) + mods(shift_row)).astype(BF)


def mod_reader(mod_ref, step):
    return lambda row: mod_ref[pl.ds(8 * step + row, 1), :]


def gelu_pair(value):
    cdf = 0.5 + 0.5 * lax.erf(value * (2.0**-0.5))
    density = jnp.exp(-0.5 * value * value) * (1.0 / math.sqrt(2.0 * math.pi))
    return (value * cdf, cdf + value * density)


def side_by_side(ref, first, count):
    return jnp.concatenate([ref[row : row + 1, :] for row in range(first, first + count)], axis=1)


def first_rows(x, rows_ref, wa_ref):
    normed, _ = layer_norm(x.astype(F32))
    hidden = modulated(normed, mod_reader(rows_ref, 0), SCALE1, SHIFT1)
    qkv = dot(hidden, wa_ref[:, : 3 * D]) + side_by_side(rows_ref, ROW_BQKV, 3)
    return qkv.astype(BF)


def middle_rows(
    x_ref, att_ref, rows_ref, wa_ref, wup_ref, wdown_ref,
    a_refs, gp_ref, act_refs, f_ref, next_ref, qkv_ref,
):
    mods = mod_reader(rows_ref, 0)
    later = mod_reader(rows_ref, 1)
    branch = dot(att_ref[...], wa_ref[:, 3 * D :]) + mods(ROW_BPROJ)
    for part, ref in enumerate(a_refs):
        ref[...] = branch[:, 128 * part : 128 * (part + 1)]
    middle = x_ref[...].astype(F32) + mods(GATE1) * branch
    normed, _ = layer_norm(middle)
    hidden = modulated(normed, mods, SCALE2, SHIFT2)
    upward = dot(hidden, wup_ref[...]) + side_by_side(rows_ref, ROW_BUP, 4)
    act, slope = gelu_pair(upward)
    gp_ref[...] = slope
    act = act.astype(BF)
    for part, ref in enumerate(act_refs):
        ref[...] = act[:, PART * part : PART * (part + 1)]
    branch = dot(act, wdown_ref[...]) + mods(ROW_BDOWN)
    f_ref[...] = branch
    stream = middle + mods(GATE2) * branch
    next_ref[...] = stream
    normed, _ = layer_norm(stream)
    hidden = modulated(normed, later, SCALE1, SHIFT1)
    qkv = dot(hidden, wa_ref[:, : 3 * D]) + side_by_side(rows_ref, ROW_BQKV, 3)
    qkv_ref[...] = qkv.astype(BF)


def ffn_back(
    mods, grad, branch_two, act, slope, hidden, wdown_ref, gdown_ref, gup_ref, wide_ref, narrow_ref
):
    df = (mods(GATE2) * grad).astype(BF)
    narrow_ref[pl.ds(GATE2, 1), :] += col_sum(grad * branch_two)
    narrow_ref[pl.ds(7, 1), :] += col_sum(df.astype(F32))
    gdown_ref[...] += dot(act, df, TN)
    dact = dot(df, wdown_ref[...], NT)
    du = (dact * slope).astype(BF)
    wide_ref[pl.ds(0, 1), :] += col_sum(du.astype(F32))
    gup_ref[...] += dot(hidden, du, TN)
    return du


def middle_back(
    mods, grad, du, normed, inverse, branch_one, att, wa_ref, wup_ref, gproj_ref, narrow_ref,
    dmid_ref, datt_ref,
):
    dh = dot(du, wup_ref[...], NT)
    narrow_ref[pl.ds(SHIFT2, 1), :] += col_sum(dh)
    narrow_ref[pl.ds(SCALE2, 1), :] += col_sum(dh * normed)
    dmid = grad + norm_back(normed, inverse, dh * (1.0 + mods(SCALE2)))
    dmid_ref[...] = dmid
    da = (mods(GATE1) * dmid).astype(BF)
    narrow_ref[pl.ds(GATE1, 1), :] += col_sum(dmid * branch_one)
    narrow_ref[pl.ds(6, 1), :] += col_sum(da.astype(F32))
    gproj_ref[...] += dot(att, da, TN)
    datt_ref[...] = dot(da, wa_ref[:, 3 * D :], NT).astype(BF)


def turn_rows(
    x_ref, att_ref, cot_ref, rows_ref, wa_ref, wup_ref, wdown_ref,
    out_ref, dmid_ref, datt_ref, gdown_ref, gup_ref, gproj_ref, wide_ref, narrow_ref,
):
    mods = mod_reader(rows_ref, 1)
    shared = mod_reader(rows_ref, 0)
    att = att_ref[...]
    branch_one = dot(att, wa_ref[:, 3 * D :]) + shared(ROW_BPROJ)
    middle = x_ref[...] + mods(GATE1) * branch_one
    normed, inverse = layer_norm(middle)
    hidden = modulated(normed, mods, SCALE2, SHIFT2)
    upward = dot(hidden, wup_ref[...]) + side_by_side(rows_ref, ROW_BUP, 4)
    act, slope = gelu_pair(upward)
    act = act.astype(BF)
    branch_two = dot(act, wdown_ref[...]) + shared(ROW_BDOWN)
    out_ref[...] = middle + mods(GATE2) * branch_two
    grad = cot_ref[...].astype(F32)
    du = ffn_back(
        mods, grad, branch_two, act, slope, hidden, wdown_ref, gdown_ref, gup_ref, wide_ref, narrow_ref
    )
    middle_back(
        mods, grad, du, normed, inverse, branch_one, att, wa_ref, wup_ref, gproj_ref, narrow_ref,
        dmid_ref, datt_ref,
    )


def qkv_back(mods, stream, dmid, dqkv, wa_ref, narrow_ref, bias_ref, gqkv_ref=None):
    normed, inverse = layer_norm(stream)
    bias_ref[pl.ds(0, 1), :] += col_sum(dqkv.astype(F32))
    if gqkv_ref is not None:
        gqkv_ref[...] += dot(modulated(normed, mods, SCALE1, SHIFT1), dqkv, TN)
    dh = dot(dqkv, wa_ref[:, : 3 * D], NT)
    narrow_ref[pl.ds(SHIFT1, 1), :] += col_sum(dh)
    narrow_ref[pl.ds(SCALE1, 1), :] += col_sum(dh * normed)
    return dmid + norm_back(normed, inverse, dh * (1.0 + mods(SCALE1)))


def middle_again(mods, x_ref, a_refs):
    branch_one = jnp.concatenate([ref[...] for ref in a_refs], axis=1)
    normed, inverse = layer_norm(x_ref[...].astype(F32) + mods(GATE1) * branch_one)
    return (branch_one, normed, inverse)


def join_rows(
    dqkv_ref, x1_ref, x0_ref, a_refs, gp_ref, act_refs, f_ref, rows_ref, wa_ref, wdown_ref,
    hidden_ref, dmid_ref, gqkv_ref, gdown_ref, gup_ref, wide_ref, narrow1_ref, narrow_ref, bias_ref,
):
    grad = qkv_back(
        mod_reader(rows_ref, 1), x1_ref[...], dmid_ref[...], dqkv_ref[...], wa_ref,
        narrow1_ref, bias_ref, gqkv_ref,
    )
    dmid_ref[...] = grad
    mods = mod_reader(rows_ref, 0)
    normed, _ = layer_norm(x0_ref[...].astype(F32))
    hidden_ref[...] = modulated(normed, mods, SCALE1, SHIFT1)
    _, normed, _ = middle_again(mods, x0_ref, a_refs)
    act = jnp.concatenate([ref[...] for ref in act_refs], axis=1)
    du = ffn_back(
        mods, grad, f_ref[...], act, gp_ref[...], modulated(normed, mods, SCALE2, SHIFT2),
        wdown_ref, gdown_ref, gup_ref, wide_ref, narrow_ref,
    )
    for part, ref in enumerate(act_refs):
        ref[...] = du[:, PART * part : PART * (part + 1)]


def join_middle_rows(
    x0_ref, a_refs, du_refs, att_ref, rows_ref, wa_ref, wup_ref,
    dmid_ref, datt_ref, gproj_ref, narrow_ref,
):
    mods = mod_reader(rows_ref, 0)
    branch_one, normed, inverse = middle_again(mods, x0_ref, a_refs)
    du = jnp.concatenate([ref[...] for ref in du_refs], axis=1)
    middle_back(
        mods, dmid_ref[...], du, normed, inverse, branch_one, att_ref[...], wa_ref, wup_ref,
        gproj_ref, narrow_ref, dmid_ref, datt_ref,
    )


def head_lanes(rows):
    lane = lax.broadcasted_iota(jnp.int32, (rows, 2 * HEAD_DIM), 1)
    return (lane < HEAD_DIM, lane >= HEAD_DIM)


def turned_heads(rows_f32, out_ref):
    turned = jnp.transpose(rows_f32)
    row = lax.broadcasted_iota(jnp.int32, turned.shape, 0)
    out_ref[0] = jnp.where(row < HEAD_DIM, turned, 0.0).astype(BF)
    out_ref[1] = jnp.where(row >= HEAD_DIM, turned, 0.0).astype(BF)


score_scale = HEAD_DIM**-0.5


def attend_pair(q, k_ref, v, o_ref, p_ref, vt_ref):
    turned_heads(v.astype(F32), vt_ref)
    queries = q * BF(score_scale)
    mixed = None
    for half, lanes in enumerate(head_lanes(queries.shape[0])):
        scores = dot(k_ref[...], jnp.where(lanes, queries, BF(0)), NT)
        top = jnp.max(scores, axis=0, keepdims=True)
        weights = jnp.exp(scores - top)
        total = jnp.sum(weights, axis=0, keepdims=True)
        low = (weights * (1.0 / total)).astype(BF)
        p_ref[half] = low
        part = dot(vt_ref[half], low)
        mixed = part if mixed is None else mixed + part
    o_ref[...] = jnp.transpose(mixed).astype(BF)


def attend_back_pair(q, k, v_ref, grads, p_ref, dq_ref, dk_ref, dv_ref, kt_ref, between):
    turned_heads(k.astype(F32) * score_scale, kt_ref)
    queries = q * BF(score_scale)
    own_lanes = head_lanes(queries.shape[0])
    for half, lanes in enumerate(own_lanes):
        grad = jnp.where(lanes, grads, BF(0))
        query = jnp.where(lanes, queries, BF(0))
        low = p_ref[half]
        weight_grad = dot(v_ref[...], grad, NT)
        weights = low.astype(F32)
        delta = jnp.sum(weights * weight_grad, axis=0, keepdims=True)
        score_grad = (weights * (weight_grad - delta)).astype(BF)
        news = (
            jnp.transpose(dot(kt_ref[half], score_grad)), dot(score_grad, query), dot(low, grad)
        )
        for ref, new in zip((dq_ref, dk_ref, dv_ref), news):
            new = new.astype(BF)
            ref[...] = new if half == 0 else jnp.where(lanes, new, ref[...])
        if half == 0 and between is not None:
            between()


class Refs:
    def __init__(self, names, refs):
        for name, ref in zip(names, refs, strict=True):
            setattr(self, name, ref)

MESH_ID = pl.DeviceIdType.MESH
GROUPS = 4
LAYERS = 4
UNITS = 3
HALF = 768


class Place:
    def __init__(self):
        self.grp = lax.axis_index("grp")
        self.dp = lax.axis_index("dp")
        self.z = self.dp // 2
        self.core = self.dp % 2

    def sibling(self):
        return (self.grp, 2 * self.z + 1 - self.core)

    def along_grp(self, step):
        return (lax.rem(self.grp + step, GROUPS), self.dp)

    def along_z(self, step):
        return (self.grp, 2 * lax.rem(self.z + step, LAYERS) + self.core)

    def across(self, step):
        return (self.grp, 2 * lax.rem(self.z + step, LAYERS) + 1 - self.core)


def greet(peers):
    barrier = pltpu.get_barrier_semaphore()
    for peer in peers:
        pl.semaphore_signal(barrier, inc=1, device_id=peer, device_id_type=MESH_ID)
    return lambda: pl.semaphore_wait(barrier, len(peers))


def remote(src, dst, sems, index, peer):
    send_sem, recv_sem = sems
    return pltpu.make_async_remote_copy(
        src_ref=src, dst_ref=dst, send_sem=send_sem.at[index], recv_sem=recv_sem.at[index],
        device_id=peer, device_id_type=MESH_ID,
    )


def condition_rows(moments, intervals, lead_ref):
    shape = (8, D)
    row = lax.broadcasted_iota(jnp.int32, shape, 0)
    lane = lax.broadcasted_iota(jnp.int32, shape, 1)
    moment = jnp.zeros(shape, F32)
    chosen = jnp.zeros(shape, jnp.int32)
    for index, (value, interval) in enumerate(zip(moments, intervals)):
        moment = jnp.where(row == index, value.astype(F32), moment)
        chosen = jnp.where(row == index, interval, chosen)
    lead = jnp.zeros(shape, F32)
    for choice in range(INTERVALS):
        picked = jnp.broadcast_to(lead_ref[choice : choice + 1, :], shape)
        lead = jnp.where(chosen == choice, picked, lead)
    half_width = D // 2
    place = jnp.where(lane < half_width, lane, lane - half_width).astype(F32)
    angles = moment * jnp.exp(place * (-math.log(10000.0) / half_width))
    wave = jnp.where(lane < half_width, jnp.sin(angles), jnp.cos(angles))
    condition = lead + wave
    return (condition / (1.0 + jnp.exp(-condition))).astype(BF).astype(F32)


def span(start, size):
    return pl.ds(pl.multiple_of(start, SLAB), size)


def local(src, dst, sem):
    made = pltpu.make_async_copy(src, dst, sem)
    made.start()
    return made


def clear_sums(r):
    def clear(i, carry):
        for ref in (r.gqkv, r.gproj, r.gup, r.gdown):
            size = ref.shape[0] // 8
            ref[span(i * size, size), :] = jnp.zeros((size, ref.shape[1]), F32)
        return carry

    lax.fori_loop(0, 8, clear, 0)
    for ref in (r.wide, r.narrow0, r.narrow1, r.bias):
        ref[...] = jnp.zeros_like(ref)


class Alone:
    def __init__(self, refs):
        self.refs = refs

    def begin(self):
        r = self.refs
        sems = r.in_sems
        first = [local(r.wa_far, r.wa, sems.at[0]), local(r.rows_far, r.rows, sems.at[3])]
        self.later = [local(r.wup_far, r.wup, sems.at[1]), local(r.wdown_far, r.wdown, sems.at[2])]
        clear_sums(r)
        for made in first:
            made.wait()

    def after_first(self):
        pass

    def after_attend_pair(self, h):
        pass

    def before_middle(self):
        for made in self.later:
            made.wait()

    def before_join(self):
        pass

    def amid_join(self):
        fill_blocks(self.refs)

    def after_join(self):
        pass

    def amid_back_pair(self, h):
        pass

    def after_back_pair(self, h):
        fill_pair(self.refs, h)

    def after_last_rows(self, i):
        pass

    def after_last(self):
        r = self.refs
        fill_vec(r)
        fill_late(r, r.late)
        r.vec[0:6, :] = r.late[0:6, :]
        r.vec[VEC_STEP : VEC_STEP + 6, :] = r.late[6:12, :]
        puts = [local(r.blocks, r.blocks_far, r.in_sems.at[0]), local(r.vec, r.vec_far, r.in_sems.at[1])]
        for made in puts:
            made.wait()


def block_rows(owner, part):
    first = HALF * (owner % 2) + 4 * SLAB * part + SLAB * (owner // 2)
    return slice(first, first + SLAB)


def fill_blocks(refs):
    share = refs.rows[ROW_SHARE : ROW_SHARE + 1, :]

    def owner(d, carry):
        for g in range(4):
            there = span(HALF * (d % 2) + 4 * SLAB * g + SLAB * (d // 2), SLAB)
            up = refs.gup[span(SLAB * d, SLAB), PART * g : PART * (g + 1)]
            down = refs.gdown[span(SLAB * (4 * d + g), SLAB), :]
            refs.blocks[1, there, :] = (up * share).astype(BF)
            refs.blocks[2, there, :] = (down * share).astype(BF)
        return carry

    lax.fori_loop(0, 8, owner, 0)


def fill_pair(refs, h):
    share = refs.rows[ROW_SHARE : ROW_SHARE + 1, 0:128]
    columns = [pl.ds(pl.multiple_of(D * g + 128 * h, 128), 128) for g in range(3)]
    grads = jnp.concatenate([refs.dqkv[:, column] for column in columns], axis=1)
    value = dot(refs.att1[...], grads, TN)
    for d in range(8):
        own = slice(SLAB * d, SLAB * (d + 1))
        for g in range(3):
            part = value[own, 128 * g : 128 * (g + 1)] + refs.gqkv[own, columns[g]]
            refs.blocks[0, block_rows(d, g), columns[0]] = (part * share).astype(BF)
        part = refs.gproj[own, columns[0]]
        refs.blocks[0, block_rows(d, 3), columns[0]] = (part * share).astype(BF)


VEC = 72
VEC_STEP = 24


def fill_vec(refs):
    share = refs.rows[ROW_SHARE : ROW_SHARE + 1, 0:128]

    def put(first_row, value):
        for j in range(value.shape[1] // 128):
            refs.vec[first_row + j : first_row + j + 1, :] = value[:, 128 * j : 128 * j + 128] * share

    refs.vec[...] = jnp.zeros_like(refs.vec)
    wide, narrow0, narrow1 = (refs.wide, refs.narrow0, refs.narrow1)
    put(6, narrow0[6:7, :] + narrow1[6:7, :])
    put(9, wide[0:1, :])
    put(21, narrow0[7:8, :] + narrow1[7:8, :])
    for r in range(6):
        if r > 1:
            put(VEC_STEP + 3 * r, narrow0[r : r + 1, :])
        put(2 * VEC_STEP + 3 * r, narrow1[r : r + 1, :])


def fill_late(refs, late_ref):
    share = refs.rows[ROW_SHARE : ROW_SHARE + 1, 0:128]
    rest = (refs.bias[0:1, :D], refs.bias[0:1, 2 * D :], refs.narrow0[0:1, :], refs.narrow0[1:2, :])
    for index, value in enumerate(rest):
        for j in range(3):
            row = 3 * index + j
            late_ref[row : row + 1, :] = value[:, 128 * j : 128 * j + 128] * share
    late_ref[12:16, :] = jnp.zeros((4, 128), F32)


class Together:
    steps = range(1, 4)

    def __init__(self, refs):
        self.refs = refs
        self.at = Place()

    def start(self, copy):
        copy.start()


    def whole(self, unit):
        return (self.refs.wa, self.refs.wup, self.refs.wdown)[unit]

    def part(self, unit, owner, grp):
        if unit == 2:
            return self.whole(2).at[span(4 * SLAB * owner + SLAB * grp, SLAB), :]
        return self.whole(unit).at[
            span(SLAB * owner, SLAB), pl.ds(pl.multiple_of(PART * grp, 128), PART)
        ]

    def slab(self, unit, owner):
        if unit == 2:
            return self.whole(2).at[span(4 * SLAB * owner, 4 * SLAB), :]
        return self.whole(unit).at[span(SLAB * owner, SLAB), :]

    def owner(self, k):
        return 2 * lax.rem(self.at.z + LAYERS - k, LAYERS) + self.at.core

    def gather_z(self, unit, k):
        own = self.part(unit, self.at.dp, self.at.grp)
        return remote(own, own, self.refs.gz, (unit, k - 1), self.at.along_z(k))

    def gather_grp(self, unit, k, m):
        part = self.part(unit, self.owner(k), self.at.grp)
        return remote(part, part, self.refs.gx, (unit, k - 1, m - 1), self.at.along_grp(m))

    def gather_sibling(self, unit, k):
        slab = self.slab(unit, self.owner(k) if k else self.at.dp)
        return remote(slab, slab, self.refs.gs, (unit, k), self.at.sibling())

    def launch(self, unit):
        for k in self.steps:
            self.start(self.gather_z(unit, k))
        self.start(self.gather_sibling(unit, 0))

    def forward_grp(self, unit):
        for k in self.steps:
            self.gather_z(unit, k).wait_recv()
            for m in self.steps:
                self.start(self.gather_grp(unit, k, m))

    def forward_sibling(self, unit):
        for k in self.steps:
            for m in self.steps:
                self.gather_grp(unit, k, m).wait_recv()
            self.start(self.gather_sibling(unit, k))

    def finish_sibling(self, unit):
        for k in range(4):
            self.gather_sibling(unit, k).wait_recv()

    def small(self, index):
        r, at = (self.refs, self.at)
        if index == 0:
            return remote(r.part_own, r.part_sib, r.gm, 0, at.sibling())
        if index == 1:
            own = r.bias_slot.at[at.z, at.core]
            return remote(own, own, r.gm, 1, at.sibling())
        if index < 5:
            own = r.part_z.at[at.z]
            return remote(own, own, r.gm, index, at.along_z(index - 1))
        own = r.bias_slot.at[at.z]
        return remote(own, own, r.gm, index, at.along_z(index - 4))

    def begin(self):
        r, at, steps = (self.refs, self.at, self.steps)
        stage = {
            "qkv": r.a.at[0:432], "proj": r.a.at[432:576], "ada": r.a.at[1728:2592],
            "up": r.a.at[576:1152], "down": r.a.at[1152:1728],
        }
        loads = {
            name: local(r.masters[name], stage[name], r.in_sems.at[index])
            for index, name in enumerate(stage)
        }
        ready = greet([self.everywhere(step) for step in range(1, 8 * LAYERS)])

        def fill(unit, source, count, offset, first=0):
            for j in range(count):
                value = source[pl.ds(first + j, SLAB, stride=count), :].astype(BF)
                where = offset + 128 * j
                if unit == 2:
                    rows = span(4 * SLAB * at.dp + offset, SLAB)
                    where = 128 * j
                else:
                    rows = span(SLAB * at.dp, SLAB)
                self.whole(unit)[rows, where : where + 128] = value

        loads["qkv"].wait()
        fill(0, stage["qkv"], 9, 0)
        loads["proj"].wait()
        fill(0, stage["proj"], 3, 3 * D)
        ready()
        self.launch(0)

        moment, interval = (r.start[at.grp], r.interval[at.grp])
        r.cond_t[...] = jnp.transpose(
            condition_rows([moment + s for s in range(ROLLOUT)], [interval] * ROLLOUT, r.lead)
        )
        own_cond = r.cond_t[span(SLAB * at.dp, SLAB), :]
        columns = [jnp.broadcast_to(own_cond[:, s : s + 1], (SLAB, 128)) for s in range(ROLLOUT)]
        loads["ada"].wait()
        for j in range(18):
            rows = stage["ada"][pl.ds(j, SLAB, stride=18), :].astype(BF).astype(F32)
            for s in range(ROLLOUT):
                r.part_own[18 * s + j : 18 * s + j + 1, :] = col_sum(rows * columns[s])
        r.part_own[36:40, :] = jnp.zeros((4, 128), F32)
        r.bias_own[...] = jnp.zeros((8, 128), F32)
        for i in range(6):
            size = 128 if i < 5 else 32
            r.bias_own[i : i + 1, 0:size] = r.bias_flat[pl.ds(128 * i, size)].reshape(1, size)
        lane = lax.broadcasted_iota(jnp.int32, (8, 128), 1)
        shift = lax.rem(32 * at.dp, 128)
        turned = pltpu.roll(r.bias_own[...].astype(BF).astype(F32), shift, axis=1)
        above = pltpu.roll(turned, 1, axis=0)
        r.bias_slot[at.z, at.core] = jnp.where(lane >= shift, turned, above)
        self.start(self.small(0))
        self.start(self.small(1))

        loads["up"].wait()
        fill(1, stage["up"], 12, 0)
        loads["down"].wait()
        for g in range(GROUPS):
            fill(2, stage["down"], 3, SLAB * g, 3 * SLAB * g)

        clear_sums(r)
        self.small(0).wait_recv()
        self.small(1).wait_recv()
        r.part_z[at.z] = r.part_own[...] + r.part_sib[...]
        for index in range(2, 8):
            self.start(self.small(index))
        self.forward_grp(0)
        self.launch(1)
        self.launch(2)

        for index in range(2, 8):
            self.small(index).wait_recv()
        total = r.part_z[0] + r.part_z[1] + r.part_z[2] + r.part_z[3]
        r.bias_full[...] = jnp.zeros_like(r.bias_full)
        for d in range(2 * LAYERS):
            first = 672 * d // 128
            r.bias_full[first : first + 7, :] += r.bias_slot[d // 2, d % 2, 0:7, :]
        counts = [r.counts[g].astype(F32) for g in range(GROUPS)]
        own_count = r.counts[at.grp].astype(F32)
        share = jnp.full((1, D), GROUPS * own_count) / jnp.full((1, D), sum(counts[1:], counts[0]))

        def put(row, value):
            r.rows[row : row + 1, :] = value

        def joined(first):
            return jnp.concatenate(
                [r.bias_full[first + j : first + j + 1, :] for j in range(3)], axis=1
            )

        for s in range(ROLLOUT):
            for row in range(6):
                first = 18 * s + 3 * row
                mod = jnp.concatenate([total[first + j : first + j + 1, :] for j in range(3)], axis=1)
                put(8 * s + row, mod + joined(24 + 3 * row))
            put(8 * s + 6, share)
            put(8 * s + 7, share)
        put(ROW_BQKV, joined(0))
        put(ROW_BQKV + 1, jnp.zeros((1, D), F32))
        put(ROW_BQKV + 2, joined(3))
        put(ROW_BPROJ, joined(6))
        for j in range(4):
            put(ROW_BUP + j, joined(9 + 3 * j))
        put(ROW_BDOWN, joined(21))
        r.rows[25:32, :] = jnp.zeros((7, D), F32)
        self.forward_sibling(0)
        self.finish_sibling(0)

    def after_first(self):
        self.forward_grp(1)

    def after_attend_pair(self, h):
        @pl.when(h == 0)
        def _():
            self.forward_grp(2)

        @pl.when(h == 1)
        def _():
            self.forward_sibling(1)

    def before_middle(self):
        self.forward_sibling(2)
        self.finish_sibling(1)
        self.finish_sibling(2)


    x_first = {3: True, 4: False}

    def columns(self, unit):
        return pl.ds(128 * unit, 128) if unit < 3 else slice(None)

    def got(self, unit, name):
        first = {"sib": 0, "piece": HALF, "grp": 0, "one": 0, "two": 8 * SLAB, "z": 12 * SLAB}[name]
        size = {"sib": HALF, "piece": 4 * SLAB, "grp": 12 * SLAB, "one": 8 * SLAB, "two": 4 * SLAB, "z": 3 * SLAB}[name]
        r, rows = (self.refs, slice(first, first + size))
        if unit < 3:
            return (r.att0 if name in ("sib", "piece") else r.act).at[rows, self.columns(unit)]
        if name in ("sib", "piece"):
            third = 0 if unit == 3 else 1
            return r.qkv1.at[rows, D * third : D * (third + 1)]
        return r.cot.at[rows] if unit == 3 else r.qkv1.at[rows, 2 * D : 3 * D]

    def half(self, unit, core):
        block = max(unit - 2, 0)
        return self.refs.blocks.at[block, span(HALF * core, HALF), self.columns(unit)]

    def parts(self, unit, part, count=1):
        return self.half(unit, self.at.core).at[span(4 * SLAB * part, 4 * SLAB * count), :]

    def sum_sibling(self, unit):
        src = self.half(unit, 1 - self.at.core)
        return remote(src, self.got(unit, "sib"), self.refs.rs, unit, self.at.sibling())

    def grp_peer(self, along_x):
        x, y = (self.at.grp % 2, self.at.grp // 2)
        grp = 2 * y + 1 - x if along_x else 2 * (1 - y) + x
        return (grp, self.at.dp)

    def stage_parts(self, unit, own):
        x, y = (self.at.grp % 2, self.at.grp // 2)
        if self.x_first[unit]:
            return [2 * j + (x if own else 1 - x) for j in range(2)]
        return [2 * (y if own else 1 - y) + j for j in range(2)]

    def sum_one(self, unit, j):
        src = self.parts(unit, self.stage_parts(unit, False)[j])
        dst = self.got(unit, "one").at[4 * SLAB * j : 4 * SLAB * (j + 1)]
        return remote(src, dst, self.refs.rx, (unit, j), self.grp_peer(self.x_first[unit]))

    def sum_two(self, unit):
        peer = self.grp_peer(not self.x_first[unit])
        return remote(self.parts(unit, peer[0]), self.got(unit, "two"), self.refs.rx, (unit, 2), peer)

    def sum_grp(self, unit, k):
        peer = self.at.along_grp(k)
        first = 4 * SLAB * (k - 1)
        dst = self.got(unit, "grp").at[first : first + 4 * SLAB]
        return remote(self.parts(unit, peer[0]), dst, self.refs.rx, (unit, k - 1), peer)

    def own_part(self, unit):
        return self.parts(unit, self.at.grp)

    def sum_z(self, unit, k):
        there = lax.rem(self.at.z + k, LAYERS)
        src = self.own_part(unit).at[span(SLAB * there, SLAB), :]
        dst = self.got(unit, "z").at[SLAB * (k - 1) : SLAB * k]
        return remote(src, dst, self.refs.rz, (unit, k - 1), self.at.along_z(k))

    def share_piece(self, unit, k):
        own = self.got(unit, "piece").at[span(SLAB * self.at.grp, SLAB), :]
        return remote(own, own, self.refs.ra, (unit, k - 1), self.at.along_grp(k))

    def add(self, mine, got, count):
        def step(i, carry):
            rows = span(SLAB * i, SLAB)
            mine[rows, :] = (mine[rows, :].astype(F32) + got[rows, :].astype(F32)).astype(BF)
            return carry

        lax.fori_loop(0, count, step, 0)

    def add_sibling(self, unit):
        self.sum_sibling(unit).wait_recv()
        self.add(self.half(unit, self.at.core), self.got(unit, "sib"), 16)
        if unit < 3:
            for k in self.steps:
                self.start(self.sum_grp(unit, k))
        else:
            for j in range(2):
                self.start(self.sum_one(unit, j))

    def add_grp(self, unit):
        for k in self.steps:
            self.sum_grp(unit, k).wait_recv()
        mine, got = (self.own_part(unit), self.got(unit, "grp"))

        def step(i, carry):
            rows = span(SLAB * i, SLAB)
            value = mine[rows, :].astype(F32)
            for k in self.steps:
                value = value + got[span(SLAB * (i + 4 * (k - 1)), SLAB), :].astype(F32)
            mine[rows, :] = value.astype(BF)
            return carry

        lax.fori_loop(0, 4, step, 0)
        for k in self.steps:
            self.start(self.sum_z(unit, k))

    def add_one(self, unit):
        for j in range(2):
            self.sum_one(unit, j).wait_recv()
            got = self.got(unit, "one").at[4 * SLAB * j : 4 * SLAB * (j + 1)]
            self.add(self.parts(unit, self.stage_parts(unit, True)[j]), got, 4)
        self.start(self.sum_two(unit))

    def add_two(self, unit):
        self.sum_two(unit).wait_recv()
        self.add(self.own_part(unit), self.got(unit, "two"), 4)
        for k in self.steps:
            self.start(self.sum_z(unit, k))

    def add_z(self, unit):
        for k in self.steps:
            self.sum_z(unit, k).wait_recv()
        value = self.own_part(unit)[span(SLAB * self.at.z, SLAB), :].astype(F32)
        for k in self.steps:
            value = value + self.got(unit, "z")[SLAB * (k - 1) : SLAB * k, :].astype(F32)
        value = value.astype(BF)
        self.got(unit, "piece")[span(SLAB * self.at.grp, SLAB), :] = value
        for k in self.steps:
            self.start(self.share_piece(unit, k))
        value = value.astype(F32)
        squares = col_sum(value * value)
        if unit < 3:
            return squares
        return squares[:, 0:128] + squares[:, 128:256] + squares[:, 256:384]

    def tell(self, sem):
        at = self.at
        for peer in (
            [at.sibling()]
            + [at.along_grp(k) for k in self.steps]
            + [at.along_z(k) for k in self.steps]
        ):
            pl.semaphore_signal(sem, inc=1, device_id=peer, device_id_type=MESH_ID)

    def before_join(self):
        self.tell(self.refs.turned_back)

    def amid_join(self):
        fill_blocks(self.refs)
        pl.semaphore_wait(self.refs.turned_back, 7)
        self.start(self.sum_sibling(3))
        self.start(self.sum_sibling(4))

    def after_join(self):
        r = self.refs
        self.tell(r.joined)
        self.add_sibling(3)
        self.add_sibling(4)
        fill_vec(r)
        self.start(self.small_sum(0))

    def amid_back_pair(self, h):
        r, at = (self.refs, self.at)

        @pl.when(h == 0)
        def _():
            self.small_sum(0).wait_recv()
            r.vec_z[at.z] = r.vec[...] + r.vec_sib[...]
            for index in self.steps:
                self.start(self.small_sum(index))

        @pl.when(h == 1)
        def _():
            self.add_one(3)
            self.add_one(4)
            self.add_sibling(0)
            for index in self.steps:
                self.small_sum(index).wait_recv()
            r.vec_g[at.grp] = r.vec_z[0] + r.vec_z[1] + r.vec_z[2] + r.vec_z[3]
            for index in self.steps:
                self.start(self.small_sum(3 + index))

        @pl.when(h == 2)
        def _():
            self.add_two(3)
            self.add_two(4)
            self.add_sibling(1)
            self.add_grp(0)

    def after_back_pair(self, h):
        r = self.refs
        fill_pair(r, h)

        @pl.when(h == 0)
        def _():
            pl.semaphore_wait(r.joined, 7)
            self.start(self.sum_sibling(0))

        @pl.when(h == 1)
        def _():
            self.start(self.sum_sibling(1))

        @pl.when(h == 2)
        def _():
            self.start(self.sum_sibling(2))

    def after_last_rows(self, i):
        @pl.when(i == 0)
        def _():
            self.add_sibling(2)

        @pl.when(i == 2)
        def _():
            self.add_grp(1)

    def small_sum(self, index):
        r, at = (self.refs, self.at)
        if index == 0:
            return remote(r.vec, r.vec_sib, r.rv, 0, at.sibling())
        if index < 4:
            own = r.vec_z.at[at.z]
            return remote(own, own, r.rv, index, at.along_z(index))
        own = r.vec_g.at[at.grp]
        return remote(own, own, r.rv, index, at.along_grp(index - 3))

    def across_dp(self, index):
        at = self.at
        if index == 0:
            return at.sibling()
        return at.along_z(index) if index < 4 else at.across(index - 3)

    def everywhere(self, step):
        device = lax.rem(2 * LAYERS * self.at.grp + self.at.dp + step, 8 * LAYERS)
        return (device // (2 * LAYERS), lax.rem(device, 2 * LAYERS))

    def square_sum(self, step):
        own = self.refs.squares.at[2 * LAYERS * self.at.grp + self.at.dp]
        return remote(own, own, self.refs.rq, step, self.everywhere(step))

    def late_sum(self, index):
        r, at = (self.refs, self.at)
        if index < 7:
            own = r.late_d.at[at.dp]
            return remote(own, own, r.rl, index, self.across_dp(index))
        own = r.late_g.at[at.grp]
        return remote(own, own, r.rl, index, at.along_grp(index - 6))

    def ada_square(self):
        r = self.refs
        left = r.cond[...]
        right = [
            r.vec_sum[g, VEC_STEP * (s + 1) : VEC_STEP * (s + 2), :]
            for g in range(GROUPS)
            for s in range(ROLLOUT)
        ]
        total = jnp.zeros((VEC_STEP, 128), F32)
        for step, weight in ((0, 1.0), (1, 2.0), (2, 2.0), (3, 2.0), (4, 1.0)):
            moved = left if step == 0 else pltpu.roll(left, step, axis=0)
            products = jnp.sum(left * moved, axis=1, keepdims=True) * weight
            for k in range(8):
                total = total + products[k : k + 1, :] * (right[k] * right[(k - step) % 8])
        return col_sum(total)

    def after_last(self):
        r, at, steps = (self.refs, self.at, self.steps)
        fill_late(r, r.late_d.at[at.dp])
        for index in range(7):
            self.start(self.late_sum(index))
        moments = [r.start[g] + s for g in range(GROUPS) for s in range(ROLLOUT)]
        intervals = [r.interval[g] for g in range(GROUPS) for s in range(ROLLOUT)]
        r.cond[...] = condition_rows(moments, intervals, r.lead)
        self.add_grp(2)
        for index in range(7):
            self.late_sum(index).wait_recv()
        total = r.late_d[0]
        for d in range(1, 2 * LAYERS):
            total = total + r.late_d[d]
        r.late_g[at.grp] = total
        for index in range(7, 10):
            self.start(self.late_sum(index))
        square = self.add_z(0) + self.add_z(3) + self.add_z(4) + self.add_z(1)
        square = square + self.add_z(2)
        own = 2 * LAYERS * at.grp + at.dp
        r.squares[own] = square
        for k in range(1, 8 * LAYERS):
            self.start(self.square_sum(k))

        for index in steps:
            self.small_sum(3 + index).wait_recv()
        for index in range(7, 10):
            self.late_sum(index).wait_recv()
        vec = r.vec_sum
        vec[...] = r.vec_g[...]
        for g in range(GROUPS):
            vec[g, 0:6, :] = r.late_g[g, 0:6, :]
            vec[g, VEC_STEP : VEC_STEP + 6, :] = r.late_g[g, 6:12, :]
        vec_sum = vec[0] + vec[1] + vec[2] + vec[3]
        r.bias_out[0:24, :] = vec_sum[0:24]
        r.bias_out[24:48, :] = vec_sum[24:48] + vec_sum[48:72]
        ada_square = self.ada_square()

        r.cond_t[...] = jnp.transpose(r.cond[...])
        own_cond = r.cond_t[span(SLAB * at.dp, SLAB), :]
        columns = [jnp.broadcast_to(own_cond[:, k : k + 1], (SLAB, 128)) for k in range(8)]
        ada = r.a.at[0 : 18 * SLAB]

        def ada_tile(j, carry):
            tile = jnp.zeros((SLAB, 128), F32)
            for k in range(8):
                row = vec[k // ROLLOUT, pl.ds(VEC_STEP * (k % ROLLOUT + 1) + j, 1), :]
                tile = tile + columns[k] * row
            ada[pl.ds(j, SLAB, stride=18), :] = tile
            return carry

        lax.fori_loop(0, 18, ada_tile, 0)
        for unit in range(5):
            for k in steps:
                self.share_piece(unit, k).wait_recv()
        whole = [r.att0.at[HALF : HALF + 4 * SLAB], self.got(3, "piece"), self.got(4, "piece")]
        puts = [local(ada, r.ada_far, r.in_sems.at[0])]
        puts += [
            local(whole[unit], r.pieces_far.at[unit], r.in_sems.at[1 + unit])
            for unit in range(UNITS)
        ]
        bias_sum = r.bias_out[...]
        total = col_sum(bias_sum * bias_sum) + ada_square
        for k in range(1, 8 * LAYERS):
            self.square_sum(k).wait_recv()
        for device in range(8 * LAYERS):
            total = total + r.squares[device]
        r.square_out[...] = jnp.broadcast_to(jnp.sum(total, axis=1, keepdims=True), (8, 128))
        for made in puts:
            made.wait()
        self.drain()

    def drain(self):
        for unit in range(UNITS):
            for k in self.steps:
                self.gather_z(unit, k).wait_send()
                for m in self.steps:
                    self.gather_grp(unit, k, m).wait_send()
            for k in range(4):
                self.gather_sibling(unit, k).wait_send()
        for unit in range(5):
            self.sum_sibling(unit).wait_send()
            if unit < 3:
                for k in self.steps:
                    self.sum_grp(unit, k).wait_send()
            else:
                self.sum_one(unit, 0).wait_send()
                self.sum_one(unit, 1).wait_send()
                self.sum_two(unit).wait_send()
            for k in self.steps:
                self.sum_z(unit, k).wait_send()
                self.share_piece(unit, k).wait_send()
        for index in range(8):
            self.small(index).wait_send()
        for index in range(7):
            self.small_sum(index).wait_send()
        for index in range(10):
            self.late_sum(index).wait_send()
        for step in range(1, 8 * LAYERS):
            self.square_sum(step).wait_send()


correction = 1.0 - 0.5**ADAM_STEP
grad_limit = math.sqrt(NPARAM)


def adam(master, first, second, clipped, decay):
    first_new = 0.5 * first + 0.5 * clipped
    second_new = 0.5 * second + 0.5 * clipped * clipped
    update = first_new / correction / (jnp.sqrt(second_new / correction) + adam_eps)
    return (master - learn_rate * (update + decay * master), first_new, second_new)


CHUNK = 48
STATE = ("qkv", "proj", "up", "down", "ada")


def finish_kernel(names, *refs):
    r = Refs(names, refs)
    loads = {
        "pieces": local(r.pieces_far, r.pieces, r.in_sems.at[0]),
        "grad": local(r.grad_ada_far, r.grad_ada, r.in_sems.at[16]),
    }
    for index, name in enumerate(STATE):
        for kind in range(3):
            loads[name, kind] = local(
                getattr(r, f"{name}_in{kind}"), getattr(r, f"{name}_{kind}"),
                r.in_sems.at[1 + 3 * index + kind],
            )
    streams = [
        local(getattr(r, name + "_in"), getattr(r, name), r.stream_sems.at[index])
        for index, name in enumerate(("y", "dx"))
    ]
    norm = jnp.sqrt(r.square[...])
    r.norm[0, 0] = jnp.max(norm)
    clip = grad_limit / jnp.maximum(norm, grad_limit)
    row_clip = clip[0:1, :]

    loads["pieces"].wait()
    piece = r.pieces

    def unpack(name):
        for j in range(3):
            columns = slice(128 * j, 128 * j + 128)
            if name == "proj":
                r.grad_proj[pl.ds(j, SLAB, stride=3), :] = piece[0, 3 * SLAB :, columns].astype(F32)
            for g in range(GROUPS):
                rows = slice(SLAB * g, SLAB * (g + 1))
                if name == "qkv" and g < 3:
                    r.grad_qkv[pl.ds(3 * g + j, SLAB, stride=9), :] = piece[0, rows, columns].astype(F32)
                if name == "up":
                    r.grad_up[pl.ds(3 * g + j, SLAB, stride=12), :] = piece[1, rows, columns].astype(F32)
                if name == "down":
                    r.grad_down[pl.ds(3 * SLAB * g + j, SLAB, stride=3), :] = piece[2, rows, columns].astype(F32)

    stores = []
    for turn, name in enumerate(("qkv", "up", "down", "ada", "proj")):
        index = STATE.index(name)
        for kind in range(3):
            loads[name, kind].wait()
        if name == "ada":
            loads["grad"].wait()
        unpack(name)
        grad, low = (getattr(r, "grad_" + name), getattr(r, name + "_low"))
        state = [getattr(r, f"{name}_{kind}") for kind in range(3)]

        def chunk(i, carry):
            rows = pl.ds(pl.multiple_of(CHUNK * i, 16), CHUNK)
            new, first_new, second_new = adam(
                *(ref[rows, :] for ref in state), grad[rows, :] * row_clip, 0.1
            )
            for ref, value in zip(state, (new, first_new, second_new)):
                ref[rows, :] = value
            low[rows, :] = new.astype(BF)
            return carry

        lax.fori_loop(0, grad.shape[0] // CHUNK, chunk, 0)
        for kind, ref in enumerate((*state, low)):
            stores.append(local(ref, getattr(r, f"{name}_out{kind}"), r.out_sems.at[4 * index + kind]))
        if turn < 2:
            name = ("y", "dx")[turn]
            streams[turn].wait()
            stores.append(local(getattr(r, name), getattr(r, name + "_out"), r.stream_sems.at[turn]))
    owner = lax.axis_index("dp")
    lane = lax.broadcasted_iota(jnp.int32, (1, 128), 1)
    first = 672 * owner // 128
    shift = lax.rem(32 * owner, 128)
    back = lax.rem(128 - shift, 128)
    for i in range(6):
        size = 128 if i < 5 else 32
        here = pltpu.roll(r.bias_sum[pl.ds(first + i, 1), :], back, axis=1)
        there = pltpu.roll(r.bias_sum[pl.ds(first + i + 1, 1), :], back, axis=1)
        grad = jnp.where(lane < 128 - shift, here, there) * row_clip
        place = pl.ds(128 * i, size)
        state = [getattr(r, f"bias_in{kind}")[place].reshape(1, size) for kind in range(3)]
        new, first_new, second_new = adam(*state, grad[:, :size], 0.0)
        r.bias_out0[place] = new.reshape(size)
        r.bias_out1[place] = first_new.reshape(size)
        r.bias_out2[place] = second_new.reshape(size)
        r.bias_out3[place] = new.reshape(size).astype(BF)

    for made in stores:
        made.wait()


def finish(y, dx, pieces, ada, bias_sum, square, masters, firsts, seconds):
    vmem, hbm, dma = (pltpu.VMEM, pl.ANY, pltpu.SemaphoreType.DMA)
    state = list(zip(masters, firsts, seconds))
    shapes = {name: (arrays[0].size // 128, 128) for name, arrays in zip(STATE, state)}
    ins = [
        ("square", square, vmem), ("bias_sum", bias_sum, vmem), ("pieces_far", pieces, hbm),
        ("grad_ada_far", ada, hbm), ("y_in", y, hbm), ("dx_in", dx, hbm),
        *[(f"bias_in{kind}", array, vmem) for kind, array in enumerate(state[5])],
        *[
            (f"{name}_in{kind}", array.reshape(-1, 128), hbm)
            for name, arrays in zip(STATE, state)
            for kind, array in enumerate(arrays)
        ],
    ]
    outs = [("norm", (1, 1), F32, pltpu.SMEM), ("y_out", y.shape, F32, hbm), ("dx_out", dx.shape, F32, hbm)]
    for kind in range(4):
        dtype = F32 if kind < 3 else BF
        outs += [(f"{name}_out{kind}", shapes[name], dtype, hbm) for name in STATE]
        outs.append((f"bias_out{kind}", state[5][0].shape, dtype, vmem))
    scratch = [
        ("pieces", vmem(pieces.shape, BF)), ("y", vmem(y.shape, F32)), ("dx", vmem(dx.shape, F32)),
        *[(f"{name}_{kind}", vmem(shapes[name], F32)) for name in STATE for kind in range(3)],
        *[(f"{name}_low", vmem(shapes[name], BF)) for name in STATE],
        *[(f"grad_{name}", vmem(shapes[name], F32)) for name in STATE],
        ("in_sems", dma((17,))), ("stream_sems", dma((2,))), ("out_sems", dma((20,))),
    ]
    names = [item[0] for item in (*ins, *outs, *scratch)]
    norm, y, dx, *rest = pl.pallas_call(
        functools.partial(finish_kernel, names),
        in_specs=[pl.BlockSpec(memory_space=space) for *_, space in ins],
        out_specs=[pl.BlockSpec(memory_space=space) for *_, space in outs],
        out_shape=[jax.ShapeDtypeStruct(shape, kind) for _, shape, kind, _ in outs],
        scratch_shapes=[kind for _, kind in scratch],
        name="finish",
    )(*(array for _, array, _ in ins))
    return (y, dx, norm.reshape(()), *(array.reshape(-1) for array in rest))


MASTERS = ("qkv", "proj", "up", "down", "ada")


def block_kernel(names, hooked, *refs):
    r = Refs(names, refs)
    if hooked is Together:
        r.masters = {name: getattr(r, "far_" + name) for name in MASTERS}
        for name in ("gz", "gx", "gs", "gm", "rs", "rx", "rz", "ra", "rv", "rq", "rl"):
            setattr(r, name, (getattr(r, name + "_out"), getattr(r, name + "_in")))
    hooks = hooked(r)
    length = r.x_far.shape[0]
    pairs = HEADS // 2
    get_x = local(r.x_far, r.x, r.out_sems.at[3])
    get_cot = local(r.cot_far, r.cot, r.out_sems.at[2])

    def over_rows(body, after=None, size=ROWS):
        def step(i, carry):
            body(pl.ds(pl.multiple_of(i * size, size), size))
            if after is not None:
                after(i)
            return carry

        lax.fori_loop(0, length // size, step, 0)

    def columns(h, offset=0):
        return pl.ds(pl.multiple_of(offset + 128 * h, 128), 128)

    def over_pairs(body):
        def step(h, carry):
            body(h)
            return carry

        lax.fori_loop(0, pairs, step, 0)

    def act_refs(rows):
        first = rows.start
        return [
            r.act.at[pl.ds(pl.multiple_of(length * part + first, ROWS), rows.size)]
            for part in range(4)
        ]

    def a_refs(rows):
        first = rows.start
        return [
            r.a.at[pl.ds(pl.multiple_of(length * part + first, ROWS), rows.size)]
            for part in range(3)
        ]

    def save(step, h):
        slot = lax.rem(h, 2)
        return pltpu.make_async_copy(
            r.p.at[slot], r.p_far.at[step, pl.ds(2 * h, 2)], r.p_sems.at[slot]
        )

    def fetch(step, h):
        slot = lax.rem(h, 2)
        return pltpu.make_async_copy(
            r.p_far.at[step, pl.ds(2 * h, 2)], r.p.at[slot], r.p_sems.at[slot]
        )

    def attend(step, qkv, att, after):
        def body(h):
            @pl.when(h >= 2)
            def _():
                save(step, h - 2).wait()

            attend_pair(
                qkv[:, columns(h)], qkv.at[:, columns(h, D)], qkv[:, columns(h, 2 * D)],
                att.at[:, columns(h)], r.p.at[lax.rem(h, 2)], r.turned,
            )
            save(step, h).start()
            after(h)

        over_pairs(body)

    def finish_saves(step):
        for h in range(pairs - 2, pairs):
            save(step, h).wait()

    def attend_back(step, qkv, between, after):
        def body(h):
            fetch(step, h).wait()
            attend_back_pair(
                qkv[:, columns(h)], qkv[:, columns(h, D)], qkv.at[:, columns(h, 2 * D)],
                r.datt[:, columns(h)], r.p.at[lax.rem(h, 2)],
                r.dqkv.at[:, columns(h)], r.dqkv.at[:, columns(h, D)],
                r.dqkv.at[:, columns(h, 2 * D)], r.turned,
                None if between is None else lambda: between(h),
            )

            @pl.when(h + 2 < pairs)
            def _():
                fetch(step, h + 2).start()

            after(h)

        over_pairs(body)

    nothing = lambda h: None
    hooks.begin()

    def first(rows):
        r.qkv0[rows, :] = first_rows(r.x[rows, :], r.rows, r.wa)

    get_x.wait()
    over_rows(first)
    hooks.after_first()
    attend(0, r.qkv0, r.att0, hooks.after_attend_pair)
    hooks.before_middle()

    def middle(rows):
        middle_rows(
            r.x.at[rows], r.att0.at[rows], r.rows, r.wa, r.wup, r.wdown,
            a_refs(rows), r.gp.at[rows], act_refs(rows), r.f.at[rows], r.x1.at[rows],
            r.qkv1.at[rows],
        )

    over_rows(middle, size=2 * ROWS)
    finish_saves(0)
    attend(1, r.qkv1, r.att1, nothing)

    def turn(rows):
        turn_rows(
            r.x1.at[rows], r.att1.at[rows], r.cot.at[rows], r.rows, r.wa, r.wup,
            r.wdown, r.y.at[rows], r.dmid.at[rows], r.datt.at[rows], r.gdown, r.gup, r.gproj,
            r.wide, r.narrow1,
        )

    finish_saves(1)
    for h in range(2):
        fetch(1, h).start()
    get_cot.wait()
    over_rows(turn, size=2 * ROWS)
    put_y = local(r.y, r.y_far, r.out_sems.at[0])
    attend_back(1, r.qkv1, None, nothing)
    for h in range(2):
        fetch(0, h).start()

    def join(rows):
        join_rows(
            r.dqkv.at[rows], r.x1.at[rows], r.x.at[rows], a_refs(rows), r.gp.at[rows],
            act_refs(rows), r.f.at[rows], r.rows, r.wa, r.wdown, r.att1.at[rows],
            r.dmid.at[rows], r.gqkv, r.gdown, r.gup, r.wide, r.narrow1, r.narrow0, r.bias,
        )

    def join_middle(rows):
        join_middle_rows(
            r.x.at[rows], a_refs(rows), act_refs(rows), r.att0.at[rows], r.rows, r.wa, r.wup,
            r.dmid.at[rows], r.datt.at[rows], r.gproj, r.narrow0,
        )

    hooks.before_join()
    over_rows(join)
    hooks.amid_join()
    over_rows(join_middle, size=2 * ROWS)
    hooks.after_join()
    attend_back(0, r.qkv0, hooks.amid_back_pair, hooks.after_back_pair)

    def last(rows):
        r.dmid[rows, :] = qkv_back(
            mod_reader(r.rows, 0), r.x[rows, :].astype(F32), r.dmid[rows, :],
            r.dqkv[rows, :], r.wa, r.narrow0, r.bias,
        )

    over_rows(last, hooks.after_last_rows)
    put_dx = local(r.dmid, r.dx_far, r.out_sems.at[1])
    hooks.after_last()
    put_y.wait()
    put_dx.wait()


def block_call(hooked, inputs, cotangent, extra_in, extra_out, extra_scratch, params):
    length = inputs.shape[0]
    vmem, hbm, dma = (pltpu.VMEM, pl.ANY, pltpu.SemaphoreType.DMA)
    weights = (ROLLOUT, HEADS, length, length)
    ins = [("x_far", inputs, hbm), ("cot_far", cotangent, hbm), *extra_in]
    outs = [
        ("y_far", (length, D), F32, hbm), ("dx_far", (length, D), F32, hbm),
        ("p_far", weights, BF, hbm), *extra_out,
    ]
    scratch = [
        ("wa", vmem((D, FF), BF)), ("wup", vmem((D, FF), BF)), ("wdown", vmem((FF, D), BF)),
        ("x", vmem((length, D), BF)), ("cot", vmem((length, D), BF)), ("qkv0", vmem((length, 3 * D), BF)),
        ("qkv1", vmem((length, 3 * D), BF)), ("p", vmem((2, 2, length, length), BF)),
        ("att0", vmem((length, D), BF)), ("att1", vmem((length, D), BF)),
        *[(name, vmem((length, D), F32)) for name in ("f", "x1", "dmid", "y")], ("a", vmem((3 * length, 128), F32)),
        ("gp", vmem((length, FF), F32)), ("act", vmem((4 * length, D), BF)),
        ("datt", vmem((length, D), BF)), ("dqkv", vmem((length, 3 * D), BF)),
        ("gqkv", vmem((D, 3 * D), F32)), ("gproj", vmem((D, D), F32)),
        ("gup", vmem((D, FF), F32)), ("gdown", vmem((FF, D), F32)),
        ("turned", vmem((2, 128, length), BF)), ("wide", vmem((8, FF), F32)),
        ("narrow0", vmem((8, D), F32)), ("narrow1", vmem((8, D), F32)),
        ("bias", vmem((8, 3 * D), F32)), ("blocks", vmem((UNITS, 2 * HALF, PART), BF)),
        ("rows", vmem((32, D), F32)), ("vec", vmem((VEC, 128), F32)), ("late", vmem((16, 128), F32)),
        ("in_sems", dma((5,))), ("p_sems", dma((2,))), ("out_sems", dma((4,))),
        *extra_scratch,
    ]
    names = [item[0] for item in (*ins, *outs, *scratch)]
    return pl.pallas_call(
        functools.partial(block_kernel, names, hooked),
        in_specs=[pl.BlockSpec(memory_space=space) for _, _, space in ins],
        out_specs=[pl.BlockSpec(memory_space=space) for *_, space in outs],
        out_shape=[jax.ShapeDtypeStruct(shape, kind) for _, shape, kind, _ in outs],
        scratch_shapes=[kind for _, kind in scratch],
        compiler_params=pltpu.CompilerParams(vmem_limit_bytes=67043328, **params),
        name="block",
    )(*(array for _, array, _ in ins))


def block_alone(inputs, cotangent, rows, wa, wup, wdown):
    hbm = pl.ANY
    y, dx, _, blocks, vec = block_call(
        Alone, inputs, cotangent,
        [("rows_far", rows, hbm), ("wa_far", wa, hbm), ("wup_far", wup, hbm), ("wdown_far", wdown, hbm)],
        [("blocks_far", (UNITS, 2 * HALF, PART), BF, hbm), ("vec_far", (VEC, 128), F32, hbm)],
        [], {},
    )
    return (y, dx, blocks, vec)


def block_together(inputs, cotangent, start, interval, counts, lead, masters):
    vmem, hbm, smem, dma = (pltpu.VMEM, pl.ANY, pltpu.SMEM, pltpu.SemaphoreType.DMA)
    qkv, proj, up, down, ada, bias = masters
    far = [
        ("far_" + name, array.reshape(-1, 128), hbm)
        for name, array in zip(MASTERS, (qkv, proj, up, down, ada))
    ]
    pairs_of = [
        ("gz", (UNITS, 3)), ("gx", (UNITS, 3, 3)), ("gs", (UNITS, 4)), ("gm", (8,)),
        ("rs", (5,)), ("rx", (5, 3)), ("rz", (5, 3)), ("ra", (5, 3)),
        ("rv", (7,)), ("rq", (8 * LAYERS,)), ("rl", (10,)),
    ]
    y, dx, _, pieces, ada_grad, bias_sum, square = block_call(
        Together, inputs, cotangent,
        [("start", start, smem), ("interval", interval, smem), ("counts", counts, smem),
         ("lead", lead, vmem), ("bias_flat", bias, vmem), *far],
        [("pieces_far", (UNITS, 4 * SLAB, PART), BF, hbm), ("ada_far", (18 * SLAB, 128), F32, hbm),
         ("bias_out", (48, 128), F32, vmem), ("square_out", (8, 128), F32, vmem)],
        [("cond_t", vmem((D, 8), F32)), ("part_own", vmem((40, 128), F32)),
         ("part_sib", vmem((40, 128), F32)), ("part_z", vmem((LAYERS, 40, 128), F32)),
         ("bias_own", vmem((8, 128), F32)), ("bias_slot", vmem((LAYERS, 2, 8, 128), F32)), ("bias_full", vmem((48, 128), F32)),
         ("vec_sib", vmem((VEC, 128), F32)), ("vec_z", vmem((LAYERS, VEC, 128), F32)),
         ("vec_g", vmem((GROUPS, VEC, 128), F32)), ("late_d", vmem((8, 16, 128), F32)),
         ("vec_sum", vmem((GROUPS, VEC, 128), F32)), ("cond", vmem((8, D), F32)),
         ("late_g", vmem((GROUPS, 16, 128), F32)), ("squares", vmem((8 * LAYERS, 1, 128), F32)), ("joined", pltpu.SemaphoreType.REGULAR), ("turned_back", pltpu.SemaphoreType.REGULAR),
         *[(name + end, dma(shape)) for name, shape in pairs_of for end in ("_out", "_in")]],
        dict(collective_id=0, has_side_effects=True),
    )
    return (y, dx, pieces, ada_grad, bias_sum, square)


def step_embedding(moment):
    half_width = D // 2
    freqs = jnp.exp(-math.log(10000.0) * jnp.arange(half_width, dtype=F32) / half_width)
    angles = moment[:, None] * freqs[None, :]
    return jnp.concatenate([jnp.sin(angles), jnp.cos(angles)], axis=1)


def all_conditions(group_interval, rollout_start, lead_table):
    chosen = group_interval[:, None] == jnp.arange(INTERVALS)[None, :]
    lead_rows = jnp.sum(jnp.where(chosen[:, :, None], lead_table[None], 0.0), axis=1)
    start = rollout_start.astype(F32)
    rows = [lead_rows + step_embedding(start + offset) for offset in range(ROLLOUT)]
    return jax.nn.silu(jnp.stack(rows, axis=1)).astype(BF)


def plain_gather(group_interval, counts, rollout_start, lead_table, masters):
    low = [master.astype(BF) for master in masters]
    owner = lax.axis_index("dp")
    group_index = lax.axis_index("grp")
    own_rows = D // lax.axis_size("dp")
    counts = counts.astype(F32)
    share = lax.axis_size("grp") * counts / jnp.sum(counts)
    share = lax.dynamic_index_in_dim(share, group_index, keepdims=False)
    conditions = all_conditions(group_interval, rollout_start, lead_table)
    owner_columns = lax.dynamic_slice_in_dim(conditions, owner * own_rows, own_rows, axis=2)
    own_condition = lax.dynamic_index_in_dim(owner_columns, group_index, keepdims=False)
    modulation = lax.psum(dot(own_condition, low[4].reshape(own_rows, 6 * D)), "dp")
    qkv, proj, up, down, bias = [
        lax.all_gather(low[index], "dp", axis=0, tiled=True) for index in (0, 1, 2, 3, 5)
    ]
    bias = bias.astype(F32)
    modulation = modulation + bias[4 * D + FF :][None]
    share_rows = jnp.broadcast_to(share, (ROLLOUT, 2, D))
    mods = jnp.concatenate([modulation.reshape(ROLLOUT, 6, D), share_rows], axis=1).reshape(-1, D)
    rows = jnp.concatenate(
        [mods, bias[:D][None], jnp.zeros((1, D), F32), bias[D : 4 * D + FF].reshape(-1, D),
         jnp.zeros((7, D), F32)]
    )
    wa = jnp.concatenate([qkv.reshape(D, 3 * D), proj.reshape(D, D)], axis=1)
    return (wa, up.reshape(D, FF), down.reshape(FF, D), rows, owner_columns)


def plain_update(owner_columns, vec, blocks, masters, firsts, seconds):
    owner = lax.axis_index("dp")
    vec = vec.reshape(-1)
    split = 4 * D + FF
    dmod = vec[split:].reshape(ROLLOUT, VEC_STEP * 128)[:, : 6 * D]
    dmod_all = lax.all_gather(lax.psum(dmod, "dp"), "grp")
    bias_sum = lax.psum(vec[:split], ("grp", "dp"))
    bias_sum = jnp.concatenate([bias_sum, jnp.sum(dmod_all, axis=(0, 1))])
    bias_rows = masters[5].shape[0]
    bias_grad = lax.dynamic_slice_in_dim(bias_sum, owner * bias_rows, bias_rows)
    ada_grad = jnp.einsum(
        "gsr,gsc->rc", owner_columns.astype(F32), dmod_all, precision=lax.Precision.HIGHEST
    )
    blocks = blocks.reshape(UNITS, 2, 4, LAYERS, SLAB, PART)
    flat_a, flat_up = [blocks[u].transpose(2, 0, 3, 1, 4).reshape(D, FF) for u in (0, 1)]
    flat_down = blocks[2].transpose(2, 0, 1, 3, 4)
    flat = [flat_a[:, : 3 * D], flat_a[:, 3 * D :], flat_up, flat_down]
    shares = []
    for grad in flat:
        summed = lax.psum(grad.reshape(-1), "grp").astype(F32)
        shares.append(lax.psum_scatter(summed, "dp", scatter_dimension=0, tiled=True))
    shares = shares + [ada_grad.reshape(-1), bias_grad]
    local_square = sum((jnp.sum(piece * piece) for piece in shares))
    grad_norm = jnp.sqrt(lax.psum(local_square, "dp"))
    clip = grad_limit / jnp.maximum(grad_norm, grad_limit)
    decays = [0.1, 0.1, 0.1, 0.1, 0.1, 0.0]
    results = [
        adam(master, first, second, grad * clip, decay)
        for master, first, second, grad, decay in zip(masters, firsts, seconds, shares, decays)
    ]
    news, first_news, second_news = zip(*results)
    return (grad_norm, *news, *first_news, *second_news, *(new.astype(BF) for new in news))


def per_device(
    inputs,
    cotangent,
    group_interval,
    sample_counts,
    rollout_start,
    lead_table,
    *state,
):
    masters, firsts, seconds = (state[0:6], state[6:12], state[12:18])
    fits = (
        lax.axis_size("dp") == 2 * LAYERS
        and lax.axis_size("grp") == GROUPS
        and inputs.shape[0] == 1024
    )
    if not fits:
        wa, wup, wdown, rows, owner_columns = plain_gather(
            group_interval, sample_counts, rollout_start, lead_table, masters
        )
        result, input_grad, blocks, vec = block_alone(inputs, cotangent, rows, wa, wup, wdown)
        rest = plain_update(owner_columns, vec, blocks, masters, firsts, seconds)
        return (result, input_grad, *rest)
    result, input_grad, pieces, ada_grad, bias_sum, square = block_together(
        inputs, cotangent, rollout_start, group_interval, sample_counts, lead_table, masters
    )
    return finish(
        result, input_grad, pieces, ada_grad, bias_sum, square, masters, firsts, seconds
    )


def solution(mesh):
    rows = P(("grp", "dp"), None)
    return jax.shard_map(
        per_device,
        mesh=mesh,
        in_specs=(rows, rows, P(), P(), P(), P(), *[P("dp")] * 18),
        out_specs=(rows, rows, P(), *[P("dp")] * 24),
        check_vma=False,
    )
```

```python
import functools
import math

import jax
import jax.numpy as jnp
from jax import lax
from jax.experimental import pallas as pl
from jax.experimental.pallas import tpu as pltpu
from jax.sharding import PartitionSpec as P

D = 384
HEADS = 6
FF = 1536
ROLLOUT = 2
INTERVALS = 3
ADAM_STEP = 10
HEAD_DIM = 64
NPARAM = 2659584

norm_eps = 1e-06
learn_rate = 0.05
adam_eps = 1e-08

BF = jnp.bfloat16
F32 = jnp.float32
NN = (((1,), (0,)), ((), ()))
NT = (((1,), (1,)), ((), ()))
TN = (((0,), (0,)), ((), ()))

ROWS = 256
SLAB = 48
PART = 384
ROW_SHARE = 6
ROW_BQKV, ROW_BPROJ, ROW_BUP, ROW_BDOWN = 16, 19, 20, 24
SHIFT1, SCALE1, GATE1, SHIFT2, SCALE2, GATE2 = range(6)


def dot(left, right, dims=NN):
    return lax.dot_general(left, right, dims, preferred_element_type=F32)


def layer_norm(stream):
    centred = stream - jnp.mean(stream, axis=-1, keepdims=True)
    inverse = lax.rsqrt(jnp.mean(centred * centred, axis=-1, keepdims=True) + norm_eps)
    return (centred * inverse, inverse)


def norm_back(normed, inverse, grad_out):
    mean_grad = jnp.mean(grad_out, axis=-1, keepdims=True)
    mean_prod = jnp.mean(grad_out * normed, axis=-1, keepdims=True)
    return inverse * (grad_out - mean_grad - normed * mean_prod)


def col_sum(value):
    return jnp.sum(value, axis=0, keepdims=True)


def modulated(normed, mods, scale_row, shift_row):
    return (normed * (1.0 + mods(scale_row)) + mods(shift_row)).astype(BF)


def mod_reader(mod_ref, step):
    return lambda row: mod_ref[pl.ds(8 * step + row, 1), :]


def gelu_pair(value):
    cdf = 0.5 + 0.5 * lax.erf(value * (2.0**-0.5))
    density = jnp.exp(-0.5 * value * value) * (1.0 / math.sqrt(2.0 * math.pi))
    return (value * cdf, cdf + value * density)


def side_by_side(ref, first, count):
    return jnp.concatenate([ref[row : row + 1, :] for row in range(first, first + count)], axis=1)


def first_rows(x, rows_ref, wa_ref):
    normed, _ = layer_norm(x.astype(F32))
    hidden = modulated(normed, mod_reader(rows_ref, 0), SCALE1, SHIFT1)
    qkv = dot(hidden, wa_ref[:, : 3 * D]) + side_by_side(rows_ref, ROW_BQKV, 3)
    return qkv.astype(BF)


def middle_rows(
    x_ref, att_ref, rows_ref, wa_ref, wup_ref, wdown_ref,
    a_refs, gp_ref, act_refs, f_ref, next_ref, qkv_ref,
):
    mods = mod_reader(rows_ref, 0)
    later = mod_reader(rows_ref, 1)
    branch = dot(att_ref[...], wa_ref[:, 3 * D :]) + mods(ROW_BPROJ)
    for part, ref in enumerate(a_refs):
        ref[...] = branch[:, 128 * part : 128 * (part + 1)]
    middle = x_ref[...].astype(F32) + mods(GATE1) * branch
    normed, _ = layer_norm(middle)
    hidden = modulated(normed, mods, SCALE2, SHIFT2)
    upward = dot(hidden, wup_ref[...]) + side_by_side(rows_ref, ROW_BUP, 4)
    act, slope = gelu_pair(upward)
    gp_ref[...] = slope
    act = act.astype(BF)
    for part, ref in enumerate(act_refs):
        ref[...] = act[:, PART * part : PART * (part + 1)]
    branch = dot(act, wdown_ref[...]) + mods(ROW_BDOWN)
    f_ref[...] = branch
    stream = middle + mods(GATE2) * branch
    next_ref[...] = stream
    normed, _ = layer_norm(stream)
    hidden = modulated(normed, later, SCALE1, SHIFT1)
    qkv = dot(hidden, wa_ref[:, : 3 * D]) + side_by_side(rows_ref, ROW_BQKV, 3)
    qkv_ref[...] = qkv.astype(BF)


def ffn_back(
    mods, grad, branch_two, act, slope, hidden, wdown_ref, gdown_ref, gup_ref, wide_ref, narrow_ref
):
    df = (mods(GATE2) * grad).astype(BF)
    narrow_ref[pl.ds(GATE2, 1), :] += col_sum(grad * branch_two)
    narrow_ref[pl.ds(7, 1), :] += col_sum(df.astype(F32))
    gdown_ref[...] += dot(act, df, TN)
    dact = dot(df, wdown_ref[...], NT)
    du = (dact * slope).astype(BF)
    wide_ref[pl.ds(0, 1), :] += col_sum(du.astype(F32))
    gup_ref[...] += dot(hidden, du, TN)
    return du


def middle_back(
    mods, grad, du, normed, inverse, branch_one, att, wa_ref, wup_ref, gproj_ref, narrow_ref,
    dmid_ref, datt_ref,
):
    dh = dot(du, wup_ref[...], NT)
    narrow_ref[pl.ds(SHIFT2, 1), :] += col_sum(dh)
    narrow_ref[pl.ds(SCALE2, 1), :] += col_sum(dh * normed)
    dmid = grad + norm_back(normed, inverse, dh * (1.0 + mods(SCALE2)))
    dmid_ref[...] = dmid
    da = (mods(GATE1) * dmid).astype(BF)
    narrow_ref[pl.ds(GATE1, 1), :] += col_sum(dmid * branch_one)
    narrow_ref[pl.ds(6, 1), :] += col_sum(da.astype(F32))
    gproj_ref[...] += dot(att, da, TN)
    datt_ref[...] = dot(da, wa_ref[:, 3 * D :], NT).astype(BF)


def turn_rows(
    x_ref, att_ref, cot_ref, rows_ref, wa_ref, wup_ref, wdown_ref,
    out_ref, dmid_ref, datt_ref, gdown_ref, gup_ref, gproj_ref, wide_ref, narrow_ref,
):
    mods = mod_reader(rows_ref, 1)
    shared = mod_reader(rows_ref, 0)
    att = att_ref[...]
    branch_one = dot(att, wa_ref[:, 3 * D :]) + shared(ROW_BPROJ)
    middle = x_ref[...] + mods(GATE1) * branch_one
    normed, inverse = layer_norm(middle)
    hidden = modulated(normed, mods, SCALE2, SHIFT2)
    upward = dot(hidden, wup_ref[...]) + side_by_side(rows_ref, ROW_BUP, 4)
    act, slope = gelu_pair(upward)
    act = act.astype(BF)
    branch_two = dot(act, wdown_ref[...]) + shared(ROW_BDOWN)
    out_ref[...] = middle + mods(GATE2) * branch_two
    grad = cot_ref[...].astype(F32)
    du = ffn_back(
        mods, grad, branch_two, act, slope, hidden, wdown_ref, gdown_ref, gup_ref, wide_ref, narrow_ref
    )
    middle_back(
        mods, grad, du, normed, inverse, branch_one, att, wa_ref, wup_ref, gproj_ref, narrow_ref,
        dmid_ref, datt_ref,
    )


def qkv_back(mods, stream, dmid, dqkv, wa_ref, narrow_ref, bias_ref, gqkv_ref=None):
    normed, inverse = layer_norm(stream)
    bias_ref[pl.ds(0, 1), :] += col_sum(dqkv.astype(F32))
    if gqkv_ref is not None:
        gqkv_ref[...] += dot(modulated(normed, mods, SCALE1, SHIFT1), dqkv, TN)
    dh = dot(dqkv, wa_ref[:, : 3 * D], NT)
    narrow_ref[pl.ds(SHIFT1, 1), :] += col_sum(dh)
    narrow_ref[pl.ds(SCALE1, 1), :] += col_sum(dh * normed)
    return dmid + norm_back(normed, inverse, dh * (1.0 + mods(SCALE1)))


def middle_again(mods, x_ref, a_refs):
    branch_one = jnp.concatenate([ref[...] for ref in a_refs], axis=1)
    normed, inverse = layer_norm(x_ref[...].astype(F32) + mods(GATE1) * branch_one)
    return (branch_one, normed, inverse)


def join_rows(
    dqkv_ref, x1_ref, x0_ref, a_refs, gp_ref, act_refs, f_ref, rows_ref, wa_ref, wdown_ref,
    hidden_ref, dmid_ref, gqkv_ref, gdown_ref, gup_ref, wide_ref, narrow1_ref, narrow_ref, bias_ref,
):
    grad = qkv_back(
        mod_reader(rows_ref, 1), x1_ref[...], dmid_ref[...], dqkv_ref[...], wa_ref,
        narrow1_ref, bias_ref, gqkv_ref,
    )
    dmid_ref[...] = grad
    mods = mod_reader(rows_ref, 0)
    normed, _ = layer_norm(x0_ref[...].astype(F32))
    hidden_ref[...] = modulated(normed, mods, SCALE1, SHIFT1)
    _, normed, _ = middle_again(mods, x0_ref, a_refs)
    act = jnp.concatenate([ref[...] for ref in act_refs], axis=1)
    du = ffn_back(
        mods, grad, f_ref[...], act, gp_ref[...], modulated(normed, mods, SCALE2, SHIFT2),
        wdown_ref, gdown_ref, gup_ref, wide_ref, narrow_ref,
    )
    for part, ref in enumerate(act_refs):
        ref[...] = du[:, PART * part : PART * (part + 1)]


def join_middle_rows(
    x0_ref, a_refs, du_refs, att_ref, rows_ref, wa_ref, wup_ref,
    dmid_ref, datt_ref, gproj_ref, narrow_ref,
):
    mods = mod_reader(rows_ref, 0)
    branch_one, normed, inverse = middle_again(mods, x0_ref, a_refs)
    du = jnp.concatenate([ref[...] for ref in du_refs], axis=1)
    middle_back(
        mods, dmid_ref[...], du, normed, inverse, branch_one, att_ref[...], wa_ref, wup_ref,
        gproj_ref, narrow_ref, dmid_ref, datt_ref,
    )


def head_lanes(rows):
    lane = lax.broadcasted_iota(jnp.int32, (rows, 2 * HEAD_DIM), 1)
    return (lane < HEAD_DIM, lane >= HEAD_DIM)


def turned_heads(rows_f32, out_ref):
    turned = jnp.transpose(rows_f32)
    row = lax.broadcasted_iota(jnp.int32, turned.shape, 0)
    out_ref[0] = jnp.where(row < HEAD_DIM, turned, 0.0).astype(BF)
    out_ref[1] = jnp.where(row >= HEAD_DIM, turned, 0.0).astype(BF)


score_scale = HEAD_DIM**-0.5


def attend_pair(q, k_ref, v, o_ref, p_ref, vt_ref):
    turned_heads(v.astype(F32), vt_ref)
    queries = q * BF(score_scale)
    mixed = None
    for half, lanes in enumerate(head_lanes(queries.shape[0])):
        scores = dot(k_ref[...], jnp.where(lanes, queries, BF(0)), NT)
        top = jnp.max(scores, axis=0, keepdims=True)
        weights = jnp.exp(scores - top)
        total = jnp.sum(weights, axis=0, keepdims=True)
        low = (weights * (1.0 / total)).astype(BF)
        p_ref[half] = low
        part = dot(vt_ref[half], low)
        mixed = part if mixed is None else mixed + part
    o_ref[...] = jnp.transpose(mixed).astype(BF)


def attend_back_pair(q, k, v_ref, grads, p_ref, dq_ref, dk_ref, dv_ref, kt_ref, between):
    turned_heads(k.astype(F32) * score_scale, kt_ref)
    queries = q * BF(score_scale)
    own_lanes = head_lanes(queries.shape[0])
    for half, lanes in enumerate(own_lanes):
        grad = jnp.where(lanes, grads, BF(0))
        query = jnp.where(lanes, queries, BF(0))
        low = p_ref[half]
        weight_grad = dot(v_ref[...], grad, NT)
        weights = low.astype(F32)
        delta = jnp.sum(weights * weight_grad, axis=0, keepdims=True)
        score_grad = (weights * (weight_grad - delta)).astype(BF)
        news = (
            jnp.transpose(dot(kt_ref[half], score_grad)), dot(score_grad, query), dot(low, grad)
        )
        for ref, new in zip((dq_ref, dk_ref, dv_ref), news):
            new = new.astype(BF)
            ref[...] = new if half == 0 else jnp.where(lanes, new, ref[...])
        if half == 0 and between is not None:
            between()


class Refs:
    def __init__(self, names, refs):
        for name, ref in zip(names, refs, strict=True):
            setattr(self, name, ref)

MESH_ID = pl.DeviceIdType.MESH
GROUPS = 4
LAYERS = 4
UNITS = 3
HALF = 768


class Place:
    def __init__(self):
        self.grp = lax.axis_index("grp")
        self.dp = lax.axis_index("dp")
        self.z = self.dp // 2
        self.core = self.dp % 2

    def sibling(self):
        return (self.grp, 2 * self.z + 1 - self.core)

    def along_grp(self, step):
        return (lax.rem(self.grp + step, GROUPS), self.dp)

    def along_z(self, step):
        return (self.grp, 2 * lax.rem(self.z + step, LAYERS) + self.core)

    def across(self, step):
        return (self.grp, 2 * lax.rem(self.z + step, LAYERS) + 1 - self.core)


def greet(peers):
    barrier = pltpu.get_barrier_semaphore()
    for peer in peers:
        pl.semaphore_signal(barrier, inc=1, device_id=peer, device_id_type=MESH_ID)
    return lambda: pl.semaphore_wait(barrier, len(peers))


def remote(src, dst, sems, index, peer):
    send_sem, recv_sem = sems
    return pltpu.make_async_remote_copy(
        src_ref=src, dst_ref=dst, send_sem=send_sem.at[index], recv_sem=recv_sem.at[index],
        device_id=peer, device_id_type=MESH_ID,
    )


def condition_rows(moments, intervals, lead_ref):
    shape = (8, D)
    row = lax.broadcasted_iota(jnp.int32, shape, 0)
    lane = lax.broadcasted_iota(jnp.int32, shape, 1)
    moment = jnp.zeros(shape, F32)
    chosen = jnp.zeros(shape, jnp.int32)
    for index, (value, interval) in enumerate(zip(moments, intervals)):
        moment = jnp.where(row == index, value.astype(F32), moment)
        chosen = jnp.where(row == index, interval, chosen)
    lead = jnp.zeros(shape, F32)
    for choice in range(INTERVALS):
        picked = jnp.broadcast_to(lead_ref[choice : choice + 1, :], shape)
        lead = jnp.where(chosen == choice, picked, lead)
    half_width = D // 2
    place = jnp.where(lane < half_width, lane, lane - half_width).astype(F32)
    angles = moment * jnp.exp(place * (-math.log(10000.0) / half_width))
    wave = jnp.where(lane < half_width, jnp.sin(angles), jnp.cos(angles))
    condition = lead + wave
    return (condition / (1.0 + jnp.exp(-condition))).astype(BF).astype(F32)


def span(start, size):
    return pl.ds(pl.multiple_of(start, SLAB), size)


def local(src, dst, sem):
    made = pltpu.make_async_copy(src, dst, sem)
    made.start()
    return made


def clear_sums(r):
    def clear(i, carry):
        for ref in (r.gqkv, r.gproj, r.gup, r.gdown):
            size = ref.shape[0] // 8
            ref[span(i * size, size), :] = jnp.zeros((size, ref.shape[1]), F32)
        return carry

    lax.fori_loop(0, 8, clear, 0)
    for ref in (r.wide, r.narrow0, r.narrow1, r.bias):
        ref[...] = jnp.zeros_like(ref)


class Alone:
    def __init__(self, refs):
        self.refs = refs

    def begin(self):
        r = self.refs
        sems = r.in_sems
        first = [local(r.wa_far, r.wa, sems.at[0]), local(r.rows_far, r.rows, sems.at[3])]
        self.later = [local(r.wup_far, r.wup, sems.at[1]), local(r.wdown_far, r.wdown, sems.at[2])]
        clear_sums(r)
        for made in first:
            made.wait()

    def after_first(self):
        pass

    def after_attend_pair(self, h):
        pass

    def before_middle(self):
        for made in self.later:
            made.wait()

    def before_join(self):
        pass

    def amid_join(self):
        fill_blocks(self.refs)

    def after_join(self):
        pass

    def amid_back_pair(self, h):
        pass

    def after_back_pair(self, h):
        fill_pair(self.refs, h)

    def after_last_rows(self, i):
        pass

    def after_last(self):
        r = self.refs
        fill_vec(r)
        fill_late(r, r.late)
        r.vec[0:6, :] = r.late[0:6, :]
        r.vec[VEC_STEP : VEC_STEP + 6, :] = r.late[6:12, :]
        puts = [local(r.blocks, r.blocks_far, r.in_sems.at[0]), local(r.vec, r.vec_far, r.in_sems.at[1])]
        for made in puts:
            made.wait()


def block_rows(owner, part):
    first = HALF * (owner % 2) + 4 * SLAB * part + SLAB * (owner // 2)
    return slice(first, first + SLAB)


def fill_blocks(refs):
    share = refs.rows[ROW_SHARE : ROW_SHARE + 1, :]

    def owner(d, carry):
        for g in range(4):
            there = span(HALF * (d % 2) + 4 * SLAB * g + SLAB * (d // 2), SLAB)
            up = refs.gup[span(SLAB * d, SLAB), PART * g : PART * (g + 1)]
            down = refs.gdown[span(SLAB * (4 * d + g), SLAB), :]
            refs.blocks[1, there, :] = (up * share).astype(BF)
            refs.blocks[2, there, :] = (down * share).astype(BF)
        return carry

    lax.fori_loop(0, 8, owner, 0)


def fill_pair(refs, h):
    share = refs.rows[ROW_SHARE : ROW_SHARE + 1, 0:128]
    columns = [pl.ds(pl.multiple_of(D * g + 128 * h, 128), 128) for g in range(3)]
    grads = jnp.concatenate([refs.dqkv[:, column] for column in columns], axis=1)
    value = dot(refs.att1[...], grads, TN)
    for d in range(8):
        own = slice(SLAB * d, SLAB * (d + 1))
        for g in range(3):
            part = value[own, 128 * g : 128 * (g + 1)] + refs.gqkv[own, columns[g]]
            refs.blocks[0, block_rows(d, g), columns[0]] = (part * share).astype(BF)
        part = refs.gproj[own, columns[0]]
        refs.blocks[0, block_rows(d, 3), columns[0]] = (part * share).astype(BF)


VEC = 72
VEC_STEP = 24


def fill_vec(refs):
    share = refs.rows[ROW_SHARE : ROW_SHARE + 1, 0:128]

    def put(first_row, value):
        for j in range(value.shape[1] // 128):
            refs.vec[first_row + j : first_row + j + 1, :] = value[:, 128 * j : 128 * j + 128] * share

    refs.vec[...] = jnp.zeros_like(refs.vec)
    wide, narrow0, narrow1 = (refs.wide, refs.narrow0, refs.narrow1)
    put(6, narrow0[6:7, :] + narrow1[6:7, :])
    put(9, wide[0:1, :])
    put(21, narrow0[7:8, :] + narrow1[7:8, :])
    for r in range(6):
        if r > 1:
            put(VEC_STEP + 3 * r, narrow0[r : r + 1, :])
        put(2 * VEC_STEP + 3 * r, narrow1[r : r + 1, :])


def fill_late(refs, late_ref):
    share = refs.rows[ROW_SHARE : ROW_SHARE + 1, 0:128]
    rest = (refs.bias[0:1, :D], refs.bias[0:1, 2 * D :], refs.narrow0[0:1, :], refs.narrow0[1:2, :])
    for index, value in enumerate(rest):
        for j in range(3):
            row = 3 * index + j
            late_ref[row : row + 1, :] = value[:, 128 * j : 128 * j + 128] * share
    late_ref[12:16, :] = jnp.zeros((4, 128), F32)


class Together:
    steps = range(1, 4)

    def __init__(self, refs):
        self.refs = refs
        self.at = Place()

    def start(self, copy):
        copy.start()


    def whole(self, unit):
        return (self.refs.wa, self.refs.wup, self.refs.wdown)[unit]

    def part(self, unit, owner, grp):
        if unit == 2:
            return self.whole(2).at[span(4 * SLAB * owner + SLAB * grp, SLAB), :]
        return self.whole(unit).at[
            span(SLAB * owner, SLAB), pl.ds(pl.multiple_of(PART * grp, 128), PART)
        ]

    def slab(self, unit, owner):
        if unit == 2:
            return self.whole(2).at[span(4 * SLAB * owner, 4 * SLAB), :]
        return self.whole(unit).at[span(SLAB * owner, SLAB), :]

    def owner(self, k):
        return 2 * lax.rem(self.at.z + LAYERS - k, LAYERS) + self.at.core

    def gather_z(self, unit, k):
        own = self.part(unit, self.at.dp, self.at.grp)
        return remote(own, own, self.refs.gz, (unit, k - 1), self.at.along_z(k))

    def gather_grp(self, unit, k, m):
        part = self.part(unit, self.owner(k), self.at.grp)
        return remote(part, part, self.refs.gx, (unit, k - 1, m - 1), self.at.along_grp(m))

    def gather_sibling(self, unit, k):
        slab = self.slab(unit, self.owner(k) if k else self.at.dp)
        return remote(slab, slab, self.refs.gs, (unit, k), self.at.sibling())

    def launch(self, unit):
        for k in self.steps:
            self.start(self.gather_z(unit, k))
        self.start(self.gather_sibling(unit, 0))

    def forward_grp(self, unit):
        for k in self.steps:
            self.gather_z(unit, k).wait_recv()
            for m in self.steps:
                self.start(self.gather_grp(unit, k, m))

    def forward_sibling(self, unit):
        for k in self.steps:
            for m in self.steps:
                self.gather_grp(unit, k, m).wait_recv()
            self.start(self.gather_sibling(unit, k))

    def finish_sibling(self, unit):
        for k in range(4):
            self.gather_sibling(unit, k).wait_recv()

    def small(self, index):
        r, at = (self.refs, self.at)
        if index == 0:
            return remote(r.part_own, r.part_sib, r.gm, 0, at.sibling())
        if index == 1:
            own = r.bias_slot.at[at.z, at.core]
            return remote(own, own, r.gm, 1, at.sibling())
        if index < 5:
            own = r.part_z.at[at.z]
            return remote(own, own, r.gm, index, at.along_z(index - 1))
        own = r.bias_slot.at[at.z]
        return remote(own, own, r.gm, index, at.along_z(index - 4))

    def begin(self):
        r, at, steps = (self.refs, self.at, self.steps)
        stage = {
            "qkv": r.a.at[0:432], "proj": r.a.at[432:576], "ada": r.a.at[1728:2592],
            "up": r.a.at[576:1152], "down": r.a.at[1152:1728],
        }
        loads = {
            name: local(r.masters[name], stage[name], r.in_sems.at[index])
            for index, name in enumerate(stage)
        }
        ready = greet([self.everywhere(step) for step in range(1, 8 * LAYERS)])

        def fill(unit, source, count, offset, first=0):
            for j in range(count):
                value = source[pl.ds(first + j, SLAB, stride=count), :].astype(BF)
                where = offset + 128 * j
                if unit == 2:
                    rows = span(4 * SLAB * at.dp + offset, SLAB)
                    where = 128 * j
                else:
                    rows = span(SLAB * at.dp, SLAB)
                self.whole(unit)[rows, where : where + 128] = value

        loads["qkv"].wait()
        fill(0, stage["qkv"], 9, 0)
        loads["proj"].wait()
        fill(0, stage["proj"], 3, 3 * D)
        ready()
        self.launch(0)

        moment, interval = (r.start[at.grp], r.interval[at.grp])
        r.cond_t[...] = jnp.transpose(
            condition_rows([moment + s for s in range(ROLLOUT)], [interval] * ROLLOUT, r.lead)
        )
        own_cond = r.cond_t[span(SLAB * at.dp, SLAB), :]
        columns = [jnp.broadcast_to(own_cond[:, s : s + 1], (SLAB, 128)) for s in range(ROLLOUT)]
        loads["ada"].wait()
        for j in range(18):
            rows = stage["ada"][pl.ds(j, SLAB, stride=18), :].astype(BF).astype(F32)
            for s in range(ROLLOUT):
                r.part_own[18 * s + j : 18 * s + j + 1, :] = col_sum(rows * columns[s])
        r.part_own[36:40, :] = jnp.zeros((4, 128), F32)
        r.bias_own[...] = jnp.zeros((8, 128), F32)
        for i in range(6):
            size = 128 if i < 5 else 32
            r.bias_own[i : i + 1, 0:size] = r.bias_flat[pl.ds(128 * i, size)].reshape(1, size)
        lane = lax.broadcasted_iota(jnp.int32, (8, 128), 1)
        shift = lax.rem(32 * at.dp, 128)
        turned = pltpu.roll(r.bias_own[...].astype(BF).astype(F32), shift, axis=1)
        above = pltpu.roll(turned, 1, axis=0)
        r.bias_slot[at.z, at.core] = jnp.where(lane >= shift, turned, above)
        self.start(self.small(0))
        self.start(self.small(1))

        loads["up"].wait()
        fill(1, stage["up"], 12, 0)
        loads["down"].wait()
        for g in range(GROUPS):
            fill(2, stage["down"], 3, SLAB * g, 3 * SLAB * g)

        clear_sums(r)
        self.small(0).wait_recv()
        self.small(1).wait_recv()
        r.part_z[at.z] = r.part_own[...] + r.part_sib[...]
        for index in range(2, 8):
            self.start(self.small(index))
        self.forward_grp(0)
        self.launch(1)
        self.launch(2)

        for index in range(2, 8):
            self.small(index).wait_recv()
        total = r.part_z[0] + r.part_z[1] + r.part_z[2] + r.part_z[3]
        r.bias_full[...] = jnp.zeros_like(r.bias_full)
        for d in range(2 * LAYERS):
            first = 672 * d // 128
            r.bias_full[first : first + 7, :] += r.bias_slot[d // 2, d % 2, 0:7, :]
        counts = [r.counts[g].astype(F32) for g in range(GROUPS)]
        own_count = r.counts[at.grp].astype(F32)
        share = jnp.full((1, D), GROUPS * own_count) / jnp.full((1, D), sum(counts[1:], counts[0]))

        def put(row, value):
            r.rows[row : row + 1, :] = value

        def joined(first):
            return jnp.concatenate(
                [r.bias_full[first + j : first + j + 1, :] for j in range(3)], axis=1
            )

        for s in range(ROLLOUT):
            for row in range(6):
                first = 18 * s + 3 * row
                mod = jnp.concatenate([total[first + j : first + j + 1, :] for j in range(3)], axis=1)
                put(8 * s + row, mod + joined(24 + 3 * row))
            put(8 * s + 6, share)
            put(8 * s + 7, share)
        put(ROW_BQKV, joined(0))
        put(ROW_BQKV + 1, jnp.zeros((1, D), F32))
        put(ROW_BQKV + 2, joined(3))
        put(ROW_BPROJ, joined(6))
        for j in range(4):
            put(ROW_BUP + j, joined(9 + 3 * j))
        put(ROW_BDOWN, joined(21))
        r.rows[25:32, :] = jnp.zeros((7, D), F32)
        self.forward_sibling(0)
        self.finish_sibling(0)

    def after_first(self):
        self.forward_grp(1)

    def after_attend_pair(self, h):
        @pl.when(h == 0)
        def _():
            self.forward_grp(2)

        @pl.when(h == 1)
        def _():
            self.forward_sibling(1)

    def before_middle(self):
        self.forward_sibling(2)
        self.finish_sibling(1)
        self.finish_sibling(2)


    x_first = {3: True, 4: False}

    def columns(self, unit):
        return pl.ds(128 * unit, 128) if unit < 3 else slice(None)

    def got(self, unit, name):
        first = {"sib": 0, "piece": HALF, "grp": 0, "one": 0, "two": 8 * SLAB, "z": 12 * SLAB}[name]
        size = {"sib": HALF, "piece": 4 * SLAB, "grp": 12 * SLAB, "one": 8 * SLAB, "two": 4 * SLAB, "z": 3 * SLAB}[name]
        r, rows = (self.refs, slice(first, first + size))
        if unit < 3:
            return (r.att0 if name in ("sib", "piece") else r.act).at[rows, self.columns(unit)]
        if name in ("sib", "piece"):
            third = 0 if unit == 3 else 1
            return r.qkv1.at[rows, D * third : D * (third + 1)]
        return r.cot.at[rows] if unit == 3 else r.qkv1.at[rows, 2 * D : 3 * D]

    def half(self, unit, core):
        block = max(unit - 2, 0)
        return self.refs.blocks.at[block, span(HALF * core, HALF), self.columns(unit)]

    def parts(self, unit, part, count=1):
        return self.half(unit, self.at.core).at[span(4 * SLAB * part, 4 * SLAB * count), :]

    def sum_sibling(self, unit):
        src = self.half(unit, 1 - self.at.core)
        return remote(src, self.got(unit, "sib"), self.refs.rs, unit, self.at.sibling())

    def grp_peer(self, along_x):
        x, y = (self.at.grp % 2, self.at.grp // 2)
        grp = 2 * y + 1 - x if along_x else 2 * (1 - y) + x
        return (grp, self.at.dp)

    def stage_parts(self, unit, own):
        x, y = (self.at.grp % 2, self.at.grp // 2)
        if self.x_first[unit]:
            return [2 * j + (x if own else 1 - x) for j in range(2)]
        return [2 * (y if own else 1 - y) + j for j in range(2)]

    def sum_one(self, unit, j):
        src = self.parts(unit, self.stage_parts(unit, False)[j])
        dst = self.got(unit, "one").at[4 * SLAB * j : 4 * SLAB * (j + 1)]
        return remote(src, dst, self.refs.rx, (unit, j), self.grp_peer(self.x_first[unit]))

    def sum_two(self, unit):
        peer = self.grp_peer(not self.x_first[unit])
        return remote(self.parts(unit, peer[0]), self.got(unit, "two"), self.refs.rx, (unit, 2), peer)

    def sum_grp(self, unit, k):
        peer = self.at.along_grp(k)
        first = 4 * SLAB * (k - 1)
        dst = self.got(unit, "grp").at[first : first + 4 * SLAB]
        return remote(self.parts(unit, peer[0]), dst, self.refs.rx, (unit, k - 1), peer)

    def own_part(self, unit):
        return self.parts(unit, self.at.grp)

    def sum_z(self, unit, k):
        there = lax.rem(self.at.z + k, LAYERS)
        src = self.own_part(unit).at[span(SLAB * there, SLAB), :]
        dst = self.got(unit, "z").at[SLAB * (k - 1) : SLAB * k]
        return remote(src, dst, self.refs.rz, (unit, k - 1), self.at.along_z(k))

    def share_piece(self, unit, k):
        own = self.got(unit, "piece").at[span(SLAB * self.at.grp, SLAB), :]
        return remote(own, own, self.refs.ra, (unit, k - 1), self.at.along_grp(k))

    def add(self, mine, got, count):
        def step(i, carry):
            rows = span(SLAB * i, SLAB)
            mine[rows, :] = (mine[rows, :].astype(F32) + got[rows, :].astype(F32)).astype(BF)
            return carry

        lax.fori_loop(0, count, step, 0)

    def add_sibling(self, unit):
        self.sum_sibling(unit).wait_recv()
        self.add(self.half(unit, self.at.core), self.got(unit, "sib"), 16)
        if unit < 3:
            for k in self.steps:
                self.start(self.sum_grp(unit, k))
        else:
            for j in range(2):
                self.start(self.sum_one(unit, j))

    def add_grp(self, unit):
        for k in self.steps:
            self.sum_grp(unit, k).wait_recv()
        mine, got = (self.own_part(unit), self.got(unit, "grp"))

        def step(i, carry):
            rows = span(SLAB * i, SLAB)
            value = mine[rows, :].astype(F32)
            for k in self.steps:
                value = value + got[span(SLAB * (i + 4 * (k - 1)), SLAB), :].astype(F32)
            mine[rows, :] = value.astype(BF)
            return carry

        lax.fori_loop(0, 4, step, 0)
        for k in self.steps:
            self.start(self.sum_z(unit, k))

    def add_one(self, unit):
        for j in range(2):
            self.sum_one(unit, j).wait_recv()
            got = self.got(unit, "one").at[4 * SLAB * j : 4 * SLAB * (j + 1)]
            self.add(self.parts(unit, self.stage_parts(unit, True)[j]), got, 4)
        self.start(self.sum_two(unit))

    def add_two(self, unit):
        self.sum_two(unit).wait_recv()
        self.add(self.own_part(unit), self.got(unit, "two"), 4)
        for k in self.steps:
            self.start(self.sum_z(unit, k))

    def add_z(self, unit):
        for k in self.steps:
            self.sum_z(unit, k).wait_recv()
        value = self.own_part(unit)[span(SLAB * self.at.z, SLAB), :].astype(F32)
        for k in self.steps:
            value = value + self.got(unit, "z")[SLAB * (k - 1) : SLAB * k, :].astype(F32)
        value = value.astype(BF)
        self.got(unit, "piece")[span(SLAB * self.at.grp, SLAB), :] = value
        for k in self.steps:
            self.start(self.share_piece(unit, k))
        value = value.astype(F32)
        squares = col_sum(value * value)
        if unit < 3:
            return squares
        return squares[:, 0:128] + squares[:, 128:256] + squares[:, 256:384]

    def tell(self, sem):
        at = self.at
        for peer in (
            [at.sibling()]
            + [at.along_grp(k) for k in self.steps]
            + [at.along_z(k) for k in self.steps]
        ):
            pl.semaphore_signal(sem, inc=1, device_id=peer, device_id_type=MESH_ID)

    def before_join(self):
        self.tell(self.refs.turned_back)

    def amid_join(self):
        fill_blocks(self.refs)
        pl.semaphore_wait(self.refs.turned_back, 7)
        self.start(self.sum_sibling(3))
        self.start(self.sum_sibling(4))

    def after_join(self):
        r = self.refs
        self.tell(r.joined)
        self.add_sibling(3)
        self.add_sibling(4)
        fill_vec(r)
        self.start(self.small_sum(0))

    def amid_back_pair(self, h):
        r, at = (self.refs, self.at)

        @pl.when(h == 0)
        def _():
            self.small_sum(0).wait_recv()
            r.vec_z[at.z] = r.vec[...] + r.vec_sib[...]
            for index in self.steps:
                self.start(self.small_sum(index))

        @pl.when(h == 1)
        def _():
            self.add_one(3)
            self.add_one(4)
            self.add_sibling(0)
            for index in self.steps:
                self.small_sum(index).wait_recv()
            r.vec_g[at.grp] = r.vec_z[0] + r.vec_z[1] + r.vec_z[2] + r.vec_z[3]
            for index in self.steps:
                self.start(self.small_sum(3 + index))

        @pl.when(h == 2)
        def _():
            self.add_two(3)
            self.add_two(4)
            self.add_sibling(1)
            self.add_grp(0)

    def after_back_pair(self, h):
        r = self.refs
        fill_pair(r, h)

        @pl.when(h == 0)
        def _():
            pl.semaphore_wait(r.joined, 7)
            self.start(self.sum_sibling(0))

        @pl.when(h == 1)
        def _():
            self.start(self.sum_sibling(1))

        @pl.when(h == 2)
        def _():
            self.start(self.sum_sibling(2))

    def after_last_rows(self, i):
        @pl.when(i == 0)
        def _():
            self.add_sibling(2)

        @pl.when(i == 2)
        def _():
            self.add_grp(1)

    def small_sum(self, index):
        r, at = (self.refs, self.at)
        if index == 0:
            return remote(r.vec, r.vec_sib, r.rv, 0, at.sibling())
        if index < 4:
            own = r.vec_z.at[at.z]
            return remote(own, own, r.rv, index, at.along_z(index))
        own = r.vec_g.at[at.grp]
        return remote(own, own, r.rv, index, at.along_grp(index - 3))

    def across_dp(self, index):
        at = self.at
        if index == 0:
            return at.sibling()
        return at.along_z(index) if index < 4 else at.across(index - 3)

    def everywhere(self, step):
        device = lax.rem(2 * LAYERS * self.at.grp + self.at.dp + step, 8 * LAYERS)
        return (device // (2 * LAYERS), lax.rem(device, 2 * LAYERS))

    def square_sum(self, step):
        own = self.refs.squares.at[2 * LAYERS * self.at.grp + self.at.dp]
        return remote(own, own, self.refs.rq, step, self.everywhere(step))

    def late_sum(self, index):
        r, at = (self.refs, self.at)
        if index < 7:
            own = r.late_d.at[at.dp]
            return remote(own, own, r.rl, index, self.across_dp(index))
        own = r.late_g.at[at.grp]
        return remote(own, own, r.rl, index, at.along_grp(index - 6))

    def ada_square(self):
        r = self.refs
        left = r.cond[...]
        right = [
            r.vec_sum[g, VEC_STEP * (s + 1) : VEC_STEP * (s + 2), :]
            for g in range(GROUPS)
            for s in range(ROLLOUT)
        ]
        total = jnp.zeros((VEC_STEP, 128), F32)
        for step, weight in ((0, 1.0), (1, 2.0), (2, 2.0), (3, 2.0), (4, 1.0)):
            moved = left if step == 0 else pltpu.roll(left, step, axis=0)
            products = jnp.sum(left * moved, axis=1, keepdims=True) * weight
            for k in range(8):
                total = total + products[k : k + 1, :] * (right[k] * right[(k - step) % 8])
        return col_sum(total)

    def after_last(self):
        r, at, steps = (self.refs, self.at, self.steps)
        fill_late(r, r.late_d.at[at.dp])
        for index in range(7):
            self.start(self.late_sum(index))
        moments = [r.start[g] + s for g in range(GROUPS) for s in range(ROLLOUT)]
        intervals = [r.interval[g] for g in range(GROUPS) for s in range(ROLLOUT)]
        r.cond[...] = condition_rows(moments, intervals, r.lead)
        self.add_grp(2)
        for index in range(7):
            self.late_sum(index).wait_recv()
        total = r.late_d[0]
        for d in range(1, 2 * LAYERS):
            total = total + r.late_d[d]
        r.late_g[at.grp] = total
        for index in range(7, 10):
            self.start(self.late_sum(index))
        square = self.add_z(0) + self.add_z(3) + self.add_z(4) + self.add_z(1)
        square = square + self.add_z(2)
        own = 2 * LAYERS * at.grp + at.dp
        r.squares[own] = square
        for k in range(1, 8 * LAYERS):
            self.start(self.square_sum(k))

        for index in steps:
            self.small_sum(3 + index).wait_recv()
        for index in range(7, 10):
            self.late_sum(index).wait_recv()
        vec = r.vec_sum
        vec[...] = r.vec_g[...]
        for g in range(GROUPS):
            vec[g, 0:6, :] = r.late_g[g, 0:6, :]
            vec[g, VEC_STEP : VEC_STEP + 6, :] = r.late_g[g, 6:12, :]
        vec_sum = vec[0] + vec[1] + vec[2] + vec[3]
        r.bias_out[0:24, :] = vec_sum[0:24]
        r.bias_out[24:48, :] = vec_sum[24:48] + vec_sum[48:72]
        ada_square = self.ada_square()

        r.cond_t[...] = jnp.transpose(r.cond[...])
        own_cond = r.cond_t[span(SLAB * at.dp, SLAB), :]
        columns = [jnp.broadcast_to(own_cond[:, k : k + 1], (SLAB, 128)) for k in range(8)]
        ada = r.a.at[0 : 18 * SLAB]

        def ada_tile(j, carry):
            tile = jnp.zeros((SLAB, 128), F32)
            for k in range(8):
                row = vec[k // ROLLOUT, pl.ds(VEC_STEP * (k % ROLLOUT + 1) + j, 1), :]
                tile = tile + columns[k] * row
            ada[pl.ds(j, SLAB, stride=18), :] = tile
            return carry

        lax.fori_loop(0, 18, ada_tile, 0)
        for unit in range(5):
            for k in steps:
                self.share_piece(unit, k).wait_recv()
        whole = [r.att0.at[HALF : HALF + 4 * SLAB], self.got(3, "piece"), self.got(4, "piece")]
        puts = [local(ada, r.ada_far, r.in_sems.at[0])]
        puts += [
            local(whole[unit], r.pieces_far.at[unit], r.in_sems.at[1 + unit])
            for unit in range(UNITS)
        ]
        bias_sum = r.bias_out[...]
        total = col_sum(bias_sum * bias_sum) + ada_square
        for k in range(1, 8 * LAYERS):
            self.square_sum(k).wait_recv()
        for device in range(8 * LAYERS):
            total = total + r.squares[device]
        r.square_out[...] = jnp.broadcast_to(jnp.sum(total, axis=1, keepdims=True), (8, 128))
        for made in puts:
            made.wait()
        self.drain()

    def drain(self):
        for unit in range(UNITS):
            for k in self.steps:
                self.gather_z(unit, k).wait_send()
                for m in self.steps:
                    self.gather_grp(unit, k, m).wait_send()
            for k in range(4):
                self.gather_sibling(unit, k).wait_send()
        for unit in range(5):
            self.sum_sibling(unit).wait_send()
            if unit < 3:
                for k in self.steps:
                    self.sum_grp(unit, k).wait_send()
            else:
                self.sum_one(unit, 0).wait_send()
                self.sum_one(unit, 1).wait_send()
                self.sum_two(unit).wait_send()
            for k in self.steps:
                self.sum_z(unit, k).wait_send()
                self.share_piece(unit, k).wait_send()
        for index in range(8):
            self.small(index).wait_send()
        for index in range(7):
            self.small_sum(index).wait_send()
        for index in range(10):
            self.late_sum(index).wait_send()
        for step in range(1, 8 * LAYERS):
            self.square_sum(step).wait_send()


correction = 1.0 - 0.5**ADAM_STEP
grad_limit = math.sqrt(NPARAM)


def adam(master, first, second, clipped, decay):
    first_new = 0.5 * first + 0.5 * clipped
    second_new = 0.5 * second + 0.5 * clipped * clipped
    update = first_new / correction / (jnp.sqrt(second_new / correction) + adam_eps)
    return (master - learn_rate * (update + decay * master), first_new, second_new)


CHUNK = 48
STATE = ("qkv", "proj", "up", "down", "ada")


def finish_kernel(names, *refs):
    r = Refs(names, refs)
    loads = {
        "pieces": local(r.pieces_far, r.pieces, r.in_sems.at[0]),
        "grad": local(r.grad_ada_far, r.grad_ada, r.in_sems.at[16]),
    }
    for index, name in enumerate(STATE):
        for kind in range(3):
            loads[name, kind] = local(
                getattr(r, f"{name}_in{kind}"), getattr(r, f"{name}_{kind}"),
                r.in_sems.at[1 + 3 * index + kind],
            )
    streams = [
        local(getattr(r, name + "_in"), getattr(r, name), r.stream_sems.at[index])
        for index, name in enumerate(("y", "dx"))
    ]
    norm = jnp.sqrt(r.square[...])
    r.norm[0, 0] = jnp.max(norm)
    clip = grad_limit / jnp.maximum(norm, grad_limit)
    row_clip = clip[0:1, :]

    loads["pieces"].wait()
    piece = r.pieces

    def unpack(name):
        for j in range(3):
            columns = slice(128 * j, 128 * j + 128)
            if name == "proj":
                r.grad_proj[pl.ds(j, SLAB, stride=3), :] = piece[0, 3 * SLAB :, columns].astype(F32)
            for g in range(GROUPS):
                rows = slice(SLAB * g, SLAB * (g + 1))
                if name == "qkv" and g < 3:
                    r.grad_qkv[pl.ds(3 * g + j, SLAB, stride=9), :] = piece[0, rows, columns].astype(F32)
                if name == "up":
                    r.grad_up[pl.ds(3 * g + j, SLAB, stride=12), :] = piece[1, rows, columns].astype(F32)
                if name == "down":
                    r.grad_down[pl.ds(3 * SLAB * g + j, SLAB, stride=3), :] = piece[2, rows, columns].astype(F32)

    stores = []
    for turn, name in enumerate(("qkv", "up", "down", "ada", "proj")):
        index = STATE.index(name)
        for kind in range(3):
            loads[name, kind].wait()
        if name == "ada":
            loads["grad"].wait()
        unpack(name)
        grad, low = (getattr(r, "grad_" + name), getattr(r, name + "_low"))
        state = [getattr(r, f"{name}_{kind}") for kind in range(3)]

        def chunk(i, carry):
            rows = pl.ds(pl.multiple_of(CHUNK * i, 16), CHUNK)
            new, first_new, second_new = adam(
                *(ref[rows, :] for ref in state), grad[rows, :] * row_clip, 0.1
            )
            for ref, value in zip(state, (new, first_new, second_new)):
                ref[rows, :] = value
            low[rows, :] = new.astype(BF)
            return carry

        lax.fori_loop(0, grad.shape[0] // CHUNK, chunk, 0)
        for kind, ref in enumerate((*state, low)):
            stores.append(local(ref, getattr(r, f"{name}_out{kind}"), r.out_sems.at[4 * index + kind]))
        if turn < 2:
            name = ("y", "dx")[turn]
            streams[turn].wait()
            stores.append(local(getattr(r, name), getattr(r, name + "_out"), r.stream_sems.at[turn]))
    owner = lax.axis_index("dp")
    lane = lax.broadcasted_iota(jnp.int32, (1, 128), 1)
    first = 672 * owner // 128
    shift = lax.rem(32 * owner, 128)
    back = lax.rem(128 - shift, 128)
    for i in range(6):
        size = 128 if i < 5 else 32
        here = pltpu.roll(r.bias_sum[pl.ds(first + i, 1), :], back, axis=1)
        there = pltpu.roll(r.bias_sum[pl.ds(first + i + 1, 1), :], back, axis=1)
        grad = jnp.where(lane < 128 - shift, here, there) * row_clip
        place = pl.ds(128 * i, size)
        state = [getattr(r, f"bias_in{kind}")[place].reshape(1, size) for kind in range(3)]
        new, first_new, second_new = adam(*state, grad[:, :size], 0.0)
        r.bias_out0[place] = new.reshape(size)
        r.bias_out1[place] = first_new.reshape(size)
        r.bias_out2[place] = second_new.reshape(size)
        r.bias_out3[place] = new.reshape(size).astype(BF)

    for made in stores:
        made.wait()


def finish(y, dx, pieces, ada, bias_sum, square, masters, firsts, seconds):
    vmem, hbm, dma = (pltpu.VMEM, pl.ANY, pltpu.SemaphoreType.DMA)
    state = list(zip(masters, firsts, seconds))
    shapes = {name: (arrays[0].size // 128, 128) for name, arrays in zip(STATE, state)}
    ins = [
        ("square", square, vmem), ("bias_sum", bias_sum, vmem), ("pieces_far", pieces, hbm),
        ("grad_ada_far", ada, hbm), ("y_in", y, hbm), ("dx_in", dx, hbm),
        *[(f"bias_in{kind}", array, vmem) for kind, array in enumerate(state[5])],
        *[
            (f"{name}_in{kind}", array.reshape(-1, 128), hbm)
            for name, arrays in zip(STATE, state)
            for kind, array in enumerate(arrays)
        ],
    ]
    outs = [("norm", (1, 1), F32, pltpu.SMEM), ("y_out", y.shape, F32, hbm), ("dx_out", dx.shape, F32, hbm)]
    for kind in range(4):
        dtype = F32 if kind < 3 else BF
        outs += [(f"{name}_out{kind}", shapes[name], dtype, hbm) for name in STATE]
        outs.append((f"bias_out{kind}", state[5][0].shape, dtype, vmem))
    scratch = [
        ("pieces", vmem(pieces.shape, BF)), ("y", vmem(y.shape, F32)), ("dx", vmem(dx.shape, F32)),
        *[(f"{name}_{kind}", vmem(shapes[name], F32)) for name in STATE for kind in range(3)],
        *[(f"{name}_low", vmem(shapes[name], BF)) for name in STATE],
        *[(f"grad_{name}", vmem(shapes[name], F32)) for name in STATE],
        ("in_sems", dma((17,))), ("stream_sems", dma((2,))), ("out_sems", dma((20,))),
    ]
    names = [item[0] for item in (*ins, *outs, *scratch)]
    norm, y, dx, *rest = pl.pallas_call(
        functools.partial(finish_kernel, names),
        in_specs=[pl.BlockSpec(memory_space=space) for *_, space in ins],
        out_specs=[pl.BlockSpec(memory_space=space) for *_, space in outs],
        out_shape=[jax.ShapeDtypeStruct(shape, kind) for _, shape, kind, _ in outs],
        scratch_shapes=[kind for _, kind in scratch],
        name="finish",
    )(*(array for _, array, _ in ins))
    return (y, dx, norm.reshape(()), *(array.reshape(-1) for array in rest))


MASTERS = ("qkv", "proj", "up", "down", "ada")


def block_kernel(names, hooked, *refs):
    r = Refs(names, refs)
    if hooked is Together:
        r.masters = {name: getattr(r, "far_" + name) for name in MASTERS}
        for name in ("gz", "gx", "gs", "gm", "rs", "rx", "rz", "ra", "rv", "rq", "rl"):
            setattr(r, name, (getattr(r, name + "_out"), getattr(r, name + "_in")))
    hooks = hooked(r)
    length = r.x_far.shape[0]
    pairs = HEADS // 2
    get_x = local(r.x_far, r.x, r.out_sems.at[3])
    get_cot = local(r.cot_far, r.cot, r.out_sems.at[2])

    def over_rows(body, after=None, size=ROWS):
        def step(i, carry):
            body(pl.ds(pl.multiple_of(i * size, size), size))
            if after is not None:
                after(i)
            return carry

        lax.fori_loop(0, length // size, step, 0)

    def columns(h, offset=0):
        return pl.ds(pl.multiple_of(offset + 128 * h, 128), 128)

    def over_pairs(body):
        def step(h, carry):
            body(h)
            return carry

        lax.fori_loop(0, pairs, step, 0)

    def act_refs(rows):
        first = rows.start
        return [
            r.act.at[pl.ds(pl.multiple_of(length * part + first, ROWS), rows.size)]
            for part in range(4)
        ]

    def a_refs(rows):
        first = rows.start
        return [
            r.a.at[pl.ds(pl.multiple_of(length * part + first, ROWS), rows.size)]
            for part in range(3)
        ]

    def save(step, h):
        slot = lax.rem(h, 2)
        return pltpu.make_async_copy(
            r.p.at[slot], r.p_far.at[step, pl.ds(2 * h, 2)], r.p_sems.at[slot]
        )

    def fetch(step, h):
        slot = lax.rem(h, 2)
        return pltpu.make_async_copy(
            r.p_far.at[step, pl.ds(2 * h, 2)], r.p.at[slot], r.p_sems.at[slot]
        )

    def attend(step, qkv, att, after):
        def body(h):
            @pl.when(h >= 2)
            def _():
                save(step, h - 2).wait()

            attend_pair(
                qkv[:, columns(h)], qkv.at[:, columns(h, D)], qkv[:, columns(h, 2 * D)],
                att.at[:, columns(h)], r.p.at[lax.rem(h, 2)], r.turned,
            )
            save(step, h).start()
            after(h)

        over_pairs(body)

    def finish_saves(step):
        for h in range(pairs - 2, pairs):
            save(step, h).wait()

    def attend_back(step, qkv, between, after):
        def body(h):
            fetch(step, h).wait()
            attend_back_pair(
                qkv[:, columns(h)], qkv[:, columns(h, D)], qkv.at[:, columns(h, 2 * D)],
                r.datt[:, columns(h)], r.p.at[lax.rem(h, 2)],
                r.dqkv.at[:, columns(h)], r.dqkv.at[:, columns(h, D)],
                r.dqkv.at[:, columns(h, 2 * D)], r.turned,
                None if between is None else lambda: between(h),
            )

            @pl.when(h + 2 < pairs)
            def _():
                fetch(step, h + 2).start()

            after(h)

        over_pairs(body)

    nothing = lambda h: None
    hooks.begin()

    def first(rows):
        r.qkv0[rows, :] = first_rows(r.x[rows, :], r.rows, r.wa)

    get_x.wait()
    over_rows(first, size=2 * ROWS)
    hooks.after_first()
    attend(0, r.qkv0, r.att0, hooks.after_attend_pair)
    hooks.before_middle()

    def middle(rows):
        middle_rows(
            r.x.at[rows], r.att0.at[rows], r.rows, r.wa, r.wup, r.wdown,
            a_refs(rows), r.gp.at[rows], act_refs(rows), r.f.at[rows], r.x1.at[rows],
            r.qkv1.at[rows],
        )

    over_rows(middle, size=2 * ROWS)
    finish_saves(0)
    attend(1, r.qkv1, r.att1, nothing)

    def turn(rows):
        turn_rows(
            r.x1.at[rows], r.att1.at[rows], r.cot.at[rows], r.rows, r.wa, r.wup,
            r.wdown, r.y.at[rows], r.dmid.at[rows], r.datt.at[rows], r.gdown, r.gup, r.gproj,
            r.wide, r.narrow1,
        )

    finish_saves(1)
    for h in range(2):
        fetch(1, h).start()
    get_cot.wait()
    over_rows(turn, size=2 * ROWS)
    put_y = local(r.y, r.y_far, r.out_sems.at[0])
    attend_back(1, r.qkv1, None, nothing)
    for h in range(2):
        fetch(0, h).start()

    def join(rows):
        join_rows(
            r.dqkv.at[rows], r.x1.at[rows], r.x.at[rows], a_refs(rows), r.gp.at[rows],
            act_refs(rows), r.f.at[rows], r.rows, r.wa, r.wdown, r.att1.at[rows],
            r.dmid.at[rows], r.gqkv, r.gdown, r.gup, r.wide, r.narrow1, r.narrow0, r.bias,
        )

    def join_middle(rows):
        join_middle_rows(
            r.x.at[rows], a_refs(rows), act_refs(rows), r.att0.at[rows], r.rows, r.wa, r.wup,
            r.dmid.at[rows], r.datt.at[rows], r.gproj, r.narrow0,
        )

    hooks.before_join()
    over_rows(join)
    hooks.amid_join()
    over_rows(join_middle, size=2 * ROWS)
    hooks.after_join()
    attend_back(0, r.qkv0, hooks.amid_back_pair, hooks.after_back_pair)

    def last(rows):
        r.dmid[rows, :] = qkv_back(
            mod_reader(r.rows, 0), r.x[rows, :].astype(F32), r.dmid[rows, :],
            r.dqkv[rows, :], r.wa, r.narrow0, r.bias,
        )

    over_rows(last, hooks.after_last_rows)
    put_dx = local(r.dmid, r.dx_far, r.out_sems.at[1])
    hooks.after_last()
    put_y.wait()
    put_dx.wait()


def block_call(hooked, inputs, cotangent, extra_in, extra_out, extra_scratch, params):
    length = inputs.shape[0]
    vmem, hbm, dma = (pltpu.VMEM, pl.ANY, pltpu.SemaphoreType.DMA)
    weights = (ROLLOUT, HEADS, length, length)
    ins = [("x_far", inputs, hbm), ("cot_far", cotangent, hbm), *extra_in]
    outs = [
        ("y_far", (length, D), F32, hbm), ("dx_far", (length, D), F32, hbm),
        ("p_far", weights, BF, hbm), *extra_out,
    ]
    scratch = [
        ("wa", vmem((D, FF), BF)), ("wup", vmem((D, FF), BF)), ("wdown", vmem((FF, D), BF)),
        ("x", vmem((length, D), BF)), ("cot", vmem((length, D), BF)), ("qkv0", vmem((length, 3 * D), BF)),
        ("qkv1", vmem((length, 3 * D), BF)), ("p", vmem((2, 2, length, length), BF)),
        ("att0", vmem((length, D), BF)), ("att1", vmem((length, D), BF)),
        *[(name, vmem((length, D), F32)) for name in ("f", "x1", "dmid", "y")], ("a", vmem((3 * length, 128), F32)),
        ("gp", vmem((length, FF), F32)), ("act", vmem((4 * length, D), BF)),
        ("datt", vmem((length, D), BF)), ("dqkv", vmem((length, 3 * D), BF)),
        ("gqkv", vmem((D, 3 * D), F32)), ("gproj", vmem((D, D), F32)),
        ("gup", vmem((D, FF), F32)), ("gdown", vmem((FF, D), F32)),
        ("turned", vmem((2, 128, length), BF)), ("wide", vmem((8, FF), F32)),
        ("narrow0", vmem((8, D), F32)), ("narrow1", vmem((8, D), F32)),
        ("bias", vmem((8, 3 * D), F32)), ("blocks", vmem((UNITS, 2 * HALF, PART), BF)),
        ("rows", vmem((32, D), F32)), ("vec", vmem((VEC, 128), F32)), ("late", vmem((16, 128), F32)),
        ("in_sems", dma((5,))), ("p_sems", dma((2,))), ("out_sems", dma((4,))),
        *extra_scratch,
    ]
    names = [item[0] for item in (*ins, *outs, *scratch)]
    return pl.pallas_call(
        functools.partial(block_kernel, names, hooked),
        in_specs=[pl.BlockSpec(memory_space=space) for _, _, space in ins],
        out_specs=[pl.BlockSpec(memory_space=space) for *_, space in outs],
        out_shape=[jax.ShapeDtypeStruct(shape, kind) for _, shape, kind, _ in outs],
        scratch_shapes=[kind for _, kind in scratch],
        compiler_params=pltpu.CompilerParams(vmem_limit_bytes=67043328, **params),
        name="block",
    )(*(array for _, array, _ in ins))


def block_alone(inputs, cotangent, rows, wa, wup, wdown):
    hbm = pl.ANY
    y, dx, _, blocks, vec = block_call(
        Alone, inputs, cotangent,
        [("rows_far", rows, hbm), ("wa_far", wa, hbm), ("wup_far", wup, hbm), ("wdown_far", wdown, hbm)],
        [("blocks_far", (UNITS, 2 * HALF, PART), BF, hbm), ("vec_far", (VEC, 128), F32, hbm)],
        [], {},
    )
    return (y, dx, blocks, vec)


def block_together(inputs, cotangent, start, interval, counts, lead, masters):
    vmem, hbm, smem, dma = (pltpu.VMEM, pl.ANY, pltpu.SMEM, pltpu.SemaphoreType.DMA)
    qkv, proj, up, down, ada, bias = masters
    far = [
        ("far_" + name, array.reshape(-1, 128), hbm)
        for name, array in zip(MASTERS, (qkv, proj, up, down, ada))
    ]
    pairs_of = [
        ("gz", (UNITS, 3)), ("gx", (UNITS, 3, 3)), ("gs", (UNITS, 4)), ("gm", (8,)),
        ("rs", (5,)), ("rx", (5, 3)), ("rz", (5, 3)), ("ra", (5, 3)),
        ("rv", (7,)), ("rq", (8 * LAYERS,)), ("rl", (10,)),
    ]
    y, dx, _, pieces, ada_grad, bias_sum, square = block_call(
        Together, inputs, cotangent,
        [("start", start, smem), ("interval", interval, smem), ("counts", counts, smem),
         ("lead", lead, vmem), ("bias_flat", bias, vmem), *far],
        [("pieces_far", (UNITS, 4 * SLAB, PART), BF, hbm), ("ada_far", (18 * SLAB, 128), F32, hbm),
         ("bias_out", (48, 128), F32, vmem), ("square_out", (8, 128), F32, vmem)],
        [("cond_t", vmem((D, 8), F32)), ("part_own", vmem((40, 128), F32)),
         ("part_sib", vmem((40, 128), F32)), ("part_z", vmem((LAYERS, 40, 128), F32)),
         ("bias_own", vmem((8, 128), F32)), ("bias_slot", vmem((LAYERS, 2, 8, 128), F32)), ("bias_full", vmem((48, 128), F32)),
         ("vec_sib", vmem((VEC, 128), F32)), ("vec_z", vmem((LAYERS, VEC, 128), F32)),
         ("vec_g", vmem((GROUPS, VEC, 128), F32)), ("late_d", vmem((8, 16, 128), F32)),
         ("vec_sum", vmem((GROUPS, VEC, 128), F32)), ("cond", vmem((8, D), F32)),
         ("late_g", vmem((GROUPS, 16, 128), F32)), ("squares", vmem((8 * LAYERS, 1, 128), F32)), ("joined", pltpu.SemaphoreType.REGULAR), ("turned_back", pltpu.SemaphoreType.REGULAR),
         *[(name + end, dma(shape)) for name, shape in pairs_of for end in ("_out", "_in")]],
        dict(collective_id=0, has_side_effects=True),
    )
    return (y, dx, pieces, ada_grad, bias_sum, square)


def step_embedding(moment):
    half_width = D // 2
    freqs = jnp.exp(-math.log(10000.0) * jnp.arange(half_width, dtype=F32) / half_width)
    angles = moment[:, None] * freqs[None, :]
    return jnp.concatenate([jnp.sin(angles), jnp.cos(angles)], axis=1)


def all_conditions(group_interval, rollout_start, lead_table):
    chosen = group_interval[:, None] == jnp.arange(INTERVALS)[None, :]
    lead_rows = jnp.sum(jnp.where(chosen[:, :, None], lead_table[None], 0.0), axis=1)
    start = rollout_start.astype(F32)
    rows = [lead_rows + step_embedding(start + offset) for offset in range(ROLLOUT)]
    return jax.nn.silu(jnp.stack(rows, axis=1)).astype(BF)


def plain_gather(group_interval, counts, rollout_start, lead_table, masters):
    low = [master.astype(BF) for master in masters]
    owner = lax.axis_index("dp")
    group_index = lax.axis_index("grp")
    own_rows = D // lax.axis_size("dp")
    counts = counts.astype(F32)
    share = lax.axis_size("grp") * counts / jnp.sum(counts)
    share = lax.dynamic_index_in_dim(share, group_index, keepdims=False)
    conditions = all_conditions(group_interval, rollout_start, lead_table)
    owner_columns = lax.dynamic_slice_in_dim(conditions, owner * own_rows, own_rows, axis=2)
    own_condition = lax.dynamic_index_in_dim(owner_columns, group_index, keepdims=False)
    modulation = lax.psum(dot(own_condition, low[4].reshape(own_rows, 6 * D)), "dp")
    qkv, proj, up, down, bias = [
        lax.all_gather(low[index], "dp", axis=0, tiled=True) for index in (0, 1, 2, 3, 5)
    ]
    bias = bias.astype(F32)
    modulation = modulation + bias[4 * D + FF :][None]
    share_rows = jnp.broadcast_to(share, (ROLLOUT, 2, D))
    mods = jnp.concatenate([modulation.reshape(ROLLOUT, 6, D), share_rows], axis=1).reshape(-1, D)
    rows = jnp.concatenate(
        [mods, bias[:D][None], jnp.zeros((1, D), F32), bias[D : 4 * D + FF].reshape(-1, D),
         jnp.zeros((7, D), F32)]
    )
    wa = jnp.concatenate([qkv.reshape(D, 3 * D), proj.reshape(D, D)], axis=1)
    return (wa, up.reshape(D, FF), down.reshape(FF, D), rows, owner_columns)


def plain_update(owner_columns, vec, blocks, masters, firsts, seconds):
    owner = lax.axis_index("dp")
    vec = vec.reshape(-1)
    split = 4 * D + FF
    dmod = vec[split:].reshape(ROLLOUT, VEC_STEP * 128)[:, : 6 * D]
    dmod_all = lax.all_gather(lax.psum(dmod, "dp"), "grp")
    bias_sum = lax.psum(vec[:split], ("grp", "dp"))
    bias_sum = jnp.concatenate([bias_sum, jnp.sum(dmod_all, axis=(0, 1))])
    bias_rows = masters[5].shape[0]
    bias_grad = lax.dynamic_slice_in_dim(bias_sum, owner * bias_rows, bias_rows)
    ada_grad = jnp.einsum(
        "gsr,gsc->rc", owner_columns.astype(F32), dmod_all, precision=lax.Precision.HIGHEST
    )
    blocks = blocks.reshape(UNITS, 2, 4, LAYERS, SLAB, PART)
    flat_a, flat_up = [blocks[u].transpose(2, 0, 3, 1, 4).reshape(D, FF) for u in (0, 1)]
    flat_down = blocks[2].transpose(2, 0, 1, 3, 4)
    flat = [flat_a[:, : 3 * D], flat_a[:, 3 * D :], flat_up, flat_down]
    shares = []
    for grad in flat:
        summed = lax.psum(grad.reshape(-1), "grp").astype(F32)
        shares.append(lax.psum_scatter(summed, "dp", scatter_dimension=0, tiled=True))
    shares = shares + [ada_grad.reshape(-1), bias_grad]
    local_square = sum((jnp.sum(piece * piece) for piece in shares))
    grad_norm = jnp.sqrt(lax.psum(local_square, "dp"))
    clip = grad_limit / jnp.maximum(grad_norm, grad_limit)
    decays = [0.1, 0.1, 0.1, 0.1, 0.1, 0.0]
    results = [
        adam(master, first, second, grad * clip, decay)
        for master, first, second, grad, decay in zip(masters, firsts, seconds, shares, decays)
    ]
    news, first_news, second_news = zip(*results)
    return (grad_norm, *news, *first_news, *second_news, *(new.astype(BF) for new in news))


def per_device(
    inputs,
    cotangent,
    group_interval,
    sample_counts,
    rollout_start,
    lead_table,
    *state,
):
    masters, firsts, seconds = (state[0:6], state[6:12], state[12:18])
    fits = (
        lax.axis_size("dp") == 2 * LAYERS
        and lax.axis_size("grp") == GROUPS
        and inputs.shape[0] == 1024
    )
    if not fits:
        wa, wup, wdown, rows, owner_columns = plain_gather(
            group_interval, sample_counts, rollout_start, lead_table, masters
        )
        result, input_grad, blocks, vec = block_alone(inputs, cotangent, rows, wa, wup, wdown)
        rest = plain_update(owner_columns, vec, blocks, masters, firsts, seconds)
        return (result, input_grad, *rest)
    result, input_grad, pieces, ada_grad, bias_sum, square = block_together(
        inputs, cotangent, rollout_start, group_interval, sample_counts, lead_table, masters
    )
    return finish(
        result, input_grad, pieces, ada_grad, bias_sum, square, masters, firsts, seconds
    )


def solution(mesh):
    rows = P(("grp", "dp"), None)
    return jax.shard_map(
        per_device,
        mesh=mesh,
        in_specs=(rows, rows, P(), P(), P(), P(), *[P("dp")] * 18),
        out_specs=(rows, rows, P(), *[P("dp")] * 24),
        check_vma=False,
    )
```
